32 devices in a mesh: dp: 4 (over y, x), seq: 8 (over z, core).
Axes of the slice: x: 2, y: 2, z: 4, core: 2. Of those that a mesh axis runs over, the one named last changes fastest.
Arguments:
- tokens: bfloat16 [4, 1024, 1024], P('dp', 'seq'), may hold values from -6 to 6
- lengths: int32 [4], P('dp'), may hold values from 256 to 1024, as said below
- cotangent: bfloat16 [4, 1024, 1024], P('dp', 'seq'), may hold values from -6 to 6
- norm_gains: float32 [2, 1024], replicated, may hold values from 0.5 to 1.5
- head_gain: float32 [256], replicated, may hold values from 0.5 to 1.5
- head_params: float32 [3, 8], replicated, may hold values from -10 to 1
- qkv_weight: bfloat16 [1024, 4096], P('dp', 'seq'), may hold values from -0.1875 to 0.1875
- gate_weight: bfloat16 [1024, 2048], P('dp', 'seq'), may hold values from -0.1875 to 0.1875
- head_weight: bfloat16 [1024, 16], replicated, may hold values from -0.1875 to 0.1875
- conv_weight: bfloat16 [4096, 4], replicated, may hold values from -3 to 3
- out_weight: bfloat16 [2048, 1024], P('dp', 'seq'), may hold values from -0.1875 to 0.1875
- ffn_in: bfloat16 [1024, 5632], P('dp', 'seq'), may hold values from -0.1875 to 0.1875
- ffn_out: bfloat16 [2816, 1024], P('dp', 'seq'), may hold values from -0.109375 to 0.109375
Outputs:
- output: bfloat16 [4, 1024, 1024], P('dp', 'seq')
- input_grad: bfloat16 [4, 1024, 1024], P('dp', 'seq')
- norm_gains_grad: float32 [2, 1024], replicated
- head_gain_grad: float32 [256], replicated
- head_params_grad: float32 [3, 8], replicated
- qkv_weight_grad: float32 [1024, 4096], P('dp', 'seq')
- gate_weight_grad: float32 [1024, 2048], P('dp', 'seq')
- head_weight_grad: float32 [1024, 16], replicated
- conv_weight_grad: float32 [4096, 4], replicated
- out_weight_grad: float32 [2048, 1024], P('dp', 'seq')
- ffn_in_grad: float32 [1024, 5632], P('dp', 'seq')
- ffn_out_grad: float32 [2816, 1024], P('dp', 'seq')
The draws below stay inside these ranges and needn't reach their ends.
Inputs may be any that keep to these rules, and one draw needn't show every extreme that they name: `lengths`: the first sequence is full: its length is 1024.
All inputs are finite; a program needn't handle non-finite values.
Results may differ from the reference program's by a relative error of at most 0.02.
Values may be sent and summed in bfloat16 or wider, within the bound.
A program may use at most 256 MiB of HBM per device.

```python
import jax
import jax.numpy as jnp
from jax import lax

D = 1024
H = 8
DK = 128
DV = 256
FF = 2816
KCONV = 4
TILE = 64
BATCH = 4
LEN = 1024
CONVF = 4096


def draw_lengths(key, part):
    drawn = jax.random.randint(key, (BATCH,), LEN // 4, LEN + 1)
    return drawn.at[0].set(LEN).astype(jnp.int32)


def draw_head_params(key, part):
    key_rate = jax.random.fold_in(key, 11)
    key_shift = jax.random.fold_in(key, 12)
    key_erase = jax.random.fold_in(key, 13)
    log_rate = jax.random.uniform(key_rate, (H,), jnp.float32, -2.0, 0.0)
    shift_bias = jax.random.uniform(key_shift, (H,), jnp.float32, -8.0, -3.0)
    erase_bias = jax.random.uniform(key_erase, (H,), jnp.float32, -5.0, 1.0)
    return jnp.stack([log_rate, shift_bias, erase_bias])


def block_levels(key, extent, shards, least, largest):
    def one(position, parts):
        steps = jax.random.uniform(jax.random.fold_in(jax.random.fold_in(key, 6), position), (parts,), jnp.float32, least / len(shards), largest / len(shards))
        return jnp.repeat(jnp.exp(steps), extent[position] // parts).reshape((-1,) + (1,) * (len(extent) - position - 1))

    level = one(*shards[0])
    for cut in shards[1:]:
        level = level * one(*cut)
    return level


def centred(own_key, shape, scale, reach, pieces=(), kind=jnp.bfloat16):
    values = scale * jax.random.normal(own_key, shape, jnp.float32)
    if pieces:
        values = values * block_levels(own_key, shape, pieces, -0.22, 0.18)
    return jnp.clip(values, -reach, reach).astype(kind)


def setup_inputs(seed: int = 0) -> dict:
    key_list = jax.random.split(jax.random.key(seed), 14)
    return {
        "tokens": centred(key_list[0], (BATCH, LEN, D), 1.0, 6.0, ((0, 4), (1, 8))),
        "lengths": draw_lengths(jax.random.fold_in(key_list[13], 71), 0),
        "cotangent": centred(key_list[2], (BATCH, LEN, D), 1.0, 6.0, ((0, 4), (1, 8))),
        "norm_gains": jnp.clip(1.0 + 0.1 * jax.random.normal(key_list[3], (2, D), jnp.float32), 0.5, 1.5),
        "head_gain": jnp.clip(1.0 + 0.1 * jax.random.normal(key_list[4], (DV,), jnp.float32), 0.5, 1.5),
        "head_params": draw_head_params(jax.random.fold_in(key_list[13], 71), 0),
        "qkv_weight": centred(key_list[6], (D, CONVF), D ** -0.5, 0.1875, ((0, 4), (1, 8))),
        "gate_weight": centred(key_list[7], (D, H * DV), D ** -0.5, 0.1875, ((0, 4), (1, 8))),
        "head_weight": centred(key_list[8], (D, 2 * H), D ** -0.5, 0.1875),
        "conv_weight": centred(key_list[9], (CONVF, KCONV), KCONV ** -0.5, 3.0),
        "out_weight": centred(key_list[10], (H * DV, D), (H * DV // 2) ** -0.5, 0.1875, ((0, 4), (1, 8))),
        "ffn_in": centred(key_list[11], (D, 2 * FF), D ** -0.5, 0.1875, ((0, 4), (1, 8))),
        "ffn_out": centred(key_list[12], (FF, D), FF ** -0.5, 0.109375, ((0, 4), (1, 8))),
    }


HIGHEST = lax.Precision.HIGHEST
epsilon = 1e-06

@jax.custom_vjp
def low(v):
    return lax.optimization_barrier(v.astype(jnp.bfloat16)).astype(jnp.float32)

@jax.custom_vjp
def low_back(v):
    return v

def low_keep(v):
    return (low(v), None)

def low_pass(kept, grad):
    return (grad,)

def back_keep(v):
    return (v, None)

def back_low(kept, grad):
    return (low(grad),)
low.defvjp(low_keep, low_pass)
low_back.defvjp(back_keep, back_low)

def rms_scale(values, gain_row):
    return values * lax.rsqrt(lax.optimization_barrier(jnp.mean(values * values, axis=-1, keepdims=True)) + epsilon) * gain_row

def unit_rows(values):
    return values * lax.rsqrt(lax.optimization_barrier(jnp.sum(values * values, axis=-1, keepdims=True)) + epsilon)

def block_step(state_now, query_vecs, key_vecs, value_vecs, log_decay, erase_rate):
    length = query_vecs.shape[1]
    cumulative = jnp.cumsum(log_decay, axis=1)
    row_index = jnp.arange(length)[:, None]
    col_index = jnp.arange(length)[None, :]
    strict = col_index < row_index
    within = col_index <= row_index
    spread = cumulative[:, :, None] - cumulative[:, None, :]
    lower_decay = jnp.where(strict, jnp.exp(jnp.where(strict, spread, 0.0)), 0.0)
    causal = jnp.where(within, jnp.exp(jnp.where(within, spread, 0.0)), 0.0)
    key_gram = jnp.einsum('htk,hsk->hts', key_vecs, key_vecs, precision=HIGHEST)
    query_gram = jnp.einsum('htk,hsk->hts', query_vecs, key_vecs, precision=HIGHEST)
    negated = -(erase_rate[:, :, None] * key_gram * lower_decay)
    identity = jnp.eye(length, dtype=jnp.float32)
    inverse = identity + negated
    powered = negated
    for level_index in range(length.bit_length() - 2):
        powered = jnp.einsum('hts,hsr->htr', powered, powered, precision=HIGHEST)
        inverse = jnp.einsum('hts,hsr->htr', inverse, identity + powered, precision=HIGHEST)
    shrink = jnp.exp(cumulative)
    recalled = jnp.einsum('htk,hkw->htw', key_vecs, state_now, precision=HIGHEST)
    target = erase_rate[:, :, None] * value_vecs - (erase_rate * shrink)[:, :, None] * recalled
    updates = jnp.einsum('hts,hsw->htw', inverse, target, precision=HIGHEST)
    read_out = shrink[:, :, None] * jnp.einsum('htk,hkw->htw', query_vecs, state_now, precision=HIGHEST)
    read_out = read_out + jnp.einsum('hts,hsw->htw', query_gram * causal, updates, precision=HIGHEST)
    remain = jnp.exp(cumulative[:, -1:] - cumulative)
    state_next = jnp.exp(cumulative[:, -1])[:, None, None] * state_now
    state_next = state_next + jnp.einsum('hsk,hsw->hkw', key_vecs * remain[:, :, None], updates, precision=HIGHEST)
    return (state_next, read_out)

def run_tiles(query_vecs, key_vecs, value_vecs, log_decay, erase_rate, state_start):
    row_count, head_count, key_width = query_vecs.shape
    tile_count = row_count // TILE

    def arrange(tensor):
        return jnp.swapaxes(tensor.reshape((tile_count, TILE, head_count) + tensor.shape[2:]), 1, 2)
    inputs = (arrange(query_vecs), arrange(key_vecs), arrange(value_vecs), arrange(log_decay), arrange(erase_rate))

    def advance(state_now, sliced):
        return jax.checkpoint(block_step)(state_now, *sliced)
    state_end, outputs = lax.scan(advance, state_start, inputs)
    outputs = jnp.swapaxes(outputs, 1, 2).reshape(row_count, head_count, outputs.shape[-1])
    return (outputs, state_end)

def mixer_inputs(conv_in, edge_rows, head_in, conv_taps, head_params):
    block_len = conv_in.shape[1]
    head_count = head_params.shape[1]
    extended = jnp.concatenate([edge_rows, conv_in], axis=1)
    conv_sum = extended[:, 0:block_len] * conv_taps[:, 0]
    for offset in range(1, conv_taps.shape[1]):
        conv_sum = conv_sum + extended[:, offset:offset + block_len] * conv_taps[:, offset]
    activated = jax.nn.silu(conv_sum)
    key_span = head_count * DK
    lead = activated.shape[:2]
    query_vecs = unit_rows(activated[..., 0:key_span].reshape(lead + (head_count, DK))) * DK ** (-0.5)
    key_vecs = unit_rows(activated[..., key_span:2 * key_span].reshape(lead + (head_count, DK)))
    value_vecs = activated[..., 2 * key_span:].reshape(lead + (head_count, DV))
    log_decay = -jnp.exp(head_params[0]) * jax.nn.softplus(head_in[..., 0:head_count] + head_params[1])
    erase_rate = jax.nn.sigmoid(head_in[..., head_count:2 * head_count] + head_params[2])
    return (query_vecs, key_vecs, value_vecs, log_decay, erase_rate)

def gated_norm(mixed, gate_in, head_gain):
    shaped = gate_in.reshape(mixed.shape)
    normed = mixed * lax.rsqrt(lax.optimization_barrier(jnp.mean(mixed * mixed, axis=-1, keepdims=True)) + epsilon) * head_gain
    return (normed * jax.nn.silu(shaped)).reshape(gate_in.shape)

def layer_forward(tokens, valid_rows, norm_gains, head_gain, head_params, qkv_weight, gate_weight, head_weight, conv_weight, out_weight, ffn_in, ffn_out):
    first_norm = low(rms_scale(tokens, norm_gains[0]))
    conv_in = low(low_back(jnp.dot(first_norm, qkv_weight, precision=HIGHEST)))
    head_in = low_back(jnp.dot(first_norm, head_weight, precision=HIGHEST))
    gate_in = low_back(jnp.dot(first_norm, gate_weight, precision=HIGHEST))
    edge_rows = jnp.zeros((1, KCONV - 1, conv_in.shape[-1]), jnp.float32)
    vectors = mixer_inputs(conv_in[None], edge_rows, head_in[None], conv_weight, head_params)
    state_zero = jnp.zeros((H, DK, DV), jnp.float32)
    mixed, unused = run_tiles(vectors[0][0], vectors[1][0], vectors[2][0], vectors[3][0], vectors[4][0], state_zero)
    normed = low(gated_norm(mixed, gate_in, head_gain))
    attended = low_back(jnp.dot(normed, out_weight, precision=HIGHEST))
    middle = tokens + attended
    second_norm = low(rms_scale(middle, norm_gains[1]))
    gate_up = low_back(jnp.dot(second_norm, ffn_in, precision=HIGHEST))
    hidden = low(jax.nn.silu(gate_up[:, 0:FF]) * gate_up[:, FF:2 * FF])
    carried = low_back(jnp.dot(hidden, ffn_out, precision=HIGHEST))
    return jnp.where(valid_rows[:, None], middle + carried, 0.0)

def reference(tokens, lengths, cotangent, norm_gains, head_gain, head_params, qkv_weight, gate_weight, head_weight, conv_weight, out_weight, ffn_in, ffn_out):
    params = tuple((tensor.astype(jnp.float32) for tensor in (norm_gains, head_gain, head_params, qkv_weight, gate_weight, head_weight, conv_weight, out_weight, ffn_in, ffn_out)))
    positions = jnp.arange(LEN)

    def one_sequence(totals, sliced):
        seq_tokens, seq_length, seq_cotangent = sliced
        valid_rows = positions < seq_length

        def apply_layer(inputs, *weights):
            return layer_forward(inputs, valid_rows, *weights)
        result, pullback = jax.vjp(apply_layer, seq_tokens.astype(jnp.float32), *params)
        gradients = pullback(seq_cotangent.astype(jnp.float32))
        totals = tuple((total + grad_part for total, grad_part in zip(totals, gradients[1:])))
        return (totals, (result.astype(jnp.bfloat16), gradients[0].astype(jnp.bfloat16)))
    start_totals = tuple((jnp.zeros_like(tensor) for tensor in params))
    totals, (outputs, input_grads) = lax.scan(one_sequence, start_totals, (tokens, lengths, cotangent))
    return (outputs, input_grads, totals[0], totals[1], totals[2], totals[3], totals[4], totals[5], totals[6], totals[7], totals[8], totals[9])
```

```python
import functools

import jax
import jax.numpy as jnp
from jax import lax
from jax.experimental import pallas as pl
from jax.experimental.pallas import tpu as pltpu
from jax.sharding import PartitionSpec as P

CH = 256
DK = 128
DV = 256
KCONV = 4
TILE = 64


HIGHEST = lax.Precision.HIGHEST
epsilon = 1e-06


def passed_along(block, axis, distance):
    devices = range(lax.axis_size(axis))
    route = [(i - distance, i) for i in devices if i - distance in devices]
    return lax.ppermute(block, axis, route)


def rms_scale(values, gain_row):
    return (
        values * lax.rsqrt(jnp.mean(values * values, axis=-1, keepdims=True) + epsilon) * gain_row
    )


def unit_rows(values):
    return values * lax.rsqrt(jnp.sum(values * values, axis=-1, keepdims=True) + epsilon)


def block_step(state_now, query_vecs, key_vecs, value_vecs, log_decay, erase_rate):
    length = query_vecs.shape[1]
    cumulative = jnp.cumsum(log_decay, axis=1)
    row_index = jnp.arange(length)[:, None]
    col_index = jnp.arange(length)[None, :]
    strict = col_index < row_index
    within = col_index <= row_index
    spread = cumulative[:, :, None] - cumulative[:, None, :]
    lower_decay = jnp.where(strict, jnp.exp(jnp.where(strict, spread, 0.0)), 0.0)
    causal = jnp.where(within, jnp.exp(jnp.where(within, spread, 0.0)), 0.0)
    key_gram = jnp.einsum("htk,hsk->hts", key_vecs, key_vecs, precision=HIGHEST)
    query_gram = jnp.einsum("htk,hsk->hts", query_vecs, key_vecs, precision=HIGHEST)
    negated = -(erase_rate[:, :, None] * key_gram * lower_decay)
    identity = jnp.eye(length, dtype=jnp.float32)
    inverse = identity + negated
    powered = negated
    for level_index in range(length.bit_length() - 2):
        powered = jnp.einsum("hts,hsr->htr", powered, powered, precision=HIGHEST)
        inverse = jnp.einsum("hts,hsr->htr", inverse, identity + powered, precision=HIGHEST)
    shrink = jnp.exp(cumulative)
    recalled = jnp.einsum("htk,hkw->htw", key_vecs, state_now, precision=HIGHEST)
    target = erase_rate[:, :, None] * value_vecs - (erase_rate * shrink)[:, :, None] * recalled
    updates = jnp.einsum("hts,hsw->htw", inverse, target, precision=HIGHEST)
    read_out = shrink[:, :, None] * jnp.einsum(
        "htk,hkw->htw", query_vecs, state_now, precision=HIGHEST
    )
    read_out = read_out + jnp.einsum(
        "hts,hsw->htw", query_gram * causal, updates, precision=HIGHEST
    )
    remain = jnp.exp(cumulative[:, -1:] - cumulative)
    state_next = jnp.exp(cumulative[:, -1])[:, None, None] * state_now
    state_next = state_next + jnp.einsum(
        "hsk,hsw->hkw", key_vecs * remain[:, :, None], updates, precision=HIGHEST
    )
    return (state_next, read_out)


def run_tiles(query_vecs, key_vecs, value_vecs, log_decay, erase_rate, state_start):
    row_count, head_count, key_width = query_vecs.shape
    tile_count = row_count // TILE

    def arrange(tensor):
        return jnp.swapaxes(tensor.reshape((tile_count, TILE, head_count) + tensor.shape[2:]), 1, 2)

    inputs = (
        arrange(query_vecs),
        arrange(key_vecs),
        arrange(value_vecs),
        arrange(log_decay),
        arrange(erase_rate),
    )

    def advance(state_now, sliced):
        return jax.checkpoint(block_step)(state_now, *sliced)

    state_end, outputs = lax.scan(advance, state_start, inputs)
    outputs = jnp.swapaxes(outputs, 1, 2).reshape(row_count, head_count, outputs.shape[-1])
    return (outputs, state_end)


def mixer_inputs(conv_in, edge_rows, head_in, conv_taps, head_params):
    block_len = conv_in.shape[1]
    head_count = head_params.shape[1]
    extended = jnp.concatenate([edge_rows, conv_in], axis=1)
    conv_sum = extended[:, 0:block_len] * conv_taps[:, 0]
    for offset in range(1, conv_taps.shape[1]):
        conv_sum = conv_sum + extended[:, offset : offset + block_len] * conv_taps[:, offset]
    activated = jax.nn.silu(conv_sum)
    key_span = head_count * DK
    lead = activated.shape[:2]
    query_vecs = unit_rows(activated[..., 0:key_span].reshape(lead + (head_count, DK))) * DK ** (
        -0.5
    )
    key_vecs = unit_rows(activated[..., key_span : 2 * key_span].reshape(lead + (head_count, DK)))
    value_vecs = activated[..., 2 * key_span :].reshape(lead + (head_count, DV))
    log_decay = -jnp.exp(head_params[0]) * jax.nn.softplus(
        head_in[..., 0:head_count] + head_params[1]
    )
    erase_rate = jax.nn.sigmoid(head_in[..., head_count : 2 * head_count] + head_params[2])
    return (query_vecs, key_vecs, value_vecs, log_decay, erase_rate)


def gated_norm(mixed, gate_in, head_gain):
    shaped = gate_in.reshape(mixed.shape)
    normed = (
        mixed * lax.rsqrt(jnp.mean(mixed * mixed, axis=-1, keepdims=True) + epsilon) * head_gain
    )
    return (normed * jax.nn.silu(shaped)).reshape(gate_in.shape)


def local_tiles(query_vecs, key_vecs, value_vecs, log_decay, erase_rate):
    key_width = key_vecs.shape[-1]
    value_width = value_vecs.shape[-1]
    head_count = key_vecs.shape[2]
    padded = jnp.concatenate(
        [jnp.zeros(value_vecs.shape[:3] + (key_width,), jnp.float32), value_vecs], axis=-1
    )
    start_map = jnp.concatenate(
        [jnp.eye(key_width, dtype=jnp.float32), jnp.zeros((key_width, value_width), jnp.float32)],
        axis=1,
    )
    start_map = jnp.broadcast_to(start_map, (head_count, key_width, key_width + value_width))

    def single(query_one, key_one, value_one, decay_one, erase_one):
        return run_tiles(query_one, key_one, value_one, decay_one, erase_one, start_map)

    return jax.vmap(single)(query_vecs, key_vecs, padded, log_decay, erase_rate)


def post_mix(local_out, incoming, gate_in, head_gain):
    mixed = local_out[..., DK:] + jnp.einsum(
        "snhk,shkv->snhv", local_out[..., 0:DK], incoming, precision=HIGHEST
    )
    return gated_norm(mixed, gate_in, head_gain)


def swiglu(gate_up):
    split_at = gate_up.shape[-1] // 2
    return jax.nn.silu(gate_up[:, 0:split_at]) * gate_up[:, split_at:]


def matmul_maps(left, right):
    return jnp.einsum("shij,shjk->shik", left, right, precision=HIGHEST)


def apply_map(maps, state_now):
    return matmul_maps(maps[0], state_now) + maps[1]


def general_body(
    tokens,
    lengths,
    cotangent,
    norm_gains,
    head_gain,
    head_params,
    qkv_weight,
    gate_weight,
    head_weight,
    conv_weight,
    out_weight,
    ffn_in,
    ffn_out,
):
    seq_count, block_len, model_width = tokens.shape
    row_count = seq_count * block_len
    position = lax.axis_index("seq") * block_len + jnp.arange(block_len, dtype=jnp.int32)
    valid_rows = (position[None, :] < lengths[:, None]).reshape(row_count, 1)
    col_parts = (
        lax.all_gather(qkv_weight, "seq", axis=1, tiled=True),
        lax.all_gather(gate_weight, "seq", axis=1, tiled=True),
        lax.all_gather(out_weight, "seq", axis=1, tiled=True),
        lax.all_gather(ffn_in, "seq", axis=1, tiled=True),
        lax.all_gather(ffn_out, "seq", axis=1, tiled=True),
    )
    gathered = (
        lax.all_gather(col_parts[0], "dp", axis=0, tiled=True),
        lax.all_gather(col_parts[1], "dp", axis=0, tiled=True),
        lax.all_gather(col_parts[2], "dp", axis=0, tiled=True),
        lax.all_gather(col_parts[3], "dp", axis=0, tiled=True),
        lax.all_gather(col_parts[4], "dp", axis=0, tiled=True),
    )
    w_qkv, w_gate, w_out, w_in, w_down = gathered
    inputs = tokens.reshape(row_count, model_width).astype(jnp.float32)
    first_norm = rms_scale(inputs, norm_gains[0]).astype(jnp.bfloat16)
    conv_in = jnp.dot(first_norm, w_qkv, preferred_element_type=jnp.float32).astype(jnp.bfloat16)
    head_in = jnp.dot(first_norm, head_weight, preferred_element_type=jnp.float32)
    gate_in = jnp.dot(first_norm, w_gate, preferred_element_type=jnp.float32)
    conv_width = conv_in.shape[-1]
    conv_rows = conv_in.reshape(seq_count, block_len, conv_width)
    edge_cut = block_len - (KCONV - 1)
    edge_rows = passed_along(conv_rows[:, edge_cut:], "seq", 1)
    mix_args = (
        conv_rows.astype(jnp.float32),
        edge_rows.astype(jnp.float32),
        head_in.reshape(seq_count, block_len, -1),
        conv_weight.astype(jnp.float32),
        head_params,
    )
    vectors = mixer_inputs(*mix_args)
    local_out, end_states = local_tiles(*vectors)
    carry_maps = (end_states[..., 0:DK], end_states[..., DK:])

    def relay_state(step_index, state_now):
        return passed_along(apply_map(carry_maps, state_now), "seq", 1)

    incoming = lax.fori_loop(
        0, lax.axis_size("seq") - 1, relay_state, jnp.zeros_like(carry_maps[1])
    )
    post_args = (local_out, incoming, gate_in, head_gain)
    normed = post_mix(*post_args).astype(jnp.bfloat16)
    attended = jnp.dot(normed, w_out, preferred_element_type=jnp.float32)
    middle = inputs + attended
    second_norm = rms_scale(middle, norm_gains[1]).astype(jnp.bfloat16)
    gate_up = jnp.dot(second_norm, w_in, preferred_element_type=jnp.float32)
    hidden = swiglu(gate_up).astype(jnp.bfloat16)
    carried = jnp.dot(hidden, w_down, preferred_element_type=jnp.float32)
    output = jnp.where(valid_rows, middle + carried, 0.0).astype(jnp.bfloat16)
    col_again = (
        lax.all_gather(qkv_weight, "seq", axis=1, tiled=True),
        lax.all_gather(gate_weight, "seq", axis=1, tiled=True),
        lax.all_gather(out_weight, "seq", axis=1, tiled=True),
        lax.all_gather(ffn_in, "seq", axis=1, tiled=True),
        lax.all_gather(ffn_out, "seq", axis=1, tiled=True),
    )
    regathered = (
        lax.all_gather(col_again[0], "dp", axis=0, tiled=True),
        lax.all_gather(col_again[1], "dp", axis=0, tiled=True),
        lax.all_gather(col_again[2], "dp", axis=0, tiled=True),
        lax.all_gather(col_again[3], "dp", axis=0, tiled=True),
        lax.all_gather(col_again[4], "dp", axis=0, tiled=True),
    )
    w_qkv, w_gate, w_out, w_in, w_down = regathered
    upstream = jnp.where(
        valid_rows, cotangent.reshape(row_count, model_width).astype(jnp.float32), 0.0
    )
    carried_grad = upstream.astype(jnp.bfloat16)
    grad_down = jnp.einsum("nf,nd->fd", hidden, carried_grad, preferred_element_type=jnp.float32)
    hidden_grad = jnp.einsum("nd,fd->nf", carried_grad, w_down, preferred_element_type=jnp.float32)
    unused, swiglu_back = jax.vjp(swiglu, gate_up)
    gate_up_grad = swiglu_back(hidden_grad)[0].astype(jnp.bfloat16)
    grad_in = jnp.einsum("nd,nf->df", second_norm, gate_up_grad, preferred_element_type=jnp.float32)
    second_grad = jnp.einsum("nf,df->nd", gate_up_grad, w_in, preferred_element_type=jnp.float32)
    unused, second_back = jax.vjp(rms_scale, middle, norm_gains[1])
    middle_back, gain_two = second_back(second_grad)
    middle_grad = upstream + middle_back
    attended_grad = middle_grad.astype(jnp.bfloat16)
    grad_out = jnp.einsum("nv,nd->vd", normed, attended_grad, preferred_element_type=jnp.float32)
    normed_grad = jnp.einsum("nd,vd->nv", attended_grad, w_out, preferred_element_type=jnp.float32)
    unused, post_back = jax.vjp(post_mix, *post_args)
    local_grad, incoming_local, gate_in_grad, head_gain_grad = post_back(normed_grad)
    flipped = (jnp.swapaxes(carry_maps[0], -1, -2), incoming_local)

    def relay_grad(step_index, grad_now):
        return passed_along(apply_map(flipped, grad_now).astype(jnp.bfloat16), "seq", -1).astype(
            jnp.float32
        )

    outgoing = lax.fori_loop(
        0, lax.axis_size("seq") - 1, relay_grad, jnp.zeros_like(incoming_local)
    )
    map_grad = jnp.einsum("shkv,shjv->shkj", outgoing, incoming, precision=HIGHEST)
    end_grad = jnp.concatenate([map_grad, outgoing], axis=-1)
    unused, tiles_back = jax.vjp(local_tiles, *vectors)
    vector_grads = tiles_back((local_grad, end_grad))
    unused, mix_back = jax.vjp(mixer_inputs, *mix_args)
    conv_own, edge_grad, head_in_grad, conv_taps_grad, params_grad = mix_back(vector_grads)
    edge_back = passed_along(edge_grad.astype(jnp.bfloat16), "seq", -1).astype(edge_grad.dtype)
    conv_total = jnp.concatenate(
        [conv_own[:, 0:edge_cut], conv_own[:, edge_cut:] + edge_back], axis=1
    )
    conv_grad = conv_total.reshape(row_count, conv_width).astype(jnp.bfloat16)
    head_grad = head_in_grad.reshape(row_count, -1).astype(jnp.bfloat16)
    gate_grad = gate_in_grad.astype(jnp.bfloat16)
    grad_qkv = jnp.einsum("nd,nc->dc", first_norm, conv_grad, preferred_element_type=jnp.float32)
    grad_head = jnp.einsum("nd,nc->dc", first_norm, head_grad, preferred_element_type=jnp.float32)
    grad_gate = jnp.einsum("nd,nc->dc", first_norm, gate_grad, preferred_element_type=jnp.float32)
    first_grad = jnp.einsum("nc,dc->nd", conv_grad, w_qkv, preferred_element_type=jnp.float32)
    first_grad = first_grad + jnp.einsum(
        "nc,dc->nd", head_grad, head_weight, preferred_element_type=jnp.float32
    )
    first_grad = first_grad + jnp.einsum(
        "nc,dc->nd", gate_grad, w_gate, preferred_element_type=jnp.float32
    )
    unused, first_back = jax.vjp(rms_scale, inputs, norm_gains[0])
    input_back, gain_one = first_back(first_grad)
    input_grad = (
        (middle_grad + input_back).astype(jnp.bfloat16).reshape(seq_count, block_len, model_width)
    )
    row_groups = (
        lax.psum_scatter(
            grad_qkv.astype(jnp.bfloat16), "dp", scatter_dimension=0, tiled=True
        ).astype(jnp.float32),
        lax.psum_scatter(
            grad_gate.astype(jnp.bfloat16), "dp", scatter_dimension=0, tiled=True
        ).astype(jnp.float32),
        lax.psum_scatter(
            grad_out.astype(jnp.bfloat16), "dp", scatter_dimension=0, tiled=True
        ).astype(jnp.float32),
        lax.psum_scatter(
            grad_in.astype(jnp.bfloat16), "dp", scatter_dimension=0, tiled=True
        ).astype(jnp.float32),
        lax.psum_scatter(
            grad_down.astype(jnp.bfloat16), "dp", scatter_dimension=0, tiled=True
        ).astype(jnp.float32),
    )
    weight_parts = (
        lax.psum_scatter(
            row_groups[0].astype(jnp.bfloat16), "seq", scatter_dimension=1, tiled=True
        ).astype(jnp.float32),
        lax.psum_scatter(
            row_groups[1].astype(jnp.bfloat16), "seq", scatter_dimension=1, tiled=True
        ).astype(jnp.float32),
        lax.psum_scatter(
            row_groups[2].astype(jnp.bfloat16), "seq", scatter_dimension=1, tiled=True
        ).astype(jnp.float32),
        lax.psum_scatter(
            row_groups[3].astype(jnp.bfloat16), "seq", scatter_dimension=1, tiled=True
        ).astype(jnp.float32),
        lax.psum_scatter(
            row_groups[4].astype(jnp.bfloat16), "seq", scatter_dimension=1, tiled=True
        ).astype(jnp.float32),
    )
    small_sums = lax.psum(
        (jnp.stack([gain_one, gain_two]), head_gain_grad, params_grad, grad_head, conv_taps_grad),
        ("dp", "seq"),
    )
    output = output.reshape(seq_count, block_len, model_width)
    return (
        output,
        input_grad,
        small_sums[0],
        small_sums[1],
        small_sums[2],
        weight_parts[0],
        weight_parts[1],
        small_sums[3],
        small_sums[4],
        weight_parts[2],
        weight_parts[3],
        weight_parts[4],
    )


def mm(a, b, dims=((1,),(0,))):
    return lax.dot_general(a, b, (dims, ((), ())), precision=HIGHEST, preferred_element_type=jnp.float32)
NT = ((1,),(1,))
TN = ((0,),(0,))
NN = ((1,),(0,))

def grid_masks():
    row = lax.broadcasted_iota(jnp.int32, (CH, CH), 0)
    col = lax.broadcasted_iota(jnp.int32, (CH, CH), 1)
    return row, col

def decay_parts(g, row, col):
    lower = (col <= row).astype(jnp.float32)
    cum = mm(lower, g)
    cum_row = mm(g, lower, ((0,), (1,)))
    within = col <= row
    decay = jnp.where(within, jnp.exp(jnp.where(within, cum - cum_row, 0.0)), 0.0)
    return cum, decay

def unit_inverse(attn, row, col):
    def same(width):
        return (row // width) == (col // width)
    power = jnp.where(same(64), -attn, 0.0)
    inverse = jnp.where(row == col, 1.0, 0.0) + power
    for level in range(5):
        power = mm(power, power)
        inverse = inverse + mm(inverse, power)
    for width in (128, 256):
        off = jnp.where(same(width) & ~same(width // 2), attn, 0.0)
        inverse = inverse - mm(inverse, mm(off, inverse))
    return inverse

def rec_fwd_kernel(q_ref, k_ref, v_ref, g_ref, e_ref, o_ref, s_ref, t_ref, u_ref, w_ref, qk_ref, cum_ref):
    n = q_ref.shape[0] // CH
    row, col = grid_masks()
    def local(i, carry):
        rows = pl.ds(pl.multiple_of(i * CH, CH), CH)
        q, k, v, g, e = q_ref[rows, :], k_ref[rows, :], v_ref[rows, :], g_ref[rows, :], e_ref[rows, :]
        cum, decay = decay_parts(g, row, col)
        attn = jnp.where(col < row, e * mm(k, k, NT) * decay, 0.0)
        t = unit_inverse(attn, row, col)
        t_ref[rows, :] = t
        w_ref[rows, :] = mm(t, (e * jnp.exp(cum)) * k)
        u_ref[rows, :] = mm(t, e * v)
        qk_ref[rows, :] = mm(q, k, NT) * decay
        cum_ref[rows, :] = cum
        return carry
    lax.fori_loop(0, n, local, 0)
    def step(i, state):
        rows = pl.ds(pl.multiple_of(i * CH, CH), CH)
        s_ref[i] = state
        cum = cum_ref[rows, :]
        last = cum[CH - 1:CH, :]
        u = u_ref[rows, :] - mm(w_ref[rows, :], state)
        u_ref[rows, :] = u
        o_ref[rows, :] = jnp.exp(cum) * mm(q_ref[rows, :], state) + mm(qk_ref[rows, :], u)
        return jnp.exp(last) * state + mm(k_ref[rows, :] * jnp.exp(last - cum), u, TN)
    lax.fori_loop(0, n, step, jnp.zeros((DK, DV), jnp.float32))

def rec_bwd_kernel(q_ref, k_ref, v_ref, g_ref, e_ref, s_ref, t_ref, u_ref, w_ref, do_ref, dq_ref, dk_ref, dv_ref, dg_ref, de_ref):
    n = q_ref.shape[0] // CH
    row, col = grid_masks()
    ones = jnp.ones((CH, 1), jnp.float32)
    def step(j, ds1):
        i = n - 1 - j
        rows = pl.ds(pl.multiple_of(i * CH, CH), CH)
        q, k, v, g, e = q_ref[rows, :], k_ref[rows, :], v_ref[rows, :], g_ref[rows, :], e_ref[rows, :]
        s0, t, u, do = s_ref[i], t_ref[rows, :], u_ref[rows, :], do_ref[rows, :]
        cum, decay = decay_parts(g, row, col)
        last = cum[CH - 1:CH, :]
        gamma = jnp.exp(last)
        shrink = jnp.exp(cum)
        remain = jnp.exp(last - cum)
        gram = jnp.where(col < row, mm(k, k, NT) * decay, 0.0)
        qk = mm(q, k, NT) * decay
        du = mm(qk, do, TN) + mm(k * remain, ds1)
        dr = mm(t, du, TN)
        ds0 = gamma * ds1 + mm(q * shrink, do, TN) - mm(w_ref[rows, :], du, TN)
        dp = jnp.where(col <= row, mm(do, u, NT), 0.0)
        da = jnp.where(col < row, -mm(dr, u, NT), 0.0)
        dqk = dp * decay
        dag = da * gram
        z = dp * qk + e * dag
        dgram = e * da * decay
        nk = mm(dr, s0, NT)
        m = mm(do, s0, NT)
        lm = mm(u, ds1, NT)
        row_nk = jnp.sum(nk * k, axis=1, keepdims=True)
        dv_ref[rows, :] = e * dr
        de_ref[rows, :] = jnp.sum(dr * v, axis=1, keepdims=True) - shrink * row_nk + jnp.sum(dag, axis=1, keepdims=True)
        dq_ref[rows, :] = mm(dqk, k) + shrink * m
        dk_ref[rows, :] = mm(dqk, q, TN) + mm(dgram, k) + mm(dgram, k, TN) - (e * shrink) * nk + remain * lm
        dshrink = jnp.sum(m * q, axis=1, keepdims=True) - e * row_nk
        rdr = remain * jnp.sum(lm * k, axis=1, keepdims=True)
        dcum = jnp.sum(z, axis=1, keepdims=True) - mm(z, ones, TN) + shrink * dshrink - rdr
        dlast = jnp.sum(rdr) + jnp.sum(gamma * s0 * ds1)
        lower = (col <= row).astype(jnp.float32)
        dg_ref[rows, :] = mm(lower, dcum, TN) + dlast
        return ds0
    lax.fori_loop(0, n, step, jnp.zeros((DK, DV), jnp.float32))

def vm(n): return [pl.BlockSpec(memory_space=pltpu.VMEM)] * n
def rec_fwd(q, k, v, g, e):
    L = q.shape[0]
    f = jnp.float32
    return pl.pallas_call(rec_fwd_kernel,
        out_shape=(jax.ShapeDtypeStruct((L, DV), f), jax.ShapeDtypeStruct((L // CH, DK, DV), f), jax.ShapeDtypeStruct((L, CH), f),
                   jax.ShapeDtypeStruct((L, DV), f), jax.ShapeDtypeStruct((L, DK), f)),
        in_specs=vm(5), out_specs=tuple(vm(5)),
        scratch_shapes=[pltpu.VMEM((L, CH), f), pltpu.VMEM((L, 1), f)],
        compiler_params=pltpu.CompilerParams(vmem_limit_bytes=48 << 20), name="rec_fwd")(q, k, v, g, e)
def rec_bwd(q, k, v, g, e, s, t, u, w, do):
    L = q.shape[0]
    f = jnp.float32
    return pl.pallas_call(rec_bwd_kernel,
        out_shape=(jax.ShapeDtypeStruct((L, DK), f), jax.ShapeDtypeStruct((L, DK), f), jax.ShapeDtypeStruct((L, DV), f),
                   jax.ShapeDtypeStruct((L, 1), f), jax.ShapeDtypeStruct((L, 1), f)),
        in_specs=vm(10), out_specs=tuple(vm(5)),
        compiler_params=pltpu.CompilerParams(vmem_limit_bytes=48 << 20), name="rec_bwd")(q, k, v, g, e, s, t, u, w, do)


MESH = pl.DeviceIdType.MESH
ANY = pl.BlockSpec(memory_space=pl.ANY)


def meet_all(dp, seq, i, j):
    barrier = pltpu.get_barrier_semaphore()
    for di in range(dp):
        for dj in range(seq):
            if di or dj:
                pl.semaphore_signal(
                    barrier, inc=1, device_id=(lax.rem(i + di, dp), lax.rem(j + dj, seq)), device_id_type=MESH
                )
    pl.semaphore_wait(barrier, dp * seq - 1)


def sender(i, j, send_sem):
    sent = []

    def push(src, dst, recv, di, dj):
        slot = send_sem.at[len(sent)]
        here = (di == i) & (dj == j)

        @pl.when(here)
        def _():
            pltpu.make_async_copy(src, dst, recv).start()

        copy = pltpu.make_async_remote_copy(
            src_ref=src, dst_ref=dst, send_sem=slot, recv_sem=recv, device_id=(di, dj), device_id_type=MESH
        )

        @pl.when(jnp.logical_not(here))
        def _():
            copy.start()

        sent.append((copy, here))

    def finish():
        for copy, here in sent:
            @pl.when(jnp.logical_not(here))
            def _():
                copy.wait_send()

    return push, finish


def arrived(dst, recv):
    pltpu.make_async_copy(dst, dst, recv).wait()


def cols(ref, start, size):
    return ref.at[:, pl.ds(pl.multiple_of(start, 128), size)]


def rows_of(ref, start, size):
    return ref.at[pl.ds(pl.multiple_of(start, 128), size), :]


def weights_in_kernel(dp, seq, qkv, w_in, w_out, w_down, qkv_o, in_o, out_o, down_o, send_sem, send2, recv):
    i, j = lax.axis_index("dp"), lax.axis_index("seq")
    meet_all(dp, seq, i, j)
    low = j < 4

    push_a, finish_a = sender(i, j, send_sem)
    push_b, finish_b = sender(i, j, send2)
    own = j // 4
    pairs = []

    @pl.when(low)
    def _():
        for t in range(4):
            push_a(
                qkv.at[:, 128 * t : 128 * t + 128],
                cols(qkv_o, 128 * (j // 2), 128),
                recv.at[j // 2],
                i,
                4 * lax.rem(j, 2) + t,
            )
        finish_a()

    @pl.when(jnp.logical_not(low))
    def _():
        push_v, finish_v = sender(i, j, send_sem)
        for t in range(2):
            push_v(qkv.at[:, 256 * t : 256 * t + 256], qkv_o.at[:, 256:512], recv.at[2], i, 2 * (j - 4) + t)
        finish_v()

    keep = pltpu.make_async_copy(cols(w_in, 384 * own, 384), cols(in_o, 384 * own, 384), recv.at[3])
    keep.start()
    push_b(cols(w_in, 384 * (1 - own), 384), cols(in_o, 384 * own, 384), recv.at[4], i, lax.rem(j + 4, 8))
    for b in range(2):
        push_b(
            w_out.at[256 * b : 256 * b + 256, :],
            cols(out_o, 128 * lax.rem(j, 2), 128),
            recv.at[5 + lax.rem(j, 2)],
            j // 2,
            2 * i + b,
        )
    for b in range(2):
        push_b(
            w_down.at[384 * b : 384 * b + 384, :],
            cols(down_o, 128 * lax.rem(j, 2), 128),
            recv.at[7 + lax.rem(j, 2)],
            j // 2,
            i + 4 * b,
        )
    arrived(qkv_o.at[:, 0:128], recv.at[0])
    arrived(qkv_o.at[:, 128:256], recv.at[1])
    arrived(qkv_o.at[:, 256:512], recv.at[2])
    keep.wait()
    arrived(in_o.at[:, 0:384], recv.at[4])
    for r in range(2):
        arrived(out_o.at[:, 128 * r : 128 * r + 128], recv.at[5 + r])
        arrived(down_o.at[:, 128 * r : 128 * r + 128], recv.at[7 + r])
    finish_b()


def weights_in(dp, seq, qkv, w_in, w_out, w_down):
    kind = jnp.bfloat16
    return pl.pallas_call(
        functools.partial(weights_in_kernel, dp, seq),
        out_shape=(
            jax.ShapeDtypeStruct((256, 512), kind),
            jax.ShapeDtypeStruct((256, 768), kind),
            jax.ShapeDtypeStruct((256, 256), kind),
            jax.ShapeDtypeStruct((384, 256), kind),
        ),
        in_specs=[ANY] * 4,
        out_specs=(ANY,) * 4,
        scratch_shapes=[
            pltpu.SemaphoreType.DMA((4,)),
            pltpu.SemaphoreType.DMA((5,)),
            pltpu.SemaphoreType.DMA((9,)),
        ],
        compiler_params=pltpu.CompilerParams(collective_id=0, has_side_effects=True),
        name="weights_in",
    )(qkv, w_in, w_out, w_down)


def grads_out_kernel(dp, seq, qkv, w_in, w_out, w_down, qkv_o, in_o, out_o, down_o, send_sem, recv):
    i, h = lax.axis_index("dp"), lax.axis_index("seq")
    meet_all(dp, seq, i, h)
    push, finish = sender(i, h, send_sem)
    quarter, pair = lax.rem(h, 4), lax.rem(h, 2)
    push(qkv.at[:, 0:128], cols(qkv_o, 128 * quarter, 128), recv.at[quarter], i, h // 4)
    push(qkv.at[:, 128:256], cols(qkv_o, 128 * quarter, 128), recv.at[quarter], i, 2 + h // 4)
    push(qkv.at[:, 256:512], cols(qkv_o, 256 * pair, 256), recv.at[pair], i, 4 + h // 2)
    push(w_in.at[:, 0:384], cols(in_o, 384 * (h // 4), 384), recv.at[4 + h // 4], i, quarter)
    push(w_in.at[:, 384:768], cols(in_o, 384 * (h // 4), 384), recv.at[4 + h // 4], i, 4 + quarter)
    for r in range(2):
        push(w_out.at[:, 128 * r : 128 * r + 128], rows_of(out_o, 256 * pair, 256), recv.at[6 + pair], h // 2, 2 * i + r)
        push(
            w_down.at[:, 128 * r : 128 * r + 128],
            rows_of(down_o, 384 * (h // 4), 384),
            recv.at[8 + h // 4],
            quarter,
            2 * i + r,
        )

    @pl.when(h < 4)
    def _():
        for t in range(4):
            arrived(qkv_o.at[:, 128 * t : 128 * t + 128], recv.at[t])

    @pl.when(h >= 4)
    def _():
        for t in range(2):
            arrived(qkv_o.at[:, 256 * t : 256 * t + 256], recv.at[t])

    for r in range(2):
        arrived(in_o.at[:, 384 * r : 384 * r + 384], recv.at[4 + r])
        arrived(out_o.at[256 * r : 256 * r + 256, :], recv.at[6 + r])
        arrived(down_o.at[384 * r : 384 * r + 384, :], recv.at[8 + r])
    finish()


def grads_out(dp, seq, qkv, w_in, w_out, w_down):
    kind = jnp.bfloat16
    return pl.pallas_call(
        functools.partial(grads_out_kernel, dp, seq),
        out_shape=(
            jax.ShapeDtypeStruct((256, 512), kind),
            jax.ShapeDtypeStruct((256, 768), kind),
            jax.ShapeDtypeStruct((512, 128), kind),
            jax.ShapeDtypeStruct((768, 128), kind),
        ),
        in_specs=[ANY] * 4,
        out_specs=(ANY,) * 4,
        scratch_shapes=[pltpu.SemaphoreType.DMA((9,)), pltpu.SemaphoreType.DMA((10,))],
        compiler_params=pltpu.CompilerParams(collective_id=1, has_side_effects=True),
        name="grads_out",
    )(qkv, w_in, w_out, w_down)


def dot(a, b, dims=((1,), (0,))):
    return lax.dot_general(a, b, (dims, ((), ())), preferred_element_type=jnp.float32)


def low(v):
    return v.astype(jnp.bfloat16)


def fast_body(
    dp,
    seq,
    tokens,
    lengths,
    cotangent,
    norm_gains,
    head_gain,
    head_params,
    qkv_weight,
    gate_weight,
    head_weight,
    conv_weight,
    out_weight,
    ffn_in,
    ffn_out,
):
    seq_count, block_len, width = tokens.shape
    h = lax.axis_index("seq")
    head_count = head_params.shape[1]
    ff_cols, ff_rows = ffn_in.shape[1], ffn_out.shape[0]
    position = h * block_len + jnp.arange(block_len, dtype=jnp.int32)
    valid = (position < lengths[0])[:, None]
    own = tokens[0].astype(jnp.float32)
    upstream = jnp.where(valid, cotangent[0].astype(jnp.float32), 0.0)
    x_all = lax.all_gather(tokens[0], "seq", axis=0, tiled=True)
    pieces = weights_in(
        dp,
        seq,
        qkv_weight,
        jnp.pad(ffn_in, ((0, 0), (0, 768 - ff_cols))),
        out_weight,
        jnp.pad(ffn_out, ((0, 768 - ff_rows), (0, 0))),
    )
    w_qkv = lax.all_gather(pieces[0], "dp", axis=0, tiled=True)
    w_gate = lax.all_gather(gate_weight, "dp", axis=0, tiled=True)
    w_out = lax.all_gather(pieces[2], "dp", axis=1, tiled=True)
    w_in = lax.all_gather(pieces[1], "dp", axis=0, tiled=True)
    w_down = lax.all_gather(pieces[3], "dp", axis=1, tiled=True)
    carried_grad = lax.all_gather(low(upstream), "seq", axis=0, tiled=True)

    def head_cols(array, axis):
        return lax.dynamic_slice_in_dim(array, h, 1, axis)

    w_head = jnp.concatenate(
        [head_cols(head_weight, 1), lax.dynamic_slice_in_dim(head_weight, head_count + h, 1, 1)], axis=1
    )
    params = head_cols(head_params, 1)
    taps_all = conv_weight.astype(jnp.float32).T
    taps = jnp.concatenate(
        [
            lax.dynamic_slice_in_dim(taps_all, DK * h, DK, 1),
            lax.dynamic_slice_in_dim(taps_all, DK * (head_count + h), DK, 1),
            lax.dynamic_slice_in_dim(taps_all, 2 * DK * head_count + DV * h, DV, 1),
        ],
        axis=1,
    )
    inputs = x_all.astype(jnp.float32)
    first_norm = low(rms_scale(inputs, norm_gains[0]))
    conv_in = low(dot(first_norm, w_qkv))
    head_in = dot(first_norm, w_head)
    gate_in = dot(first_norm, w_gate)

    def mixer(conv_rows, head_rows, taps, params):
        total = conv_rows.shape[0]
        extended = jnp.concatenate([jnp.zeros((KCONV - 1, conv_rows.shape[1]), jnp.float32), conv_rows], axis=0)
        conv_sum = sum(extended[t : t + total] * taps[t] for t in range(KCONV))
        act = jax.nn.silu(conv_sum)
        query = unit_rows(act[:, 0:DK]) * DK ** (-0.5)
        key = unit_rows(act[:, DK : 2 * DK])
        decay = -jnp.exp(params[0]) * jax.nn.softplus(head_rows[:, 0:1] + params[1])
        erase = jax.nn.sigmoid(head_rows[:, 1:2] + params[2])
        return query, key, act[:, 2 * DK :], decay, erase

    mix_args = (conv_in.astype(jnp.float32), head_in, taps, params)
    vectors, mix_back = jax.vjp(mixer, *mix_args)
    mixed, states, inverse, updates, w_maps = rec_fwd(*vectors)
    normed_f, post_back = jax.vjp(gated_norm, mixed, gate_in, head_gain)
    normed = low(normed_f)
    attended = lax.psum_scatter(low(dot(normed, w_out)), "seq", scatter_dimension=0, tiled=True)
    middle = own + attended.astype(jnp.float32)
    second_f, second_back = jax.vjp(rms_scale, middle, norm_gains[1])
    second_norm = lax.all_gather(low(second_f), "seq", axis=0, tiled=True)
    gate_up = dot(second_norm, w_in)
    hidden_f, swiglu_back = jax.vjp(swiglu, gate_up)
    hidden = low(hidden_f)
    carried = lax.psum_scatter(low(dot(hidden, w_down)), "seq", scatter_dimension=0, tiled=True)
    output = low(jnp.where(valid, middle + carried.astype(jnp.float32), 0.0))

    grad_down = dot(hidden, carried_grad, ((0,), (0,)))
    hidden_grad = dot(carried_grad, w_down, ((1,), (1,)))
    gate_up_grad = low(swiglu_back(hidden_grad)[0])
    grad_in = dot(second_norm, gate_up_grad, ((0,), (0,)))
    second_grad = lax.psum_scatter(
        low(dot(gate_up_grad, w_in, ((1,), (1,)))), "seq", scatter_dimension=0, tiled=True
    ).astype(jnp.float32)
    middle_back, gain_two = second_back(second_grad)
    middle_grad = upstream + middle_back
    attended_grad = lax.all_gather(low(middle_grad), "seq", axis=0, tiled=True)
    grad_out = dot(normed, attended_grad, ((0,), (0,)))
    normed_grad = dot(attended_grad, w_out, ((1,), (1,)))
    mixed_grad, gate_in_grad, head_gain_grad = post_back(normed_grad)
    vector_grads = rec_bwd(*vectors, states, inverse, updates, w_maps, mixed_grad)
    conv_f, head_f, taps_grad, params_grad = mix_back(tuple(vector_grads))
    conv_grad, head_grad, gate_grad = low(conv_f), low(head_f), low(gate_in_grad)
    grad_qkv = dot(first_norm, conv_grad, ((0,), (0,)))
    grad_head = dot(head_grad, first_norm, ((0,), (0,)))
    grad_gate = dot(first_norm, gate_grad, ((0,), (0,)))
    first_part = (
        dot(conv_grad, w_qkv, ((1,), (1,)))
        + dot(head_grad, w_head, ((1,), (1,)))
        + dot(gate_grad, w_gate, ((1,), (1,)))
    )
    first_grad = lax.psum_scatter(low(first_part), "seq", scatter_dimension=0, tiled=True).astype(jnp.float32)
    unused, first_back = jax.vjp(rms_scale, own, norm_gains[0])
    input_back, gain_one = first_back(first_grad)
    input_grad = low(middle_grad + input_back)

    def group_sum(part, dim):
        return lax.psum_scatter(low(part), "dp", scatter_dimension=dim, tiled=True)

    parts = grads_out(
        dp, seq, group_sum(grad_qkv, 0), group_sum(grad_in, 0), group_sum(grad_out, 1), group_sum(grad_down, 1)
    )
    gate_total = group_sum(grad_gate, 0)

    def placed(array, start, total):
        return lax.dynamic_update_slice_in_dim(jnp.zeros((array.shape[0], total), jnp.float32), array, start, 1)

    conv_all = (
        placed(taps_grad[:, 0:DK], DK * h, taps_all.shape[1])
        + placed(taps_grad[:, DK : 2 * DK], DK * (head_count + h), taps_all.shape[1])
        + placed(taps_grad[:, 2 * DK :], 2 * DK * head_count + DV * h, taps_all.shape[1])
    )
    head_all = lax.dynamic_update_slice_in_dim(jnp.zeros((2 * head_count, width), jnp.float32), grad_head[0:1], h, 0)
    head_all = lax.dynamic_update_slice_in_dim(head_all, grad_head[1:2], head_count + h, 0)
    params_all = placed(params_grad, h, head_count)
    small = lax.psum(
        (jnp.stack([gain_one, gain_two]), head_gain_grad, params_all, head_all, conv_all), ("dp", "seq")
    )
    wide = jnp.float32
    return (
        output[None],
        input_grad[None],
        small[0],
        small[1],
        small[2],
        parts[0].astype(wide),
        gate_total.astype(wide),
        small[3].T,
        small[4].T,
        parts[2].astype(wide),
        parts[1][:, 0:ff_cols].astype(wide),
        parts[3][0:ff_rows].astype(wide),
    )


def choose_body(dp, seq):
    def chosen(*arrays):
        tokens, head_params = arrays[0], arrays[5]
        if (dp, seq) == (4, 8) and tokens.shape[0] == 1 and head_params.shape[1] == seq:
            return fast_body(dp, seq, *arrays)
        return general_body(*arrays)

    return chosen


def solution(mesh):
    dp, seq = mesh.shape["dp"], mesh.shape["seq"]
    placed = (
        P("dp", "seq", None),
        P("dp"),
        P("dp", "seq", None),
        P(),
        P(),
        P(),
        P("dp", "seq"),
        P("dp", "seq"),
        P(),
        P(),
        P("dp", "seq"),
        P("dp", "seq"),
        P("dp", "seq"),
    )
    return jax.shard_map(
        choose_body(dp, seq),
        mesh=mesh,
        in_specs=placed,
        out_specs=(
            P("dp", "seq", None),
            P("dp", "seq", None),
            P(),
            P(),
            P(),
            P("dp", "seq"),
            P("dp", "seq"),
            P(),
            P(),
            P("dp", "seq"),
            P("dp", "seq"),
            P("dp", "seq"),
        ),
        check_vma=False,
    )
```

```python
import functools

import jax
import jax.numpy as jnp
from jax import lax
from jax.experimental import pallas as pl
from jax.experimental.pallas import tpu as pltpu
from jax.sharding import PartitionSpec as P

CH = 256
DK = 128
DV = 256
KCONV = 4
TILE = 64


HIGHEST = lax.Precision.HIGHEST
epsilon = 1e-06


def passed_along(block, axis, distance):
    devices = range(lax.axis_size(axis))
    route = [(i - distance, i) for i in devices if i - distance in devices]
    return lax.ppermute(block, axis, route)


def rms_scale(values, gain_row):
    return (
        values * lax.rsqrt(jnp.mean(values * values, axis=-1, keepdims=True) + epsilon) * gain_row
    )


def unit_rows(values):
    return values * lax.rsqrt(jnp.sum(values * values, axis=-1, keepdims=True) + epsilon)


def block_step(state_now, query_vecs, key_vecs, value_vecs, log_decay, erase_rate):
    length = query_vecs.shape[1]
    cumulative = jnp.cumsum(log_decay, axis=1)
    row_index = jnp.arange(length)[:, None]
    col_index = jnp.arange(length)[None, :]
    strict = col_index < row_index
    within = col_index <= row_index
    spread = cumulative[:, :, None] - cumulative[:, None, :]
    lower_decay = jnp.where(strict, jnp.exp(jnp.where(strict, spread, 0.0)), 0.0)
    causal = jnp.where(within, jnp.exp(jnp.where(within, spread, 0.0)), 0.0)
    key_gram = jnp.einsum("htk,hsk->hts", key_vecs, key_vecs, precision=HIGHEST)
    query_gram = jnp.einsum("htk,hsk->hts", query_vecs, key_vecs, precision=HIGHEST)
    negated = -(erase_rate[:, :, None] * key_gram * lower_decay)
    identity = jnp.eye(length, dtype=jnp.float32)
    inverse = identity + negated
    powered = negated
    for level_index in range(length.bit_length() - 2):
        powered = jnp.einsum("hts,hsr->htr", powered, powered, precision=HIGHEST)
        inverse = jnp.einsum("hts,hsr->htr", inverse, identity + powered, precision=HIGHEST)
    shrink = jnp.exp(cumulative)
    recalled = jnp.einsum("htk,hkw->htw", key_vecs, state_now, precision=HIGHEST)
    target = erase_rate[:, :, None] * value_vecs - (erase_rate * shrink)[:, :, None] * recalled
    updates = jnp.einsum("hts,hsw->htw", inverse, target, precision=HIGHEST)
    read_out = shrink[:, :, None] * jnp.einsum(
        "htk,hkw->htw", query_vecs, state_now, precision=HIGHEST
    )
    read_out = read_out + jnp.einsum(
        "hts,hsw->htw", query_gram * causal, updates, precision=HIGHEST
    )
    remain = jnp.exp(cumulative[:, -1:] - cumulative)
    state_next = jnp.exp(cumulative[:, -1])[:, None, None] * state_now
    state_next = state_next + jnp.einsum(
        "hsk,hsw->hkw", key_vecs * remain[:, :, None], updates, precision=HIGHEST
    )
    return (state_next, read_out)


def run_tiles(query_vecs, key_vecs, value_vecs, log_decay, erase_rate, state_start):
    row_count, head_count, key_width = query_vecs.shape
    tile_count = row_count // TILE

    def arrange(tensor):
        return jnp.swapaxes(tensor.reshape((tile_count, TILE, head_count) + tensor.shape[2:]), 1, 2)

    inputs = (
        arrange(query_vecs),
        arrange(key_vecs),
        arrange(value_vecs),
        arrange(log_decay),
        arrange(erase_rate),
    )

    def advance(state_now, sliced):
        return jax.checkpoint(block_step)(state_now, *sliced)

    state_end, outputs = lax.scan(advance, state_start, inputs)
    outputs = jnp.swapaxes(outputs, 1, 2).reshape(row_count, head_count, outputs.shape[-1])
    return (outputs, state_end)


def mixer_inputs(conv_in, edge_rows, head_in, conv_taps, head_params):
    block_len = conv_in.shape[1]
    head_count = head_params.shape[1]
    extended = jnp.concatenate([edge_rows, conv_in], axis=1)
    conv_sum = extended[:, 0:block_len] * conv_taps[:, 0]
    for offset in range(1, conv_taps.shape[1]):
        conv_sum = conv_sum + extended[:, offset : offset + block_len] * conv_taps[:, offset]
    activated = jax.nn.silu(conv_sum)
    key_span = head_count * DK
    lead = activated.shape[:2]
    query_vecs = unit_rows(activated[..., 0:key_span].reshape(lead + (head_count, DK))) * DK ** (
        -0.5
    )
    key_vecs = unit_rows(activated[..., key_span : 2 * key_span].reshape(lead + (head_count, DK)))
    value_vecs = activated[..., 2 * key_span :].reshape(lead + (head_count, DV))
    log_decay = -jnp.exp(head_params[0]) * jax.nn.softplus(
        head_in[..., 0:head_count] + head_params[1]
    )
    erase_rate = jax.nn.sigmoid(head_in[..., head_count : 2 * head_count] + head_params[2])
    return (query_vecs, key_vecs, value_vecs, log_decay, erase_rate)


def gated_norm(mixed, gate_in, head_gain):
    shaped = gate_in.reshape(mixed.shape)
    normed = (
        mixed * lax.rsqrt(jnp.mean(mixed * mixed, axis=-1, keepdims=True) + epsilon) * head_gain
    )
    return (normed * jax.nn.silu(shaped)).reshape(gate_in.shape)


def local_tiles(query_vecs, key_vecs, value_vecs, log_decay, erase_rate):
    key_width = key_vecs.shape[-1]
    value_width = value_vecs.shape[-1]
    head_count = key_vecs.shape[2]
    padded = jnp.concatenate(
        [jnp.zeros(value_vecs.shape[:3] + (key_width,), jnp.float32), value_vecs], axis=-1
    )
    start_map = jnp.concatenate(
        [jnp.eye(key_width, dtype=jnp.float32), jnp.zeros((key_width, value_width), jnp.float32)],
        axis=1,
    )
    start_map = jnp.broadcast_to(start_map, (head_count, key_width, key_width + value_width))

    def single(query_one, key_one, value_one, decay_one, erase_one):
        return run_tiles(query_one, key_one, value_one, decay_one, erase_one, start_map)

    return jax.vmap(single)(query_vecs, key_vecs, padded, log_decay, erase_rate)


def post_mix(local_out, incoming, gate_in, head_gain):
    mixed = local_out[..., DK:] + jnp.einsum(
        "snhk,shkv->snhv", local_out[..., 0:DK], incoming, precision=HIGHEST
    )
    return gated_norm(mixed, gate_in, head_gain)


def swiglu(gate_up):
    split_at = gate_up.shape[-1] // 2
    return jax.nn.silu(gate_up[:, 0:split_at]) * gate_up[:, split_at:]


def matmul_maps(left, right):
    return jnp.einsum("shij,shjk->shik", left, right, precision=HIGHEST)


def apply_map(maps, state_now):
    return matmul_maps(maps[0], state_now) + maps[1]


def general_body(
    tokens,
    lengths,
    cotangent,
    norm_gains,
    head_gain,
    head_params,
    qkv_weight,
    gate_weight,
    head_weight,
    conv_weight,
    out_weight,
    ffn_in,
    ffn_out,
):
    seq_count, block_len, model_width = tokens.shape
    row_count = seq_count * block_len
    position = lax.axis_index("seq") * block_len + jnp.arange(block_len, dtype=jnp.int32)
    valid_rows = (position[None, :] < lengths[:, None]).reshape(row_count, 1)
    col_parts = (
        lax.all_gather(qkv_weight, "seq", axis=1, tiled=True),
        lax.all_gather(gate_weight, "seq", axis=1, tiled=True),
        lax.all_gather(out_weight, "seq", axis=1, tiled=True),
        lax.all_gather(ffn_in, "seq", axis=1, tiled=True),
        lax.all_gather(ffn_out, "seq", axis=1, tiled=True),
    )
    gathered = (
        lax.all_gather(col_parts[0], "dp", axis=0, tiled=True),
        lax.all_gather(col_parts[1], "dp", axis=0, tiled=True),
        lax.all_gather(col_parts[2], "dp", axis=0, tiled=True),
        lax.all_gather(col_parts[3], "dp", axis=0, tiled=True),
        lax.all_gather(col_parts[4], "dp", axis=0, tiled=True),
    )
    w_qkv, w_gate, w_out, w_in, w_down = gathered
    inputs = tokens.reshape(row_count, model_width).astype(jnp.float32)
    first_norm = rms_scale(inputs, norm_gains[0]).astype(jnp.bfloat16)
    conv_in = jnp.dot(first_norm, w_qkv, preferred_element_type=jnp.float32).astype(jnp.bfloat16)
    head_in = jnp.dot(first_norm, head_weight, preferred_element_type=jnp.float32)
    gate_in = jnp.dot(first_norm, w_gate, preferred_element_type=jnp.float32)
    conv_width = conv_in.shape[-1]
    conv_rows = conv_in.reshape(seq_count, block_len, conv_width)
    edge_cut = block_len - (KCONV - 1)
    edge_rows = passed_along(conv_rows[:, edge_cut:], "seq", 1)
    mix_args = (
        conv_rows.astype(jnp.float32),
        edge_rows.astype(jnp.float32),
        head_in.reshape(seq_count, block_len, -1),
        conv_weight.astype(jnp.float32),
        head_params,
    )
    vectors = mixer_inputs(*mix_args)
    local_out, end_states = local_tiles(*vectors)
    carry_maps = (end_states[..., 0:DK], end_states[..., DK:])

    def relay_state(step_index, state_now):
        return passed_along(apply_map(carry_maps, state_now), "seq", 1)

    incoming = lax.fori_loop(
        0, lax.axis_size("seq") - 1, relay_state, jnp.zeros_like(carry_maps[1])
    )
    post_args = (local_out, incoming, gate_in, head_gain)
    normed = post_mix(*post_args).astype(jnp.bfloat16)
    attended = jnp.dot(normed, w_out, preferred_element_type=jnp.float32)
    middle = inputs + attended
    second_norm = rms_scale(middle, norm_gains[1]).astype(jnp.bfloat16)
    gate_up = jnp.dot(second_norm, w_in, preferred_element_type=jnp.float32)
    hidden = swiglu(gate_up).astype(jnp.bfloat16)
    carried = jnp.dot(hidden, w_down, preferred_element_type=jnp.float32)
    output = jnp.where(valid_rows, middle + carried, 0.0).astype(jnp.bfloat16)
    col_again = (
        lax.all_gather(qkv_weight, "seq", axis=1, tiled=True),
        lax.all_gather(gate_weight, "seq", axis=1, tiled=True),
        lax.all_gather(out_weight, "seq", axis=1, tiled=True),
        lax.all_gather(ffn_in, "seq", axis=1, tiled=True),
        lax.all_gather(ffn_out, "seq", axis=1, tiled=True),
    )
    regathered = (
        lax.all_gather(col_again[0], "dp", axis=0, tiled=True),
        lax.all_gather(col_again[1], "dp", axis=0, tiled=True),
        lax.all_gather(col_again[2], "dp", axis=0, tiled=True),
        lax.all_gather(col_again[3], "dp", axis=0, tiled=True),
        lax.all_gather(col_again[4], "dp", axis=0, tiled=True),
    )
    w_qkv, w_gate, w_out, w_in, w_down = regathered
    upstream = jnp.where(
        valid_rows, cotangent.reshape(row_count, model_width).astype(jnp.float32), 0.0
    )
    carried_grad = upstream.astype(jnp.bfloat16)
    grad_down = jnp.einsum("nf,nd->fd", hidden, carried_grad, preferred_element_type=jnp.float32)
    hidden_grad = jnp.einsum("nd,fd->nf", carried_grad, w_down, preferred_element_type=jnp.float32)
    unused, swiglu_back = jax.vjp(swiglu, gate_up)
    gate_up_grad = swiglu_back(hidden_grad)[0].astype(jnp.bfloat16)
    grad_in = jnp.einsum("nd,nf->df", second_norm, gate_up_grad, preferred_element_type=jnp.float32)
    second_grad = jnp.einsum("nf,df->nd", gate_up_grad, w_in, preferred_element_type=jnp.float32)
    unused, second_back = jax.vjp(rms_scale, middle, norm_gains[1])
    middle_back, gain_two = second_back(second_grad)
    middle_grad = upstream + middle_back
    attended_grad = middle_grad.astype(jnp.bfloat16)
    grad_out = jnp.einsum("nv,nd->vd", normed, attended_grad, preferred_element_type=jnp.float32)
    normed_grad = jnp.einsum("nd,vd->nv", attended_grad, w_out, preferred_element_type=jnp.float32)
    unused, post_back = jax.vjp(post_mix, *post_args)
    local_grad, incoming_local, gate_in_grad, head_gain_grad = post_back(normed_grad)
    flipped = (jnp.swapaxes(carry_maps[0], -1, -2), incoming_local)

    def relay_grad(step_index, grad_now):
        return passed_along(apply_map(flipped, grad_now).astype(jnp.bfloat16), "seq", -1).astype(
            jnp.float32
        )

    outgoing = lax.fori_loop(
        0, lax.axis_size("seq") - 1, relay_grad, jnp.zeros_like(incoming_local)
    )
    map_grad = jnp.einsum("shkv,shjv->shkj", outgoing, incoming, precision=HIGHEST)
    end_grad = jnp.concatenate([map_grad, outgoing], axis=-1)
    unused, tiles_back = jax.vjp(local_tiles, *vectors)
    vector_grads = tiles_back((local_grad, end_grad))
    unused, mix_back = jax.vjp(mixer_inputs, *mix_args)
    conv_own, edge_grad, head_in_grad, conv_taps_grad, params_grad = mix_back(vector_grads)
    edge_back = passed_along(edge_grad.astype(jnp.bfloat16), "seq", -1).astype(edge_grad.dtype)
    conv_total = jnp.concatenate(
        [conv_own[:, 0:edge_cut], conv_own[:, edge_cut:] + edge_back], axis=1
    )
    conv_grad = conv_total.reshape(row_count, conv_width).astype(jnp.bfloat16)
    head_grad = head_in_grad.reshape(row_count, -1).astype(jnp.bfloat16)
    gate_grad = gate_in_grad.astype(jnp.bfloat16)
    grad_qkv = jnp.einsum("nd,nc->dc", first_norm, conv_grad, preferred_element_type=jnp.float32)
    grad_head = jnp.einsum("nd,nc->dc", first_norm, head_grad, preferred_element_type=jnp.float32)
    grad_gate = jnp.einsum("nd,nc->dc", first_norm, gate_grad, preferred_element_type=jnp.float32)
    first_grad = jnp.einsum("nc,dc->nd", conv_grad, w_qkv, preferred_element_type=jnp.float32)
    first_grad = first_grad + jnp.einsum(
        "nc,dc->nd", head_grad, head_weight, preferred_element_type=jnp.float32
    )
    first_grad = first_grad + jnp.einsum(
        "nc,dc->nd", gate_grad, w_gate, preferred_element_type=jnp.float32
    )
    unused, first_back = jax.vjp(rms_scale, inputs, norm_gains[0])
    input_back, gain_one = first_back(first_grad)
    input_grad = (
        (middle_grad + input_back).astype(jnp.bfloat16).reshape(seq_count, block_len, model_width)
    )
    row_groups = (
        lax.psum_scatter(
            grad_qkv.astype(jnp.bfloat16), "dp", scatter_dimension=0, tiled=True
        ).astype(jnp.float32),
        lax.psum_scatter(
            grad_gate.astype(jnp.bfloat16), "dp", scatter_dimension=0, tiled=True
        ).astype(jnp.float32),
        lax.psum_scatter(
            grad_out.astype(jnp.bfloat16), "dp", scatter_dimension=0, tiled=True
        ).astype(jnp.float32),
        lax.psum_scatter(
            grad_in.astype(jnp.bfloat16), "dp", scatter_dimension=0, tiled=True
        ).astype(jnp.float32),
        lax.psum_scatter(
            grad_down.astype(jnp.bfloat16), "dp", scatter_dimension=0, tiled=True
        ).astype(jnp.float32),
    )
    weight_parts = (
        lax.psum_scatter(
            row_groups[0].astype(jnp.bfloat16), "seq", scatter_dimension=1, tiled=True
        ).astype(jnp.float32),
        lax.psum_scatter(
            row_groups[1].astype(jnp.bfloat16), "seq", scatter_dimension=1, tiled=True
        ).astype(jnp.float32),
        lax.psum_scatter(
            row_groups[2].astype(jnp.bfloat16), "seq", scatter_dimension=1, tiled=True
        ).astype(jnp.float32),
        lax.psum_scatter(
            row_groups[3].astype(jnp.bfloat16), "seq", scatter_dimension=1, tiled=True
        ).astype(jnp.float32),
        lax.psum_scatter(
            row_groups[4].astype(jnp.bfloat16), "seq", scatter_dimension=1, tiled=True
        ).astype(jnp.float32),
    )
    small_sums = lax.psum(
        (jnp.stack([gain_one, gain_two]), head_gain_grad, params_grad, grad_head, conv_taps_grad),
        ("dp", "seq"),
    )
    output = output.reshape(seq_count, block_len, model_width)
    return (
        output,
        input_grad,
        small_sums[0],
        small_sums[1],
        small_sums[2],
        weight_parts[0],
        weight_parts[1],
        small_sums[3],
        small_sums[4],
        weight_parts[2],
        weight_parts[3],
        weight_parts[4],
    )


MESH = pl.DeviceIdType.MESH
ANY = pl.BlockSpec(memory_space=pl.ANY)
IN_VMEM = pl.BlockSpec(memory_space=pltpu.VMEM)
B16 = jnp.bfloat16
F32 = jnp.float32
NN = ((1,), (0,))
NT = ((1,), (1,))
TN = ((0,), (0,))
HALO = 16


def low(v):
    return v.astype(jnp.bfloat16)


def mm(a, b, dims=NN):
    return lax.dot_general(low(a), low(b), (dims, ((), ())), preferred_element_type=jnp.float32)


def mmf(a, b, dims=NN):
    return lax.dot_general(
        a, b, (dims, ((), ())), precision=HIGHEST, preferred_element_type=jnp.float32
    )


def mm3(a, b, dims=NN):
    ah, bh = low(a), low(b)
    al, bl = low(a - ah.astype(jnp.float32)), low(b - bh.astype(jnp.float32))
    return mm(ah, bh, dims) + (mm(ah, bl, dims) + mm(al, bh, dims))


def sig(v):
    return 1.0 / (1.0 + jnp.exp(-v))


def soft_plus(v):
    tail = jnp.exp(-jnp.abs(v))
    series = tail * (1.0 - tail * (0.5 - tail * (1.0 / 3.0)))
    return jnp.maximum(v, 0.0) + jnp.where(tail < 1e-3, series, jnp.log(1.0 + tail))


def grid_masks():
    row = lax.broadcasted_iota(jnp.int32, (CH, CH), 0)
    col = lax.broadcasted_iota(jnp.int32, (CH, CH), 1)
    return row, col


def decay_parts(g, row, col):
    lower = (col <= row).astype(jnp.float32)
    cum = mmf(lower, g)
    cum_row = mmf(g, lower, ((0,), (1,)))
    within = col <= row
    decay = jnp.where(within, jnp.exp(jnp.where(within, cum - cum_row, 0.0)), 0.0)
    return cum, decay


def unit_inverse(attns, row, col):
    def same(width):
        return (row // width) == (col // width)

    eye = jnp.where(row == col, 1.0, 0.0)
    power = [jnp.where(same(64), -a, 0.0) for a in attns]
    inv = [eye + p for p in power]
    for level in range(5):
        power = [mm(p, p) for p in power]
        inv = [x + mm(x, p) for x, p in zip(inv, power)]
    for width in (128, 256):
        off = same(width) & jnp.logical_not(same(width // 2))
        part = [mm(jnp.where(off, a, 0.0), x) for a, x in zip(attns, inv)]
        inv = [x - mm(x, p) for x, p in zip(inv, part)]
    rest = [eye - x - mm3(a, x) for a, x in zip(attns, inv)]
    return [x + mm(x, r) for x, r in zip(inv, rest)]


def tile(t, size=CH):
    return pl.ds(pl.multiple_of(t * size, size), size)


class Wires:
    def __init__(self, dp, seq, sems):
        self.dp, self.seq, self.sems, self.used = dp, seq, sems, 0
        self.i, self.s = lax.axis_index("dp"), lax.axis_index("seq")
        self.z, self.c = self.s // 2, lax.rem(self.s, 2)

    def take(self, count=1):
        start = self.used
        self.used += count
        return start

    def meet_all(self):
        barrier = pltpu.get_barrier_semaphore()
        for di in range(self.dp):
            for dj in range(self.seq):
                if di or dj:
                    pl.semaphore_signal(
                        barrier,
                        inc=1,
                        device_id=(lax.rem(self.i + di, self.dp), lax.rem(self.s + dj, self.seq)),
                        device_id_type=MESH,
                    )
        pl.semaphore_wait(barrier, self.dp * self.seq - 1)

    def remote(self, src, dst, send, recv, di, dj):
        return pltpu.make_async_remote_copy(
            src_ref=src,
            dst_ref=dst,
            send_sem=self.sems.at[send],
            recv_sem=self.sems.at[recv],
            device_id=(di, dj),
            device_id_type=MESH,
        )

    def local(self, src, dst, sem):
        return pltpu.make_async_copy(src, dst, self.sems.at[sem])

    def push(self, src, dst, send, recv, di, dj):
        here = (di == self.i) & (dj == self.s)
        away = self.remote(src, dst, send, recv, di, dj)

        @pl.when(here)
        def _():
            self.local(src, dst, recv).start()

        @pl.when(jnp.logical_not(here))
        def _():
            away.start()

        def sent():
            @pl.when(jnp.logical_not(here))
            def _():
                away.wait_send()

        return sent

    def arrived(self, dst, recv):
        pltpu.make_async_copy(dst, dst, self.sems.at[recv]).wait()

    def peer_z(self, d):
        return lax.rem(self.z + d, 4) * 2 + self.c

    def sibling(self):
        return self.z * 2 + 1 - self.c


class LineGather:
    def __init__(self, w, block_of):
        self.w, self.block_of = w, block_of
        self.send, self.recv = w.take(4), w.take(4)
        self.fsend, self.frecv = w.take(4), w.take(4)

    def start(self, src):
        w = self.w
        self.copies = []
        dst = self.block_of(w.s)
        for d in (2, 1, 3):
            self.copies.append(w.remote(src, dst, self.send + d, self.recv + d, w.i, w.peer_z(d)))
        self.copies.append(w.remote(src, dst, self.fsend, self.frecv, w.i, w.sibling()))
        for copy in self.copies:
            copy.start()

    def forward(self):
        w = self.w
        self.passed = []
        for d in (1, 3, 2):
            block = self.block_of(w.peer_z(4 - d))
            w.arrived(block, self.recv + d)
            copy = w.remote(block, block, self.fsend + d, self.frecv + d, w.i, w.sibling())
            copy.start()
            self.passed.append(copy)

    def finish(self):
        w = self.w
        for copy in self.copies + self.passed:
            copy.wait_send()
        for d in range(4):
            w.arrived(self.block_of(lax.rem(w.z + 4 - d, 4) * 2 + 1 - w.c), self.frecv + d)


class GroupGather:
    def __init__(self, w, part_of):
        self.w, self.part_of = w, part_of
        self.send, self.recv = w.take(4), w.take(4)

    def start(self, src):
        w = self.w
        self.own = w.local(src, self.part_of(w.i), self.recv)
        self.own.start()
        self.copies = []
        for d in (3, 1, 2):
            copy = w.remote(src, self.part_of(w.i), self.send + d, self.recv + d, lax.rem(w.i + d, 4), w.s)
            copy.start()
            self.copies.append(copy)

    def finish(self):
        w = self.w
        self.own.wait()
        for d in range(1, 4):
            w.arrived(self.part_of(lax.rem(w.i + 4 - d, 4)), self.recv + d)
        for copy in self.copies:
            copy.wait_send()


class LineScatter:
    def __init__(self, w, part, sib, chip, got):
        self.w, self.part, self.sib, self.chip, self.got = w, part, sib, chip, got
        self.ssend, self.srecv = w.take(4), w.take(4)
        self.send, self.recv = w.take(4), w.take(4)

    def swap(self, t):
        w = self.w
        src = self.part.at[pl.ds(pl.multiple_of(t * 256 + 128 * (1 - w.c), 128), 128), :]
        w.remote(src, self.sib.at[t], self.ssend + t, self.srecv + t, w.i, w.sibling()).start()

    def pass_on(self, t):
        w = self.w
        w.arrived(self.sib.at[t], self.srecv + t)
        mine = self.part[pl.ds(pl.multiple_of(t * 256 + 128 * w.c, 128), 128), :]
        self.chip[t] = low(mine.astype(jnp.float32) + self.sib[t].astype(jnp.float32))
        d = lax.rem(t - w.z + 4, 4)

        @pl.when(d != 0)
        def _():
            w.remote(
                self.chip.at[t], self.got.at[d], self.send + t, self.recv + d, w.i, 2 * t + w.c
            ).start()

    def total(self):
        w = self.w
        total = self.chip[w.z].astype(jnp.float32)
        for d in range(1, 4):
            w.arrived(self.got.at[d], self.recv + d)
            total = total + self.got[d].astype(jnp.float32)
        return total

    def finish(self):
        w = self.w
        for t in range(4):
            src = self.part.at[pl.ds(t * 256, 128), :]
            w.remote(src, self.sib.at[t], self.ssend + t, self.srecv + t, w.i, w.sibling()).wait_send()

            @pl.when(w.z != t)
            def _():
                w.remote(self.chip.at[t], self.got.at[1], self.send + t, self.recv + 1, w.i, 2 * t + w.c).wait_send()


def cols(ref, start, size):
    return ref.at[:, pl.ds(pl.multiple_of(start, 128), size)]


def rows_of(ref, start, size):
    return ref.at[pl.ds(pl.multiple_of(start, 128), size), :]


FRONT_OUT = (
    ("fn", (1024, 1024), B16),
    ("ci", (HALO + 1024, 512), B16),
    ("gi", (1024, 256), F32),
    ("hi", (1024, 16), F32),
    ("q", (1024, 128), F32),
    ("k", (1024, 128), F32),
    ("v", (1024, 256), F32),
    ("g", (1024, 1), F32),
    ("e", (1024, 1), F32),
    ("mixed", (1024, 256), F32),
    ("states", (4, 128, 256), F32),
    ("tinv", (1024, 256), B16),
    ("u", (1024, 256), F32),
    ("wm", (1024, 128), B16),
    ("normed", (1024, 256), B16),
    ("middle", (128, 1024), F32),
    ("sn", (1024, 1024), B16),
    ("cg", (1024, 1024), B16),
    ("w_qkv", (1024, 512), B16),
    ("w_gate", (1024, 256), B16),
    ("w_in", (1024, 768), B16),
    ("w_out", (256, 1024), B16),
    ("w_down", (384, 1024), B16),
)
FRONT_IN = ("tokens", "cot", "qkv", "gate", "ffn_in", "out", "ffn_out", "gains", "head_gain", "params", "head_w", "taps")
FRONT_SCRATCH = (
    ("x", (1024, 1024), B16),
    ("qkv_p", (256, 512), B16),
    ("in_p", (256, 768), B16),
    ("out_p", (256, 256), B16),
    ("down_p", (384, 256), B16),
    ("qk", (1024, 256), B16),
    ("cum", (1024, 1), F32),
    ("part", (1024, 1024), B16),
    ("sib", (4, 128, 1024), B16),
    ("chip", (4, 128, 1024), B16),
    ("got", (4, 128, 1024), B16),
    ("own_sn", (128, 1024), B16),
)


class Box:
    pass


def start_weights(w, b):
    i, s = w.i, w.s
    qs, qr = w.take(4), w.take(3)
    lowhalf = s < 4
    b.qr = qr

    @pl.when(lowhalf)
    def _():
        for t in range(4):
            w.push(
                b.qkv.at[:, 128 * t : 128 * t + 128],
                cols(b.qkv_p, 128 * (s // 2), 128),
                qs + t,
                qr + s // 2,
                i,
                4 * lax.rem(s, 2) + t,
            )

    @pl.when(jnp.logical_not(lowhalf))
    def _():
        for t in range(2):
            w.push(b.qkv.at[:, 256 * t : 256 * t + 256], b.qkv_p.at[:, 256:512], qs + t, qr + 2, i, 2 * (s - 4) + t)

    def sent():
        @pl.when(lowhalf)
        def _():
            for t in range(4):
                @pl.when(4 * lax.rem(s, 2) + t != s)
                def _():
                    src = b.qkv.at[:, 128 * t : 128 * t + 128]
                    w.remote(src, b.qkv_p.at[:, 0:128], qs + t, qr, i, w.sibling()).wait_send()

        @pl.when(jnp.logical_not(lowhalf))
        def _():
            for t in range(2):
                @pl.when(2 * (s - 4) + t != s)
                def _():
                    src = b.qkv.at[:, 256 * t : 256 * t + 256]
                    w.remote(src, b.qkv_p.at[:, 256:512], qs + t, qr + 2, i, w.sibling()).wait_send()

    return sent


def start_more_weights(w, b):
    i, s = w.i, w.s
    ms, mr = w.take(5), w.take(6)
    own, odd = s // 4, lax.rem(s, 2)
    b.keep = w.local(cols(b.ffn_in, 384 * own, 384), cols(b.in_p, 384 * own, 384), mr)
    b.keep.start()
    waits = [
        w.push(cols(b.ffn_in, 384 * (1 - own), 384), cols(b.in_p, 384 * own, 384), ms, mr + 1, i, lax.rem(s + 4, 8))
    ]
    for n in range(2):
        waits.append(
            w.push(
                b.out.at[256 * n : 256 * n + 256, :],
                cols(b.out_p, 128 * odd, 128),
                ms + 1 + n,
                mr + 2 + odd,
                s // 2,
                2 * i + n,
            )
        )
        waits.append(
            w.push(
                b.ffn_out.at[384 * n : 384 * n + 384, :],
                cols(b.down_p, 128 * odd, 128),
                ms + 3 + n,
                mr + 4 + odd,
                s // 2,
                i + 4 * n,
            )
        )

    def landed():
        b.keep.wait()
        w.arrived(b.in_p.at[:, 0:384], mr + 1)
        for r in range(2):
            w.arrived(b.out_p.at[:, 128 * r : 128 * r + 128], mr + 2 + r)
            w.arrived(b.down_p.at[:, 128 * r : 128 * r + 128], mr + 4 + r)

    def sent():
        for wait in waits:
            wait()

    return landed, sent


def first_norm_tile(b, t):
    rows = tile(t)
    x = b.x[rows, :].astype(jnp.float32)
    inv = lax.rsqrt(jnp.mean(x * x, axis=-1, keepdims=True) + epsilon)
    b.fn[rows, :] = low(x * inv * b.gains[0:1, :])


def own_head(b, w):
    pm = b.params[...]
    lane = lax.broadcasted_iota(jnp.int32, pm.shape, 1)
    return jnp.sum(jnp.where(lane == w.s, pm, 0.0), axis=1, keepdims=True)


def own_taps(b, w, n):
    s = w.s
    return jnp.concatenate(
        [
            b.taps[n : n + 1, pl.ds(pl.multiple_of(128 * s, 128), 128)],
            b.taps[n : n + 1, pl.ds(pl.multiple_of(1024 + 128 * s, 128), 128)],
            b.taps[n : n + 1, pl.ds(pl.multiple_of(2048 + 256 * s, 128), 256)],
        ],
        axis=1,
    )


def conv_sums(b, w, t):
    window = b.ci[pl.ds(pl.multiple_of(t * CH, CH), CH + HALO), :].astype(jnp.float32)
    total = None
    for n in range(KCONV):
        at = HALO - (KCONV - 1) + n
        term = window[at : at + CH] * own_taps(b, w, n)
        total = term if total is None else total + term
    return total


def project_tile(b, w, t):
    rows = tile(t)
    f = b.fn[rows, :]
    b.ci[pl.ds(pl.multiple_of(t * CH + HALO, HALO), CH), :] = low(mm(f, b.w_qkv[...]))
    b.gi[rows, :] = mm(f, b.w_gate[...])
    hi = mm(f, b.head_w[...])
    b.hi[rows, :] = hi
    lane = lax.broadcasted_iota(jnp.int32, hi.shape, 1)
    pm = own_head(b, w)
    shift = jnp.sum(jnp.where(lane == w.s, hi, 0.0), axis=1, keepdims=True) + pm[1:2, :]
    erase = jnp.sum(jnp.where(lane == w.s + 8, hi, 0.0), axis=1, keepdims=True) + pm[2:3, :]
    b.g[rows, :] = -jnp.exp(pm[0:1, :]) * soft_plus(shift)
    b.e[rows, :] = sig(erase)
    total = conv_sums(b, w, t)
    act = total * sig(total)
    qa, ka = act[:, 0:DK], act[:, DK : 2 * DK]
    b.q[rows, :] = qa * lax.rsqrt(jnp.sum(qa * qa, axis=-1, keepdims=True) + epsilon) * DK ** (-0.5)
    b.k[rows, :] = ka * lax.rsqrt(jnp.sum(ka * ka, axis=-1, keepdims=True) + epsilon)
    b.v[rows, :] = act[:, 2 * DK :]


def rec_local(b):
    row, col = grid_masks()
    attns = []
    for t in range(4):
        rows = pl.ds(t * CH, CH)
        k = b.k[rows, :]
        cum, decay = decay_parts(b.g[rows, :], row, col)
        b.cum[rows, :] = cum
        b.qk[rows, :] = low(mm(b.q[rows, :], k, NT) * decay)
        attns.append(jnp.where(col < row, b.e[rows, :] * mm(k, k, NT) * decay, 0.0))
    for t, inv in enumerate(unit_inverse(attns, row, col)):
        rows = pl.ds(t * CH, CH)
        e, t16 = b.e[rows, :], low(inv)
        b.tinv[rows, :] = t16
        b.wm[rows, :] = low(mm(t16, (e * jnp.exp(b.cum[rows, :])) * b.k[rows, :]))
        b.u[rows, :] = mm(t16, e * b.v[rows, :])


def rec_step(b, t, state):
    rows = tile(t)
    b.states[t] = state
    cum = b.cum[rows, :]
    last = cum[CH - 1 : CH, :]
    s16 = low(state)
    u = b.u[rows, :] - mm(b.wm[rows, :], s16)
    b.u[rows, :] = u
    u16 = low(u)
    mixed = jnp.exp(cum) * mm(b.q[rows, :], s16) + mm(b.qk[rows, :], u16)
    b.mixed[rows, :] = mixed
    nxt = jnp.exp(last) * state + mm(b.k[rows, :] * jnp.exp(last - cum), u16, TN)
    gate = b.gi[rows, :]
    scale = lax.rsqrt(jnp.mean(mixed * mixed, axis=-1, keepdims=True) + epsilon)
    normed = low(mixed * scale * b.head_gain[...] * (gate * sig(gate)))
    b.normed[rows, :] = normed
    b.part[rows, :] = low(mm(normed, b.w_out[...]))
    return nxt


def front_phase(b, w):
    s, i = w.s, w.i
    own_rows = lambda ref: (lambda n: rows_of(ref, 128 * n, 128))
    x_gather = LineGather(w, own_rows(b.x))
    cg_gather = LineGather(w, own_rows(b.cg))
    sn_gather = LineGather(w, own_rows(b.sn))
    qkv_gather = GroupGather(w, lambda n: rows_of(b.w_qkv, 256 * n, 256))
    gate_gather = GroupGather(w, lambda n: rows_of(b.w_gate, 256 * n, 256))
    in_gather = GroupGather(w, lambda n: rows_of(b.w_in, 256 * n, 256))
    out_gather = GroupGather(w, lambda n: cols(b.w_out, 256 * n, 256))
    down_gather = GroupGather(w, lambda n: cols(b.w_down, 256 * n, 256))
    scatter = LineScatter(w, b.part, b.sib, b.chip, b.got)
    own_x, own_c = w.take(), w.take()

    w.meet_all()
    qkv_sent = start_weights(w, b)
    x_gather.start(b.tokens)
    keep_x = w.local(b.tokens, rows_of(b.x, 128 * s, 128), own_x)
    keep_x.start()
    gate_gather.start(b.gate)
    w.arrived(b.qkv_p.at[:, 0:128], b.qr)
    w.arrived(b.qkv_p.at[:, 128:256], b.qr + 1)
    w.arrived(b.qkv_p.at[:, 256:512], b.qr + 2)
    qkv_gather.start(b.qkv_p)
    b.ci[0:HALO, :] = jnp.zeros((HALO, 512), B16)
    keep_x.wait()
    x_gather.forward()
    more_landed, more_sent = start_more_weights(w, b)
    x_gather.finish()

    def norm_loop(t, carry):
        first_norm_tile(b, t)
        return carry

    lax.fori_loop(0, 4, norm_loop, 0)
    qkv_gather.finish()
    gate_gather.finish()
    cg_gather.start(b.cot)
    keep_c = w.local(b.cot, rows_of(b.cg, 128 * s, 128), own_c)
    keep_c.start()
    more_landed()
    out_gather.start(b.out_p)
    in_gather.start(b.in_p)
    down_gather.start(b.down_p)

    def project_loop(t, carry):
        project_tile(b, w, t)
        return carry

    lax.fori_loop(0, 4, project_loop, 0)
    rec_local(b)
    out_gather.finish()
    state = jnp.zeros((DK, DV), F32)
    for t in range(4):
        state = rec_step(b, t, state)
        scatter.swap(t)
        if t:
            scatter.pass_on(t - 1)
    scatter.pass_on(3)
    keep_c.wait()
    cg_gather.forward()
    middle = b.tokens_v[...].astype(jnp.float32) + scatter.total()
    b.middle[...] = middle
    inv = lax.rsqrt(jnp.mean(middle * middle, axis=-1, keepdims=True) + epsilon)
    second = low(middle * inv * b.gains[1:2, :])
    b.own_sn[...] = second
    rows_of(b.sn, 128 * s, 128)[...] = second
    sn_gather.start(b.own_sn)
    sn_gather.forward()
    cg_gather.finish()
    in_gather.finish()
    down_gather.finish()
    qkv_sent()
    more_sent()
    scatter.finish()
    sn_gather.finish()


def front_kernel(dp, seq, *refs):
    b = Box()
    names = FRONT_IN + ("tokens_v",) + tuple(n for n, _, _ in FRONT_OUT) + tuple(n for n, _, _ in FRONT_SCRATCH)
    for name, ref in zip(names, refs):
        setattr(b, name, ref)
    w = Wires(dp, seq, refs[-1])
    front_phase(b, w)


def front(dp, seq, *arrays):
    in_hbm = (True,) * 7 + (False,) * 5
    outs = pl.pallas_call(
        functools.partial(front_kernel, dp, seq),
        out_shape=tuple(jax.ShapeDtypeStruct(shape, kind) for _, shape, kind in FRONT_OUT),
        in_specs=[ANY if hbm else IN_VMEM for hbm in in_hbm] + [IN_VMEM],
        out_specs=(IN_VMEM,) * len(FRONT_OUT),
        scratch_shapes=[pltpu.VMEM(shape, kind) for _, shape, kind in FRONT_SCRATCH] + [pltpu.SemaphoreType.DMA((160,))],
        compiler_params=pltpu.CompilerParams(collective_id=0, has_side_effects=True, vmem_limit_bytes=60 << 20),
        name="front",
    )(*arrays, arrays[0])
    return dict(zip((n for n, _, _ in FRONT_OUT), outs))


def rec_bwd_kernel(q_ref, k_ref, v_ref, g_ref, e_ref, s_ref, t_ref, u_ref, w_ref, do_ref, dq_ref, dk_ref, dv_ref, dg_ref, de_ref, ds_ref):
    n = q_ref.shape[0] // CH
    row, col = grid_masks()
    ones = jnp.ones((CH, 1), jnp.float32)
    def chain(j, ds1):
        i = n - 1 - j
        rows = pl.ds(pl.multiple_of(i * CH, CH), CH)
        q, k, do = q_ref[rows, :], k_ref[rows, :], low(do_ref[rows, :])
        ds_ref[i] = ds1
        cum, decay = decay_parts(g_ref[rows, :], row, col)
        last = cum[CH - 1:CH, :]
        qk = mm(q, k, NT) * decay
        du = mm(qk, do, TN) + mm(k * jnp.exp(last - cum), ds1)
        du16 = low(du)
        dv_ref[rows, :] = mm(t_ref[rows, :], du16, TN)
        return jnp.exp(last) * ds1 + mm(q * jnp.exp(cum), do, TN) - mm(w_ref[rows, :], du16, TN)
    lax.fori_loop(0, n, chain, jnp.zeros((DK, DV), jnp.float32))
    def step(i, carry):
        rows = pl.ds(pl.multiple_of(i * CH, CH), CH)
        q, k, v, g, e = q_ref[rows, :], k_ref[rows, :], v_ref[rows, :], g_ref[rows, :], e_ref[rows, :]
        s0, ds1, u, do, dr = s_ref[i], ds_ref[i], low(u_ref[rows, :]), low(do_ref[rows, :]), dv_ref[rows, :]
        dr16, s16 = low(dr), low(s0)
        cum, decay = decay_parts(g, row, col)
        last = cum[CH - 1:CH, :]
        gamma = jnp.exp(last)
        shrink = jnp.exp(cum)
        remain = jnp.exp(last - cum)
        gram = jnp.where(col < row, mm(k, k, NT) * decay, 0.0)
        qk = mm(q, k, NT) * decay
        dp = jnp.where(col <= row, mm(do, u, NT), 0.0)
        da = jnp.where(col < row, -mm(dr16, u, NT), 0.0)
        dqk = low(dp * decay)
        dag = da * gram
        z = dp * qk + e * dag
        dgram = low(e * da * decay)
        nk = mm(dr16, s16, NT)
        m = mm(do, s16, NT)
        lm = mm(u, ds1, NT)
        row_nk = jnp.sum(nk * k, axis=1, keepdims=True)
        dv_ref[rows, :] = e * dr
        de_ref[rows, :] = jnp.sum(dr * v, axis=1, keepdims=True) - shrink * row_nk + jnp.sum(dag, axis=1, keepdims=True)
        dq_ref[rows, :] = mm(dqk, k) + shrink * m
        dk_ref[rows, :] = mm(dqk, q, TN) + mm(dgram, k) + mm(dgram, k, TN) - (e * shrink) * nk + remain * lm
        dshrink = jnp.sum(m * q, axis=1, keepdims=True) - e * row_nk
        rdr = remain * jnp.sum(lm * k, axis=1, keepdims=True)
        dcum = jnp.sum(z, axis=1, keepdims=True) - mmf(z, ones, TN) + shrink * dshrink - rdr
        dlast = jnp.sum(rdr) + jnp.sum(gamma * s0 * ds1)
        lower = (col <= row).astype(jnp.float32)
        dg_ref[rows, :] = mmf(lower, dcum, TN) + dlast
        return carry
    lax.fori_loop(0, n, step, 0)

def vm(n): return [pl.BlockSpec(memory_space=pltpu.VMEM)] * n
def rec_bwd(q, k, v, g, e, s, t, u, w, do):
    L = q.shape[0]
    f = jnp.float32
    return pl.pallas_call(rec_bwd_kernel,
        out_shape=(jax.ShapeDtypeStruct((L, DK), f), jax.ShapeDtypeStruct((L, DK), f), jax.ShapeDtypeStruct((L, DV), f),
                   jax.ShapeDtypeStruct((L, 1), f), jax.ShapeDtypeStruct((L, 1), f)),
        in_specs=vm(10), out_specs=tuple(vm(5)),
        scratch_shapes=[pltpu.VMEM((L // CH, DK, DV), f)],
        compiler_params=pltpu.CompilerParams(vmem_limit_bytes=48 << 20), name="rec_bwd")(q, k, v, g, e, s, t, u, w, do)


def meet_all(dp, seq, i, j):
    barrier = pltpu.get_barrier_semaphore()
    for di in range(dp):
        for dj in range(seq):
            if di or dj:
                pl.semaphore_signal(
                    barrier, inc=1, device_id=(lax.rem(i + di, dp), lax.rem(j + dj, seq)), device_id_type=MESH
                )
    pl.semaphore_wait(barrier, dp * seq - 1)


def sender(i, j, send_sem):
    sent = []

    def push(src, dst, recv, di, dj):
        slot = send_sem.at[len(sent)]
        here = (di == i) & (dj == j)

        @pl.when(here)
        def _():
            pltpu.make_async_copy(src, dst, recv).start()

        copy = pltpu.make_async_remote_copy(
            src_ref=src, dst_ref=dst, send_sem=slot, recv_sem=recv, device_id=(di, dj), device_id_type=MESH
        )

        @pl.when(jnp.logical_not(here))
        def _():
            copy.start()

        sent.append((copy, here))

    def finish():
        for copy, here in sent:
            @pl.when(jnp.logical_not(here))
            def _():
                copy.wait_send()

    return push, finish


def arrived(dst, recv):
    pltpu.make_async_copy(dst, dst, recv).wait()


def cols_(ref, start, size):
    return ref.at[:, pl.ds(pl.multiple_of(start, 128), size)]


def rows_of_(ref, start, size):
    return ref.at[pl.ds(pl.multiple_of(start, 128), size), :]


def grads_out_kernel(dp, seq, qkv, w_in, w_out, w_down, qkv_o, in_o, out_o, down_o, send_sem, recv):
    i, h = lax.axis_index("dp"), lax.axis_index("seq")
    meet_all(dp, seq, i, h)
    push, finish = sender(i, h, send_sem)
    quarter, pair = lax.rem(h, 4), lax.rem(h, 2)
    push(qkv.at[:, 0:128], cols(qkv_o, 128 * quarter, 128), recv.at[quarter], i, h // 4)
    push(qkv.at[:, 128:256], cols(qkv_o, 128 * quarter, 128), recv.at[quarter], i, 2 + h // 4)
    push(qkv.at[:, 256:512], cols(qkv_o, 256 * pair, 256), recv.at[pair], i, 4 + h // 2)
    push(w_in.at[:, 0:384], cols(in_o, 384 * (h // 4), 384), recv.at[4 + h // 4], i, quarter)
    push(w_in.at[:, 384:768], cols(in_o, 384 * (h // 4), 384), recv.at[4 + h // 4], i, 4 + quarter)
    for r in range(2):
        push(w_out.at[:, 128 * r : 128 * r + 128], rows_of(out_o, 256 * pair, 256), recv.at[6 + pair], h // 2, 2 * i + r)
        push(
            w_down.at[:, 128 * r : 128 * r + 128],
            rows_of(down_o, 384 * (h // 4), 384),
            recv.at[8 + h // 4],
            quarter,
            2 * i + r,
        )

    @pl.when(h < 4)
    def _():
        for t in range(4):
            arrived(qkv_o.at[:, 128 * t : 128 * t + 128], recv.at[t])

    @pl.when(h >= 4)
    def _():
        for t in range(2):
            arrived(qkv_o.at[:, 256 * t : 256 * t + 256], recv.at[t])

    for r in range(2):
        arrived(in_o.at[:, 384 * r : 384 * r + 384], recv.at[4 + r])
        arrived(out_o.at[256 * r : 256 * r + 256, :], recv.at[6 + r])
        arrived(down_o.at[384 * r : 384 * r + 384, :], recv.at[8 + r])
    finish()


def grads_out(dp, seq, qkv, w_in, w_out, w_down):
    kind = jnp.bfloat16
    return pl.pallas_call(
        functools.partial(grads_out_kernel, dp, seq),
        out_shape=(
            jax.ShapeDtypeStruct((256, 512), kind),
            jax.ShapeDtypeStruct((256, 768), kind),
            jax.ShapeDtypeStruct((512, 128), kind),
            jax.ShapeDtypeStruct((768, 128), kind),
        ),
        in_specs=[ANY] * 4,
        out_specs=(ANY,) * 4,
        scratch_shapes=[pltpu.SemaphoreType.DMA((9,)), pltpu.SemaphoreType.DMA((10,))],
        compiler_params=pltpu.CompilerParams(collective_id=1, has_side_effects=True),
        name="grads_out",
    )(qkv, w_in, w_out, w_down)


def dot(a, b, dims=((1,), (0,))):
    return lax.dot_general(a, b, (dims, ((), ())), preferred_element_type=jnp.float32)


def fast_body(
    dp,
    seq,
    tokens,
    lengths,
    cotangent,
    norm_gains,
    head_gain,
    head_params,
    qkv_weight,
    gate_weight,
    head_weight,
    conv_weight,
    out_weight,
    ffn_in,
    ffn_out,
):
    seq_count, block_len, width = tokens.shape
    h = lax.axis_index("seq")
    head_count = head_params.shape[1]
    ff_cols, ff_rows = ffn_in.shape[1], ffn_out.shape[0]
    position = h * block_len + jnp.arange(block_len, dtype=jnp.int32)
    valid = (position < lengths[0])[:, None]
    own = tokens[0].astype(jnp.float32)
    upstream = jnp.where(valid, cotangent[0].astype(jnp.float32), 0.0)
    taps_all = conv_weight.astype(jnp.float32).T
    fr = front(
        dp,
        seq,
        tokens[0],
        low(upstream),
        qkv_weight,
        gate_weight,
        jnp.pad(ffn_in, ((0, 0), (0, 768 - ff_cols))),
        out_weight,
        jnp.pad(ffn_out, ((0, 768 - ff_rows), (0, 0))),
        norm_gains,
        head_gain[None],
        head_params,
        head_weight,
        taps_all,
    )
    w_qkv, w_gate, w_out, w_in, w_down = fr["w_qkv"], fr["w_gate"], fr["w_out"], fr["w_in"], fr["w_down"]
    carried_grad = fr["cg"]

    def head_cols(array, axis):
        return lax.dynamic_slice_in_dim(array, h, 1, axis)

    w_head = jnp.concatenate(
        [head_cols(head_weight, 1), lax.dynamic_slice_in_dim(head_weight, head_count + h, 1, 1)], axis=1
    )
    params = head_cols(head_params, 1)
    taps = jnp.concatenate(
        [
            lax.dynamic_slice_in_dim(taps_all, DK * h, DK, 1),
            lax.dynamic_slice_in_dim(taps_all, DK * (head_count + h), DK, 1),
            lax.dynamic_slice_in_dim(taps_all, 2 * DK * head_count + DV * h, DV, 1),
        ],
        axis=1,
    )
    first_norm = fr["fn"]
    conv_in = fr["ci"][HALO:]
    head_in = jnp.concatenate(
        [lax.dynamic_slice_in_dim(fr["hi"], h, 1, 1), lax.dynamic_slice_in_dim(fr["hi"], head_count + h, 1, 1)], axis=1
    )
    gate_in = fr["gi"]

    def mixer(conv_rows, head_rows, taps, params):
        total = conv_rows.shape[0]
        extended = jnp.concatenate([jnp.zeros((KCONV - 1, conv_rows.shape[1]), jnp.float32), conv_rows], axis=0)
        conv_sum = sum(extended[t : t + total] * taps[t] for t in range(KCONV))
        act = jax.nn.silu(conv_sum)
        query = unit_rows(act[:, 0:DK]) * DK ** (-0.5)
        key = unit_rows(act[:, DK : 2 * DK])
        decay = -jnp.exp(params[0]) * jax.nn.softplus(head_rows[:, 0:1] + params[1])
        erase = jax.nn.sigmoid(head_rows[:, 1:2] + params[2])
        return query, key, act[:, 2 * DK :], decay, erase

    mix_args = (conv_in.astype(jnp.float32), head_in, taps, params)
    vectors, mix_back = jax.vjp(mixer, *mix_args)
    mixed, states, inverse, updates, w_maps = fr["mixed"], fr["states"], fr["tinv"], fr["u"], fr["wm"]
    unused, post_back = jax.vjp(gated_norm, mixed, gate_in, head_gain)
    normed = fr["normed"]
    middle = fr["middle"]
    unused, second_back = jax.vjp(rms_scale, middle, norm_gains[1])
    second_norm = fr["sn"]
    gate_up = dot(second_norm, w_in)
    hidden_f, swiglu_back = jax.vjp(swiglu, gate_up)
    hidden = low(hidden_f)
    carried = lax.psum_scatter(low(dot(hidden, w_down)), "seq", scatter_dimension=0, tiled=True)
    output = low(jnp.where(valid, middle + carried.astype(jnp.float32), 0.0))

    grad_down = dot(hidden, carried_grad, ((0,), (0,)))
    hidden_grad = dot(carried_grad, w_down, ((1,), (1,)))
    gate_up_grad = low(swiglu_back(hidden_grad)[0])
    grad_in = dot(second_norm, gate_up_grad, ((0,), (0,)))
    second_grad = lax.psum_scatter(
        low(dot(gate_up_grad, w_in, ((1,), (1,)))), "seq", scatter_dimension=0, tiled=True
    ).astype(jnp.float32)
    middle_back, gain_two = second_back(second_grad)
    middle_grad = upstream + middle_back
    attended_grad = lax.all_gather(low(middle_grad), "seq", axis=0, tiled=True)
    grad_out = dot(normed, attended_grad, ((0,), (0,)))
    normed_grad = dot(attended_grad, w_out, ((1,), (1,)))
    mixed_grad, gate_in_grad, head_gain_grad = post_back(normed_grad)
    vector_grads = rec_bwd(*vectors, states, inverse, updates, w_maps, mixed_grad)
    conv_f, head_f, taps_grad, params_grad = mix_back(tuple(vector_grads))
    conv_grad, head_grad, gate_grad = low(conv_f), low(head_f), low(gate_in_grad)
    grad_qkv = dot(first_norm, conv_grad, ((0,), (0,)))
    grad_head = dot(head_grad, first_norm, ((0,), (0,)))
    grad_gate = dot(first_norm, gate_grad, ((0,), (0,)))
    first_part = (
        dot(conv_grad, w_qkv, ((1,), (1,)))
        + dot(head_grad, w_head, ((1,), (1,)))
        + dot(gate_grad, w_gate, ((1,), (1,)))
    )
    first_grad = lax.psum_scatter(low(first_part), "seq", scatter_dimension=0, tiled=True).astype(jnp.float32)
    unused, first_back = jax.vjp(rms_scale, own, norm_gains[0])
    input_back, gain_one = first_back(first_grad)
    input_grad = low(middle_grad + input_back)

    def group_sum(part, dim):
        return lax.psum_scatter(low(part), "dp", scatter_dimension=dim, tiled=True)

    parts = grads_out(
        dp, seq, group_sum(grad_qkv, 0), group_sum(grad_in, 0), group_sum(grad_out, 1), group_sum(grad_down, 1)
    )
    gate_total = group_sum(grad_gate, 0)

    def placed(array, start, total):
        return lax.dynamic_update_slice_in_dim(jnp.zeros((array.shape[0], total), jnp.float32), array, start, 1)

    conv_all = (
        placed(taps_grad[:, 0:DK], DK * h, taps_all.shape[1])
        + placed(taps_grad[:, DK : 2 * DK], DK * (head_count + h), taps_all.shape[1])
        + placed(taps_grad[:, 2 * DK :], 2 * DK * head_count + DV * h, taps_all.shape[1])
    )
    head_all = lax.dynamic_update_slice_in_dim(jnp.zeros((2 * head_count, width), jnp.float32), grad_head[0:1], h, 0)
    head_all = lax.dynamic_update_slice_in_dim(head_all, grad_head[1:2], head_count + h, 0)
    params_all = placed(params_grad, h, head_count)
    small = lax.psum(
        (jnp.stack([gain_one, gain_two]), head_gain_grad, params_all, head_all, conv_all), ("dp", "seq")
    )
    wide = jnp.float32
    return (
        output[None],
        input_grad[None],
        small[0],
        small[1],
        small[2],
        parts[0].astype(wide),
        gate_total.astype(wide),
        small[3].T,
        small[4].T,
        parts[2].astype(wide),
        parts[1][:, 0:ff_cols].astype(wide),
        parts[3][0:ff_rows].astype(wide),
    )


def choose_body(dp, seq):
    def chosen(*arrays):
        tokens, head_params = arrays[0], arrays[5]
        if (dp, seq) == (4, 8) and tokens.shape[0] == 1 and head_params.shape[1] == seq:
            return fast_body(dp, seq, *arrays)
        return general_body(*arrays)

    return chosen


def solution(mesh):
    dp, seq = mesh.shape["dp"], mesh.shape["seq"]
    placed = (
        P("dp", "seq", None),
        P("dp"),
        P("dp", "seq", None),
        P(),
        P(),
        P(),
        P("dp", "seq"),
        P("dp", "seq"),
        P(),
        P(),
        P("dp", "seq"),
        P("dp", "seq"),
        P("dp", "seq"),
    )
    return jax.shard_map(
        choose_body(dp, seq),
        mesh=mesh,
        in_specs=placed,
        out_specs=(
            P("dp", "seq", None),
            P("dp", "seq", None),
            P(),
            P(),
            P(),
            P("dp", "seq"),
            P("dp", "seq"),
            P(),
            P(),
            P("dp", "seq"),
            P("dp", "seq"),
            P("dp", "seq"),
        ),
        check_vma=False,
    )
```

```python
import functools

import jax
import jax.numpy as jnp
from jax import lax
from jax.experimental import pallas as pl
from jax.experimental.pallas import tpu as pltpu
from jax.sharding import PartitionSpec as P

CH = 256
DK = 128
DV = 256
KCONV = 4
TILE = 64


HIGHEST = lax.Precision.HIGHEST
epsilon = 1e-06


def passed_along(block, axis, distance):
    devices = range(lax.axis_size(axis))
    route = [(i - distance, i) for i in devices if i - distance in devices]
    return lax.ppermute(block, axis, route)


def rms_scale(values, gain_row):
    return (
        values * lax.rsqrt(jnp.mean(values * values, axis=-1, keepdims=True) + epsilon) * gain_row
    )


def unit_rows(values):
    return values * lax.rsqrt(jnp.sum(values * values, axis=-1, keepdims=True) + epsilon)


def block_step(state_now, query_vecs, key_vecs, value_vecs, log_decay, erase_rate):
    length = query_vecs.shape[1]
    cumulative = jnp.cumsum(log_decay, axis=1)
    row_index = jnp.arange(length)[:, None]
    col_index = jnp.arange(length)[None, :]
    strict = col_index < row_index
    within = col_index <= row_index
    spread = cumulative[:, :, None] - cumulative[:, None, :]
    lower_decay = jnp.where(strict, jnp.exp(jnp.where(strict, spread, 0.0)), 0.0)
    causal = jnp.where(within, jnp.exp(jnp.where(within, spread, 0.0)), 0.0)
    key_gram = jnp.einsum("htk,hsk->hts", key_vecs, key_vecs, precision=HIGHEST)
    query_gram = jnp.einsum("htk,hsk->hts", query_vecs, key_vecs, precision=HIGHEST)
    negated = -(erase_rate[:, :, None] * key_gram * lower_decay)
    identity = jnp.eye(length, dtype=jnp.float32)
    inverse = identity + negated
    powered = negated
    for level_index in range(length.bit_length() - 2):
        powered = jnp.einsum("hts,hsr->htr", powered, powered, precision=HIGHEST)
        inverse = jnp.einsum("hts,hsr->htr", inverse, identity + powered, precision=HIGHEST)
    shrink = jnp.exp(cumulative)
    recalled = jnp.einsum("htk,hkw->htw", key_vecs, state_now, precision=HIGHEST)
    target = erase_rate[:, :, None] * value_vecs - (erase_rate * shrink)[:, :, None] * recalled
    updates = jnp.einsum("hts,hsw->htw", inverse, target, precision=HIGHEST)
    read_out = shrink[:, :, None] * jnp.einsum(
        "htk,hkw->htw", query_vecs, state_now, precision=HIGHEST
    )
    read_out = read_out + jnp.einsum(
        "hts,hsw->htw", query_gram * causal, updates, precision=HIGHEST
    )
    remain = jnp.exp(cumulative[:, -1:] - cumulative)
    state_next = jnp.exp(cumulative[:, -1])[:, None, None] * state_now
    state_next = state_next + jnp.einsum(
        "hsk,hsw->hkw", key_vecs * remain[:, :, None], updates, precision=HIGHEST
    )
    return (state_next, read_out)


def run_tiles(query_vecs, key_vecs, value_vecs, log_decay, erase_rate, state_start):
    row_count, head_count, key_width = query_vecs.shape
    tile_count = row_count // TILE

    def arrange(tensor):
        return jnp.swapaxes(tensor.reshape((tile_count, TILE, head_count) + tensor.shape[2:]), 1, 2)

    inputs = (
        arrange(query_vecs),
        arrange(key_vecs),
        arrange(value_vecs),
        arrange(log_decay),
        arrange(erase_rate),
    )

    def advance(state_now, sliced):
        return jax.checkpoint(block_step)(state_now, *sliced)

    state_end, outputs = lax.scan(advance, state_start, inputs)
    outputs = jnp.swapaxes(outputs, 1, 2).reshape(row_count, head_count, outputs.shape[-1])
    return (outputs, state_end)


def mixer_inputs(conv_in, edge_rows, head_in, conv_taps, head_params):
    block_len = conv_in.shape[1]
    head_count = head_params.shape[1]
    extended = jnp.concatenate([edge_rows, conv_in], axis=1)
    conv_sum = extended[:, 0:block_len] * conv_taps[:, 0]
    for offset in range(1, conv_taps.shape[1]):
        conv_sum = conv_sum + extended[:, offset : offset + block_len] * conv_taps[:, offset]
    activated = jax.nn.silu(conv_sum)
    key_span = head_count * DK
    lead = activated.shape[:2]
    query_vecs = unit_rows(activated[..., 0:key_span].reshape(lead + (head_count, DK))) * DK ** (
        -0.5
    )
    key_vecs = unit_rows(activated[..., key_span : 2 * key_span].reshape(lead + (head_count, DK)))
    value_vecs = activated[..., 2 * key_span :].reshape(lead + (head_count, DV))
    log_decay = -jnp.exp(head_params[0]) * jax.nn.softplus(
        head_in[..., 0:head_count] + head_params[1]
    )
    erase_rate = jax.nn.sigmoid(head_in[..., head_count : 2 * head_count] + head_params[2])
    return (query_vecs, key_vecs, value_vecs, log_decay, erase_rate)


def gated_norm(mixed, gate_in, head_gain):
    shaped = gate_in.reshape(mixed.shape)
    normed = (
        mixed * lax.rsqrt(jnp.mean(mixed * mixed, axis=-1, keepdims=True) + epsilon) * head_gain
    )
    return (normed * jax.nn.silu(shaped)).reshape(gate_in.shape)


def local_tiles(query_vecs, key_vecs, value_vecs, log_decay, erase_rate):
    key_width = key_vecs.shape[-1]
    value_width = value_vecs.shape[-1]
    head_count = key_vecs.shape[2]
    padded = jnp.concatenate(
        [jnp.zeros(value_vecs.shape[:3] + (key_width,), jnp.float32), value_vecs], axis=-1
    )
    start_map = jnp.concatenate(
        [jnp.eye(key_width, dtype=jnp.float32), jnp.zeros((key_width, value_width), jnp.float32)],
        axis=1,
    )
    start_map = jnp.broadcast_to(start_map, (head_count, key_width, key_width + value_width))

    def single(query_one, key_one, value_one, decay_one, erase_one):
        return run_tiles(query_one, key_one, value_one, decay_one, erase_one, start_map)

    return jax.vmap(single)(query_vecs, key_vecs, padded, log_decay, erase_rate)


def post_mix(local_out, incoming, gate_in, head_gain):
    mixed = local_out[..., DK:] + jnp.einsum(
        "snhk,shkv->snhv", local_out[..., 0:DK], incoming, precision=HIGHEST
    )
    return gated_norm(mixed, gate_in, head_gain)


def swiglu(gate_up):
    split_at = gate_up.shape[-1] // 2
    return jax.nn.silu(gate_up[:, 0:split_at]) * gate_up[:, split_at:]


def matmul_maps(left, right):
    return jnp.einsum("shij,shjk->shik", left, right, precision=HIGHEST)


def apply_map(maps, state_now):
    return matmul_maps(maps[0], state_now) + maps[1]


def general_body(
    tokens,
    lengths,
    cotangent,
    norm_gains,
    head_gain,
    head_params,
    qkv_weight,
    gate_weight,
    head_weight,
    conv_weight,
    out_weight,
    ffn_in,
    ffn_out,
):
    seq_count, block_len, model_width = tokens.shape
    row_count = seq_count * block_len
    position = lax.axis_index("seq") * block_len + jnp.arange(block_len, dtype=jnp.int32)
    valid_rows = (position[None, :] < lengths[:, None]).reshape(row_count, 1)
    col_parts = (
        lax.all_gather(qkv_weight, "seq", axis=1, tiled=True),
        lax.all_gather(gate_weight, "seq", axis=1, tiled=True),
        lax.all_gather(out_weight, "seq", axis=1, tiled=True),
        lax.all_gather(ffn_in, "seq", axis=1, tiled=True),
        lax.all_gather(ffn_out, "seq", axis=1, tiled=True),
    )
    gathered = (
        lax.all_gather(col_parts[0], "dp", axis=0, tiled=True),
        lax.all_gather(col_parts[1], "dp", axis=0, tiled=True),
        lax.all_gather(col_parts[2], "dp", axis=0, tiled=True),
        lax.all_gather(col_parts[3], "dp", axis=0, tiled=True),
        lax.all_gather(col_parts[4], "dp", axis=0, tiled=True),
    )
    w_qkv, w_gate, w_out, w_in, w_down = gathered
    inputs = tokens.reshape(row_count, model_width).astype(jnp.float32)
    first_norm = rms_scale(inputs, norm_gains[0]).astype(jnp.bfloat16)
    conv_in = jnp.dot(first_norm, w_qkv, preferred_element_type=jnp.float32).astype(jnp.bfloat16)
    head_in = jnp.dot(first_norm, head_weight, preferred_element_type=jnp.float32)
    gate_in = jnp.dot(first_norm, w_gate, preferred_element_type=jnp.float32)
    conv_width = conv_in.shape[-1]
    conv_rows = conv_in.reshape(seq_count, block_len, conv_width)
    edge_cut = block_len - (KCONV - 1)
    edge_rows = passed_along(conv_rows[:, edge_cut:], "seq", 1)
    mix_args = (
        conv_rows.astype(jnp.float32),
        edge_rows.astype(jnp.float32),
        head_in.reshape(seq_count, block_len, -1),
        conv_weight.astype(jnp.float32),
        head_params,
    )
    vectors = mixer_inputs(*mix_args)
    local_out, end_states = local_tiles(*vectors)
    carry_maps = (end_states[..., 0:DK], end_states[..., DK:])

    def relay_state(step_index, state_now):
        return passed_along(apply_map(carry_maps, state_now), "seq", 1)

    incoming = lax.fori_loop(
        0, lax.axis_size("seq") - 1, relay_state, jnp.zeros_like(carry_maps[1])
    )
    post_args = (local_out, incoming, gate_in, head_gain)
    normed = post_mix(*post_args).astype(jnp.bfloat16)
    attended = jnp.dot(normed, w_out, preferred_element_type=jnp.float32)
    middle = inputs + attended
    second_norm = rms_scale(middle, norm_gains[1]).astype(jnp.bfloat16)
    gate_up = jnp.dot(second_norm, w_in, preferred_element_type=jnp.float32)
    hidden = swiglu(gate_up).astype(jnp.bfloat16)
    carried = jnp.dot(hidden, w_down, preferred_element_type=jnp.float32)
    output = jnp.where(valid_rows, middle + carried, 0.0).astype(jnp.bfloat16)
    col_again = (
        lax.all_gather(qkv_weight, "seq", axis=1, tiled=True),
        lax.all_gather(gate_weight, "seq", axis=1, tiled=True),
        lax.all_gather(out_weight, "seq", axis=1, tiled=True),
        lax.all_gather(ffn_in, "seq", axis=1, tiled=True),
        lax.all_gather(ffn_out, "seq", axis=1, tiled=True),
    )
    regathered = (
        lax.all_gather(col_again[0], "dp", axis=0, tiled=True),
        lax.all_gather(col_again[1], "dp", axis=0, tiled=True),
        lax.all_gather(col_again[2], "dp", axis=0, tiled=True),
        lax.all_gather(col_again[3], "dp", axis=0, tiled=True),
        lax.all_gather(col_again[4], "dp", axis=0, tiled=True),
    )
    w_qkv, w_gate, w_out, w_in, w_down = regathered
    upstream = jnp.where(
        valid_rows, cotangent.reshape(row_count, model_width).astype(jnp.float32), 0.0
    )
    carried_grad = upstream.astype(jnp.bfloat16)
    grad_down = jnp.einsum("nf,nd->fd", hidden, carried_grad, preferred_element_type=jnp.float32)
    hidden_grad = jnp.einsum("nd,fd->nf", carried_grad, w_down, preferred_element_type=jnp.float32)
    unused, swiglu_back = jax.vjp(swiglu, gate_up)
    gate_up_grad = swiglu_back(hidden_grad)[0].astype(jnp.bfloat16)
    grad_in = jnp.einsum("nd,nf->df", second_norm, gate_up_grad, preferred_element_type=jnp.float32)
    second_grad = jnp.einsum("nf,df->nd", gate_up_grad, w_in, preferred_element_type=jnp.float32)
    unused, second_back = jax.vjp(rms_scale, middle, norm_gains[1])
    middle_back, gain_two = second_back(second_grad)
    middle_grad = upstream + middle_back
    attended_grad = middle_grad.astype(jnp.bfloat16)
    grad_out = jnp.einsum("nv,nd->vd", normed, attended_grad, preferred_element_type=jnp.float32)
    normed_grad = jnp.einsum("nd,vd->nv", attended_grad, w_out, preferred_element_type=jnp.float32)
    unused, post_back = jax.vjp(post_mix, *post_args)
    local_grad, incoming_local, gate_in_grad, head_gain_grad = post_back(normed_grad)
    flipped = (jnp.swapaxes(carry_maps[0], -1, -2), incoming_local)

    def relay_grad(step_index, grad_now):
        return passed_along(apply_map(flipped, grad_now).astype(jnp.bfloat16), "seq", -1).astype(
            jnp.float32
        )

    outgoing = lax.fori_loop(
        0, lax.axis_size("seq") - 1, relay_grad, jnp.zeros_like(incoming_local)
    )
    map_grad = jnp.einsum("shkv,shjv->shkj", outgoing, incoming, precision=HIGHEST)
    end_grad = jnp.concatenate([map_grad, outgoing], axis=-1)
    unused, tiles_back = jax.vjp(local_tiles, *vectors)
    vector_grads = tiles_back((local_grad, end_grad))
    unused, mix_back = jax.vjp(mixer_inputs, *mix_args)
    conv_own, edge_grad, head_in_grad, conv_taps_grad, params_grad = mix_back(vector_grads)
    edge_back = passed_along(edge_grad.astype(jnp.bfloat16), "seq", -1).astype(edge_grad.dtype)
    conv_total = jnp.concatenate(
        [conv_own[:, 0:edge_cut], conv_own[:, edge_cut:] + edge_back], axis=1
    )
    conv_grad = conv_total.reshape(row_count, conv_width).astype(jnp.bfloat16)
    head_grad = head_in_grad.reshape(row_count, -1).astype(jnp.bfloat16)
    gate_grad = gate_in_grad.astype(jnp.bfloat16)
    grad_qkv = jnp.einsum("nd,nc->dc", first_norm, conv_grad, preferred_element_type=jnp.float32)
    grad_head = jnp.einsum("nd,nc->dc", first_norm, head_grad, preferred_element_type=jnp.float32)
    grad_gate = jnp.einsum("nd,nc->dc", first_norm, gate_grad, preferred_element_type=jnp.float32)
    first_grad = jnp.einsum("nc,dc->nd", conv_grad, w_qkv, preferred_element_type=jnp.float32)
    first_grad = first_grad + jnp.einsum(
        "nc,dc->nd", head_grad, head_weight, preferred_element_type=jnp.float32
    )
    first_grad = first_grad + jnp.einsum(
        "nc,dc->nd", gate_grad, w_gate, preferred_element_type=jnp.float32
    )
    unused, first_back = jax.vjp(rms_scale, inputs, norm_gains[0])
    input_back, gain_one = first_back(first_grad)
    input_grad = (
        (middle_grad + input_back).astype(jnp.bfloat16).reshape(seq_count, block_len, model_width)
    )
    row_groups = (
        lax.psum_scatter(
            grad_qkv.astype(jnp.bfloat16), "dp", scatter_dimension=0, tiled=True
        ).astype(jnp.float32),
        lax.psum_scatter(
            grad_gate.astype(jnp.bfloat16), "dp", scatter_dimension=0, tiled=True
        ).astype(jnp.float32),
        lax.psum_scatter(
            grad_out.astype(jnp.bfloat16), "dp", scatter_dimension=0, tiled=True
        ).astype(jnp.float32),
        lax.psum_scatter(
            grad_in.astype(jnp.bfloat16), "dp", scatter_dimension=0, tiled=True
        ).astype(jnp.float32),
        lax.psum_scatter(
            grad_down.astype(jnp.bfloat16), "dp", scatter_dimension=0, tiled=True
        ).astype(jnp.float32),
    )
    weight_parts = (
        lax.psum_scatter(
            row_groups[0].astype(jnp.bfloat16), "seq", scatter_dimension=1, tiled=True
        ).astype(jnp.float32),
        lax.psum_scatter(
            row_groups[1].astype(jnp.bfloat16), "seq", scatter_dimension=1, tiled=True
        ).astype(jnp.float32),
        lax.psum_scatter(
            row_groups[2].astype(jnp.bfloat16), "seq", scatter_dimension=1, tiled=True
        ).astype(jnp.float32),
        lax.psum_scatter(
            row_groups[3].astype(jnp.bfloat16), "seq", scatter_dimension=1, tiled=True
        ).astype(jnp.float32),
        lax.psum_scatter(
            row_groups[4].astype(jnp.bfloat16), "seq", scatter_dimension=1, tiled=True
        ).astype(jnp.float32),
    )
    small_sums = lax.psum(
        (jnp.stack([gain_one, gain_two]), head_gain_grad, params_grad, grad_head, conv_taps_grad),
        ("dp", "seq"),
    )
    output = output.reshape(seq_count, block_len, model_width)
    return (
        output,
        input_grad,
        small_sums[0],
        small_sums[1],
        small_sums[2],
        weight_parts[0],
        weight_parts[1],
        small_sums[3],
        small_sums[4],
        weight_parts[2],
        weight_parts[3],
        weight_parts[4],
    )


MESH = pl.DeviceIdType.MESH
ANY = pl.BlockSpec(memory_space=pl.ANY)
IN_VMEM = pl.BlockSpec(memory_space=pltpu.VMEM)
B16 = jnp.bfloat16
F32 = jnp.float32
NN = ((1,), (0,))
NT = ((1,), (1,))
TN = ((0,), (0,))
HALO = 16


def low(v):
    return v.astype(jnp.bfloat16)


def mm(a, b, dims=NN):
    return lax.dot_general(low(a), low(b), (dims, ((), ())), preferred_element_type=jnp.float32)


def mmf(a, b, dims=NN):
    return lax.dot_general(
        a, b, (dims, ((), ())), precision=HIGHEST, preferred_element_type=jnp.float32
    )


def mm3(a, b, dims=NN):
    ah, bh = low(a), low(b)
    al, bl = low(a - ah.astype(jnp.float32)), low(b - bh.astype(jnp.float32))
    return mm(ah, bh, dims) + (mm(ah, bl, dims) + mm(al, bh, dims))


def sig(v):
    return 1.0 / (1.0 + jnp.exp(-v))


def soft_plus(v):
    tail = jnp.exp(-jnp.abs(v))
    series = tail * (1.0 - tail * (0.5 - tail * (1.0 / 3.0)))
    return jnp.maximum(v, 0.0) + jnp.where(tail < 1e-3, series, jnp.log(1.0 + tail))


def grid_masks():
    row = lax.broadcasted_iota(jnp.int32, (CH, CH), 0)
    col = lax.broadcasted_iota(jnp.int32, (CH, CH), 1)
    return row, col


def decay_parts(g, row, col):
    lower = (col <= row).astype(jnp.float32)
    cum = mmf(lower, g)
    cum_row = mmf(g, lower, ((0,), (1,)))
    within = col <= row
    decay = jnp.where(within, jnp.exp(jnp.where(within, cum - cum_row, 0.0)), 0.0)
    return cum, decay


def unit_inverse(attns, row, col):
    def same(width):
        return (row // width) == (col // width)

    eye = jnp.where(row == col, 1.0, 0.0)
    power = [jnp.where(same(64), -a, 0.0) for a in attns]
    inv = [eye + p for p in power]
    for level in range(5):
        power = [mm(p, p) for p in power]
        inv = [x + mm(x, p) for x, p in zip(inv, power)]
    for width in (128, 256):
        off = same(width) & jnp.logical_not(same(width // 2))
        part = [mm(jnp.where(off, a, 0.0), x) for a, x in zip(attns, inv)]
        inv = [x - mm(x, p) for x, p in zip(inv, part)]
    rest = [eye - x - mm3(a, x) for a, x in zip(attns, inv)]
    return [x + mm(x, r) for x, r in zip(inv, rest)]


def tile(t, size=CH):
    return pl.ds(pl.multiple_of(t * size, size), size)


class Wires:
    def __init__(self, dp, seq, sems):
        self.dp, self.seq, self.sems, self.used = dp, seq, sems, 0
        self.i, self.s = lax.axis_index("dp"), lax.axis_index("seq")
        self.z, self.c = self.s // 2, lax.rem(self.s, 2)
        self.half, self.partner = self.z // 2, self.z + 1 - 2 * lax.rem(self.z, 2)
        self.inner = lax.rem((self.z + 1) // 2, 2)

    def take(self, count=1):
        start = self.used
        self.used += count
        return start

    def meet_all(self):
        barrier = pltpu.get_barrier_semaphore()
        for di in range(self.dp):
            for dj in range(self.seq):
                if di or dj:
                    pl.semaphore_signal(
                        barrier,
                        inc=1,
                        device_id=(lax.rem(self.i + di, self.dp), lax.rem(self.s + dj, self.seq)),
                        device_id_type=MESH,
                    )
        pl.semaphore_wait(barrier, self.dp * self.seq - 1)

    def remote(self, src, dst, send, recv, di, dj):
        return pltpu.make_async_remote_copy(
            src_ref=src,
            dst_ref=dst,
            send_sem=self.sems.at[send],
            recv_sem=self.sems.at[recv],
            device_id=(di, dj),
            device_id_type=MESH,
        )

    def local(self, src, dst, sem):
        return pltpu.make_async_copy(src, dst, self.sems.at[sem])

    def push(self, src, dst, send, recv, di, dj):
        here = (di == self.i) & (dj == self.s)
        away = self.remote(src, dst, send, recv, di, dj)

        @pl.when(here)
        def _():
            self.local(src, dst, recv).start()

        @pl.when(jnp.logical_not(here))
        def _():
            away.start()

        def sent():
            @pl.when(jnp.logical_not(here))
            def _():
                away.wait_send()

        return sent

    def arrived(self, dst, recv):
        pltpu.make_async_copy(dst, dst, self.sems.at[recv]).wait()

    def chip(self, z):
        return z * 2 + self.c

    def order(self, n):
        near = self.z + n * (1 - 2 * lax.rem(self.z, 2))
        return (1 - n // 2) * near + (n // 2) * (n + self.half * (3 - 2 * n))

    def sibling(self):
        return self.z * 2 + 1 - self.c


class LineGather:
    parts = 2

    def __init__(self, w, block_of):
        self.w, self.block_of = w, block_of
        n = 4 * self.parts
        self.send, self.recv = w.take(n), w.take(n)
        self.fsend, self.frecv = w.take(n), w.take(n)

    def piece(self, block, part):
        size = block.shape[0] // self.parts
        return block.at[part * size : part * size + size, :]

    def start(self, src):
        w = self.w
        dst = self.block_of(w.s)
        self.src = src
        for part in range(self.parts):
            a, b = self.piece(src, part), self.piece(dst, part)
            w.remote(a, b, self.send + part, self.recv + self.parts + part, w.i, w.chip(w.partner)).start()
            w.remote(
                a,
                b,
                self.send + self.parts + part,
                self.recv + (3 - w.inner) * self.parts + part,
                w.i,
                w.chip(2 - w.half),
            ).start()
        for part in range(self.parts):
            a, b = self.piece(src, part), self.piece(dst, part)
            w.remote(a, b, self.fsend + part, self.frecv + part, w.i, w.sibling()).start()

    def arrive(self, n):
        w = self.w
        block = self.block_of(w.chip(w.order(n)))
        for part in range(self.parts):
            ref, slot = self.piece(block, part), n * self.parts + part
            w.arrived(ref, self.recv + slot)

            @pl.when((w.inner == 1) & (n > 1))
            def _():
                w.remote(ref, ref, self.send + slot, self.recv + slot, w.i, w.chip(w.partner)).start()

            w.remote(ref, ref, self.fsend + slot, self.frecv + slot, w.i, w.sibling()).start()

    def other(self, n):
        w = self.w
        block = self.block_of(w.order(n) * 2 + 1 - w.c)
        for part in range(self.parts):
            w.arrived(self.piece(block, part), self.frecv + n * self.parts + part)

    def finish(self):
        w = self.w
        for part in range(self.parts):
            ref = self.piece(self.src, part)
            for n in range(4):
                copy = w.remote(ref, ref, self.send + n * self.parts + part, self.recv, w.i, w.sibling())
                if n < 2:
                    copy.wait_send()
                else:
                    @pl.when(w.inner == 1)
                    def _():
                        copy.wait_send()

                w.remote(ref, ref, self.fsend + n * self.parts + part, self.recv, w.i, w.sibling()).wait_send()


class GroupGather:
    def __init__(self, w, part_of):
        self.w, self.part_of = w, part_of
        self.send, self.recv = w.take(4), w.take(4)

    def start(self, src):
        w = self.w
        self.own = w.local(src, self.part_of(w.i), self.recv)
        self.own.start()
        self.copies = []
        for d in (3, 1, 2):
            copy = w.remote(src, self.part_of(w.i), self.send + d, self.recv + d, lax.rem(w.i + d, 4), w.s)
            copy.start()
            self.copies.append(copy)

    def finish(self):
        w = self.w
        self.own.wait()
        for d in range(1, 4):
            w.arrived(self.part_of(lax.rem(w.i + 4 - d, 4)), self.recv + d)
        for copy in self.copies:
            copy.wait_send()


class LineScatter:
    def __init__(self, w, part, sib, chip, got):
        self.w, self.part, self.sib, self.chip, self.got = w, part, sib, chip, got
        self.ssend, self.srecv = w.take(4), w.take(4)
        self.send, self.recv = w.take(4), w.take(4)

    def swap(self, t):
        w = self.w
        src = self.part.at[pl.ds(pl.multiple_of(t * 256 + 128 * (1 - w.c), 128), 128), :]
        w.remote(src, self.sib.at[t], self.ssend + t, self.srecv + t, w.i, w.sibling()).start()

    def out(self, t, slot, chip):
        w = self.w
        w.remote(self.chip.at[t], self.got.at[slot], self.send + t, self.recv + slot, w.i, w.chip(chip)).start()

    def pass_on(self, t):
        w = self.w
        w.arrived(self.sib.at[t], self.srecv + t)
        mine = self.part[pl.ds(pl.multiple_of(t * 256 + 128 * w.c, 128), 128), :]
        self.chip[t] = low(mine.astype(jnp.float32) + self.sib[t].astype(jnp.float32))

        @pl.when(t == w.partner)
        def _():
            self.out(t, 0, t)

        @pl.when((t // 2 != w.half) & (w.inner == 0))
        def _():
            self.out(t, 2 + lax.rem(t, 2), w.partner)

    def relay(self, t):
        w = self.w

        @pl.when((t // 2 != w.half) & (w.inner == 1))
        def _():
            slot = 2 + lax.rem(t, 2)
            w.arrived(self.got.at[slot], self.recv + slot)
            self.chip[t] = low(self.chip[t].astype(jnp.float32) + self.got[slot].astype(jnp.float32))
            self.out(t, 1, t)

    def total(self):
        w = self.w
        total = self.chip[w.z].astype(jnp.float32)
        for slot in range(2):
            w.arrived(self.got.at[slot], self.recv + slot)
            total = total + self.got[slot].astype(jnp.float32)
        return total

    def finish(self):
        w = self.w
        for t in range(4):
            src = self.part.at[pl.ds(t * 256, 128), :]
            w.remote(src, self.sib.at[t], self.ssend + t, self.srecv + t, w.i, w.sibling()).wait_send()

            @pl.when(w.z != t)
            def _():
                w.remote(self.chip.at[t], self.got.at[0], self.send + t, self.recv, w.i, w.sibling()).wait_send()


def cols(ref, start, size):
    return ref.at[:, pl.ds(pl.multiple_of(start, 128), size)]


def rows_of(ref, start, size):
    return ref.at[pl.ds(pl.multiple_of(start, 128), size), :]


class Box:
    pass


def fields(kind):
    return [(name, *value) for name, value in vars(kind).items() if name[0] != "_"]


class FrontKept:
    fn = ((1024, 1024), B16)
    ci = ((HALO + 1024, 512), B16)
    gi = ((1024, 256), F32)
    q = ((1024, 128), F32)
    k = ((1024, 128), F32)
    v = ((1024, 256), F32)
    ge = ((1024, 128), F32)
    mixed = ((1024, 256), F32)
    states = ((4, 128, 256), F32)
    tinv = ((1024, 256), B16)
    u = ((1024, 256), F32)
    wm = ((1024, 128), B16)
    normed = ((1024, 256), B16)
    middle = ((128, 1024), F32)
    sn = ((1024, 1024), B16)
    cg = ((1024, 1024), B16)
    w_qkv = ((1024, 512), B16)
    w_gate = ((1024, 256), B16)
    w_in = ((1024, 768), B16)
    w_out = ((256, 1024), B16)
    w_down = ((384, 1024), B16)
class FrontScratch:
    x = ((1024, 1024), B16)
    qkv_p = ((256, 512), B16)
    in_p = ((256, 768), B16)
    out_p = ((256, 256), B16)
    down_p = ((384, 256), B16)
    qk = ((1024, 256), B16)
    cum = ((1024, 1), F32)
    part = ((1024, 1024), B16)
    sib = ((4, 128, 1024), B16)
    chip = ((4, 128, 1024), B16)
    got = ((4, 128, 1024), B16)
    own_sn = ((128, 1024), B16)


def start_weights(w, b):
    i, s = w.i, w.s
    qs, qr = w.take(4), w.take(3)
    lowhalf = s < 4
    b.qr = qr

    @pl.when(lowhalf)
    def _():
        for t in range(4):
            w.push(
                b.qkv.at[:, 128 * t : 128 * t + 128],
                cols(b.qkv_p, 128 * (s // 2), 128),
                qs + t,
                qr + s // 2,
                i,
                4 * lax.rem(s, 2) + t,
            )

    @pl.when(jnp.logical_not(lowhalf))
    def _():
        for t in range(2):
            w.push(b.qkv.at[:, 256 * t : 256 * t + 256], b.qkv_p.at[:, 256:512], qs + t, qr + 2, i, 2 * (s - 4) + t)

    def sent():
        @pl.when(lowhalf)
        def _():
            for t in range(4):
                @pl.when(4 * lax.rem(s, 2) + t != s)
                def _():
                    src = b.qkv.at[:, 128 * t : 128 * t + 128]
                    w.remote(src, b.qkv_p.at[:, 0:128], qs + t, qr, i, w.sibling()).wait_send()

        @pl.when(jnp.logical_not(lowhalf))
        def _():
            for t in range(2):
                @pl.when(2 * (s - 4) + t != s)
                def _():
                    src = b.qkv.at[:, 256 * t : 256 * t + 256]
                    w.remote(src, b.qkv_p.at[:, 256:512], qs + t, qr + 2, i, w.sibling()).wait_send()

    return sent


def start_more_weights(w, b):
    i, s = w.i, w.s
    ms, mr = w.take(5), w.take(6)
    own, odd = s // 4, lax.rem(s, 2)
    b.keep = w.local(cols(b.ffn_in, 384 * own, 384), cols(b.in_p, 384 * own, 384), mr)
    b.keep.start()
    waits = [
        w.push(cols(b.ffn_in, 384 * (1 - own), 384), cols(b.in_p, 384 * own, 384), ms, mr + 1, i, lax.rem(s + 4, 8))
    ]
    for n in range(2):
        waits.append(
            w.push(
                b.out.at[256 * n : 256 * n + 256, :],
                cols(b.out_p, 128 * odd, 128),
                ms + 1 + n,
                mr + 2 + odd,
                s // 2,
                2 * i + n,
            )
        )
        waits.append(
            w.push(
                b.ffn_out.at[384 * n : 384 * n + 384, :],
                cols(b.down_p, 128 * odd, 128),
                ms + 3 + n,
                mr + 4 + odd,
                s // 2,
                i + 4 * n,
            )
        )

    def landed():
        b.keep.wait()
        w.arrived(b.in_p.at[:, 0:384], mr + 1)
        for r in range(2):
            w.arrived(b.out_p.at[:, 128 * r : 128 * r + 128], mr + 2 + r)
            w.arrived(b.down_p.at[:, 128 * r : 128 * r + 128], mr + 4 + r)

    def sent():
        for wait in waits:
            wait()

    return landed, sent


def first_norm_tile(b, t):
    rows = tile(t)
    x = b.x[rows, :].astype(jnp.float32)
    inv = lax.rsqrt(jnp.mean(x * x, axis=-1, keepdims=True) + epsilon)
    b.fn[rows, :] = low(x * inv * b.gains[0:1, :])


def own_head(b, w):
    pm = b.params[...]
    lane = lax.broadcasted_iota(jnp.int32, pm.shape, 1)
    return jnp.sum(jnp.where(lane == w.s, pm, 0.0), axis=1, keepdims=True)


def own_taps(b, w, n):
    s = w.s
    return jnp.concatenate(
        [
            b.taps[n : n + 1, pl.ds(pl.multiple_of(128 * s, 128), 128)],
            b.taps[n : n + 1, pl.ds(pl.multiple_of(1024 + 128 * s, 128), 128)],
            b.taps[n : n + 1, pl.ds(pl.multiple_of(2048 + 256 * s, 128), 256)],
        ],
        axis=1,
    )


def conv_sums(b, w, t):
    window = b.ci[pl.ds(pl.multiple_of(t * CH, CH), CH + HALO), :].astype(jnp.float32)
    total = None
    for n in range(KCONV):
        at = HALO - (KCONV - 1) + n
        term = window[at : at + CH] * own_taps(b, w, n)
        total = term if total is None else total + term
    return total


def project_tile(b, w, t):
    rows = tile(t)
    f = b.fn[rows, :]
    b.ci[pl.ds(pl.multiple_of(t * CH + HALO, HALO), CH), :] = low(mm(f, b.w_qkv[...]))
    b.gi[rows, :] = mm(f, b.w_gate[...])
    hi = mm(f, b.head_w[...])
    lane = lax.broadcasted_iota(jnp.int32, hi.shape, 1)
    pm = own_head(b, w)
    shift = jnp.sum(jnp.where(lane == w.s, hi, 0.0), axis=1, keepdims=True) + pm[1:2, :]
    erase = jnp.sum(jnp.where(lane == w.s + 8, hi, 0.0), axis=1, keepdims=True) + pm[2:3, :]
    line = lax.broadcasted_iota(jnp.int32, (CH, 128), 1)
    decay = -jnp.exp(pm[0:1, :]) * soft_plus(shift)
    b.ge[rows, :] = jnp.where(line == 0, decay, jnp.where(line == 1, sig(erase), shift))


def vectors_tile(b, w, t):
    rows = tile(t)
    total = conv_sums(b, w, t)
    act = total * sig(total)
    qa, ka = act[:, 0:DK], act[:, DK : 2 * DK]
    b.q[rows, :] = qa * lax.rsqrt(jnp.sum(qa * qa, axis=-1, keepdims=True) + epsilon) * DK ** (-0.5)
    b.k[rows, :] = ka * lax.rsqrt(jnp.sum(ka * ka, axis=-1, keepdims=True) + epsilon)
    b.v[rows, :] = act[:, 2 * DK :]


def rec_local(b, w, ts):
    row, col = grid_masks()
    attns = []
    for t in ts:
        vectors_tile(b, w, t)
        rows = tile(t)
        k = b.k[rows, :]
        cum, decay = decay_parts(b.ge[rows, 0:1], row, col)
        b.cum[rows, :] = cum
        b.qk[rows, :] = low(mm(b.q[rows, :], k, NT) * decay)
        attns.append(jnp.where(col < row, b.ge[rows, 1:2] * mm(k, k, NT) * decay, 0.0))
    for t, inv in zip(ts, unit_inverse(attns, row, col)):
        rows = tile(t)
        e, t16 = b.ge[rows, 1:2], low(inv)
        b.tinv[rows, :] = t16
        b.wm[rows, :] = low(mm(t16, (e * jnp.exp(b.cum[rows, :])) * b.k[rows, :]))
        b.u[rows, :] = mm(t16, e * b.v[rows, :])


def rec_step(b, t, state):
    rows = tile(t)
    b.states[t] = state
    cum = b.cum[rows, :]
    last = cum[CH - 1 : CH, :]
    s16 = low(state)
    u = b.u[rows, :] - mm(b.wm[rows, :], s16)
    b.u[rows, :] = u
    u16 = low(u)
    mixed = jnp.exp(cum) * mm(b.q[rows, :], s16) + mm(b.qk[rows, :], u16)
    b.mixed[rows, :] = mixed
    nxt = jnp.exp(last) * state + mm(b.k[rows, :] * jnp.exp(last - cum), u16, TN)
    gate = b.gi[rows, :]
    scale = lax.rsqrt(jnp.mean(mixed * mixed, axis=-1, keepdims=True) + epsilon)
    normed = low(mixed * scale * b.head_gain[...] * (gate * sig(gate)))
    b.normed[rows, :] = normed
    b.part[rows, :] = low(mm(normed, b.w_out[...]))
    return nxt


def front_phase(b, w):
    s, i = w.s, w.i
    own_rows = lambda ref: (lambda n: rows_of(ref, 128 * n, 128))
    x_gather = LineGather(w, own_rows(b.x))
    cg_gather = LineGather(w, own_rows(b.cg))
    sn_gather = LineGather(w, own_rows(b.sn))
    qkv_gather = GroupGather(w, lambda n: rows_of(b.w_qkv, 256 * n, 256))
    gate_gather = GroupGather(w, lambda n: rows_of(b.w_gate, 256 * n, 256))
    in_gather = GroupGather(w, lambda n: rows_of(b.w_in, 256 * n, 256))
    out_gather = GroupGather(w, lambda n: cols(b.w_out, 256 * n, 256))
    down_gather = GroupGather(w, lambda n: cols(b.w_down, 256 * n, 256))
    scatter = LineScatter(w, b.part, b.sib, b.chip, b.got)
    own_x, own_c = w.take(), w.take()

    w.meet_all()
    qkv_sent = start_weights(w, b)
    gate_gather.start(b.gate)
    keep_x = w.local(b.tokens, rows_of(b.x, 128 * s, 128), own_x)
    keep_x.start()
    b.ci[0:HALO, :] = jnp.zeros((HALO, 512), B16)
    w.arrived(b.qkv_p.at[:, 0:128], b.qr)
    w.arrived(b.qkv_p.at[:, 128:256], b.qr + 1)
    w.arrived(b.qkv_p.at[:, 256:512], b.qr + 2)
    x_gather.start(b.tokens)
    qkv_gather.start(b.qkv_p)
    keep_x.wait()

    def norm_loop(n, carry):
        @pl.when(n > 0)
        def _():
            x_gather.arrive(n)

        x_gather.other(n)
        first_norm_tile(b, w.order(n))
        return carry

    lax.fori_loop(0, 4, norm_loop, 0)
    more_landed, more_sent = start_more_weights(w, b)
    cg_gather.start(b.cot)
    keep_c = w.local(b.cot, rows_of(b.cg, 128 * s, 128), own_c)
    keep_c.start()
    qkv_gather.finish()
    gate_gather.finish()

    def project_loop(t, carry):
        project_tile(b, w, t)
        return carry

    lax.fori_loop(0, 4, project_loop, 0)
    x_gather.finish()
    more_landed()
    out_gather.start(b.out_p)
    in_gather.start(b.in_p)
    down_gather.start(b.down_p)

    def pair_loop(pair, state):
        rec_local(b, w, (2 * pair, 2 * pair + 1))

        @pl.when(pair == 0)
        def _():
            out_gather.finish()

        @pl.when(pair == 1)
        def _():
            scatter.pass_on(1)

        for k in range(2):
            t = 2 * pair + k
            state = rec_step(b, t, state)
            scatter.swap(t)
            if k:
                scatter.pass_on(t - 1)
        return state

    lax.fori_loop(0, 2, pair_loop, jnp.zeros((DK, DV), F32))
    scatter.pass_on(3)
    scatter.relay(0)
    scatter.relay(1)
    keep_c.wait()
    for n in range(1, 4):
        cg_gather.arrive(n)
    scatter.relay(2)
    scatter.relay(3)
    middle = b.tokens_v[...].astype(jnp.float32) + scatter.total()
    b.middle[...] = middle
    inv = lax.rsqrt(jnp.mean(middle * middle, axis=-1, keepdims=True) + epsilon)
    second = low(middle * inv * b.gains[1:2, :])
    b.own_sn[...] = second
    rows_of(b.sn, 128 * s, 128)[...] = second
    sn_gather.start(b.own_sn)
    in_gather.finish()
    down_gather.finish()
    qkv_sent()
    more_sent()
    scatter.finish()

    def finish():
        cg_gather.finish()
        sn_gather.finish()

    return sn_gather, cg_gather, finish


class GroupScatter:
    def __init__(self, w, out, got):
        self.w, self.out, self.got = w, out, got
        self.send, self.recv = w.take(4), w.take(4)

    def start(self, piece_of):
        w = self.w
        self.copies = []
        for d in (2, 1, 3):
            to = lax.rem(w.i + d, 4)
            self.out[d - 1] = low(piece_of(to))
            copy = w.remote(self.out.at[d - 1], self.got.at[d - 1], self.send + d, self.recv + d, to, w.s)
            copy.start()
            self.copies.append(copy)

    def total(self, own):
        w = self.w
        total = own
        for d in range(1, 4):
            w.arrived(self.got.at[d - 1], self.recv + d)
            total = total + self.got[d - 1].astype(jnp.float32)
        for copy in self.copies:
            copy.wait_send()
        return total


def ffn_tile(b, t):
    rows = tile(t)
    sn, cg = b.sn[rows, :], b.cg[rows, :]
    half = b.w_in.shape[1] // 2
    both = mm(sn, b.w_in[...])
    gate, up = both[:, 0:half], both[:, half:]
    open_ = sig(gate)
    act = gate * open_
    hidden = low(act * up)
    b.hid[rows, :] = hidden
    b.part4[rows, :] = low(mm(hidden, b.w_down[...]))
    hgrad = mm(cg, b.w_down[...], NT)
    both_grad = jnp.concatenate(
        [low(hgrad * up * (open_ * (1.0 + gate * (1.0 - open_)))), low(hgrad * act)], axis=1
    )
    b.gug[rows, :] = both_grad
    b.part[rows, :] = low(mm(both_grad, b.w_in[...], NT))


def norm_back(x, gain, grad):
    inv = lax.rsqrt(jnp.mean(x * x, axis=-1, keepdims=True) + epsilon)
    unit = x * inv
    dunit = grad * gain
    return inv * (dunit - unit * jnp.mean(dunit * unit, axis=-1, keepdims=True)), grad * unit


def mixer_out_back(b, t, head_gain_sum):
    rows = tile(t)
    ng = mm(b.agr[rows, :], b.w_out[...], NT)
    gate = b.gi[rows, :]
    open_ = sig(gate)
    act = gate * open_
    gain = b.head_gain[...]
    mixed = b.mixed[rows, :]
    inv = lax.rsqrt(jnp.mean(mixed * mixed, axis=-1, keepdims=True) + epsilon)
    unit = mixed * inv
    dunit = ng * act * gain
    b.do[rows, :] = inv * (dunit - unit * jnp.mean(dunit * unit, axis=-1, keepdims=True))
    nu = ng * unit
    b.gg[rows, :] = low(nu * gain * (open_ * (1.0 + gate * (1.0 - open_))))
    return head_gain_sum + jnp.sum(nu * act, axis=0, keepdims=True)


def rec_back_chain(b, t, ds1, row, col):
    rows = tile(t)
    do = low(b.do[rows, :])
    b.dstates[t] = ds1
    cum = b.cum[rows, :]
    last = cum[CH - 1 : CH, :]
    du = mm(b.qk[rows, :], do, TN) + mm(b.k[rows, :] * jnp.exp(last - cum), ds1)
    du16 = low(du)
    b.dr[rows, :] = mm(b.tinv[rows, :], du16, TN)
    return jnp.exp(last) * ds1 + mm(b.q[rows, :] * jnp.exp(cum), do, TN) - mm(b.wm[rows, :], du16, TN)


def rec_back_tile(b, t, row, col):
    rows = tile(t)
    q, k, v, e = b.q[rows, :], b.k[rows, :], b.v[rows, :], b.ge[rows, 1:2]
    s0, ds1, u, do, dr = b.states[t], b.dstates[t], b.u[rows, :], b.do[rows, :], b.dr[rows, :]
    cum, decay = decay_parts(b.ge[rows, 0:1], row, col)
    last = cum[CH - 1 : CH, :]
    gamma, shrink, remain = jnp.exp(last), jnp.exp(cum), jnp.exp(last - cum)
    gram = jnp.where(col < row, mm(k, k, NT) * decay, 0.0)
    qk = mm(q, k, NT) * decay
    dp = jnp.where(col <= row, mm3(do, u, NT), 0.0)
    da = jnp.where(col < row, -mm3(dr, u, NT), 0.0)
    dqk = low(dp * decay)
    dag = da * gram
    zed = dp * qk + e * dag
    dgram = low(e * da * decay)
    nk = mm3(dr, s0, NT)
    m = mm3(do, s0, NT)
    lm = mm3(u, ds1, NT)
    row_nk = jnp.sum(nk * k, axis=1, keepdims=True)
    dv = e * dr
    de = (
        jnp.sum(dr * v, axis=1, keepdims=True)
        - shrink * row_nk
        + jnp.sum(dag, axis=1, keepdims=True)
    )
    dq = mm(dqk, k) + shrink * m
    dk = mm(dqk, q, TN) + mm(dgram, k) + mm(dgram, k, TN) - (e * shrink) * nk + remain * lm
    dshrink = jnp.sum(m * q, axis=1, keepdims=True) - e * row_nk
    rdr = remain * jnp.sum(lm * k, axis=1, keepdims=True)
    ones = jnp.ones((CH, 1), jnp.float32)
    dcum = jnp.sum(zed, axis=1, keepdims=True) - mmf(zed, ones, TN) + shrink * dshrink - rdr
    dlast = jnp.sum(rdr, axis=0, keepdims=True) + gamma * jnp.sum(
        jnp.sum(s0 * ds1, axis=1, keepdims=True), axis=0, keepdims=True
    )
    lower = (col <= row).astype(jnp.float32)
    dg = mmf(lower, dcum, TN) + dlast
    return dq, dk, dv, dg, de


def unit_back(x, grad):
    inv = lax.rsqrt(jnp.sum(x * x, axis=-1, keepdims=True) + epsilon)
    unit = x * inv
    return inv * (grad - unit * jnp.sum(grad * unit, axis=-1, keepdims=True))


def mixer_back_tile(b, w, t, row, col, sums):
    rows = tile(t)
    dq, dk, dv, dg, de = rec_back_tile(b, t, row, col)
    total = conv_sums(b, w, t)
    open_ = sig(total)
    act = total * open_
    dact = jnp.concatenate(
        [unit_back(act[:, 0:DK], dq * DK ** (-0.5)), unit_back(act[:, DK : 2 * DK], dk), dv], axis=1
    )
    dcs = dact * (open_ * (1.0 + total * (1.0 - open_)))
    b.dcs[0:CH, :] = dcs
    window = b.ci[pl.ds(pl.multiple_of(t * CH, CH), CH + HALO), :].astype(jnp.float32)
    ahead = b.dcs[...]
    taps_sums, p0, p1, p2, gain_sum = sums
    dci = None
    new_taps = []
    for n in range(KCONV):
        at = HALO - (KCONV - 1) + n
        new_taps.append(taps_sums[n] + jnp.sum(dcs * window[at : at + CH], axis=0, keepdims=True))
        back = KCONV - 1 - n
        term = ahead[back : back + CH] * own_taps(b, w, n)
        dci = term if dci is None else dci + term
    b.dcs[CH : CH + HALO, :] = dcs[0:HALO]
    dci16 = low(dci)
    b.cgd[rows, :] = dci16
    lane = lax.broadcasted_iota(jnp.int32, (CH, 16), 1)
    pm = own_head(b, w)
    shift = b.ge[rows, 2:3]
    dshift = dg * (-jnp.exp(pm[0:1, :])) * sig(shift)
    e = b.ge[rows, 1:2]
    dlogit = de * e * (1.0 - e)
    hg = low(jnp.where(lane == w.s, dshift, jnp.where(lane == w.s + 8, dlogit, 0.0)))
    b.hg[rows, :] = hg
    fp = mm(dci16, b.w_qkv[...], NT) + mm(hg, b.head_w[...], NT) + mm(b.gg[rows, :], b.w_gate[...], NT)
    b.part[rows, :] = low(fp)
    gain_part = jnp.sum(fp * b.fn[rows, :].astype(jnp.float32), axis=0, keepdims=True)
    return (
        tuple(new_taps),
        p0 + jnp.sum(dg * b.ge[rows, 0:1], axis=0, keepdims=True),
        p1 + jnp.sum(dshift, axis=0, keepdims=True),
        p2 + jnp.sum(dlogit, axis=0, keepdims=True),
        gain_sum + gain_part,
    )


class LayerOut:
    output = ((128, 1024), B16)
    input_grad = ((128, 1024), B16)
    gains_grad = ((2, 1024), F32)
    head_gain_grad = ((1, 256), F32)
    params_grad = ((8, 128), F32)
    head_w_grad = ((16, 1024), F32)
    conv_grad = ((4, 4096), F32)
    qkv_back = ((256, 512), B16)
    gate_back = ((256, 256), B16)
    in_back = ((256, 768), B16)
    out_back = ((512, 128), B16)
    down_back = ((768, 128), B16)
class RestScratch:
    hid = ((1024, 384), B16)
    gug = ((1024, 768), B16)
    part4 = ((1024, 1024), B16)
    sib4 = ((4, 128, 1024), B16)
    chip4 = ((4, 128, 1024), B16)
    got4 = ((4, 128, 1024), B16)
    sib6 = ((4, 128, 1024), B16)
    got6 = ((4, 128, 1024), B16)
    own_ag = ((128, 1024), B16)
    mgrad = ((128, 1024), F32)
    gg = ((1024, 256), B16)
    dstates = ((4, 128, 256), F32)
    dcs = ((CH + HALO, 512), F32)
    cgd = ((1024, 512), B16)
    hg = ((1024, 16), B16)
    in_out = ((3, 256, 768), B16)
    in_got = ((3, 256, 768), B16)
    down_out = ((3, 384, 256), B16)
    down_got = ((3, 384, 256), B16)
    out_out = ((3, 256, 256), B16)
    out_got = ((3, 256, 256), B16)
    qkv_out = ((3, 256, 512), B16)
    qkv_got = ((3, 256, 512), B16)
    gate_out = ((3, 256, 256), B16)
    gate_got = ((3, 256, 256), B16)
    in_sum = ((256, 768), B16)
    down_sum = ((384, 256), B16)
    out_sum = ((256, 256), B16)
    qkv_sum = ((256, 512), B16)
    small = ((8, 1024), F32)
    small_got = ((4, 8, 1024), F32)
    small_sum = ((8, 1024), F32)
    small_all = ((8, 8, 1024), F32)


def grads_home(w, b):
    i, h = w.i, w.s
    send, recv = w.take(9), w.take(10)
    quarter, pair, half = lax.rem(h, 4), lax.rem(h, 2), h // 4

    def ffn():
        waits = [
            w.push(b.in_sum.at[:, 0:384], cols(b.in_back, 384 * half, 384), send, recv + 4 + half, i, quarter),
            w.push(b.in_sum.at[:, 384:768], cols(b.in_back, 384 * half, 384), send + 1, recv + 4 + half, i, 4 + quarter),
        ]
        for r in range(2):
            waits.append(
                w.push(
                    b.down_sum.at[:, 128 * r : 128 * r + 128],
                    rows_of(b.down_back, 384 * half, 384),
                    send + 2 + r,
                    recv + 8 + half,
                    quarter,
                    2 * i + r,
                )
            )
        return waits

    def mixer():
        waits = [
            w.push(b.qkv_sum.at[:, 0:128], cols(b.qkv_back, 128 * quarter, 128), send + 4, recv + quarter, i, half),
            w.push(b.qkv_sum.at[:, 128:256], cols(b.qkv_back, 128 * quarter, 128), send + 5, recv + quarter, i, 2 + half),
            w.push(b.qkv_sum.at[:, 256:512], cols(b.qkv_back, 256 * pair, 256), send + 6, recv + pair, i, 4 + h // 2),
        ]
        return waits

    def mixer_out():
        waits = []
        for r in range(2):
            waits.append(
                w.push(
                    b.out_sum.at[:, 128 * r : 128 * r + 128],
                    rows_of(b.out_back, 256 * pair, 256),
                    send + 7 + r,
                    recv + 6 + pair,
                    h // 2,
                    2 * i + r,
                )
            )
        return waits

    def landed():
        @pl.when(h < 4)
        def _():
            for t in range(4):
                w.arrived(b.qkv_back.at[:, 128 * t : 128 * t + 128], recv + t)

        @pl.when(h >= 4)
        def _():
            for t in range(2):
                w.arrived(b.qkv_back.at[:, 256 * t : 256 * t + 256], recv + t)

        for r in range(2):
            w.arrived(b.in_back.at[:, 384 * r : 384 * r + 384], recv + 4 + r)
            w.arrived(b.out_back.at[256 * r : 256 * r + 256, :], recv + 6 + r)
            w.arrived(b.down_back.at[384 * r : 384 * r + 384, :], recv + 8 + r)

    return ffn, mixer, mixer_out, landed


def small_sums(w, b, send, recv, send2, recv2):
    copies = []
    for d in range(1, 4):
        copy = w.remote(b.small, b.small_got.at[d], send + d, recv + d, lax.rem(w.i + d, 4), w.s)
        copy.start()
        copies.append(copy)

    def middle():
        total = b.small[...]
        for d in range(1, 4):
            w.arrived(b.small_got.at[d], recv + d)
            total = total + b.small_got[d]
        b.small_sum[...] = total
        b.small_all[w.s] = total
        for d in range(1, 8):
            copy = w.remote(b.small_sum, b.small_all.at[w.s], send2 + d, recv2 + d, w.i, lax.rem(w.s + d, 8))
            copy.start()
            copies.append(copy)

    def end():
        for d in range(1, 8):
            w.arrived(b.small_all.at[lax.rem(w.s + 8 - d, 8)], recv2 + d)
        for copy in copies:
            copy.wait_send()
        gains = b.small_all[0, 0:2, :]
        head_gain = b.small_all[0, 2:3, 0:256]
        for n in range(1, 8):
            gains = gains + b.small_all[n, 0:2, :]
            head_gain = head_gain + b.small_all[n, 2:3, 0:256]
        b.gains_grad[...] = gains
        b.head_gain_grad[...] = head_gain
        for n in range(8):
            b.params_grad[n : n + 1, :] = b.small_all[n, 3:4, 0:128]
            b.head_w_grad[n : n + 1, :] = b.small_all[n, 4:5, :]
            b.head_w_grad[8 + n : 9 + n, :] = b.small_all[n, 5:6, :]
            for k in range(KCONV):
                line = b.small_all[n, 6 + k // 2 : 7 + k // 2, 512 * (k % 2) : 512 * (k % 2) + 512]
                b.conv_grad[k : k + 1, 128 * n : 128 * n + 128] = line[:, 0:128]
                b.conv_grad[k : k + 1, 1024 + 128 * n : 1152 + 128 * n] = line[:, 128:256]
                b.conv_grad[k : k + 1, 2048 + 256 * n : 2304 + 256 * n] = line[:, 256:512]

    return middle, end


def rest_phase(b, w, sn_gather, cg_gather, front_finish):
    s = w.s
    half_rows = lambda ref: (lambda n: rows_of(ref, 128 * n, 128))
    ag_gather = LineGather(w, half_rows(b.agr))
    scatter4 = LineScatter(w, b.part4, b.sib4, b.chip4, b.got4)
    scatter6 = LineScatter(w, b.part, b.sib6, b.chip, b.got6)
    scatter8 = LineScatter(w, b.part, b.sib, b.chip, b.got)
    in_sum = GroupScatter(w, b.in_out, b.in_got)
    down_sum = GroupScatter(w, b.down_out, b.down_got)
    out_sum = GroupScatter(w, b.out_out, b.out_got)
    qkv_sum = GroupScatter(w, b.qkv_out, b.qkv_got)
    gate_sum = GroupScatter(w, b.gate_out, b.gate_got)
    home_ffn, home_qkv, home_out, home_landed = grads_home(w, b)
    sm = (w.take(4), w.take(4), w.take(8), w.take(8))

    def ffn_loop(n, carry):
        @pl.when(n > 0)
        def _():
            sn_gather.arrive(n)

        sn_gather.other(n)
        cg_gather.other(n)
        t = w.order(n)
        ffn_tile(b, t)
        scatter6.swap(t)
        scatter4.swap(t)

        @pl.when(n > 0)
        def _():
            scatter6.pass_on(w.order(n - 1))

        return carry

    lax.fori_loop(0, 4, ffn_loop, 0)
    scatter6.pass_on(w.order(3))
    scatter6.relay(w.order(2))
    scatter6.relay(w.order(3))

    def in_piece(n):
        return mm(cols(b.sn, 256 * n, 256)[...], b.gug[...], TN)

    def down_piece(n):
        return mm(b.hid[...], cols(b.cg, 256 * n, 256)[...], TN)

    in_sum.start(in_piece)
    down_sum.start(down_piece)
    second_grad = scatter6.total()
    back, share = norm_back(b.middle[...], b.gains[1:2, :], second_grad)
    b.small[1:2, :] = jnp.sum(share, axis=0, keepdims=True)
    mgrad = b.cot_v[...].astype(jnp.float32) + back
    b.mgrad[...] = mgrad
    own = low(mgrad)
    b.own_ag[...] = own
    rows_of(b.agr, 128 * s, 128)[...] = own
    ag_gather.start(b.own_ag)
    for n in range(1, 4):
        ag_gather.arrive(n)
    scatter6.finish()
    for n in range(4):
        ag_gather.other(n)
    for t in range(4):
        scatter4.pass_on(t)
    b.in_sum[...] = low(in_sum.total(in_piece(w.i)))
    b.down_sum[...] = low(down_sum.total(down_piece(w.i)))
    waits = home_ffn()

    def out_piece(n):
        return mm(b.normed[...], cols(b.agr, 256 * n, 256)[...], TN)

    out_sum.start(out_piece)
    row, col = grid_masks()

    def chain_loop(n, carry):
        ds1, head_gain_sum = carry
        t = 3 - n
        head_gain_sum = mixer_out_back(b, t, head_gain_sum)
        return rec_back_chain(b, t, ds1, row, col), head_gain_sum

    unused, head_gain_sum = lax.fori_loop(
        0, 4, chain_loop, (jnp.zeros((DK, DV), F32), jnp.zeros((1, DV), F32))
    )
    for t in range(4):
        scatter4.relay(t)
    b.dcs[CH : CH + HALO, :] = jnp.zeros((HALO, 512), F32)

    def back_loop(n, sums):
        t = 3 - n
        sums = mixer_back_tile(b, w, t, row, col, sums)
        scatter8.swap(t)

        @pl.when(n > 0)
        def _():
            scatter8.pass_on(t + 1)

        @pl.when(n > 1)
        def _():
            scatter8.relay(t + 2)

        return sums

    one = jnp.zeros((1, 1), F32)
    taps_sums, p0, p1, p2, gain_sum = lax.fori_loop(
        0, 4, back_loop, (tuple(jnp.zeros((1, 512), F32) for n in range(KCONV)), one, one, one, jnp.zeros((1, 1024), F32))
    )
    scatter8.pass_on(0)
    scatter8.relay(1)
    scatter8.relay(0)

    def qkv_piece(n):
        return mm(cols(b.fn, 256 * n, 256)[...], b.cgd[...], TN)

    def gate_piece(n):
        return mm(cols(b.fn, 256 * n, 256)[...], b.gg[...], TN)

    qkv_sum.start(qkv_piece)
    gate_sum.start(gate_piece)
    b.small[0:1, :] = gain_sum / b.gains[0:1, :]
    b.small[2:3, :] = jnp.concatenate([head_gain_sum, jnp.zeros((1, 1024 - DV), F32)], axis=1)
    lane = lax.broadcasted_iota(jnp.int32, (1, 1024), 1)
    b.small[3:4, :] = jnp.where(lane == 0, p0, jnp.where(lane == 1, p1, jnp.where(lane == 2, p2, 0.0)))
    head_rows = mm(b.hg[...], b.fn[...], TN)
    line = lax.broadcasted_iota(jnp.int32, head_rows.shape, 0)
    b.small[4:5, :] = jnp.sum(jnp.where(line == s, head_rows, 0.0), axis=0, keepdims=True)
    b.small[5:6, :] = jnp.sum(jnp.where(line == s + 8, head_rows, 0.0), axis=0, keepdims=True)
    b.small[6:7, :] = jnp.concatenate([taps_sums[0], taps_sums[1]], axis=1)
    b.small[7:8, :] = jnp.concatenate([taps_sums[2], taps_sums[3]], axis=1)
    small_middle, small_end = small_sums(w, b, *sm)
    b.out_sum[...] = low(out_sum.total(out_piece(w.i)))
    waits = waits + home_out()
    b.qkv_sum[...] = low(qkv_sum.total(qkv_piece(w.i)))
    waits = waits + home_qkv()
    b.gate_back[...] = low(gate_sum.total(gate_piece(w.i)))
    small_middle()
    b.output[...] = low(jnp.where(b.valid[...] > 0.0, b.middle[...] + scatter4.total(), 0.0))
    first_grad = scatter8.total()
    back, unused_share = norm_back(b.tokens_v[...].astype(jnp.float32), b.gains[0:1, :], first_grad)
    b.input_grad[...] = low(b.mgrad[...] + back)
    small_end()
    home_landed()
    for wait in waits:
        wait()
    scatter4.finish()
    scatter8.finish()
    ag_gather.finish()
    front_finish()


def layer_kernel(dp, seq, *refs):
    b = Box()
    (
        b.tokens,
        b.cot,
        b.qkv,
        b.gate,
        b.ffn_in,
        b.out,
        b.ffn_out,
        b.gains,
        b.head_gain,
        b.params,
        b.head_w,
        b.taps,
        b.tokens_v,
        b.cot_v,
        b.valid,
    ) = refs[:15]
    kinds = fields(LayerOut) + fields(FrontKept) + fields(FrontScratch) + fields(RestScratch)
    for (name, shape, kind), ref in zip(kinds, refs[15:]):
        setattr(b, name, ref)
    b.do, b.dr, b.agr = b.mixed, b.gi, b.x
    w = Wires(dp, seq, refs[-1])
    rest_phase(b, w, *front_phase(b, w))


def layer(dp, seq, *arrays):
    outs = pl.pallas_call(
        functools.partial(layer_kernel, dp, seq),
        out_shape=tuple(jax.ShapeDtypeStruct(shape, kind) for _, shape, kind in fields(LayerOut)),
        in_specs=[ANY] * 7 + [IN_VMEM] * 8,
        out_specs=(IN_VMEM,) * len(fields(LayerOut)),
        scratch_shapes=[
            pltpu.VMEM(shape, kind)
            for _, shape, kind in fields(FrontKept) + fields(FrontScratch) + fields(RestScratch)
        ]
        + [pltpu.SemaphoreType.DMA((500,))],
        compiler_params=pltpu.CompilerParams(collective_id=0, has_side_effects=True, vmem_limit_bytes=62 << 20),
        name="layer",
    )(*arrays)
    made = Box()
    for (name, shape, kind), out in zip(fields(LayerOut), outs):
        setattr(made, name, out)
    return made


def fast_body(
    dp,
    seq,
    tokens,
    lengths,
    cotangent,
    norm_gains,
    head_gain,
    head_params,
    qkv_weight,
    gate_weight,
    head_weight,
    conv_weight,
    out_weight,
    ffn_in,
    ffn_out,
):
    seq_count, block_len, width = tokens.shape
    ff_cols, ff_rows = ffn_in.shape[1], ffn_out.shape[0]
    position = lax.axis_index("seq") * block_len + jnp.arange(block_len, dtype=jnp.int32)
    valid = (position < lengths[0])[:, None]
    cot = jnp.where(valid, cotangent[0], jnp.zeros_like(cotangent[0]))
    r = layer(
        dp,
        seq,
        tokens[0],
        cot,
        qkv_weight,
        gate_weight,
        jnp.pad(ffn_in, ((0, 0), (0, 768 - ff_cols))),
        out_weight,
        jnp.pad(ffn_out, ((0, 768 - ff_rows), (0, 0))),
        norm_gains,
        head_gain[None],
        head_params,
        head_weight,
        conv_weight.astype(jnp.float32).T,
        tokens[0],
        cot,
        valid.astype(jnp.float32),
    )
    wide = jnp.float32
    return (
        r.output[None],
        r.input_grad[None],
        r.gains_grad,
        r.head_gain_grad[0],
        r.params_grad[:, 0:3].T,
        r.qkv_back.astype(wide),
        r.gate_back.astype(wide),
        r.head_w_grad.T,
        r.conv_grad.T,
        r.out_back.astype(wide),
        r.in_back[:, 0:ff_cols].astype(wide),
        r.down_back[0:ff_rows].astype(wide),
    )


def choose_body(dp, seq):
    def chosen(*arrays):
        tokens, head_params = arrays[0], arrays[5]
        if (dp, seq) == (4, 8) and tokens.shape[0] == 1 and head_params.shape[1] == seq:
            return fast_body(dp, seq, *arrays)
        return general_body(*arrays)

    return chosen


def solution(mesh):
    dp, seq = mesh.shape["dp"], mesh.shape["seq"]
    placed = (
        P("dp", "seq", None),
        P("dp"),
        P("dp", "seq", None),
        P(),
        P(),
        P(),
        P("dp", "seq"),
        P("dp", "seq"),
        P(),
        P(),
        P("dp", "seq"),
        P("dp", "seq"),
        P("dp", "seq"),
    )
    return jax.shard_map(
        choose_body(dp, seq),
        mesh=mesh,
        in_specs=placed,
        out_specs=(
            P("dp", "seq", None),
            P("dp", "seq", None),
            P(),
            P(),
            P(),
            P("dp", "seq"),
            P("dp", "seq"),
            P(),
            P(),
            P("dp", "seq"),
            P("dp", "seq"),
            P("dp", "seq"),
        ),
        check_vma=False,
    )
```

```python
import functools

import jax
import jax.numpy as jnp
from jax import lax
from jax.experimental import pallas as pl
from jax.experimental.pallas import tpu as pltpu
from jax.sharding import PartitionSpec as P

CH = 256
DK = 128
DV = 256
KCONV = 4
TILE = 64


HIGHEST = lax.Precision.HIGHEST
epsilon = 1e-06


def passed_along(block, axis, distance):
    devices = range(lax.axis_size(axis))
    route = [(i - distance, i) for i in devices if i - distance in devices]
    return lax.ppermute(block, axis, route)


def rms_scale(values, gain_row):
    return (
        values * lax.rsqrt(jnp.mean(values * values, axis=-1, keepdims=True) + epsilon) * gain_row
    )


def unit_rows(values):
    return values * lax.rsqrt(jnp.sum(values * values, axis=-1, keepdims=True) + epsilon)


def block_step(state_now, query_vecs, key_vecs, value_vecs, log_decay, erase_rate):
    length = query_vecs.shape[1]
    cumulative = jnp.cumsum(log_decay, axis=1)
    row_index = jnp.arange(length)[:, None]
    col_index = jnp.arange(length)[None, :]
    strict = col_index < row_index
    within = col_index <= row_index
    spread = cumulative[:, :, None] - cumulative[:, None, :]
    lower_decay = jnp.where(strict, jnp.exp(jnp.where(strict, spread, 0.0)), 0.0)
    causal = jnp.where(within, jnp.exp(jnp.where(within, spread, 0.0)), 0.0)
    key_gram = jnp.einsum("htk,hsk->hts", key_vecs, key_vecs, precision=HIGHEST)
    query_gram = jnp.einsum("htk,hsk->hts", query_vecs, key_vecs, precision=HIGHEST)
    negated = -(erase_rate[:, :, None] * key_gram * lower_decay)
    identity = jnp.eye(length, dtype=jnp.float32)
    inverse = identity + negated
    powered = negated
    for level_index in range(length.bit_length() - 2):
        powered = jnp.einsum("hts,hsr->htr", powered, powered, precision=HIGHEST)
        inverse = jnp.einsum("hts,hsr->htr", inverse, identity + powered, precision=HIGHEST)
    shrink = jnp.exp(cumulative)
    recalled = jnp.einsum("htk,hkw->htw", key_vecs, state_now, precision=HIGHEST)
    target = erase_rate[:, :, None] * value_vecs - (erase_rate * shrink)[:, :, None] * recalled
    updates = jnp.einsum("hts,hsw->htw", inverse, target, precision=HIGHEST)
    read_out = shrink[:, :, None] * jnp.einsum(
        "htk,hkw->htw", query_vecs, state_now, precision=HIGHEST
    )
    read_out = read_out + jnp.einsum(
        "hts,hsw->htw", query_gram * causal, updates, precision=HIGHEST
    )
    remain = jnp.exp(cumulative[:, -1:] - cumulative)
    state_next = jnp.exp(cumulative[:, -1])[:, None, None] * state_now
    state_next = state_next + jnp.einsum(
        "hsk,hsw->hkw", key_vecs * remain[:, :, None], updates, precision=HIGHEST
    )
    return (state_next, read_out)


def run_tiles(query_vecs, key_vecs, value_vecs, log_decay, erase_rate, state_start):
    row_count, head_count, key_width = query_vecs.shape
    tile_count = row_count // TILE

    def arrange(tensor):
        return jnp.swapaxes(tensor.reshape((tile_count, TILE, head_count) + tensor.shape[2:]), 1, 2)

    inputs = (
        arrange(query_vecs),
        arrange(key_vecs),
        arrange(value_vecs),
        arrange(log_decay),
        arrange(erase_rate),
    )

    def advance(state_now, sliced):
        return jax.checkpoint(block_step)(state_now, *sliced)

    state_end, outputs = lax.scan(advance, state_start, inputs)
    outputs = jnp.swapaxes(outputs, 1, 2).reshape(row_count, head_count, outputs.shape[-1])
    return (outputs, state_end)


def mixer_inputs(conv_in, edge_rows, head_in, conv_taps, head_params):
    block_len = conv_in.shape[1]
    head_count = head_params.shape[1]
    extended = jnp.concatenate([edge_rows, conv_in], axis=1)
    conv_sum = extended[:, 0:block_len] * conv_taps[:, 0]
    for offset in range(1, conv_taps.shape[1]):
        conv_sum = conv_sum + extended[:, offset : offset + block_len] * conv_taps[:, offset]
    activated = jax.nn.silu(conv_sum)
    key_span = head_count * DK
    lead = activated.shape[:2]
    query_vecs = unit_rows(activated[..., 0:key_span].reshape(lead + (head_count, DK))) * DK ** (
        -0.5
    )
    key_vecs = unit_rows(activated[..., key_span : 2 * key_span].reshape(lead + (head_count, DK)))
    value_vecs = activated[..., 2 * key_span :].reshape(lead + (head_count, DV))
    log_decay = -jnp.exp(head_params[0]) * jax.nn.softplus(
        head_in[..., 0:head_count] + head_params[1]
    )
    erase_rate = jax.nn.sigmoid(head_in[..., head_count : 2 * head_count] + head_params[2])
    return (query_vecs, key_vecs, value_vecs, log_decay, erase_rate)


def gated_norm(mixed, gate_in, head_gain):
    shaped = gate_in.reshape(mixed.shape)
    normed = (
        mixed * lax.rsqrt(jnp.mean(mixed * mixed, axis=-1, keepdims=True) + epsilon) * head_gain
    )
    return (normed * jax.nn.silu(shaped)).reshape(gate_in.shape)


def local_tiles(query_vecs, key_vecs, value_vecs, log_decay, erase_rate):
    key_width = key_vecs.shape[-1]
    value_width = value_vecs.shape[-1]
    head_count = key_vecs.shape[2]
    padded = jnp.concatenate(
        [jnp.zeros(value_vecs.shape[:3] + (key_width,), jnp.float32), value_vecs], axis=-1
    )
    start_map = jnp.concatenate(
        [jnp.eye(key_width, dtype=jnp.float32), jnp.zeros((key_width, value_width), jnp.float32)],
        axis=1,
    )
    start_map = jnp.broadcast_to(start_map, (head_count, key_width, key_width + value_width))

    def single(query_one, key_one, value_one, decay_one, erase_one):
        return run_tiles(query_one, key_one, value_one, decay_one, erase_one, start_map)

    return jax.vmap(single)(query_vecs, key_vecs, padded, log_decay, erase_rate)


def post_mix(local_out, incoming, gate_in, head_gain):
    mixed = local_out[..., DK:] + jnp.einsum(
        "snhk,shkv->snhv", local_out[..., 0:DK], incoming, precision=HIGHEST
    )
    return gated_norm(mixed, gate_in, head_gain)


def swiglu(gate_up):
    split_at = gate_up.shape[-1] // 2
    return jax.nn.silu(gate_up[:, 0:split_at]) * gate_up[:, split_at:]


def matmul_maps(left, right):
    return jnp.einsum("shij,shjk->shik", left, right, precision=HIGHEST)


def apply_map(maps, state_now):
    return matmul_maps(maps[0], state_now) + maps[1]


def general_body(
    tokens,
    lengths,
    cotangent,
    norm_gains,
    head_gain,
    head_params,
    qkv_weight,
    gate_weight,
    head_weight,
    conv_weight,
    out_weight,
    ffn_in,
    ffn_out,
):
    seq_count, block_len, model_width = tokens.shape
    row_count = seq_count * block_len
    position = lax.axis_index("seq") * block_len + jnp.arange(block_len, dtype=jnp.int32)
    valid_rows = (position[None, :] < lengths[:, None]).reshape(row_count, 1)
    col_parts = (
        lax.all_gather(qkv_weight, "seq", axis=1, tiled=True),
        lax.all_gather(gate_weight, "seq", axis=1, tiled=True),
        lax.all_gather(out_weight, "seq", axis=1, tiled=True),
        lax.all_gather(ffn_in, "seq", axis=1, tiled=True),
        lax.all_gather(ffn_out, "seq", axis=1, tiled=True),
    )
    gathered = (
        lax.all_gather(col_parts[0], "dp", axis=0, tiled=True),
        lax.all_gather(col_parts[1], "dp", axis=0, tiled=True),
        lax.all_gather(col_parts[2], "dp", axis=0, tiled=True),
        lax.all_gather(col_parts[3], "dp", axis=0, tiled=True),
        lax.all_gather(col_parts[4], "dp", axis=0, tiled=True),
    )
    w_qkv, w_gate, w_out, w_in, w_down = gathered
    inputs = tokens.reshape(row_count, model_width).astype(jnp.float32)
    first_norm = rms_scale(inputs, norm_gains[0]).astype(jnp.bfloat16)
    conv_in = jnp.dot(first_norm, w_qkv, preferred_element_type=jnp.float32).astype(jnp.bfloat16)
    head_in = jnp.dot(first_norm, head_weight, preferred_element_type=jnp.float32)
    gate_in = jnp.dot(first_norm, w_gate, preferred_element_type=jnp.float32)
    conv_width = conv_in.shape[-1]
    conv_rows = conv_in.reshape(seq_count, block_len, conv_width)
    edge_cut = block_len - (KCONV - 1)
    edge_rows = passed_along(conv_rows[:, edge_cut:], "seq", 1)
    mix_args = (
        conv_rows.astype(jnp.float32),
        edge_rows.astype(jnp.float32),
        head_in.reshape(seq_count, block_len, -1),
        conv_weight.astype(jnp.float32),
        head_params,
    )
    vectors = mixer_inputs(*mix_args)
    local_out, end_states = local_tiles(*vectors)
    carry_maps = (end_states[..., 0:DK], end_states[..., DK:])

    def relay_state(step_index, state_now):
        return passed_along(apply_map(carry_maps, state_now), "seq", 1)

    incoming = lax.fori_loop(
        0, lax.axis_size("seq") - 1, relay_state, jnp.zeros_like(carry_maps[1])
    )
    post_args = (local_out, incoming, gate_in, head_gain)
    normed = post_mix(*post_args).astype(jnp.bfloat16)
    attended = jnp.dot(normed, w_out, preferred_element_type=jnp.float32)
    middle = inputs + attended
    second_norm = rms_scale(middle, norm_gains[1]).astype(jnp.bfloat16)
    gate_up = jnp.dot(second_norm, w_in, preferred_element_type=jnp.float32)
    hidden = swiglu(gate_up).astype(jnp.bfloat16)
    carried = jnp.dot(hidden, w_down, preferred_element_type=jnp.float32)
    output = jnp.where(valid_rows, middle + carried, 0.0).astype(jnp.bfloat16)
    col_again = (
        lax.all_gather(qkv_weight, "seq", axis=1, tiled=True),
        lax.all_gather(gate_weight, "seq", axis=1, tiled=True),
        lax.all_gather(out_weight, "seq", axis=1, tiled=True),
        lax.all_gather(ffn_in, "seq", axis=1, tiled=True),
        lax.all_gather(ffn_out, "seq", axis=1, tiled=True),
    )
    regathered = (
        lax.all_gather(col_again[0], "dp", axis=0, tiled=True),
        lax.all_gather(col_again[1], "dp", axis=0, tiled=True),
        lax.all_gather(col_again[2], "dp", axis=0, tiled=True),
        lax.all_gather(col_again[3], "dp", axis=0, tiled=True),
        lax.all_gather(col_again[4], "dp", axis=0, tiled=True),
    )
    w_qkv, w_gate, w_out, w_in, w_down = regathered
    upstream = jnp.where(
        valid_rows, cotangent.reshape(row_count, model_width).astype(jnp.float32), 0.0
    )
    carried_grad = upstream.astype(jnp.bfloat16)
    grad_down = jnp.einsum("nf,nd->fd", hidden, carried_grad, preferred_element_type=jnp.float32)
    hidden_grad = jnp.einsum("nd,fd->nf", carried_grad, w_down, preferred_element_type=jnp.float32)
    unused, swiglu_back = jax.vjp(swiglu, gate_up)
    gate_up_grad = swiglu_back(hidden_grad)[0].astype(jnp.bfloat16)
    grad_in = jnp.einsum("nd,nf->df", second_norm, gate_up_grad, preferred_element_type=jnp.float32)
    second_grad = jnp.einsum("nf,df->nd", gate_up_grad, w_in, preferred_element_type=jnp.float32)
    unused, second_back = jax.vjp(rms_scale, middle, norm_gains[1])
    middle_back, gain_two = second_back(second_grad)
    middle_grad = upstream + middle_back
    attended_grad = middle_grad.astype(jnp.bfloat16)
    grad_out = jnp.einsum("nv,nd->vd", normed, attended_grad, preferred_element_type=jnp.float32)
    normed_grad = jnp.einsum("nd,vd->nv", attended_grad, w_out, preferred_element_type=jnp.float32)
    unused, post_back = jax.vjp(post_mix, *post_args)
    local_grad, incoming_local, gate_in_grad, head_gain_grad = post_back(normed_grad)
    flipped = (jnp.swapaxes(carry_maps[0], -1, -2), incoming_local)

    def relay_grad(step_index, grad_now):
        return passed_along(apply_map(flipped, grad_now).astype(jnp.bfloat16), "seq", -1).astype(
            jnp.float32
        )

    outgoing = lax.fori_loop(
        0, lax.axis_size("seq") - 1, relay_grad, jnp.zeros_like(incoming_local)
    )
    map_grad = jnp.einsum("shkv,shjv->shkj", outgoing, incoming, precision=HIGHEST)
    end_grad = jnp.concatenate([map_grad, outgoing], axis=-1)
    unused, tiles_back = jax.vjp(local_tiles, *vectors)
    vector_grads = tiles_back((local_grad, end_grad))
    unused, mix_back = jax.vjp(mixer_inputs, *mix_args)
    conv_own, edge_grad, head_in_grad, conv_taps_grad, params_grad = mix_back(vector_grads)
    edge_back = passed_along(edge_grad.astype(jnp.bfloat16), "seq", -1).astype(edge_grad.dtype)
    conv_total = jnp.concatenate(
        [conv_own[:, 0:edge_cut], conv_own[:, edge_cut:] + edge_back], axis=1
    )
    conv_grad = conv_total.reshape(row_count, conv_width).astype(jnp.bfloat16)
    head_grad = head_in_grad.reshape(row_count, -1).astype(jnp.bfloat16)
    gate_grad = gate_in_grad.astype(jnp.bfloat16)
    grad_qkv = jnp.einsum("nd,nc->dc", first_norm, conv_grad, preferred_element_type=jnp.float32)
    grad_head = jnp.einsum("nd,nc->dc", first_norm, head_grad, preferred_element_type=jnp.float32)
    grad_gate = jnp.einsum("nd,nc->dc", first_norm, gate_grad, preferred_element_type=jnp.float32)
    first_grad = jnp.einsum("nc,dc->nd", conv_grad, w_qkv, preferred_element_type=jnp.float32)
    first_grad = first_grad + jnp.einsum(
        "nc,dc->nd", head_grad, head_weight, preferred_element_type=jnp.float32
    )
    first_grad = first_grad + jnp.einsum(
        "nc,dc->nd", gate_grad, w_gate, preferred_element_type=jnp.float32
    )
    unused, first_back = jax.vjp(rms_scale, inputs, norm_gains[0])
    input_back, gain_one = first_back(first_grad)
    input_grad = (
        (middle_grad + input_back).astype(jnp.bfloat16).reshape(seq_count, block_len, model_width)
    )
    row_groups = (
        lax.psum_scatter(
            grad_qkv.astype(jnp.bfloat16), "dp", scatter_dimension=0, tiled=True
        ).astype(jnp.float32),
        lax.psum_scatter(
            grad_gate.astype(jnp.bfloat16), "dp", scatter_dimension=0, tiled=True
        ).astype(jnp.float32),
        lax.psum_scatter(
            grad_out.astype(jnp.bfloat16), "dp", scatter_dimension=0, tiled=True
        ).astype(jnp.float32),
        lax.psum_scatter(
            grad_in.astype(jnp.bfloat16), "dp", scatter_dimension=0, tiled=True
        ).astype(jnp.float32),
        lax.psum_scatter(
            grad_down.astype(jnp.bfloat16), "dp", scatter_dimension=0, tiled=True
        ).astype(jnp.float32),
    )
    weight_parts = (
        lax.psum_scatter(
            row_groups[0].astype(jnp.bfloat16), "seq", scatter_dimension=1, tiled=True
        ).astype(jnp.float32),
        lax.psum_scatter(
            row_groups[1].astype(jnp.bfloat16), "seq", scatter_dimension=1, tiled=True
        ).astype(jnp.float32),
        lax.psum_scatter(
            row_groups[2].astype(jnp.bfloat16), "seq", scatter_dimension=1, tiled=True
        ).astype(jnp.float32),
        lax.psum_scatter(
            row_groups[3].astype(jnp.bfloat16), "seq", scatter_dimension=1, tiled=True
        ).astype(jnp.float32),
        lax.psum_scatter(
            row_groups[4].astype(jnp.bfloat16), "seq", scatter_dimension=1, tiled=True
        ).astype(jnp.float32),
    )
    small_sums = lax.psum(
        (jnp.stack([gain_one, gain_two]), head_gain_grad, params_grad, grad_head, conv_taps_grad),
        ("dp", "seq"),
    )
    output = output.reshape(seq_count, block_len, model_width)
    return (
        output,
        input_grad,
        small_sums[0],
        small_sums[1],
        small_sums[2],
        weight_parts[0],
        weight_parts[1],
        small_sums[3],
        small_sums[4],
        weight_parts[2],
        weight_parts[3],
        weight_parts[4],
    )


MESH = pl.DeviceIdType.MESH
ANY = pl.BlockSpec(memory_space=pl.ANY)
IN_VMEM = pl.BlockSpec(memory_space=pltpu.VMEM)
B16 = jnp.bfloat16
F32 = jnp.float32
NN = ((1,), (0,))
NT = ((1,), (1,))
TN = ((0,), (0,))
HALO = 16


def low(v):
    return v.astype(jnp.bfloat16)


def mm(a, b, dims=NN):
    return lax.dot_general(low(a), low(b), (dims, ((), ())), preferred_element_type=jnp.float32)


def mmf(a, b, dims=NN):
    return lax.dot_general(
        a, b, (dims, ((), ())), precision=HIGHEST, preferred_element_type=jnp.float32
    )


def mm3(a, b, dims=NN):
    ah, bh = low(a), low(b)
    al, bl = low(a - ah.astype(jnp.float32)), low(b - bh.astype(jnp.float32))
    return mm(ah, bh, dims) + (mm(ah, bl, dims) + mm(al, bh, dims))


def sig(v):
    return 1.0 / (1.0 + jnp.exp(-v))


def soft_plus(v):
    tail = jnp.exp(-jnp.abs(v))
    series = tail * (1.0 - tail * (0.5 - tail * (1.0 / 3.0)))
    return jnp.maximum(v, 0.0) + jnp.where(tail < 1e-3, series, jnp.log(1.0 + tail))


def grid_masks():
    row = lax.broadcasted_iota(jnp.int32, (CH, CH), 0)
    col = lax.broadcasted_iota(jnp.int32, (CH, CH), 1)
    return row, col


def decay_parts(g, row, col):
    lower = (col <= row).astype(jnp.float32)
    cum = mmf(lower, g)
    cum_row = mmf(g, lower, ((0,), (1,)))
    within = col <= row
    decay = jnp.where(within, jnp.exp(jnp.where(within, cum - cum_row, 0.0)), 0.0)
    return cum, decay


def unit_inverse(attns, row, col):
    def same(width):
        return (row // width) == (col // width)

    eye = jnp.where(row == col, 1.0, 0.0)
    power = [jnp.where(same(64), -a, 0.0) for a in attns]
    inv = [eye + p for p in power]
    for level in range(5):
        power = [mm(p, p) for p in power]
        inv = [x + mm(x, p) for x, p in zip(inv, power)]
    for width in (128, 256):
        off = same(width) & jnp.logical_not(same(width // 2))
        part = [mm(jnp.where(off, a, 0.0), x) for a, x in zip(attns, inv)]
        inv = [x - mm(x, p) for x, p in zip(inv, part)]
    rest = [eye - x - mm3(a, x) for a, x in zip(attns, inv)]
    return [x + mm(x, r) for x, r in zip(inv, rest)]


def odd(t):
    return t % 2 if isinstance(t, int) else lax.rem(t, 2)


def tile(t, size=CH):
    return pl.ds(pl.multiple_of(t * size, size), size)


class Wires:
    def __init__(self, dp, seq, sems):
        self.dp, self.seq, self.sems, self.used = dp, seq, sems, 0
        self.i, self.s = lax.axis_index("dp"), lax.axis_index("seq")
        self.z, self.c = self.s // 2, lax.rem(self.s, 2)
        self.half, self.partner = self.z // 2, self.z + 1 - 2 * lax.rem(self.z, 2)
        self.inner = lax.rem((self.z + 1) // 2, 2)
        self.place = lax.rem(self.z, 2)

    def take(self, count=1):
        start = self.used
        self.used += count
        return start

    def meet_all(self):
        barrier = pltpu.get_barrier_semaphore()
        for di in range(self.dp):
            for dj in range(self.seq):
                if di or dj:
                    pl.semaphore_signal(
                        barrier,
                        inc=1,
                        device_id=(lax.rem(self.i + di, self.dp), lax.rem(self.s + dj, self.seq)),
                        device_id_type=MESH,
                    )
        pl.semaphore_wait(barrier, self.dp * self.seq - 1)

    def remote(self, src, dst, send, recv, di, dj):
        return pltpu.make_async_remote_copy(
            src_ref=src,
            dst_ref=dst,
            send_sem=self.sems.at[send],
            recv_sem=self.sems.at[recv],
            device_id=(di, dj),
            device_id_type=MESH,
        )

    def local(self, src, dst, sem):
        return pltpu.make_async_copy(src, dst, self.sems.at[sem])

    def push(self, src, dst, send, recv, di, dj):
        here = (di == self.i) & (dj == self.s)
        away = self.remote(src, dst, send, recv, di, dj)

        @pl.when(here)
        def _():
            self.local(src, dst, recv).start()

        @pl.when(jnp.logical_not(here))
        def _():
            away.start()

        def sent():
            @pl.when(jnp.logical_not(here))
            def _():
                away.wait_send()

        return sent

    def arrived(self, dst, recv):
        pltpu.make_async_copy(dst, dst, self.sems.at[recv]).wait()

    def chip(self, z):
        return z * 2 + self.c

    def order(self, n):
        near = self.z + n * (1 - 2 * lax.rem(self.z, 2))
        return (1 - n // 2) * near + (n // 2) * (n + self.half * (3 - 2 * n))

    def sibling(self):
        return self.z * 2 + 1 - self.c


class LineGather:
    parts = 2

    def __init__(self, w, block_of):
        self.w, self.block_of = w, block_of
        n = 4 * self.parts
        self.send, self.recv = w.take(n), w.take(n)
        self.fsend, self.frecv = w.take(n), w.take(n)

    def piece(self, block, part):
        size = block.shape[0] // self.parts
        return block.at[part * size : part * size + size, :]

    def start(self, src):
        w = self.w
        dst = self.block_of(w.s)
        for part in range(self.parts):
            a, b = self.piece(src, part), self.piece(dst, part)
            slot = w.z * self.parts + part
            near, far = self.send + part, self.send + self.parts + part
            w.remote(a, b, near, self.recv + slot, w.i, w.chip(w.partner)).start()
            w.remote(a, b, far, self.recv + slot, w.i, w.chip(2 - w.half)).start()
        for part in range(self.parts):
            a, b = self.piece(src, part), self.piece(dst, part)
            slot = w.z * self.parts + part
            w.remote(a, b, self.fsend + slot, self.frecv + slot, w.i, w.sibling()).start()

    def arrive(self, t):
        w = self.w

        @pl.when(t != w.z)
        def _():
            block = self.block_of(w.chip(t))
            for part in range(self.parts):
                ref, slot = self.piece(block, part), t * self.parts + part
                w.arrived(ref, self.recv + slot)

                @pl.when((w.inner == 1) & (t // 2 != w.half))
                def _():
                    on = self.send + (2 + odd(t)) * self.parts + part
                    w.remote(ref, ref, on, self.recv + slot, w.i, w.chip(w.partner)).start()

                w.remote(ref, ref, self.fsend + slot, self.frecv + slot, w.i, w.sibling()).start()

    def other(self, t):
        w = self.w
        block = self.block_of(t * 2 + 1 - w.c)
        for part in range(self.parts):
            w.arrived(self.piece(block, part), self.frecv + t * self.parts + part)

    def finish(self):
        w = self.w
        block = self.block_of(w.s)
        for part in range(self.parts):
            ref = self.piece(block, part)
            for n in range(4):
                copy = w.remote(ref, ref, self.send + n * self.parts + part, self.recv, w.i, w.sibling())
                if n < 2:
                    copy.wait_send()
                else:
                    @pl.when(w.inner == 1)
                    def _():
                        copy.wait_send()

                w.remote(ref, ref, self.fsend + n * self.parts + part, self.recv, w.i, w.sibling()).wait_send()


class GroupGather:
    def __init__(self, w, part_of):
        self.w, self.part_of = w, part_of
        self.send, self.recv = w.take(4), w.take(4)

    def start(self, src):
        w = self.w
        w.local(src, self.part_of(w.i), self.recv).start()
        for d in (3, 1, 2):
            to = lax.rem(w.i + d, 4)
            w.remote(src, self.part_of(w.i), self.send + d, self.recv + d, to, w.s).start()

    def finish(self):
        w = self.w
        for d in range(4):
            w.arrived(self.part_of(lax.rem(w.i + 4 - d, 4)), self.recv + d)
        for d in range(1, 4):
            part = self.part_of(w.i)
            w.remote(part, part, self.send + d, self.recv + d, lax.rem(w.i + d, 4), w.s).wait_send()


class LineScatter:
    def __init__(self, w, part, sib, chip, got):
        self.w, self.part, self.sib, self.chip, self.got = w, part, sib, chip, got
        self.ssend, self.srecv = w.take(4), w.take(4)
        self.send, self.recv = w.take(4), w.take(4)

    def swap(self, t):
        w = self.w
        src = self.part.at[pl.ds(pl.multiple_of(t * 256 + 128 * (1 - w.c), 128), 128), :]
        w.remote(src, self.sib.at[t], self.ssend + t, self.srecv + t, w.i, w.sibling()).start()

    def out(self, t, slot, chip):
        w = self.w
        w.remote(self.chip.at[t], self.got.at[slot], self.send + t, self.recv + slot, w.i, w.chip(chip)).start()

    def pass_on(self, t):
        w = self.w
        w.arrived(self.sib.at[t], self.srecv + t)
        mine = self.part[pl.ds(pl.multiple_of(t * 256 + 128 * w.c, 128), 128), :]
        self.chip[t] = low(mine.astype(jnp.float32) + self.sib[t].astype(jnp.float32))

        @pl.when(t == w.partner)
        def _():
            self.out(t, 0, t)

        @pl.when((t // 2 != w.half) & (w.inner == 0))
        def _():
            self.out(t, 2 + odd(t), w.partner)

    def relay(self, t):
        w = self.w

        @pl.when((t // 2 != w.half) & (w.inner == 1))
        def _():
            slot = 2 + odd(t)
            w.arrived(self.got.at[slot], self.recv + slot)
            self.chip[t] = low(self.chip[t].astype(jnp.float32) + self.got[slot].astype(jnp.float32))
            self.out(t, 1, t)

    def total(self):
        w = self.w
        total = self.chip[w.z].astype(jnp.float32)
        for slot in range(2):
            w.arrived(self.got.at[slot], self.recv + slot)
            total = total + self.got[slot].astype(jnp.float32)
        return total

    def finish(self):
        w = self.w
        for t in range(4):
            src = self.part.at[pl.ds(t * 256, 128), :]
            w.remote(src, self.sib.at[t], self.ssend + t, self.srecv + t, w.i, w.sibling()).wait_send()

            @pl.when(w.z != t)
            def _():
                w.remote(self.chip.at[t], self.got.at[0], self.send + t, self.recv, w.i, w.sibling()).wait_send()


class PairGather:
    def __init__(self, w, buffer):
        self.w, self.buffer = w, buffer
        self.send, self.recv = w.take(3), w.take(3)

    def block(self, q, c):
        return rows_of(self.buffer, 256 * q + 128 * c, 128)

    def copies(self):
        w = self.w
        mine, theirs = self.block(w.place, w.c), self.block(1 - w.place, w.c)
        send, recv = self.send, self.recv
        return (
            w.remote(mine, mine, send, recv, w.i, w.chip(w.partner)),
            w.remote(mine, mine, send + 1, recv + 1, w.i, w.sibling()),
            w.remote(theirs, theirs, send + 2, recv + 2, w.i, w.sibling()),
        )

    def start(self):
        near, core, unused = self.copies()
        near.start()
        core.start()

    def arrive(self):
        w = self.w
        w.arrived(self.block(1 - w.place, w.c), self.recv)
        self.copies()[2].start()

    def other(self, n):
        w = self.w
        q = w.place + n * (1 - 2 * w.place)
        w.arrived(self.block(q, 1 - w.c), self.recv + 1 + n)

    def finish(self):
        for copy in self.copies():
            copy.wait_send()


class PairScatter:
    def __init__(self, w, part, sib, chip, got):
        self.w, self.part, self.sib, self.chip, self.got = w, part, sib, chip, got
        self.ssend, self.srecv = w.take(2), w.take(2)
        self.send, self.recv = w.take(), w.take()

    def swapped(self, q):
        w = self.w
        src = rows_of(self.part, 256 * q + 128 * (1 - w.c), 128)
        return w.remote(src, self.sib.at[q], self.ssend + q, self.srecv + q, w.i, w.sibling())

    def away(self):
        w = self.w
        return w.remote(self.chip.at[1 - w.place], self.got, self.send, self.recv, w.i, w.chip(w.partner))

    def add(self, q):
        w = self.w
        w.arrived(self.sib.at[q], self.srecv + q)
        mine = rows_of(self.part, 256 * q + 128 * w.c, 128)[...]
        self.chip[q] = low(mine.astype(jnp.float32) + self.sib[q].astype(jnp.float32))

    def total(self):
        self.w.arrived(self.got, self.recv)
        return self.chip[self.w.place].astype(jnp.float32) + self.got[...].astype(jnp.float32)

    def finish(self):
        self.swapped(0).wait_send()
        self.swapped(1).wait_send()
        self.away().wait_send()


def cols(ref, start, size):
    return ref.at[:, pl.ds(pl.multiple_of(start, 128), size)]


def rows_of(ref, start, size):
    return ref.at[pl.ds(pl.multiple_of(start, 128), size), :]


class Box:
    pass


def fields(kind):
    return [(name, *value) for name, value in vars(kind).items() if name[0] != "_"]


class FrontKept:
    fn = ((1024, 1024), B16)
    ci = ((HALO + 1024, 512), B16)
    gi = ((1024, 256), F32)
    q = ((1024, 128), F32)
    k = ((1024, 128), F32)
    v = ((1024, 256), F32)
    ge = ((1024, 128), F32)
    mixed = ((1024, 256), F32)
    states = ((4, 128, 256), F32)
    tinv = ((1024, 256), B16)
    u = ((1024, 256), F32)
    wm = ((1024, 128), B16)
    normed = ((1024, 256), B16)
    middle = ((128, 1024), F32)
    sn = ((512, 1024), B16)
    cg = ((512, 1024), B16)
    w_qkv = ((1024, 512), B16)
    w_gate = ((1024, 256), B16)
    w_in = ((1024, 1536), B16)
    w_out = ((256, 1024), B16)
    w_down = ((768, 1024), B16)
class FrontScratch:
    x = ((1024, 1024), B16)
    qkv_p = ((256, 512), B16)
    in_p = ((256, 1536), B16)
    out_p = ((256, 256), B16)
    down_p = ((768, 256), B16)
    down_pad = ((768, 128), B16)
    taps32 = ((8, 4096), F32)
    own_cot = ((128, 1024), B16)
    qk = ((1024, 256), B16)
    cum = ((1024, 1), F32)
    part = ((1024, 1024), B16)
    sib = ((4, 128, 1024), B16)
    chip = ((4, 128, 1024), B16)
    got = ((4, 128, 1024), B16)


def start_weights(w, b):
    i, s = w.i, w.s
    qs, qr = w.take(4), w.take(3)
    lowhalf = s < 4
    b.qr = qr

    @pl.when(lowhalf)
    def _():
        for t in range(4):
            w.push(
                b.qkv.at[:, 128 * t : 128 * t + 128],
                cols(b.qkv_p, 128 * (s // 2), 128),
                qs + t,
                qr + s // 2,
                i,
                4 * lax.rem(s, 2) + t,
            )

    @pl.when(jnp.logical_not(lowhalf))
    def _():
        for t in range(2):
            w.push(b.qkv.at[:, 256 * t : 256 * t + 256], b.qkv_p.at[:, 256:512], qs + t, qr + 2, i, 2 * (s - 4) + t)

    def sent():
        @pl.when(lowhalf)
        def _():
            for t in range(4):
                @pl.when(4 * lax.rem(s, 2) + t != s)
                def _():
                    src = b.qkv.at[:, 128 * t : 128 * t + 128]
                    w.remote(src, b.qkv_p.at[:, 0:128], qs + t, qr, i, w.sibling()).wait_send()

        @pl.when(jnp.logical_not(lowhalf))
        def _():
            for t in range(2):
                @pl.when(2 * (s - 4) + t != s)
                def _():
                    src = b.qkv.at[:, 256 * t : 256 * t + 256]
                    w.remote(src, b.qkv_p.at[:, 256:512], qs + t, qr + 2, i, w.sibling()).wait_send()

    return sent


def start_out_weights(w, b):
    send, recv = w.take(2), w.take(2)
    odd = lax.rem(w.s, 2)
    waits = []
    for n in range(2):
        src = b.out.at[256 * n : 256 * n + 256, :]
        waits.append(w.push(src, cols(b.out_p, 128 * odd, 128), send + n, recv + odd, w.s // 2, 2 * w.i + n))

    def landed():
        for r in range(2):
            w.arrived(b.out_p.at[:, 128 * r : 128 * r + 128], recv + r)

    def sent():
        for wait in waits:
            wait()

    return landed, sent


def start_ffn_weights(w, b):
    i, s = w.i, w.s
    send, recv = w.take(3), w.take(3)
    own, half = lax.rem(s, 2), s // 4
    block = cols(b.in_p, 768 * half, 768)
    across = w.remote(block, block, send, recv, i, lax.rem(s + 4, 8))
    across.start()
    waits = [across.wait_send]
    for n in range(2):
        dst = cols(b.down_p, 128 * own, 128)
        waits.append(w.push(b.down_pad, dst, send + 1 + n, recv + 1 + own, s // 2, i + 4 * n))

    def landed():
        w.arrived(cols(b.in_p, 768 * (1 - half), 768), recv)
        for r in range(2):
            w.arrived(b.down_p.at[:, 128 * r : 128 * r + 128], recv + 1 + r)

    def sent():
        for wait in waits:
            wait()

    return landed, sent


def valid_rows(b, w):
    place = w.s * 128 + lax.broadcasted_iota(jnp.int32, (128, 1), 0)
    return place < b.lengths[0]


def first_norm_tile(b, t):
    rows = tile(t)
    x = b.x[rows, :].astype(jnp.float32)
    inv = lax.rsqrt(jnp.mean(x * x, axis=-1, keepdims=True) + epsilon)
    b.fn[rows, :] = low(x * inv * b.gains[0:1, :])


def own_head(b, w):
    pm = b.params[...]
    lane = lax.broadcasted_iota(jnp.int32, pm.shape, 1)
    return jnp.sum(jnp.where(lane == w.s, pm, 0.0), axis=1, keepdims=True)


def own_taps(b, w, n):
    s = w.s
    return jnp.concatenate(
        [
            b.taps32[n : n + 1, pl.ds(pl.multiple_of(128 * s, 128), 128)],
            b.taps32[n : n + 1, pl.ds(pl.multiple_of(1024 + 128 * s, 128), 128)],
            b.taps32[n : n + 1, pl.ds(pl.multiple_of(2048 + 256 * s, 128), 256)],
        ],
        axis=1,
    )


def conv_sums(b, w, t):
    window = b.ci[pl.ds(pl.multiple_of(t * CH, CH), CH + HALO), :].astype(jnp.float32)
    total = None
    for n in range(KCONV):
        at = HALO - (KCONV - 1) + n
        term = window[at : at + CH] * own_taps(b, w, n)
        total = term if total is None else total + term
    return total


def project_tile(b, w, t):
    rows = tile(t)
    f = b.fn[rows, :]
    b.ci[pl.ds(pl.multiple_of(t * CH + HALO, HALO), CH), :] = low(mm(f, b.w_qkv[...]))
    b.gi[rows, :] = mm(f, b.w_gate[...])
    hi = mm(f, b.head_w[...], NT)
    lane = lax.broadcasted_iota(jnp.int32, hi.shape, 1)
    pm = own_head(b, w)
    shift = jnp.sum(jnp.where(lane == w.s, hi, 0.0), axis=1, keepdims=True) + pm[1:2, :]
    erase = jnp.sum(jnp.where(lane == w.s + 8, hi, 0.0), axis=1, keepdims=True) + pm[2:3, :]
    line = lax.broadcasted_iota(jnp.int32, (CH, 128), 1)
    decay = -jnp.exp(pm[0:1, :]) * soft_plus(shift)
    b.ge[rows, :] = jnp.where(line == 0, decay, jnp.where(line == 1, sig(erase), shift))


def vectors_tile(b, w, t):
    rows = tile(t)
    total = conv_sums(b, w, t)
    act = total * sig(total)
    qa, ka = act[:, 0:DK], act[:, DK : 2 * DK]
    b.q[rows, :] = qa * lax.rsqrt(jnp.sum(qa * qa, axis=-1, keepdims=True) + epsilon) * DK ** (-0.5)
    b.k[rows, :] = ka * lax.rsqrt(jnp.sum(ka * ka, axis=-1, keepdims=True) + epsilon)
    b.v[rows, :] = act[:, 2 * DK :]


def rec_local(b, w, ts):
    row, col = grid_masks()
    attns = []
    for t in ts:
        vectors_tile(b, w, t)
        rows = tile(t)
        k = b.k[rows, :]
        cum, decay = decay_parts(b.ge[rows, 0:1], row, col)
        b.cum[rows, :] = cum
        b.qk[rows, :] = low(mm(b.q[rows, :], k, NT) * decay)
        attns.append(jnp.where(col < row, b.ge[rows, 1:2] * mm(k, k, NT) * decay, 0.0))
    for t, inv in zip(ts, unit_inverse(attns, row, col)):
        rows = tile(t)
        e, t16 = b.ge[rows, 1:2], low(inv)
        b.tinv[rows, :] = t16
        b.wm[rows, :] = low(mm(t16, (e * jnp.exp(b.cum[rows, :])) * b.k[rows, :]))
        b.u[rows, :] = mm(t16, e * b.v[rows, :])


def rec_step(b, t, state):
    rows = tile(t)
    b.states[t] = state
    cum = b.cum[rows, :]
    last = cum[CH - 1 : CH, :]
    s16 = low(state)
    u = b.u[rows, :] - mm(b.wm[rows, :], s16)
    b.u[rows, :] = u
    u16 = low(u)
    mixed = jnp.exp(cum) * mm(b.q[rows, :], s16) + mm(b.qk[rows, :], u16)
    b.mixed[rows, :] = mixed
    nxt = jnp.exp(last) * state + mm(b.k[rows, :] * jnp.exp(last - cum), u16, TN)
    gate = b.gi[rows, :]
    scale = lax.rsqrt(jnp.mean(mixed * mixed, axis=-1, keepdims=True) + epsilon)
    normed = low(mixed * scale * b.head_gain[...] * (gate * sig(gate)))
    b.normed[rows, :] = normed
    b.part[rows, :] = low(mm(normed, b.w_out[...]))
    return nxt


def front_phase(b, w):
    s, i = w.s, w.i
    own_rows = lambda ref: (lambda n: rows_of(ref, 128 * n, 128))
    x_gather = LineGather(w, own_rows(b.x))
    cg_gather = PairGather(w, b.cg)
    sn_gather = PairGather(w, b.sn)
    qkv_gather = GroupGather(w, lambda n: rows_of(b.w_qkv, 256 * n, 256))
    gate_gather = GroupGather(w, lambda n: rows_of(b.w_gate, 256 * n, 256))
    half = s // 4

    def in_block(n, start, size):
        return b.w_in.at[pl.ds(pl.multiple_of(256 * n, 256), 256), pl.ds(pl.multiple_of(start, 128), size)]

    def own_third(k):
        return GroupGather(w, lambda n: in_block(n, 768 * half + 256 * k, 256))

    in_gathers = [own_third(k) for k in range(3)]
    across_gather = GroupGather(w, lambda n: in_block(n, 768 * (1 - half), 768))

    def start_third(k):
        in_gathers[k].start(cols(b.in_p, 768 * half + 256 * k, 256))

    out_gather = GroupGather(w, lambda n: cols(b.w_out, 256 * n, 256))
    down_gather = GroupGather(w, lambda n: cols(b.w_down, 256 * n, 256))
    scatter = LineScatter(w, b.part, b.sib, b.chip, b.got)
    own_x, own_c = w.take(), w.take()

    ff_cols, ff_rows = b.ffn_in.shape[1], b.ffn_out.shape[0]
    block = jnp.concatenate([b.ffn_in[...], jnp.zeros((256, 768 - ff_cols), B16)], axis=1)
    b.in_p[:, pl.ds(pl.multiple_of(768 * half, 128), 768)] = block
    b.down_pad[0:ff_rows, :] = b.ffn_out[...]
    b.down_pad[ff_rows:, :] = jnp.zeros((768 - ff_rows, 128), B16)
    w.meet_all()
    qkv_sent = start_weights(w, b)
    out_landed, out_sent = start_out_weights(w, b)
    x_gather.start(b.tokens)
    gate_gather.start(b.gate)
    start_third(0)
    keep_x = w.local(b.tokens, rows_of(b.x, 128 * s, 128), own_x)
    keep_x.start()
    b.ci[0:HALO, :] = jnp.zeros((HALO, 512), B16)
    b.taps32[0:KCONV, :] = b.taps[...].astype(jnp.float32)
    cot = jnp.where(valid_rows(b, w), b.cot_v[...].astype(jnp.float32), 0.0)
    b.own_cot[...] = low(cot)
    rows_of(b.cg, 128 * lax.rem(s, 4), 128)[...] = low(cot)
    w.arrived(b.qkv_p.at[:, 0:128], b.qr)
    w.arrived(b.qkv_p.at[:, 128:256], b.qr + 1)
    w.arrived(b.qkv_p.at[:, 256:512], b.qr + 2)
    qkv_gather.start(b.qkv_p)
    out_landed()
    out_gather.start(b.out_p)
    ffn_landed, ffn_sent = start_ffn_weights(w, b)
    keep_x.wait()

    def norm_loop(n, carry):
        t = w.order(n)
        x_gather.arrive(t)
        x_gather.other(t)
        first_norm_tile(b, t)
        return carry

    lax.fori_loop(0, 4, norm_loop, 0)
    cg_gather.start()
    qkv_gather.finish()
    gate_gather.finish()
    start_third(1)
    start_third(2)

    def project_loop(t, carry):
        project_tile(b, w, t)
        return carry

    lax.fori_loop(0, 4, project_loop, 0)
    x_gather.finish()
    out_gather.finish()

    def pair_loop(pair, state):
        rec_local(b, w, (2 * pair, 2 * pair + 1))

        @pl.when(pair == 1)
        def _():
            scatter.relay(0)
            scatter.relay(1)

        @pl.when(pair == 0)
        def _():
            ffn_landed()
            across_gather.start(cols(b.in_p, 768 * (1 - half), 768))
            down_gather.start(b.down_p)

        for k in range(2):
            t = 2 * pair + k
            state = rec_step(b, t, state)
            scatter.swap(t)
        scatter.pass_on(2 * pair)
        scatter.pass_on(2 * pair + 1)
        return state

    lax.fori_loop(0, 2, pair_loop, jnp.zeros((DK, DV), F32))

    def own_half(which):
        @pl.when(w.half == which)
        def _():
            middle = b.tokens_v[...].astype(jnp.float32) + scatter.total()
            b.middle[...] = middle
            inv = lax.rsqrt(jnp.mean(middle * middle, axis=-1, keepdims=True) + epsilon)
            rows_of(b.sn, 128 * lax.rem(s, 4), 128)[...] = low(middle * inv * b.gains[1:2, :])
            sn_gather.start()

    own_half(0)
    cg_gather.arrive()
    scatter.relay(2)
    scatter.relay(3)
    own_half(1)
    for third in in_gathers:
        third.finish()
    across_gather.finish()
    down_gather.finish()
    qkv_sent()
    out_sent()
    ffn_sent()
    scatter.finish()

    def finish():
        cg_gather.finish()
        sn_gather.finish()

    return sn_gather, cg_gather, finish


class GroupScatter:
    def __init__(self, w, out, got):
        self.w, self.out, self.got = w, out, got
        self.send, self.recv = w.take(4), w.take(4)

    def start(self, piece_of):
        w = self.w
        self.copies = []
        for d in (2, 1, 3):
            to = lax.rem(w.i + d, 4)
            self.out[d - 1] = low(piece_of(to))
            copy = w.remote(self.out.at[d - 1], self.got.at[d - 1], self.send + d, self.recv + d, to, w.s)
            copy.start()
            self.copies.append(copy)

    def total(self, own):
        w = self.w
        total = own
        for d in range(1, 4):
            w.arrived(self.got.at[d - 1], self.recv + d)
            total = total + self.got[d - 1].astype(jnp.float32)
        for copy in self.copies:
            copy.wait_send()
        return total


def ffn_tile(b, t):
    rows = tile(t)
    sn, cg = b.sn[rows, :], b.cg[rows, :]
    half = b.w_in.shape[1] // 2
    both = mm(sn, b.w_in[...])
    gate, up = both[:, 0:half], both[:, half:]
    open_ = sig(gate)
    act = gate * open_
    hidden = low(act * up)
    b.hid[rows, :] = hidden
    b.part4[rows, :] = low(mm(hidden, b.w_down[...]))
    hgrad = mm(cg, b.w_down[...], NT)
    both_grad = jnp.concatenate(
        [low(hgrad * up * (open_ * (1.0 + gate * (1.0 - open_)))), low(hgrad * act)], axis=1
    )
    b.gug[rows, :] = both_grad
    b.part[rows, :] = low(mm(both_grad, b.w_in[...], NT))


def norm_back(x, gain, grad):
    inv = lax.rsqrt(jnp.mean(x * x, axis=-1, keepdims=True) + epsilon)
    unit = x * inv
    dunit = grad * gain
    return inv * (dunit - unit * jnp.mean(dunit * unit, axis=-1, keepdims=True)), grad * unit


def mixer_out_back(b, t, head_gain_sum):
    rows = tile(t)
    ng = mm(b.agr[rows, :], b.w_out[...], NT)
    gate = b.gi[rows, :]
    open_ = sig(gate)
    act = gate * open_
    gain = b.head_gain[...]
    mixed = b.mixed[rows, :]
    inv = lax.rsqrt(jnp.mean(mixed * mixed, axis=-1, keepdims=True) + epsilon)
    unit = mixed * inv
    dunit = ng * act * gain
    b.do[rows, :] = inv * (dunit - unit * jnp.mean(dunit * unit, axis=-1, keepdims=True))
    nu = ng * unit
    b.gg[rows, :] = low(nu * gain * (open_ * (1.0 + gate * (1.0 - open_))))
    return head_gain_sum + jnp.sum(nu * act, axis=0, keepdims=True)


def rec_back_chain(b, t, ds1, row, col):
    rows = tile(t)
    do = low(b.do[rows, :])
    b.dstates[t] = ds1
    cum = b.cum[rows, :]
    last = cum[CH - 1 : CH, :]
    du = mm(b.qk[rows, :], do, TN) + mm(b.k[rows, :] * jnp.exp(last - cum), ds1)
    du16 = low(du)
    b.dr[rows, :] = mm(b.tinv[rows, :], du16, TN)
    return jnp.exp(last) * ds1 + mm(b.q[rows, :] * jnp.exp(cum), do, TN) - mm(b.wm[rows, :], du16, TN)


def rec_back_tile(b, t, row, col):
    rows = tile(t)
    q, k, v, e = b.q[rows, :], b.k[rows, :], b.v[rows, :], b.ge[rows, 1:2]
    s0, ds1, u, do, dr = b.states[t], b.dstates[t], b.u[rows, :], b.do[rows, :], b.dr[rows, :]
    cum, decay = decay_parts(b.ge[rows, 0:1], row, col)
    last = cum[CH - 1 : CH, :]
    gamma, shrink, remain = jnp.exp(last), jnp.exp(cum), jnp.exp(last - cum)
    gram = jnp.where(col < row, mm(k, k, NT) * decay, 0.0)
    qk = mm(q, k, NT) * decay
    dp = jnp.where(col <= row, mm3(do, u, NT), 0.0)
    da = jnp.where(col < row, -mm3(dr, u, NT), 0.0)
    dqk = low(dp * decay)
    dag = da * gram
    zed = dp * qk + e * dag
    dgram = low(e * da * decay)
    nk = mm3(dr, s0, NT)
    m = mm3(do, s0, NT)
    lm = mm3(u, ds1, NT)
    row_nk = jnp.sum(nk * k, axis=1, keepdims=True)
    dv = e * dr
    de = (
        jnp.sum(dr * v, axis=1, keepdims=True)
        - shrink * row_nk
        + jnp.sum(dag, axis=1, keepdims=True)
    )
    dq = mm(dqk, k) + shrink * m
    dk = mm(dqk, q, TN) + mm(dgram, k) + mm(dgram, k, TN) - (e * shrink) * nk + remain * lm
    dshrink = jnp.sum(m * q, axis=1, keepdims=True) - e * row_nk
    rdr = remain * jnp.sum(lm * k, axis=1, keepdims=True)
    ones = jnp.ones((CH, 1), jnp.float32)
    dcum = jnp.sum(zed, axis=1, keepdims=True) - mmf(zed, ones, TN) + shrink * dshrink - rdr
    dlast = jnp.sum(rdr, axis=0, keepdims=True) + gamma * jnp.sum(
        jnp.sum(s0 * ds1, axis=1, keepdims=True), axis=0, keepdims=True
    )
    lower = (col <= row).astype(jnp.float32)
    dg = mmf(lower, dcum, TN) + dlast
    return dq, dk, dv, dg, de


def unit_back(x, grad):
    inv = lax.rsqrt(jnp.sum(x * x, axis=-1, keepdims=True) + epsilon)
    unit = x * inv
    return inv * (grad - unit * jnp.sum(grad * unit, axis=-1, keepdims=True))


def mixer_back_tile(b, w, t, row, col, sums):
    rows = tile(t)
    dq, dk, dv, dg, de = rec_back_tile(b, t, row, col)
    total = conv_sums(b, w, t)
    open_ = sig(total)
    act = total * open_
    dact = jnp.concatenate(
        [unit_back(act[:, 0:DK], dq * DK ** (-0.5)), unit_back(act[:, DK : 2 * DK], dk), dv], axis=1
    )
    dcs = dact * (open_ * (1.0 + total * (1.0 - open_)))
    b.dcs[0:CH, :] = dcs
    window = b.ci[pl.ds(pl.multiple_of(t * CH, CH), CH + HALO), :].astype(jnp.float32)
    ahead = b.dcs[...]
    taps_sums, p0, p1, p2, gain_sum = sums
    dci = None
    new_taps = []
    for n in range(KCONV):
        at = HALO - (KCONV - 1) + n
        new_taps.append(taps_sums[n] + jnp.sum(dcs * window[at : at + CH], axis=0, keepdims=True))
        back = KCONV - 1 - n
        term = ahead[back : back + CH] * own_taps(b, w, n)
        dci = term if dci is None else dci + term
    b.dcs[CH : CH + HALO, :] = dcs[0:HALO]
    dci16 = low(dci)
    b.cgd[rows, :] = dci16
    lane = lax.broadcasted_iota(jnp.int32, (CH, 16), 1)
    pm = own_head(b, w)
    shift = b.ge[rows, 2:3]
    dshift = dg * (-jnp.exp(pm[0:1, :])) * sig(shift)
    e = b.ge[rows, 1:2]
    dlogit = de * e * (1.0 - e)
    hg = low(jnp.where(lane == w.s, dshift, jnp.where(lane == w.s + 8, dlogit, 0.0)))
    b.hg[rows, :] = hg
    fp = mm(dci16, b.w_qkv[...], NT) + mm(hg, b.head_w[...]) + mm(b.gg[rows, :], b.w_gate[...], NT)
    b.part[rows, :] = low(fp)
    gain_part = jnp.sum(fp * b.fn[rows, :].astype(jnp.float32), axis=0, keepdims=True)
    return (
        tuple(new_taps),
        p0 + jnp.sum(dg * b.ge[rows, 0:1], axis=0, keepdims=True),
        p1 + jnp.sum(dshift, axis=0, keepdims=True),
        p2 + jnp.sum(dlogit, axis=0, keepdims=True),
        gain_sum + gain_part,
    )


class LayerOut:
    output = ((128, 1024), B16)
    input_grad = ((128, 1024), B16)
    gains_grad = ((2, 1024), F32)
    head_gain_grad = ((1, 256), F32)
    params_grad = ((8, 128), F32)
    head_w_grad = ((16, 1024), F32)
    conv_grad = ((4, 4096), F32)
    qkv_back = ((256, 512), B16)
    gate_back = ((256, 256), B16)
    in_back = ((256, 768), B16)
    out_back = ((512, 128), B16)
    down_back = ((768, 128), B16)
class RestScratch:
    hid = ((512, 768), B16)
    gug = ((512, 1536), B16)
    part4 = ((512, 1024), B16)
    sib4 = ((2, 128, 1024), B16)
    chip4 = ((2, 128, 1024), B16)
    got4 = ((128, 1024), B16)
    sib6 = ((2, 128, 1024), B16)
    chip6 = ((2, 128, 1024), B16)
    got6 = ((128, 1024), B16)
    own_ag = ((128, 1024), B16)
    mgrad = ((128, 1024), F32)
    gg = ((1024, 256), B16)
    dstates = ((4, 128, 256), F32)
    dcs = ((CH + HALO, 512), F32)
    cgd = ((1024, 512), B16)
    hg = ((1024, 16), B16)
    in_out = ((3, 256, 1536), B16)
    in_got = ((3, 256, 1536), B16)
    down_out = ((3, 768, 256), B16)
    down_got = ((3, 768, 256), B16)
    out_out = ((3, 256, 256), B16)
    out_got = ((3, 256, 256), B16)
    qkv_out = ((3, 256, 512), B16)
    qkv_got = ((3, 256, 512), B16)
    gate_out = ((3, 256, 256), B16)
    gate_got = ((3, 256, 256), B16)
    in_sum = ((256, 1536), B16)
    in_other = ((256, 768), B16)
    down_sum = ((768, 256), B16)
    down_parts = ((2, 768, 128), B16)
    out_sum = ((256, 256), B16)
    qkv_sum = ((256, 512), B16)
    small = ((8, 1024), F32)
    small_got = ((4, 8, 1024), F32)
    small_sum = ((8, 1024), F32)
    small_all = ((8, 8, 1024), F32)


def grads_home(w, b):
    i, h = w.i, w.s
    send, recv = w.take(9), w.take(10)
    quarter, pair, half = lax.rem(h, 4), lax.rem(h, 2), h // 4

    def ffn():
        block = cols(b.in_sum, 768 * (1 - half), 768)
        across = w.remote(block, b.in_other, send, recv + 4, i, lax.rem(h + 4, 8))
        across.start()
        waits = [across.wait_send]
        for r in range(2):
            src, dst = b.down_sum.at[:, 128 * r : 128 * r + 128], b.down_parts.at[half]
            waits.append(w.push(src, dst, send + 2 + r, recv + 8 + half, quarter, 2 * i + r))
        return waits

    def ffn_done():
        w.arrived(b.in_other, recv + 4)
        mine = cols(b.in_sum, 768 * half, 768)[...]
        b.in_back[...] = low(mine.astype(jnp.float32) + b.in_other[...].astype(jnp.float32))
        for r in range(2):
            w.arrived(b.down_parts.at[r], recv + 8 + r)
        b.down_back[...] = low(b.down_parts[0].astype(jnp.float32) + b.down_parts[1].astype(jnp.float32))

    def mixer():
        waits = [
            w.push(b.qkv_sum.at[:, 0:128], cols(b.qkv_back, 128 * quarter, 128), send + 4, recv + quarter, i, half),
            w.push(b.qkv_sum.at[:, 128:256], cols(b.qkv_back, 128 * quarter, 128), send + 5, recv + quarter, i, 2 + half),
            w.push(b.qkv_sum.at[:, 256:512], cols(b.qkv_back, 256 * pair, 256), send + 6, recv + pair, i, 4 + h // 2),
        ]
        return waits

    def mixer_out():
        waits = []
        for r in range(2):
            waits.append(
                w.push(
                    b.out_sum.at[:, 128 * r : 128 * r + 128],
                    rows_of(b.out_back, 256 * pair, 256),
                    send + 7 + r,
                    recv + 6 + pair,
                    h // 2,
                    2 * i + r,
                )
            )
        return waits

    def landed():
        @pl.when(h < 4)
        def _():
            for t in range(4):
                w.arrived(b.qkv_back.at[:, 128 * t : 128 * t + 128], recv + t)

        @pl.when(h >= 4)
        def _():
            for t in range(2):
                w.arrived(b.qkv_back.at[:, 256 * t : 256 * t + 256], recv + t)

        for r in range(2):
            w.arrived(b.out_back.at[256 * r : 256 * r + 256, :], recv + 6 + r)

    return ffn, ffn_done, mixer, mixer_out, landed


def small_sums(w, b, send, recv, send2, recv2):
    copies = []
    for d in range(1, 4):
        copy = w.remote(b.small, b.small_got.at[d], send + d, recv + d, lax.rem(w.i + d, 4), w.s)
        copy.start()
        copies.append(copy)

    def middle():
        total = b.small[...]
        for d in range(1, 4):
            w.arrived(b.small_got.at[d], recv + d)
            total = total + b.small_got[d]
        b.small_sum[...] = total
        b.small_all[w.s] = total
        for d in range(1, 8):
            copy = w.remote(b.small_sum, b.small_all.at[w.s], send2 + d, recv2 + d, w.i, lax.rem(w.s + d, 8))
            copy.start()
            copies.append(copy)

    def end():
        for d in range(1, 8):
            w.arrived(b.small_all.at[lax.rem(w.s + 8 - d, 8)], recv2 + d)
        for copy in copies:
            copy.wait_send()
        gains = b.small_all[0, 0:2, :]
        head_gain = b.small_all[0, 2:3, 0:256]
        for n in range(1, 8):
            gains = gains + b.small_all[n, 0:2, :]
            head_gain = head_gain + b.small_all[n, 2:3, 0:256]
        b.gains_grad[...] = gains
        b.head_gain_grad[...] = head_gain
        for n in range(8):
            b.params_grad[n : n + 1, :] = b.small_all[n, 3:4, 0:128]
            b.head_w_grad[n : n + 1, :] = b.small_all[n, 4:5, :]
            b.head_w_grad[8 + n : 9 + n, :] = b.small_all[n, 5:6, :]
            for k in range(KCONV):
                line = b.small_all[n, 6 + k // 2 : 7 + k // 2, 512 * (k % 2) : 512 * (k % 2) + 512]
                b.conv_grad[k : k + 1, 128 * n : 128 * n + 128] = line[:, 0:128]
                b.conv_grad[k : k + 1, 1024 + 128 * n : 1152 + 128 * n] = line[:, 128:256]
                b.conv_grad[k : k + 1, 2048 + 256 * n : 2304 + 256 * n] = line[:, 256:512]

    return middle, end


def rest_phase(b, w, sn_gather, cg_gather, front_finish):
    s = w.s
    half_rows = lambda ref: (lambda n: rows_of(ref, 128 * n, 128))
    ag_gather = LineGather(w, half_rows(b.agr))
    scatter4 = PairScatter(w, b.part4, b.sib4, b.chip4, b.got4)
    scatter6 = PairScatter(w, b.part, b.sib6, b.chip6, b.got6)
    scatter8 = LineScatter(w, b.part, b.sib, b.chip, b.got)
    in_sum = GroupScatter(w, b.in_out, b.in_got)
    down_sum = GroupScatter(w, b.down_out, b.down_got)
    out_sum = GroupScatter(w, b.out_out, b.out_got)
    qkv_sum = GroupScatter(w, b.qkv_out, b.qkv_got)
    gate_sum = GroupScatter(w, b.gate_out, b.gate_got)
    home_ffn, home_ffn_done, home_qkv, home_out, home_landed = grads_home(w, b)
    sm = (w.take(4), w.take(4), w.take(8), w.take(8))

    def ffn_loop(n, carry):
        @pl.when(n == 1)
        def _():
            sn_gather.arrive()

        sn_gather.other(n)
        cg_gather.other(n)
        q = w.place + n * (1 - 2 * w.place)
        ffn_tile(b, q)
        scatter6.swapped(q).start()
        scatter4.swapped(q).start()
        return carry

    lax.fori_loop(0, 2, ffn_loop, 0)
    scatter6.add(1 - w.place)
    scatter6.away().start()
    scatter6.add(w.place)

    def in_piece(n):
        return mm(cols(b.sn, 256 * n, 256)[...], b.gug[...], TN)

    def down_piece(n):
        return mm(b.hid[...], cols(b.cg, 256 * n, 256)[...], TN)

    second_grad = scatter6.total()
    back, share = norm_back(b.middle[...], b.gains[1:2, :], second_grad)
    b.small[1:2, :] = jnp.sum(share, axis=0, keepdims=True)
    mgrad = b.own_cot[...].astype(jnp.float32) + back
    b.mgrad[...] = mgrad
    own = low(mgrad)
    b.own_ag[...] = own
    rows_of(b.agr, 128 * s, 128)[...] = own
    ag_gather.start(b.own_ag)
    in_sum.start(in_piece)
    down_sum.start(down_piece)
    scatter4.add(1 - w.place)
    scatter4.away().start()
    scatter4.add(w.place)
    row, col = grid_masks()

    def out_loop(n, head_gain_sum):
        t = w.order(n)
        ag_gather.arrive(t)
        ag_gather.other(t)
        return mixer_out_back(b, t, head_gain_sum)

    head_gain_sum = lax.fori_loop(0, 4, out_loop, jnp.zeros((1, DV), F32))
    scatter6.finish()
    def out_piece(n):
        return mm(b.normed[...], cols(b.agr, 256 * n, 256)[...], TN)

    out_sum.start(out_piece)

    def chain_loop(n, ds1):
        return rec_back_chain(b, 3 - n, ds1, row, col)

    lax.fori_loop(0, 4, chain_loop, jnp.zeros((DK, DV), F32))
    b.dcs[CH : CH + HALO, :] = jnp.zeros((HALO, 512), F32)

    def back_loop(n, sums):
        t = 3 - n
        sums = mixer_back_tile(b, w, t, row, col, sums)
        scatter8.swap(t)

        @pl.when(n > 0)
        def _():
            scatter8.pass_on(t + 1)

        @pl.when(n > 1)
        def _():
            scatter8.relay(t + 2)

        return sums

    one = jnp.zeros((1, 1), F32)
    taps_sums, p0, p1, p2, gain_sum = lax.fori_loop(
        0, 4, back_loop, (tuple(jnp.zeros((1, 512), F32) for n in range(KCONV)), one, one, one, jnp.zeros((1, 1024), F32))
    )
    scatter8.pass_on(0)
    scatter8.relay(1)

    def qkv_piece(n):
        return mm(cols(b.fn, 256 * n, 256)[...], b.cgd[...], TN)

    def gate_piece(n):
        return mm(cols(b.fn, 256 * n, 256)[...], b.gg[...], TN)

    qkv_sum.start(qkv_piece)
    scatter8.relay(0)
    gate_sum.start(gate_piece)
    b.in_sum[...] = low(in_sum.total(in_piece(w.i)))
    b.down_sum[...] = low(down_sum.total(down_piece(w.i)))
    waits = home_ffn()
    b.small[0:1, :] = gain_sum / b.gains[0:1, :]
    b.small[2:3, :] = jnp.concatenate([head_gain_sum, jnp.zeros((1, 1024 - DV), F32)], axis=1)
    lane = lax.broadcasted_iota(jnp.int32, (1, 1024), 1)
    b.small[3:4, :] = jnp.where(lane == 0, p0, jnp.where(lane == 1, p1, jnp.where(lane == 2, p2, 0.0)))
    head_rows = mm(b.hg[...], b.fn[...], TN)
    line = lax.broadcasted_iota(jnp.int32, head_rows.shape, 0)
    b.small[4:5, :] = jnp.sum(jnp.where(line == s, head_rows, 0.0), axis=0, keepdims=True)
    b.small[5:6, :] = jnp.sum(jnp.where(line == s + 8, head_rows, 0.0), axis=0, keepdims=True)
    b.small[6:7, :] = jnp.concatenate([taps_sums[0], taps_sums[1]], axis=1)
    b.small[7:8, :] = jnp.concatenate([taps_sums[2], taps_sums[3]], axis=1)
    small_middle, small_end = small_sums(w, b, *sm)
    b.out_sum[...] = low(out_sum.total(out_piece(w.i)))
    waits = waits + home_out()
    b.qkv_sum[...] = low(qkv_sum.total(qkv_piece(w.i)))
    waits = waits + home_qkv()
    b.gate_back[...] = low(gate_sum.total(gate_piece(w.i)))
    small_middle()
    b.output[...] = low(jnp.where(valid_rows(b, w), b.middle[...] + scatter4.total(), 0.0))
    first_grad = scatter8.total()
    back, unused_share = norm_back(b.tokens_v[...].astype(jnp.float32), b.gains[0:1, :], first_grad)
    b.input_grad[...] = low(b.mgrad[...] + back)
    home_ffn_done()
    small_end()
    home_landed()
    for wait in waits:
        wait()
    scatter4.finish()
    scatter8.finish()
    ag_gather.finish()
    front_finish()


def layer_kernel(dp, seq, *refs):
    b = Box()
    (
        b.tokens,
        b.qkv,
        b.gate,
        b.ffn_in,
        b.out,
        b.ffn_out,
        b.gains,
        b.head_gain,
        b.params,
        b.head_w,
        b.taps,
        b.tokens_v,
        b.cot_v,
        b.lengths,
    ) = refs[:14]
    kinds = fields(LayerOut) + fields(FrontKept) + fields(FrontScratch) + fields(RestScratch)
    for (name, shape, kind), ref in zip(kinds, refs[14:]):
        setattr(b, name, ref)
    b.do, b.dr, b.agr = b.mixed, b.gi, b.x
    w = Wires(dp, seq, refs[-1])
    rest_phase(b, w, *front_phase(b, w))


def layer(dp, seq, *arrays):
    outs = pl.pallas_call(
        functools.partial(layer_kernel, dp, seq),
        out_shape=tuple(jax.ShapeDtypeStruct(shape, kind) for _, shape, kind in fields(LayerOut)),
        in_specs=[ANY] * 3 + [IN_VMEM, ANY] + [IN_VMEM] * 8 + [pl.BlockSpec(memory_space=pltpu.SMEM)],
        out_specs=(IN_VMEM,) * len(fields(LayerOut)),
        scratch_shapes=[
            pltpu.VMEM(shape, kind)
            for _, shape, kind in fields(FrontKept) + fields(FrontScratch) + fields(RestScratch)
        ]
        + [pltpu.SemaphoreType.DMA((500,))],
        compiler_params=pltpu.CompilerParams(collective_id=0, has_side_effects=True, vmem_limit_bytes=62 << 20),
        name="layer",
    )(*arrays)
    made = Box()
    for (name, shape, kind), out in zip(fields(LayerOut), outs):
        setattr(made, name, out)
    return made


def fast_body(
    dp,
    seq,
    tokens,
    lengths,
    cotangent,
    norm_gains,
    head_gain,
    head_params,
    qkv_weight,
    gate_weight,
    head_weight,
    conv_weight,
    out_weight,
    ffn_in,
    ffn_out,
):
    ff_cols, ff_rows = ffn_in.shape[1], ffn_out.shape[0]
    r = layer(
        dp,
        seq,
        tokens[0],
        qkv_weight,
        gate_weight,
        ffn_in,
        out_weight,
        ffn_out,
        norm_gains,
        head_gain[None],
        head_params,
        head_weight.T,
        conv_weight.T,
        tokens[0],
        cotangent[0],
        lengths,
    )
    wide = jnp.float32
    return (
        r.output[None],
        r.input_grad[None],
        r.gains_grad,
        r.head_gain_grad[0],
        r.params_grad[:, 0:3].T,
        r.qkv_back.astype(wide),
        r.gate_back.astype(wide),
        r.head_w_grad.T,
        r.conv_grad.T,
        r.out_back.astype(wide),
        r.in_back[:, 0:ff_cols].astype(wide),
        r.down_back[0:ff_rows].astype(wide),
    )


def choose_body(dp, seq):
    def chosen(*arrays):
        tokens, head_params = arrays[0], arrays[5]
        if (dp, seq) == (4, 8) and tokens.shape[0] == 1 and head_params.shape[1] == seq:
            return fast_body(dp, seq, *arrays)
        return general_body(*arrays)

    return chosen


def solution(mesh):
    dp, seq = mesh.shape["dp"], mesh.shape["seq"]
    placed = (
        P("dp", "seq", None),
        P("dp"),
        P("dp", "seq", None),
        P(),
        P(),
        P(),
        P("dp", "seq"),
        P("dp", "seq"),
        P(),
        P(),
        P("dp", "seq"),
        P("dp", "seq"),
        P("dp", "seq"),
    )
    return jax.shard_map(
        choose_body(dp, seq),
        mesh=mesh,
        in_specs=placed,
        out_specs=(
            P("dp", "seq", None),
            P("dp", "seq", None),
            P(),
            P(),
            P(),
            P("dp", "seq"),
            P("dp", "seq"),
            P(),
            P(),
            P("dp", "seq"),
            P("dp", "seq"),
            P("dp", "seq"),
        ),
        check_vma=False,
    )
```

```python
import functools

import jax
import jax.numpy as jnp
from jax import lax
from jax.experimental import pallas as pl
from jax.experimental.pallas import tpu as pltpu
from jax.sharding import PartitionSpec as P

CH = 256
DK = 128
DV = 256
KCONV = 4
TILE = 64


HIGHEST = lax.Precision.HIGHEST
epsilon = 1e-06


def passed_along(block, axis, distance):
    devices = range(lax.axis_size(axis))
    route = [(i - distance, i) for i in devices if i - distance in devices]
    return lax.ppermute(block, axis, route)


def rms_scale(values, gain_row):
    return (
        values * lax.rsqrt(jnp.mean(values * values, axis=-1, keepdims=True) + epsilon) * gain_row
    )


def unit_rows(values):
    return values * lax.rsqrt(jnp.sum(values * values, axis=-1, keepdims=True) + epsilon)


def block_step(state_now, query_vecs, key_vecs, value_vecs, log_decay, erase_rate):
    length = query_vecs.shape[1]
    cumulative = jnp.cumsum(log_decay, axis=1)
    row_index = jnp.arange(length)[:, None]
    col_index = jnp.arange(length)[None, :]
    strict = col_index < row_index
    within = col_index <= row_index
    spread = cumulative[:, :, None] - cumulative[:, None, :]
    lower_decay = jnp.where(strict, jnp.exp(jnp.where(strict, spread, 0.0)), 0.0)
    causal = jnp.where(within, jnp.exp(jnp.where(within, spread, 0.0)), 0.0)
    key_gram = jnp.einsum("htk,hsk->hts", key_vecs, key_vecs, precision=HIGHEST)
    query_gram = jnp.einsum("htk,hsk->hts", query_vecs, key_vecs, precision=HIGHEST)
    negated = -(erase_rate[:, :, None] * key_gram * lower_decay)
    identity = jnp.eye(length, dtype=jnp.float32)
    inverse = identity + negated
    powered = negated
    for level_index in range(length.bit_length() - 2):
        powered = jnp.einsum("hts,hsr->htr", powered, powered, precision=HIGHEST)
        inverse = jnp.einsum("hts,hsr->htr", inverse, identity + powered, precision=HIGHEST)
    shrink = jnp.exp(cumulative)
    recalled = jnp.einsum("htk,hkw->htw", key_vecs, state_now, precision=HIGHEST)
    target = erase_rate[:, :, None] * value_vecs - (erase_rate * shrink)[:, :, None] * recalled
    updates = jnp.einsum("hts,hsw->htw", inverse, target, precision=HIGHEST)
    read_out = shrink[:, :, None] * jnp.einsum(
        "htk,hkw->htw", query_vecs, state_now, precision=HIGHEST
    )
    read_out = read_out + jnp.einsum(
        "hts,hsw->htw", query_gram * causal, updates, precision=HIGHEST
    )
    remain = jnp.exp(cumulative[:, -1:] - cumulative)
    state_next = jnp.exp(cumulative[:, -1])[:, None, None] * state_now
    state_next = state_next + jnp.einsum(
        "hsk,hsw->hkw", key_vecs * remain[:, :, None], updates, precision=HIGHEST
    )
    return (state_next, read_out)


def run_tiles(query_vecs, key_vecs, value_vecs, log_decay, erase_rate, state_start):
    row_count, head_count, key_width = query_vecs.shape
    tile_count = row_count // TILE

    def arrange(tensor):
        return jnp.swapaxes(tensor.reshape((tile_count, TILE, head_count) + tensor.shape[2:]), 1, 2)

    inputs = (
        arrange(query_vecs),
        arrange(key_vecs),
        arrange(value_vecs),
        arrange(log_decay),
        arrange(erase_rate),
    )

    def advance(state_now, sliced):
        return jax.checkpoint(block_step)(state_now, *sliced)

    state_end, outputs = lax.scan(advance, state_start, inputs)
    outputs = jnp.swapaxes(outputs, 1, 2).reshape(row_count, head_count, outputs.shape[-1])
    return (outputs, state_end)


def mixer_inputs(conv_in, edge_rows, head_in, conv_taps, head_params):
    block_len = conv_in.shape[1]
    head_count = head_params.shape[1]
    extended = jnp.concatenate([edge_rows, conv_in], axis=1)
    conv_sum = extended[:, 0:block_len] * conv_taps[:, 0]
    for offset in range(1, conv_taps.shape[1]):
        conv_sum = conv_sum + extended[:, offset : offset + block_len] * conv_taps[:, offset]
    activated = jax.nn.silu(conv_sum)
    key_span = head_count * DK
    lead = activated.shape[:2]
    query_vecs = unit_rows(activated[..., 0:key_span].reshape(lead + (head_count, DK))) * DK ** (
        -0.5
    )
    key_vecs = unit_rows(activated[..., key_span : 2 * key_span].reshape(lead + (head_count, DK)))
    value_vecs = activated[..., 2 * key_span :].reshape(lead + (head_count, DV))
    log_decay = -jnp.exp(head_params[0]) * jax.nn.softplus(
        head_in[..., 0:head_count] + head_params[1]
    )
    erase_rate = jax.nn.sigmoid(head_in[..., head_count : 2 * head_count] + head_params[2])
    return (query_vecs, key_vecs, value_vecs, log_decay, erase_rate)


def gated_norm(mixed, gate_in, head_gain):
    shaped = gate_in.reshape(mixed.shape)
    normed = (
        mixed * lax.rsqrt(jnp.mean(mixed * mixed, axis=-1, keepdims=True) + epsilon) * head_gain
    )
    return (normed * jax.nn.silu(shaped)).reshape(gate_in.shape)


def local_tiles(query_vecs, key_vecs, value_vecs, log_decay, erase_rate):
    key_width = key_vecs.shape[-1]
    value_width = value_vecs.shape[-1]
    head_count = key_vecs.shape[2]
    padded = jnp.concatenate(
        [jnp.zeros(value_vecs.shape[:3] + (key_width,), jnp.float32), value_vecs], axis=-1
    )
    start_map = jnp.concatenate(
        [jnp.eye(key_width, dtype=jnp.float32), jnp.zeros((key_width, value_width), jnp.float32)],
        axis=1,
    )
    start_map = jnp.broadcast_to(start_map, (head_count, key_width, key_width + value_width))

    def single(query_one, key_one, value_one, decay_one, erase_one):
        return run_tiles(query_one, key_one, value_one, decay_one, erase_one, start_map)

    return jax.vmap(single)(query_vecs, key_vecs, padded, log_decay, erase_rate)


def post_mix(local_out, incoming, gate_in, head_gain):
    mixed = local_out[..., DK:] + jnp.einsum(
        "snhk,shkv->snhv", local_out[..., 0:DK], incoming, precision=HIGHEST
    )
    return gated_norm(mixed, gate_in, head_gain)


def swiglu(gate_up):
    split_at = gate_up.shape[-1] // 2
    return jax.nn.silu(gate_up[:, 0:split_at]) * gate_up[:, split_at:]


def matmul_maps(left, right):
    return jnp.einsum("shij,shjk->shik", left, right, precision=HIGHEST)


def apply_map(maps, state_now):
    return matmul_maps(maps[0], state_now) + maps[1]


def general_body(
    tokens,
    lengths,
    cotangent,
    norm_gains,
    head_gain,
    head_params,
    qkv_weight,
    gate_weight,
    head_weight,
    conv_weight,
    out_weight,
    ffn_in,
    ffn_out,
):
    seq_count, block_len, model_width = tokens.shape
    row_count = seq_count * block_len
    position = lax.axis_index("seq") * block_len + jnp.arange(block_len, dtype=jnp.int32)
    valid_rows = (position[None, :] < lengths[:, None]).reshape(row_count, 1)
    col_parts = (
        lax.all_gather(qkv_weight, "seq", axis=1, tiled=True),
        lax.all_gather(gate_weight, "seq", axis=1, tiled=True),
        lax.all_gather(out_weight, "seq", axis=1, tiled=True),
        lax.all_gather(ffn_in, "seq", axis=1, tiled=True),
        lax.all_gather(ffn_out, "seq", axis=1, tiled=True),
    )
    gathered = (
        lax.all_gather(col_parts[0], "dp", axis=0, tiled=True),
        lax.all_gather(col_parts[1], "dp", axis=0, tiled=True),
        lax.all_gather(col_parts[2], "dp", axis=0, tiled=True),
        lax.all_gather(col_parts[3], "dp", axis=0, tiled=True),
        lax.all_gather(col_parts[4], "dp", axis=0, tiled=True),
    )
    w_qkv, w_gate, w_out, w_in, w_down = gathered
    inputs = tokens.reshape(row_count, model_width).astype(jnp.float32)
    first_norm = rms_scale(inputs, norm_gains[0]).astype(jnp.bfloat16)
    conv_in = jnp.dot(first_norm, w_qkv, preferred_element_type=jnp.float32).astype(jnp.bfloat16)
    head_in = jnp.dot(first_norm, head_weight, preferred_element_type=jnp.float32)
    gate_in = jnp.dot(first_norm, w_gate, preferred_element_type=jnp.float32)
    conv_width = conv_in.shape[-1]
    conv_rows = conv_in.reshape(seq_count, block_len, conv_width)
    edge_cut = block_len - (KCONV - 1)
    edge_rows = passed_along(conv_rows[:, edge_cut:], "seq", 1)
    mix_args = (
        conv_rows.astype(jnp.float32),
        edge_rows.astype(jnp.float32),
        head_in.reshape(seq_count, block_len, -1),
        conv_weight.astype(jnp.float32),
        head_params,
    )
    vectors = mixer_inputs(*mix_args)
    local_out, end_states = local_tiles(*vectors)
    carry_maps = (end_states[..., 0:DK], end_states[..., DK:])

    def relay_state(step_index, state_now):
        return passed_along(apply_map(carry_maps, state_now), "seq", 1)

    incoming = lax.fori_loop(
        0, lax.axis_size("seq") - 1, relay_state, jnp.zeros_like(carry_maps[1])
    )
    post_args = (local_out, incoming, gate_in, head_gain)
    normed = post_mix(*post_args).astype(jnp.bfloat16)
    attended = jnp.dot(normed, w_out, preferred_element_type=jnp.float32)
    middle = inputs + attended
    second_norm = rms_scale(middle, norm_gains[1]).astype(jnp.bfloat16)
    gate_up = jnp.dot(second_norm, w_in, preferred_element_type=jnp.float32)
    hidden = swiglu(gate_up).astype(jnp.bfloat16)
    carried = jnp.dot(hidden, w_down, preferred_element_type=jnp.float32)
    output = jnp.where(valid_rows, middle + carried, 0.0).astype(jnp.bfloat16)
    col_again = (
        lax.all_gather(qkv_weight, "seq", axis=1, tiled=True),
        lax.all_gather(gate_weight, "seq", axis=1, tiled=True),
        lax.all_gather(out_weight, "seq", axis=1, tiled=True),
        lax.all_gather(ffn_in, "seq", axis=1, tiled=True),
        lax.all_gather(ffn_out, "seq", axis=1, tiled=True),
    )
    regathered = (
        lax.all_gather(col_again[0], "dp", axis=0, tiled=True),
        lax.all_gather(col_again[1], "dp", axis=0, tiled=True),
        lax.all_gather(col_again[2], "dp", axis=0, tiled=True),
        lax.all_gather(col_again[3], "dp", axis=0, tiled=True),
        lax.all_gather(col_again[4], "dp", axis=0, tiled=True),
    )
    w_qkv, w_gate, w_out, w_in, w_down = regathered
    upstream = jnp.where(
        valid_rows, cotangent.reshape(row_count, model_width).astype(jnp.float32), 0.0
    )
    carried_grad = upstream.astype(jnp.bfloat16)
    grad_down = jnp.einsum("nf,nd->fd", hidden, carried_grad, preferred_element_type=jnp.float32)
    hidden_grad = jnp.einsum("nd,fd->nf", carried_grad, w_down, preferred_element_type=jnp.float32)
    unused, swiglu_back = jax.vjp(swiglu, gate_up)
    gate_up_grad = swiglu_back(hidden_grad)[0].astype(jnp.bfloat16)
    grad_in = jnp.einsum("nd,nf->df", second_norm, gate_up_grad, preferred_element_type=jnp.float32)
    second_grad = jnp.einsum("nf,df->nd", gate_up_grad, w_in, preferred_element_type=jnp.float32)
    unused, second_back = jax.vjp(rms_scale, middle, norm_gains[1])
    middle_back, gain_two = second_back(second_grad)
    middle_grad = upstream + middle_back
    attended_grad = middle_grad.astype(jnp.bfloat16)
    grad_out = jnp.einsum("nv,nd->vd", normed, attended_grad, preferred_element_type=jnp.float32)
    normed_grad = jnp.einsum("nd,vd->nv", attended_grad, w_out, preferred_element_type=jnp.float32)
    unused, post_back = jax.vjp(post_mix, *post_args)
    local_grad, incoming_local, gate_in_grad, head_gain_grad = post_back(normed_grad)
    flipped = (jnp.swapaxes(carry_maps[0], -1, -2), incoming_local)

    def relay_grad(step_index, grad_now):
        return passed_along(apply_map(flipped, grad_now).astype(jnp.bfloat16), "seq", -1).astype(
            jnp.float32
        )

    outgoing = lax.fori_loop(
        0, lax.axis_size("seq") - 1, relay_grad, jnp.zeros_like(incoming_local)
    )
    map_grad = jnp.einsum("shkv,shjv->shkj", outgoing, incoming, precision=HIGHEST)
    end_grad = jnp.concatenate([map_grad, outgoing], axis=-1)
    unused, tiles_back = jax.vjp(local_tiles, *vectors)
    vector_grads = tiles_back((local_grad, end_grad))
    unused, mix_back = jax.vjp(mixer_inputs, *mix_args)
    conv_own, edge_grad, head_in_grad, conv_taps_grad, params_grad = mix_back(vector_grads)
    edge_back = passed_along(edge_grad.astype(jnp.bfloat16), "seq", -1).astype(edge_grad.dtype)
    conv_total = jnp.concatenate(
        [conv_own[:, 0:edge_cut], conv_own[:, edge_cut:] + edge_back], axis=1
    )
    conv_grad = conv_total.reshape(row_count, conv_width).astype(jnp.bfloat16)
    head_grad = head_in_grad.reshape(row_count, -1).astype(jnp.bfloat16)
    gate_grad = gate_in_grad.astype(jnp.bfloat16)
    grad_qkv = jnp.einsum("nd,nc->dc", first_norm, conv_grad, preferred_element_type=jnp.float32)
    grad_head = jnp.einsum("nd,nc->dc", first_norm, head_grad, preferred_element_type=jnp.float32)
    grad_gate = jnp.einsum("nd,nc->dc", first_norm, gate_grad, preferred_element_type=jnp.float32)
    first_grad = jnp.einsum("nc,dc->nd", conv_grad, w_qkv, preferred_element_type=jnp.float32)
    first_grad = first_grad + jnp.einsum(
        "nc,dc->nd", head_grad, head_weight, preferred_element_type=jnp.float32
    )
    first_grad = first_grad + jnp.einsum(
        "nc,dc->nd", gate_grad, w_gate, preferred_element_type=jnp.float32
    )
    unused, first_back = jax.vjp(rms_scale, inputs, norm_gains[0])
    input_back, gain_one = first_back(first_grad)
    input_grad = (
        (middle_grad + input_back).astype(jnp.bfloat16).reshape(seq_count, block_len, model_width)
    )
    row_groups = (
        lax.psum_scatter(
            grad_qkv.astype(jnp.bfloat16), "dp", scatter_dimension=0, tiled=True
        ).astype(jnp.float32),
        lax.psum_scatter(
            grad_gate.astype(jnp.bfloat16), "dp", scatter_dimension=0, tiled=True
        ).astype(jnp.float32),
        lax.psum_scatter(
            grad_out.astype(jnp.bfloat16), "dp", scatter_dimension=0, tiled=True
        ).astype(jnp.float32),
        lax.psum_scatter(
            grad_in.astype(jnp.bfloat16), "dp", scatter_dimension=0, tiled=True
        ).astype(jnp.float32),
        lax.psum_scatter(
            grad_down.astype(jnp.bfloat16), "dp", scatter_dimension=0, tiled=True
        ).astype(jnp.float32),
    )
    weight_parts = (
        lax.psum_scatter(
            row_groups[0].astype(jnp.bfloat16), "seq", scatter_dimension=1, tiled=True
        ).astype(jnp.float32),
        lax.psum_scatter(
            row_groups[1].astype(jnp.bfloat16), "seq", scatter_dimension=1, tiled=True
        ).astype(jnp.float32),
        lax.psum_scatter(
            row_groups[2].astype(jnp.bfloat16), "seq", scatter_dimension=1, tiled=True
        ).astype(jnp.float32),
        lax.psum_scatter(
            row_groups[3].astype(jnp.bfloat16), "seq", scatter_dimension=1, tiled=True
        ).astype(jnp.float32),
        lax.psum_scatter(
            row_groups[4].astype(jnp.bfloat16), "seq", scatter_dimension=1, tiled=True
        ).astype(jnp.float32),
    )
    small_sums = lax.psum(
        (jnp.stack([gain_one, gain_two]), head_gain_grad, params_grad, grad_head, conv_taps_grad),
        ("dp", "seq"),
    )
    output = output.reshape(seq_count, block_len, model_width)
    return (
        output,
        input_grad,
        small_sums[0],
        small_sums[1],
        small_sums[2],
        weight_parts[0],
        weight_parts[1],
        small_sums[3],
        small_sums[4],
        weight_parts[2],
        weight_parts[3],
        weight_parts[4],
    )


MESH = pl.DeviceIdType.MESH
ANY = pl.BlockSpec(memory_space=pl.ANY)
IN_VMEM = pl.BlockSpec(memory_space=pltpu.VMEM)
B16 = jnp.bfloat16
F32 = jnp.float32
NN = ((1,), (0,))
NT = ((1,), (1,))
TN = ((0,), (0,))
HALO = 16


def low(v):
    return v.astype(jnp.bfloat16)


def mm(a, b, dims=NN):
    return lax.dot_general(low(a), low(b), (dims, ((), ())), preferred_element_type=jnp.float32)


def mmf(a, b, dims=NN):
    return lax.dot_general(
        a, b, (dims, ((), ())), precision=HIGHEST, preferred_element_type=jnp.float32
    )


def mm3(a, b, dims=NN):
    ah, bh = low(a), low(b)
    al, bl = low(a - ah.astype(jnp.float32)), low(b - bh.astype(jnp.float32))
    return mm(ah, bh, dims) + (mm(ah, bl, dims) + mm(al, bh, dims))


def sig(v):
    return 1.0 / (1.0 + jnp.exp(-v))


def soft_plus(v):
    tail = jnp.exp(-jnp.abs(v))
    series = tail * (1.0 - tail * (0.5 - tail * (1.0 / 3.0)))
    return jnp.maximum(v, 0.0) + jnp.where(tail < 1e-3, series, jnp.log(1.0 + tail))


def grid_masks():
    row = lax.broadcasted_iota(jnp.int32, (CH, CH), 0)
    col = lax.broadcasted_iota(jnp.int32, (CH, CH), 1)
    return row, col


def decay_parts(g, row, col):
    lower = (col <= row).astype(jnp.float32)
    cum = mmf(lower, g)
    cum_row = mmf(g, lower, ((0,), (1,)))
    within = col <= row
    decay = jnp.where(within, jnp.exp(jnp.where(within, cum - cum_row, 0.0)), 0.0)
    return cum, decay


def unit_inverse(attns, row, col):
    def same(width):
        return (row // width) == (col // width)

    eye = jnp.where(row == col, 1.0, 0.0)
    power = [jnp.where(same(64), -a, 0.0) for a in attns]
    inv = [eye + p for p in power]
    for level in range(5):
        power = [mm(p, p) for p in power]
        inv = [x + mm(x, p) for x, p in zip(inv, power)]
    for width in (128, 256):
        off = same(width) & jnp.logical_not(same(width // 2))
        part = [mm(jnp.where(off, a, 0.0), x) for a, x in zip(attns, inv)]
        inv = [x - mm(x, p) for x, p in zip(inv, part)]
    rest = [eye - x - mm3(a, x) for a, x in zip(attns, inv)]
    return [x + mm(x, r) for x, r in zip(inv, rest)]


def odd(t):
    return t % 2 if isinstance(t, int) else lax.rem(t, 2)


def tile(t, size=CH):
    return pl.ds(pl.multiple_of(t * size, size), size)


class Wires:
    def __init__(self, dp, seq, sems):
        self.dp, self.seq, self.sems, self.used = dp, seq, sems, 0
        self.i, self.s = lax.axis_index("dp"), lax.axis_index("seq")
        self.z, self.c = self.s // 2, lax.rem(self.s, 2)
        self.half, self.partner = self.z // 2, self.z + 1 - 2 * lax.rem(self.z, 2)
        self.inner = lax.rem((self.z + 1) // 2, 2)
        self.place = lax.rem(self.z, 2)
        self.beside = (self.i + 1 - 2 * lax.rem(self.i, 2), lax.rem(self.i + 2, 4))

    def take(self, count=1):
        start = self.used
        self.used += count
        return start

    def meet_all(self):
        barrier = pltpu.get_barrier_semaphore()
        for di in range(self.dp):
            for dj in range(self.seq):
                if di or dj:
                    pl.semaphore_signal(
                        barrier,
                        inc=1,
                        device_id=(lax.rem(self.i + di, self.dp), lax.rem(self.s + dj, self.seq)),
                        device_id_type=MESH,
                    )
        pl.semaphore_wait(barrier, self.dp * self.seq - 1)

    def remote(self, src, dst, send, recv, di, dj):
        return pltpu.make_async_remote_copy(
            src_ref=src,
            dst_ref=dst,
            send_sem=self.sems.at[send],
            recv_sem=self.sems.at[recv],
            device_id=(di, dj),
            device_id_type=MESH,
        )

    def local(self, src, dst, sem):
        return pltpu.make_async_copy(src, dst, self.sems.at[sem])

    def push(self, src, dst, send, recv, di, dj):
        here = (di == self.i) & (dj == self.s)
        away = self.remote(src, dst, send, recv, di, dj)

        @pl.when(here)
        def _():
            self.local(src, dst, recv).start()

        @pl.when(jnp.logical_not(here))
        def _():
            away.start()

        def sent():
            @pl.when(jnp.logical_not(here))
            def _():
                away.wait_send()

        return sent

    def arrived(self, dst, recv):
        pltpu.make_async_copy(dst, dst, self.sems.at[recv]).wait()

    def chip(self, z):
        return z * 2 + self.c

    def order(self, n):
        near = self.z + n * (1 - 2 * lax.rem(self.z, 2))
        return (1 - n // 2) * near + (n // 2) * (n + self.half * (3 - 2 * n))

    def sibling(self):
        return self.z * 2 + 1 - self.c


class LineGather:
    parts = 2

    def __init__(self, w, block_of):
        self.w, self.block_of = w, block_of
        n = 4 * self.parts
        self.send, self.recv = w.take(n), w.take(n)
        self.fsend, self.frecv = w.take(n), w.take(n)

    def piece(self, block, part):
        size = block.shape[0] // self.parts
        return block.at[part * size : part * size + size, :]

    def start(self, src):
        w = self.w
        dst = self.block_of(w.s)
        for part in range(self.parts):
            a, b = self.piece(src, part), self.piece(dst, part)
            slot = w.z * self.parts + part
            near, far = self.send + part, self.send + self.parts + part
            w.remote(a, b, near, self.recv + slot, w.i, w.chip(w.partner)).start()
            w.remote(a, b, far, self.recv + slot, w.i, w.chip(2 - w.half)).start()
        for part in range(self.parts):
            a, b = self.piece(src, part), self.piece(dst, part)
            slot = w.z * self.parts + part
            w.remote(a, b, self.fsend + slot, self.frecv + slot, w.i, w.sibling()).start()

    def arrive(self, t):
        w = self.w

        @pl.when(t != w.z)
        def _():
            block = self.block_of(w.chip(t))
            for part in range(self.parts):
                ref, slot = self.piece(block, part), t * self.parts + part
                w.arrived(ref, self.recv + slot)

                @pl.when((w.inner == 1) & (t // 2 != w.half))
                def _():
                    on = self.send + (2 + odd(t)) * self.parts + part
                    w.remote(ref, ref, on, self.recv + slot, w.i, w.chip(w.partner)).start()

                w.remote(ref, ref, self.fsend + slot, self.frecv + slot, w.i, w.sibling()).start()

    def other(self, t):
        w = self.w
        block = self.block_of(t * 2 + 1 - w.c)
        for part in range(self.parts):
            w.arrived(self.piece(block, part), self.frecv + t * self.parts + part)

    def finish(self):
        w = self.w
        block = self.block_of(w.s)
        for part in range(self.parts):
            ref = self.piece(block, part)
            for n in range(4):
                copy = w.remote(ref, ref, self.send + n * self.parts + part, self.recv, w.i, w.sibling())
                if n < 2:
                    copy.wait_send()
                else:
                    @pl.when(w.inner == 1)
                    def _():
                        copy.wait_send()

                w.remote(ref, ref, self.fsend + n * self.parts + part, self.recv, w.i, w.sibling()).wait_send()


class GroupGather:
    def __init__(self, w, part_of):
        self.w, self.part_of = w, part_of
        self.send, self.recv = w.take(4), w.take(4)

    def start(self, src):
        w = self.w
        w.local(src, self.part_of(w.i), self.recv).start()
        for d in (3, 1, 2):
            to = lax.rem(w.i + d, 4)
            w.remote(src, self.part_of(w.i), self.send + d, self.recv + d, to, w.s).start()

    def finish(self):
        w = self.w
        for d in range(4):
            w.arrived(self.part_of(lax.rem(w.i + 4 - d, 4)), self.recv + d)
        for d in range(1, 4):
            part = self.part_of(w.i)
            w.remote(part, part, self.send + d, self.recv + d, lax.rem(w.i + d, 4), w.s).wait_send()


class SquareGather:
    def __init__(self, w, part_of):
        self.w, self.part_of = w, part_of
        self.send, self.recv = w.take(4), w.take(5)

    def half(self, n, k):
        part = self.part_of(n)
        size = part.shape[0] // 2
        return part.at[size * k : size * k + size, :]

    def near(self, src):
        w = self.w
        part = self.part_of(w.i)
        return [w.remote(src, part, self.send + k, self.recv + k, w.beside[k], w.s) for k in range(2)]

    def far(self, k):
        w = self.w
        half = self.half(w.beside[k], k)
        return w.remote(half, half, self.send + 2 + k, self.recv + 2 + k, w.beside[1 - k], w.s)

    def start(self, src):
        w = self.w
        w.local(src, self.part_of(w.i), self.recv + 4).start()
        for copy in self.near(src):
            copy.start()

    def relay(self):
        w = self.w
        for k in range(2):
            w.arrived(self.part_of(w.beside[k]), self.recv + k)
            self.far(k).start()

    def finish(self):
        w = self.w
        w.arrived(self.part_of(w.i), self.recv + 4)
        for k in range(2):
            w.arrived(self.half(3 - w.i, k), self.recv + 2 + k)
        for copy in self.near(self.part_of(w.i)) + [self.far(0), self.far(1)]:
            copy.wait_send()


class LineScatter:
    def __init__(self, w, part, sib, chip, got):
        self.w, self.part, self.sib, self.chip, self.got = w, part, sib, chip, got
        self.ssend, self.srecv = w.take(4), w.take(4)
        self.send, self.recv = w.take(4), w.take(4)

    def swap(self, t):
        w = self.w
        src = self.part.at[pl.ds(pl.multiple_of(t * 256 + 128 * (1 - w.c), 128), 128), :]
        w.remote(src, self.sib.at[t], self.ssend + t, self.srecv + t, w.i, w.sibling()).start()

    def out(self, t, slot, chip):
        w = self.w
        w.remote(self.chip.at[t], self.got.at[slot], self.send + t, self.recv + slot, w.i, w.chip(chip)).start()

    def pass_on(self, t):
        w = self.w
        w.arrived(self.sib.at[t], self.srecv + t)
        mine = self.part[pl.ds(pl.multiple_of(t * 256 + 128 * w.c, 128), 128), :]
        self.chip[t] = low(mine.astype(jnp.float32) + self.sib[t].astype(jnp.float32))

        @pl.when(t == w.partner)
        def _():
            self.out(t, 0, t)

        @pl.when((t // 2 != w.half) & (w.inner == 0))
        def _():
            self.out(t, 2 + odd(t), w.partner)

    def relay(self, t):
        w = self.w

        @pl.when((t // 2 != w.half) & (w.inner == 1))
        def _():
            slot = 2 + odd(t)
            w.arrived(self.got.at[slot], self.recv + slot)
            self.chip[t] = low(self.chip[t].astype(jnp.float32) + self.got[slot].astype(jnp.float32))
            self.out(t, 1, t)

    def total(self):
        w = self.w
        total = self.chip[w.z].astype(jnp.float32)
        for slot in range(2):
            w.arrived(self.got.at[slot], self.recv + slot)
            total = total + self.got[slot].astype(jnp.float32)
        return total

    def finish(self):
        w = self.w
        for t in range(4):
            src = self.part.at[pl.ds(t * 256, 128), :]
            w.remote(src, self.sib.at[t], self.ssend + t, self.srecv + t, w.i, w.sibling()).wait_send()

            @pl.when(w.z != t)
            def _():
                w.remote(self.chip.at[t], self.got.at[0], self.send + t, self.recv, w.i, w.sibling()).wait_send()


class PairGather:
    def __init__(self, w, buffer):
        self.w, self.buffer = w, buffer
        self.send, self.recv = w.take(3), w.take(3)

    def block(self, q, c):
        return rows_of(self.buffer, 256 * q + 128 * c, 128)

    def copies(self):
        w = self.w
        mine, theirs = self.block(w.place, w.c), self.block(1 - w.place, w.c)
        send, recv = self.send, self.recv
        return (
            w.remote(mine, mine, send, recv, w.i, w.chip(w.partner)),
            w.remote(mine, mine, send + 1, recv + 1, w.i, w.sibling()),
            w.remote(theirs, theirs, send + 2, recv + 2, w.i, w.sibling()),
        )

    def start(self):
        near, core, unused = self.copies()
        near.start()
        core.start()

    def arrive(self):
        w = self.w
        w.arrived(self.block(1 - w.place, w.c), self.recv)
        self.copies()[2].start()

    def other(self, n):
        w = self.w
        q = w.place + n * (1 - 2 * w.place)
        w.arrived(self.block(q, 1 - w.c), self.recv + 1 + n)

    def finish(self):
        for copy in self.copies():
            copy.wait_send()


class PairScatter:
    def __init__(self, w, part, sib, chip, got):
        self.w, self.part, self.sib, self.chip, self.got = w, part, sib, chip, got
        self.ssend, self.srecv = w.take(2), w.take(2)
        self.send, self.recv = w.take(), w.take()

    def swapped(self, q):
        w = self.w
        src = rows_of(self.part, 256 * q + 128 * (1 - w.c), 128)
        return w.remote(src, self.sib.at[q], self.ssend + q, self.srecv + q, w.i, w.sibling())

    def away(self):
        w = self.w
        return w.remote(self.chip.at[1 - w.place], self.got, self.send, self.recv, w.i, w.chip(w.partner))

    def add(self, q):
        w = self.w
        w.arrived(self.sib.at[q], self.srecv + q)
        mine = rows_of(self.part, 256 * q + 128 * w.c, 128)[...]
        self.chip[q] = low(mine.astype(jnp.float32) + self.sib[q].astype(jnp.float32))

    def total(self):
        self.w.arrived(self.got, self.recv)
        return self.chip[self.w.place].astype(jnp.float32) + self.got[...].astype(jnp.float32)

    def finish(self):
        self.swapped(0).wait_send()
        self.swapped(1).wait_send()
        self.away().wait_send()


def cols(ref, start, size):
    return ref.at[:, pl.ds(pl.multiple_of(start, 128), size)]


def rows_of(ref, start, size):
    return ref.at[pl.ds(pl.multiple_of(start, 128), size), :]


class Box:
    pass


def fields(kind):
    return [(name, *value) for name, value in vars(kind).items() if name[0] != "_"]


class FrontKept:
    fn = ((1024, 1024), B16)
    ci = ((HALO + 1024, 512), B16)
    gi = ((1024, 256), F32)
    q = ((1024, 128), F32)
    k = ((1024, 128), F32)
    v = ((1024, 256), F32)
    ge = ((1024, 128), F32)
    mixed = ((1024, 256), F32)
    states = ((4, 128, 256), F32)
    tinv = ((1024, 256), B16)
    u = ((1024, 256), F32)
    wm = ((1024, 128), B16)
    normed = ((1024, 256), B16)
    middle = ((128, 1024), F32)
    sn = ((512, 1024), B16)
    cg = ((512, 1024), B16)
    w_qkv = ((1024, 512), B16)
    w_gate = ((1024, 256), B16)
    w_in = ((1536, 1024), B16)
    w_out = ((256, 1024), B16)
    w_down = ((768, 1024), B16)
class FrontScratch:
    x = ((1024, 1024), B16)
    qkv_p = ((256, 512), B16)
    in_p = ((1536, 256), B16)
    out_p = ((256, 256), B16)
    down_p = ((768, 256), B16)
    down_pad = ((768, 128), B16)
    taps32 = ((8, 4096), F32)
    own_cot = ((128, 1024), B16)
    qk = ((1024, 256), B16)
    cum = ((1024, 1), F32)
    part = ((1024, 1024), B16)
    sib = ((4, 128, 1024), B16)
    chip = ((4, 128, 1024), B16)
    got = ((4, 128, 1024), B16)


def start_weights(w, b):
    i, s = w.i, w.s
    qs, qr = w.take(4), w.take(3)
    lowhalf = s < 4
    b.qr = qr

    @pl.when(lowhalf)
    def _():
        for t in range(4):
            w.push(
                b.qkv.at[:, 128 * t : 128 * t + 128],
                cols(b.qkv_p, 128 * (s // 2), 128),
                qs + t,
                qr + s // 2,
                i,
                4 * lax.rem(s, 2) + t,
            )

    @pl.when(jnp.logical_not(lowhalf))
    def _():
        for t in range(2):
            w.push(b.qkv.at[:, 256 * t : 256 * t + 256], b.qkv_p.at[:, 256:512], qs + t, qr + 2, i, 2 * (s - 4) + t)

    def sent():
        @pl.when(lowhalf)
        def _():
            for t in range(4):
                @pl.when(4 * lax.rem(s, 2) + t != s)
                def _():
                    src = b.qkv.at[:, 128 * t : 128 * t + 128]
                    w.remote(src, b.qkv_p.at[:, 0:128], qs + t, qr, i, w.sibling()).wait_send()

        @pl.when(jnp.logical_not(lowhalf))
        def _():
            for t in range(2):
                @pl.when(2 * (s - 4) + t != s)
                def _():
                    src = b.qkv.at[:, 256 * t : 256 * t + 256]
                    w.remote(src, b.qkv_p.at[:, 256:512], qs + t, qr + 2, i, w.sibling()).wait_send()

    return sent


def start_out_weights(w, b):
    send, recv = w.take(2), w.take(2)
    odd = lax.rem(w.s, 2)
    waits = []
    for n in range(2):
        src = b.out.at[256 * n : 256 * n + 256, :]
        waits.append(w.push(src, cols(b.out_p, 128 * odd, 128), send + n, recv + odd, w.s // 2, 2 * w.i + n))

    def landed():
        for r in range(2):
            w.arrived(b.out_p.at[:, 128 * r : 128 * r + 128], recv + r)

    def sent():
        for wait in waits:
            wait()

    return landed, sent


def start_ffn_weights(w, b):
    i, s = w.i, w.s
    send, recv = w.take(3), w.take(3)
    own, half = lax.rem(s, 2), s // 4
    block = rows_of(b.in_p, 768 * half, 768)
    across = w.remote(block, block, send, recv, i, lax.rem(s + 4, 8))
    across.start()
    waits = [across.wait_send]
    for n in range(2):
        dst = cols(b.down_p, 128 * own, 128)
        waits.append(w.push(b.down_pad, dst, send + 1 + n, recv + 1 + own, s // 2, i + 4 * n))

    def landed():
        w.arrived(rows_of(b.in_p, 768 * (1 - half), 768), recv)
        for r in range(2):
            w.arrived(b.down_p.at[:, 128 * r : 128 * r + 128], recv + 1 + r)

    def sent():
        for wait in waits:
            wait()

    return landed, sent


def valid_rows(b, w):
    place = w.s * 128 + lax.broadcasted_iota(jnp.int32, (128, 1), 0)
    return place < b.lengths[0]


def first_norm_tile(b, t):
    rows = tile(t)
    x = b.x[rows, :].astype(jnp.float32)
    inv = lax.rsqrt(jnp.mean(x * x, axis=-1, keepdims=True) + epsilon)
    b.fn[rows, :] = low(x * inv * b.gains[0:1, :])


def own_head(b, w):
    pm = b.params[...]
    lane = lax.broadcasted_iota(jnp.int32, pm.shape, 1)
    return jnp.sum(jnp.where(lane == w.s, pm, 0.0), axis=1, keepdims=True)


def own_taps(b, w, n):
    s = w.s
    return jnp.concatenate(
        [
            b.taps32[n : n + 1, pl.ds(pl.multiple_of(128 * s, 128), 128)],
            b.taps32[n : n + 1, pl.ds(pl.multiple_of(1024 + 128 * s, 128), 128)],
            b.taps32[n : n + 1, pl.ds(pl.multiple_of(2048 + 256 * s, 128), 256)],
        ],
        axis=1,
    )


def conv_sums(b, w, t):
    window = b.ci[pl.ds(pl.multiple_of(t * CH, CH), CH + HALO), :].astype(jnp.float32)
    total = None
    for n in range(KCONV):
        at = HALO - (KCONV - 1) + n
        term = window[at : at + CH] * own_taps(b, w, n)
        total = term if total is None else total + term
    return total


def project_tile(b, w, t):
    rows = tile(t)
    f = b.fn[rows, :]
    b.ci[pl.ds(pl.multiple_of(t * CH + HALO, HALO), CH), :] = low(mm(f, b.w_qkv[...]))
    b.gi[rows, :] = mm(f, b.w_gate[...])
    hi = mm(f, b.head_w[...], NT)
    lane = lax.broadcasted_iota(jnp.int32, hi.shape, 1)
    pm = own_head(b, w)
    shift = jnp.sum(jnp.where(lane == w.s, hi, 0.0), axis=1, keepdims=True) + pm[1:2, :]
    erase = jnp.sum(jnp.where(lane == w.s + 8, hi, 0.0), axis=1, keepdims=True) + pm[2:3, :]
    line = lax.broadcasted_iota(jnp.int32, (CH, 128), 1)
    decay = -jnp.exp(pm[0:1, :]) * soft_plus(shift)
    b.ge[rows, :] = jnp.where(line == 0, decay, jnp.where(line == 1, sig(erase), shift))


def vectors_tile(b, w, t):
    rows = tile(t)
    total = conv_sums(b, w, t)
    act = total * sig(total)
    qa, ka = act[:, 0:DK], act[:, DK : 2 * DK]
    b.q[rows, :] = qa * lax.rsqrt(jnp.sum(qa * qa, axis=-1, keepdims=True) + epsilon) * DK ** (-0.5)
    b.k[rows, :] = ka * lax.rsqrt(jnp.sum(ka * ka, axis=-1, keepdims=True) + epsilon)
    b.v[rows, :] = act[:, 2 * DK :]


def rec_local(b, w, ts):
    row, col = grid_masks()
    attns = []
    for t in ts:
        vectors_tile(b, w, t)
        rows = tile(t)
        k = b.k[rows, :]
        cum, decay = decay_parts(b.ge[rows, 0:1], row, col)
        b.cum[rows, :] = cum
        b.qk[rows, :] = low(mm(b.q[rows, :], k, NT) * decay)
        attns.append(jnp.where(col < row, b.ge[rows, 1:2] * mm(k, k, NT) * decay, 0.0))
    for t, inv in zip(ts, unit_inverse(attns, row, col)):
        rows = tile(t)
        e, t16 = b.ge[rows, 1:2], low(inv)
        b.tinv[rows, :] = t16
        b.wm[rows, :] = low(mm(t16, (e * jnp.exp(b.cum[rows, :])) * b.k[rows, :]))
        b.u[rows, :] = mm(t16, e * b.v[rows, :])


def rec_step(b, t, state):
    rows = tile(t)
    b.states[t] = state
    cum = b.cum[rows, :]
    last = cum[CH - 1 : CH, :]
    s16 = low(state)
    u = b.u[rows, :] - mm(b.wm[rows, :], s16)
    b.u[rows, :] = u
    u16 = low(u)
    mixed = jnp.exp(cum) * mm(b.q[rows, :], s16) + mm(b.qk[rows, :], u16)
    b.mixed[rows, :] = mixed
    nxt = jnp.exp(last) * state + mm(b.k[rows, :] * jnp.exp(last - cum), u16, TN)
    gate = b.gi[rows, :]
    scale = lax.rsqrt(jnp.mean(mixed * mixed, axis=-1, keepdims=True) + epsilon)
    normed = low(mixed * scale * b.head_gain[...] * (gate * sig(gate)))
    b.normed[rows, :] = normed
    b.part[rows, :] = low(mm(normed, b.w_out[...]))
    return nxt


def front_phase(b, w):
    s, i = w.s, w.i
    own_rows = lambda ref: (lambda n: rows_of(ref, 128 * n, 128))
    x_gather = LineGather(w, own_rows(b.x))
    cg_gather = PairGather(w, b.cg)
    sn_gather = PairGather(w, b.sn)
    qkv_gather = GroupGather(w, lambda n: rows_of(b.w_qkv, 256 * n, 256))
    gate_gather = GroupGather(w, lambda n: rows_of(b.w_gate, 256 * n, 256))
    half = s // 4

    def in_block(n, start, size):
        return b.w_in.at[pl.ds(pl.multiple_of(start, 128), size), pl.ds(pl.multiple_of(256 * n, 256), 256)]

    def own_third(k):
        return GroupGather(w, lambda n: in_block(n, 768 * half + 256 * k, 256))

    in_gathers = [own_third(k) for k in range(3)]
    across_gather = SquareGather(w, lambda n: in_block(n, 768 * (1 - half), 768))

    def start_third(k):
        in_gathers[k].start(rows_of(b.in_p, 768 * half + 256 * k, 256))

    out_gather = GroupGather(w, lambda n: cols(b.w_out, 256 * n, 256))
    down_gather = SquareGather(w, lambda n: cols(b.w_down, 256 * n, 256))
    scatter = LineScatter(w, b.part, b.sib, b.chip, b.got)
    own_x, own_c = w.take(), w.take()

    ff_cols, ff_rows = b.ffn_in.shape[0], b.ffn_out.shape[0]
    b.in_p[pl.ds(pl.multiple_of(768 * half, 128), ff_cols), :] = b.ffn_in[...]
    b.in_p[pl.ds(pl.multiple_of(768 * half + ff_cols, 64), 768 - ff_cols), :] = jnp.zeros((768 - ff_cols, 256), B16)
    b.down_pad[0:ff_rows, :] = b.ffn_out[...]
    b.down_pad[ff_rows:, :] = jnp.zeros((768 - ff_rows, 128), B16)
    w.meet_all()
    qkv_sent = start_weights(w, b)
    out_landed, out_sent = start_out_weights(w, b)
    x_gather.start(b.tokens)
    gate_gather.start(b.gate)
    start_third(0)
    keep_x = w.local(b.tokens, rows_of(b.x, 128 * s, 128), own_x)
    keep_x.start()
    b.ci[0:HALO, :] = jnp.zeros((HALO, 512), B16)
    b.taps32[0:KCONV, :] = b.taps[...].astype(jnp.float32)
    cot = jnp.where(valid_rows(b, w), b.cot_v[...].astype(jnp.float32), 0.0)
    b.own_cot[...] = low(cot)
    rows_of(b.cg, 128 * lax.rem(s, 4), 128)[...] = low(cot)
    w.arrived(b.qkv_p.at[:, 0:128], b.qr)
    w.arrived(b.qkv_p.at[:, 128:256], b.qr + 1)
    w.arrived(b.qkv_p.at[:, 256:512], b.qr + 2)
    qkv_gather.start(b.qkv_p)
    out_landed()
    out_gather.start(b.out_p)
    ffn_landed, ffn_sent = start_ffn_weights(w, b)
    keep_x.wait()

    def norm_loop(n, carry):
        t = w.order(n)
        x_gather.arrive(t)
        x_gather.other(t)
        first_norm_tile(b, t)
        return carry

    lax.fori_loop(0, 4, norm_loop, 0)
    cg_gather.start()
    qkv_gather.finish()
    gate_gather.finish()
    start_third(1)
    start_third(2)

    def project_loop(t, carry):
        project_tile(b, w, t)
        return carry

    lax.fori_loop(0, 4, project_loop, 0)
    x_gather.finish()
    out_gather.finish()

    def pair_loop(pair, state):
        rec_local(b, w, (2 * pair, 2 * pair + 1))

        @pl.when(pair == 1)
        def _():
            scatter.relay(0)
            scatter.relay(1)

        @pl.when(pair == 0)
        def _():
            ffn_landed()
            across_gather.start(rows_of(b.in_p, 768 * (1 - half), 768))
            down_gather.start(b.down_p)

        for k in range(2):
            t = 2 * pair + k
            state = rec_step(b, t, state)
            scatter.swap(t)
        scatter.pass_on(2 * pair)
        scatter.pass_on(2 * pair + 1)
        return state

    lax.fori_loop(0, 2, pair_loop, jnp.zeros((DK, DV), F32))

    across_gather.relay()
    down_gather.relay()

    def own_half(which):
        @pl.when(w.half == which)
        def _():
            middle = b.tokens_v[...].astype(jnp.float32) + scatter.total()
            b.middle[...] = middle
            inv = lax.rsqrt(jnp.mean(middle * middle, axis=-1, keepdims=True) + epsilon)
            rows_of(b.sn, 128 * lax.rem(s, 4), 128)[...] = low(middle * inv * b.gains[1:2, :])
            sn_gather.start()

    own_half(0)
    cg_gather.arrive()
    scatter.relay(2)
    scatter.relay(3)
    own_half(1)
    for third in in_gathers:
        third.finish()
    across_gather.finish()
    down_gather.finish()
    qkv_sent()
    out_sent()
    ffn_sent()
    scatter.finish()

    def finish():
        cg_gather.finish()
        sn_gather.finish()

    return sn_gather, cg_gather, finish


class SquareScatter:
    def __init__(self, w, out, got):
        self.w, self.out, self.got = w, out, got
        self.send, self.recv = w.take(6), w.take(6)

    def half(self, ref, n, k):
        size = ref.shape[1] // 2
        return ref.at[n, size * k : size * k + size, :]

    def copy(self, n, k):
        w = self.w
        to = k if n == 2 else n
        slot = 2 * n + k
        return w.remote(
            self.half(self.out, n, k), self.half(self.got, n, k), self.send + slot, self.recv + slot, w.beside[to], w.s
        )

    def start_far(self, piece_of):
        self.out[2] = low(piece_of(3 - self.w.i))
        self.copy(2, 0).start()
        self.copy(2, 1).start()

    def start_near(self, piece_of):
        for n in range(2):
            self.out[n] = low(piece_of(self.w.beside[n]))
            self.copy(n, n).start()

    def relay(self):
        w = self.w
        for k in range(2):
            half = self.half(self.out, 1 - k, k)
            w.arrived(self.half(self.got, 2, k), self.recv + 4 + k)
            half[...] = low(half[...].astype(jnp.float32) + self.half(self.got, 2, k)[...].astype(jnp.float32))
            self.copy(1 - k, k).start()

    def total(self, own):
        w = self.w
        total = own
        for n in range(2):
            for k in range(2):
                w.arrived(self.half(self.got, n, k), self.recv + 2 * n + k)
            total = total + self.got[n].astype(jnp.float32)
        return total

    def finish(self):
        for n in range(3):
            for k in range(2):
                self.copy(n, k).wait_send()


def ffn_tile(b, t):
    rows = tile(t)
    sn, cg = b.sn[rows, :], b.cg[rows, :]
    half = b.w_in.shape[0] // 2
    both = mm(sn, b.w_in[...], NT)
    gate, up = both[:, 0:half], both[:, half:]
    open_ = sig(gate)
    act = gate * open_
    hidden = low(act * up)
    b.hid[rows, :] = hidden
    b.part4[rows, :] = low(mm(hidden, b.w_down[...]))
    hgrad = mm(cg, b.w_down[...], NT)
    both_grad = jnp.concatenate(
        [low(hgrad * up * (open_ * (1.0 + gate * (1.0 - open_)))), low(hgrad * act)], axis=1
    )
    b.gug[rows, :] = both_grad
    b.part[rows, :] = low(mm(both_grad, b.w_in[...]))


def norm_back(x, gain, grad):
    inv = lax.rsqrt(jnp.mean(x * x, axis=-1, keepdims=True) + epsilon)
    unit = x * inv
    dunit = grad * gain
    return inv * (dunit - unit * jnp.mean(dunit * unit, axis=-1, keepdims=True)), grad * unit


def mixer_out_back(b, t, head_gain_sum):
    rows = tile(t)
    ng = mm(b.agr[rows, :], b.w_out[...], NT)
    gate = b.gi[rows, :]
    open_ = sig(gate)
    act = gate * open_
    gain = b.head_gain[...]
    mixed = b.mixed[rows, :]
    inv = lax.rsqrt(jnp.mean(mixed * mixed, axis=-1, keepdims=True) + epsilon)
    unit = mixed * inv
    dunit = ng * act * gain
    b.do[rows, :] = inv * (dunit - unit * jnp.mean(dunit * unit, axis=-1, keepdims=True))
    nu = ng * unit
    b.gg[rows, :] = low(nu * gain * (open_ * (1.0 + gate * (1.0 - open_))))
    return head_gain_sum + jnp.sum(nu * act, axis=0, keepdims=True)


def rec_back_chain(b, t, ds1, row, col):
    rows = tile(t)
    do = low(b.do[rows, :])
    b.dstates[t] = ds1
    cum = b.cum[rows, :]
    last = cum[CH - 1 : CH, :]
    du = mm(b.qk[rows, :], do, TN) + mm(b.k[rows, :] * jnp.exp(last - cum), ds1)
    du16 = low(du)
    b.dr[rows, :] = mm(b.tinv[rows, :], du16, TN)
    return jnp.exp(last) * ds1 + mm(b.q[rows, :] * jnp.exp(cum), do, TN) - mm(b.wm[rows, :], du16, TN)


def rec_back_tile(b, t, row, col):
    rows = tile(t)
    q, k, v, e = b.q[rows, :], b.k[rows, :], b.v[rows, :], b.ge[rows, 1:2]
    s0, ds1, u, do, dr = b.states[t], b.dstates[t], b.u[rows, :], b.do[rows, :], b.dr[rows, :]
    cum, decay = decay_parts(b.ge[rows, 0:1], row, col)
    last = cum[CH - 1 : CH, :]
    gamma, shrink, remain = jnp.exp(last), jnp.exp(cum), jnp.exp(last - cum)
    gram = jnp.where(col < row, mm(k, k, NT) * decay, 0.0)
    qk = mm(q, k, NT) * decay
    dp = jnp.where(col <= row, mm3(do, u, NT), 0.0)
    da = jnp.where(col < row, -mm3(dr, u, NT), 0.0)
    dqk = low(dp * decay)
    dag = da * gram
    zed = dp * qk + e * dag
    dgram = low(e * da * decay)
    nk = mm3(dr, s0, NT)
    m = mm3(do, s0, NT)
    lm = mm3(u, ds1, NT)
    row_nk = jnp.sum(nk * k, axis=1, keepdims=True)
    dv = e * dr
    de = (
        jnp.sum(dr * v, axis=1, keepdims=True)
        - shrink * row_nk
        + jnp.sum(dag, axis=1, keepdims=True)
    )
    dq = mm(dqk, k) + shrink * m
    dk = mm(dqk, q, TN) + mm(dgram, k) + mm(dgram, k, TN) - (e * shrink) * nk + remain * lm
    dshrink = jnp.sum(m * q, axis=1, keepdims=True) - e * row_nk
    rdr = remain * jnp.sum(lm * k, axis=1, keepdims=True)
    ones = jnp.ones((CH, 1), jnp.float32)
    dcum = jnp.sum(zed, axis=1, keepdims=True) - mmf(zed, ones, TN) + shrink * dshrink - rdr
    dlast = jnp.sum(rdr, axis=0, keepdims=True) + gamma * jnp.sum(
        jnp.sum(s0 * ds1, axis=1, keepdims=True), axis=0, keepdims=True
    )
    lower = (col <= row).astype(jnp.float32)
    dg = mmf(lower, dcum, TN) + dlast
    return dq, dk, dv, dg, de


def unit_back(x, grad):
    inv = lax.rsqrt(jnp.sum(x * x, axis=-1, keepdims=True) + epsilon)
    unit = x * inv
    return inv * (grad - unit * jnp.sum(grad * unit, axis=-1, keepdims=True))


def mixer_back_tile(b, w, t, row, col, sums):
    rows = tile(t)
    dq, dk, dv, dg, de = rec_back_tile(b, t, row, col)
    total = conv_sums(b, w, t)
    open_ = sig(total)
    act = total * open_
    dact = jnp.concatenate(
        [unit_back(act[:, 0:DK], dq * DK ** (-0.5)), unit_back(act[:, DK : 2 * DK], dk), dv], axis=1
    )
    dcs = dact * (open_ * (1.0 + total * (1.0 - open_)))
    b.dcs[0:CH, :] = dcs
    window = b.ci[pl.ds(pl.multiple_of(t * CH, CH), CH + HALO), :].astype(jnp.float32)
    ahead = b.dcs[...]
    taps_sums, p0, p1, p2, gain_sum = sums
    dci = None
    new_taps = []
    for n in range(KCONV):
        at = HALO - (KCONV - 1) + n
        new_taps.append(taps_sums[n] + jnp.sum(dcs * window[at : at + CH], axis=0, keepdims=True))
        back = KCONV - 1 - n
        term = ahead[back : back + CH] * own_taps(b, w, n)
        dci = term if dci is None else dci + term
    b.dcs[CH : CH + HALO, :] = dcs[0:HALO]
    dci16 = low(dci)
    b.cgd[rows, :] = dci16
    lane = lax.broadcasted_iota(jnp.int32, (CH, 16), 1)
    pm = own_head(b, w)
    shift = b.ge[rows, 2:3]
    dshift = dg * (-jnp.exp(pm[0:1, :])) * sig(shift)
    e = b.ge[rows, 1:2]
    dlogit = de * e * (1.0 - e)
    hg = low(jnp.where(lane == w.s, dshift, jnp.where(lane == w.s + 8, dlogit, 0.0)))
    b.hg[rows, :] = hg
    fp = mm(dci16, b.w_qkv[...], NT) + mm(hg, b.head_w[...]) + mm(b.gg[rows, :], b.w_gate[...], NT)
    b.part[rows, :] = low(fp)
    gain_part = jnp.sum(fp * b.fn[rows, :].astype(jnp.float32), axis=0, keepdims=True)
    return (
        tuple(new_taps),
        p0 + jnp.sum(dg * b.ge[rows, 0:1], axis=0, keepdims=True),
        p1 + jnp.sum(dshift, axis=0, keepdims=True),
        p2 + jnp.sum(dlogit, axis=0, keepdims=True),
        gain_sum + gain_part,
    )


class LayerOut:
    output = ((128, 1024), B16)
    input_grad = ((128, 1024), B16)
    gains_grad = ((2, 1024), F32)
    head_gain_grad = ((1, 256), F32)
    params_grad = ((8, 128), F32)
    head_w_grad = ((16, 1024), F32)
    conv_grad = ((4, 4096), F32)
    qkv_back = ((256, 512), B16)
    gate_back = ((256, 256), B16)
    in_back = ((768, 256), B16)
    out_back = ((512, 128), B16)
    down_back = ((768, 128), B16)
class RestScratch:
    hid = ((512, 768), B16)
    gug = ((512, 1536), B16)
    part4 = ((512, 1024), B16)
    sib4 = ((2, 128, 1024), B16)
    chip4 = ((2, 128, 1024), B16)
    got4 = ((128, 1024), B16)
    sib6 = ((2, 128, 1024), B16)
    chip6 = ((2, 128, 1024), B16)
    got6 = ((128, 1024), B16)
    own_ag = ((128, 1024), B16)
    mgrad = ((128, 1024), F32)
    gg = ((1024, 256), B16)
    dstates = ((4, 128, 256), F32)
    dcs = ((CH + HALO, 512), F32)
    cgd = ((1024, 512), B16)
    hg = ((1024, 16), B16)
    in_out = ((3, 1536, 256), B16)
    in_got = ((3, 1536, 256), B16)
    down_out = ((3, 768, 256), B16)
    down_got = ((3, 768, 256), B16)
    out_out = ((3, 256, 256), B16)
    out_got = ((3, 256, 256), B16)
    qkv_out = ((3, 256, 512), B16)
    qkv_got = ((3, 256, 512), B16)
    gate_out = ((3, 256, 256), B16)
    gate_got = ((3, 256, 256), B16)
    in_sum = ((1536, 256), B16)
    in_other = ((768, 256), B16)
    down_sum = ((768, 256), B16)
    down_parts = ((2, 768, 128), B16)
    out_sum = ((256, 256), B16)
    qkv_sum = ((256, 512), B16)
    small = ((8, 1024), F32)
    small_got = ((4, 8, 1024), F32)
    small_sum = ((8, 1024), F32)
    small_all = ((8, 8, 1024), F32)


def grads_home(w, b):
    i, h = w.i, w.s
    send, recv = w.take(9), w.take(10)
    quarter, pair, half = lax.rem(h, 4), lax.rem(h, 2), h // 4

    def across():
        block = rows_of(b.in_sum, 768 * (1 - half), 768)
        return w.remote(block, b.in_other, send, recv + 4, i, lax.rem(h + 4, 8))

    down_to = [(b.down_sum.at[:, 128 * r : 128 * r + 128], quarter, 2 * i + r) for r in range(2)]

    def ffn():
        across().start()
        for r, (src, di, dj) in enumerate(down_to):
            w.push(src, b.down_parts.at[half], send + 2 + r, recv + 8 + half, di, dj)

    def ffn_done():
        across().wait_send()
        for r, (src, di, dj) in enumerate(down_to):
            @pl.when((di != i) | (dj != h))
            def _():
                w.remote(src, src, send + 2 + r, recv, i, w.sibling()).wait_send()

        w.arrived(b.in_other, recv + 4)
        mine = rows_of(b.in_sum, 768 * half, 768)[...]
        b.in_back[...] = low(mine.astype(jnp.float32) + b.in_other[...].astype(jnp.float32))
        for r in range(2):
            w.arrived(b.down_parts.at[r], recv + 8 + r)
        b.down_back[...] = low(b.down_parts[0].astype(jnp.float32) + b.down_parts[1].astype(jnp.float32))

    def mixer():
        to = (
            (b.qkv_sum.at[:, 0:128], cols(b.qkv_back, 128 * quarter, 128), recv + quarter, half),
            (b.qkv_sum.at[:, 128:256], cols(b.qkv_back, 128 * quarter, 128), recv + quarter, 2 + half),
            (b.qkv_sum.at[:, 256:512], cols(b.qkv_back, 256 * pair, 256), recv + pair, 4 + h // 2),
        )
        return [w.push(src, dst, send + 4 + n, sem, i, dj) for n, (src, dst, sem, dj) in enumerate(to)]

    def mixer_out():
        waits = []
        for r in range(2):
            src = b.out_sum.at[:, 128 * r : 128 * r + 128]
            dst = rows_of(b.out_back, 256 * pair, 256)
            waits.append(w.push(src, dst, send + 7 + r, recv + 6 + pair, h // 2, 2 * i + r))
        return waits

    def landed():
        @pl.when(h < 4)
        def _():
            for t in range(4):
                w.arrived(b.qkv_back.at[:, 128 * t : 128 * t + 128], recv + t)

        @pl.when(h >= 4)
        def _():
            for t in range(2):
                w.arrived(b.qkv_back.at[:, 256 * t : 256 * t + 256], recv + t)

        for r in range(2):
            w.arrived(b.out_back.at[256 * r : 256 * r + 256, :], recv + 6 + r)

    return ffn, ffn_done, mixer, mixer_out, landed


def small_sums(w, b, send, recv, send2, recv2):
    copies = []
    for d in range(1, 4):
        copy = w.remote(b.small, b.small_got.at[d], send + d, recv + d, lax.rem(w.i + d, 4), w.s)
        copy.start()
        copies.append(copy)

    def middle():
        total = b.small[...]
        for d in range(1, 4):
            w.arrived(b.small_got.at[d], recv + d)
            total = total + b.small_got[d]
        b.small_sum[...] = total
        b.small_all[w.s] = total
        for d in range(1, 8):
            copy = w.remote(b.small_sum, b.small_all.at[w.s], send2 + d, recv2 + d, w.i, lax.rem(w.s + d, 8))
            copy.start()
            copies.append(copy)

    def end():
        for d in range(1, 8):
            w.arrived(b.small_all.at[lax.rem(w.s + 8 - d, 8)], recv2 + d)
        for copy in copies:
            copy.wait_send()
        gains = b.small_all[0, 0:2, :]
        head_gain = b.small_all[0, 2:3, 0:256]
        for n in range(1, 8):
            gains = gains + b.small_all[n, 0:2, :]
            head_gain = head_gain + b.small_all[n, 2:3, 0:256]
        b.gains_grad[...] = gains
        b.head_gain_grad[...] = head_gain
        for n in range(8):
            b.params_grad[n : n + 1, :] = b.small_all[n, 3:4, 0:128]
            b.head_w_grad[n : n + 1, :] = b.small_all[n, 4:5, :]
            b.head_w_grad[8 + n : 9 + n, :] = b.small_all[n, 5:6, :]
            for k in range(KCONV):
                line = b.small_all[n, 6 + k // 2 : 7 + k // 2, 512 * (k % 2) : 512 * (k % 2) + 512]
                b.conv_grad[k : k + 1, 128 * n : 128 * n + 128] = line[:, 0:128]
                b.conv_grad[k : k + 1, 1024 + 128 * n : 1152 + 128 * n] = line[:, 128:256]
                b.conv_grad[k : k + 1, 2048 + 256 * n : 2304 + 256 * n] = line[:, 256:512]

    return middle, end


def rest_phase(b, w, sn_gather, cg_gather, front_finish):
    s = w.s
    half_rows = lambda ref: (lambda n: rows_of(ref, 128 * n, 128))
    ag_gather = LineGather(w, half_rows(b.agr))
    scatter4 = PairScatter(w, b.part4, b.sib4, b.chip4, b.got4)
    scatter6 = PairScatter(w, b.part, b.sib6, b.chip6, b.got6)
    scatter8 = LineScatter(w, b.part, b.sib, b.chip, b.got)
    in_sum = SquareScatter(w, b.in_out, b.in_got)
    down_sum = SquareScatter(w, b.down_out, b.down_got)
    out_sum = SquareScatter(w, b.out_out, b.out_got)
    qkv_sum = SquareScatter(w, b.qkv_out, b.qkv_got)
    gate_sum = SquareScatter(w, b.gate_out, b.gate_got)
    home_ffn, home_ffn_done, home_qkv, home_out, home_landed = grads_home(w, b)
    sm = (w.take(4), w.take(4), w.take(8), w.take(8))

    def ffn_loop(n, carry):
        @pl.when(n == 1)
        def _():
            sn_gather.arrive()

        sn_gather.other(n)
        cg_gather.other(n)
        q = w.place + n * (1 - 2 * w.place)
        ffn_tile(b, q)
        scatter6.swapped(q).start()
        scatter4.swapped(q).start()
        return carry

    lax.fori_loop(0, 2, ffn_loop, 0)
    scatter6.add(1 - w.place)
    scatter6.away().start()
    scatter6.add(w.place)

    def in_piece(n):
        return mm(b.gug[...], cols(b.sn, 256 * n, 256)[...], TN)

    def down_piece(n):
        return mm(b.hid[...], cols(b.cg, 256 * n, 256)[...], TN)

    in_sum.start_far(in_piece)
    down_sum.start_far(down_piece)
    second_grad = scatter6.total()
    back, share = norm_back(b.middle[...], b.gains[1:2, :], second_grad)
    b.small[1:2, :] = jnp.sum(share, axis=0, keepdims=True)
    mgrad = b.own_cot[...].astype(jnp.float32) + back
    b.mgrad[...] = mgrad
    own = low(mgrad)
    b.own_ag[...] = own
    rows_of(b.agr, 128 * s, 128)[...] = own
    ag_gather.start(b.own_ag)
    in_sum.start_near(in_piece)
    down_sum.start_near(down_piece)
    scatter4.add(1 - w.place)
    scatter4.away().start()
    scatter4.add(w.place)
    row, col = grid_masks()

    def out_loop(n, head_gain_sum):
        t = w.order(n)
        ag_gather.arrive(t)
        ag_gather.other(t)
        out = mixer_out_back(b, t, head_gain_sum)

        @pl.when(n == 2)
        def _():
            in_sum.relay()
            down_sum.relay()

        return out

    head_gain_sum = lax.fori_loop(0, 4, out_loop, jnp.zeros((1, DV), F32))
    scatter6.finish()
    def out_piece(n):
        return mm(b.normed[...], cols(b.agr, 256 * n, 256)[...], TN)


    out_sum.start_far(out_piece)
    out_sum.start_near(out_piece)

    def chain_loop(n, ds1):
        return rec_back_chain(b, 3 - n, ds1, row, col)

    lax.fori_loop(0, 4, chain_loop, jnp.zeros((DK, DV), F32))
    b.dcs[CH : CH + HALO, :] = jnp.zeros((HALO, 512), F32)

    def back_loop(n, sums):
        t = 3 - n
        sums = mixer_back_tile(b, w, t, row, col, sums)
        scatter8.swap(t)

        @pl.when(n == 0)
        def _():
            out_sum.relay()
            b.in_sum[...] = low(in_sum.total(in_piece(w.i)))
            b.down_sum[...] = low(down_sum.total(down_piece(w.i)))
            home_ffn()

        @pl.when(n > 0)
        def _():
            scatter8.pass_on(t + 1)

        @pl.when(n > 1)
        def _():
            scatter8.relay(t + 2)

        return sums

    one = jnp.zeros((1, 1), F32)
    taps_sums, p0, p1, p2, gain_sum = lax.fori_loop(
        0, 4, back_loop, (tuple(jnp.zeros((1, 512), F32) for n in range(KCONV)), one, one, one, jnp.zeros((1, 1024), F32))
    )
    scatter8.pass_on(0)
    scatter8.relay(1)

    def qkv_piece(n):
        return mm(cols(b.fn, 256 * n, 256)[...], b.cgd[...], TN)

    def gate_piece(n):
        return mm(cols(b.fn, 256 * n, 256)[...], b.gg[...], TN)

    qkv_sum.start_far(qkv_piece)
    gate_sum.start_far(gate_piece)
    qkv_sum.start_near(qkv_piece)
    gate_sum.start_near(gate_piece)
    scatter8.relay(0)
    b.small[0:1, :] = gain_sum / b.gains[0:1, :]
    b.small[2:3, :] = jnp.concatenate([head_gain_sum, jnp.zeros((1, 1024 - DV), F32)], axis=1)
    lane = lax.broadcasted_iota(jnp.int32, (1, 1024), 1)
    b.small[3:4, :] = jnp.where(lane == 0, p0, jnp.where(lane == 1, p1, jnp.where(lane == 2, p2, 0.0)))
    head_rows = mm(b.hg[...], b.fn[...], TN)
    line = lax.broadcasted_iota(jnp.int32, head_rows.shape, 0)
    b.small[4:5, :] = jnp.sum(jnp.where(line == s, head_rows, 0.0), axis=0, keepdims=True)
    b.small[5:6, :] = jnp.sum(jnp.where(line == s + 8, head_rows, 0.0), axis=0, keepdims=True)
    b.small[6:7, :] = jnp.concatenate([taps_sums[0], taps_sums[1]], axis=1)
    b.small[7:8, :] = jnp.concatenate([taps_sums[2], taps_sums[3]], axis=1)
    small_middle, small_end = small_sums(w, b, *sm)
    b.out_sum[...] = low(out_sum.total(out_piece(w.i)))
    waits = home_out()
    qkv_sum.relay()
    gate_sum.relay()
    b.qkv_sum[...] = low(qkv_sum.total(qkv_piece(w.i)))
    waits = waits + home_qkv()
    b.gate_back[...] = low(gate_sum.total(gate_piece(w.i)))
    small_middle()
    b.output[...] = low(jnp.where(valid_rows(b, w), b.middle[...] + scatter4.total(), 0.0))
    first_grad = scatter8.total()
    back, unused_share = norm_back(b.tokens_v[...].astype(jnp.float32), b.gains[0:1, :], first_grad)
    b.input_grad[...] = low(b.mgrad[...] + back)
    home_ffn_done()
    small_end()
    home_landed()
    for wait in waits:
        wait()
    for part in (in_sum, down_sum, out_sum, qkv_sum, gate_sum):
        part.finish()
    scatter4.finish()
    scatter8.finish()
    ag_gather.finish()
    front_finish()


def layer_kernel(dp, seq, *refs):
    b = Box()
    (
        b.tokens,
        b.qkv,
        b.gate,
        b.ffn_in,
        b.out,
        b.ffn_out,
        b.gains,
        b.head_gain,
        b.params,
        b.head_w,
        b.taps,
        b.tokens_v,
        b.cot_v,
        b.lengths,
    ) = refs[:14]
    kinds = fields(LayerOut) + fields(FrontKept) + fields(FrontScratch) + fields(RestScratch)
    for (name, shape, kind), ref in zip(kinds, refs[14:]):
        setattr(b, name, ref)
    b.do, b.dr, b.agr = b.mixed, b.gi, b.x
    w = Wires(dp, seq, refs[-1])
    rest_phase(b, w, *front_phase(b, w))


def layer(dp, seq, *arrays):
    outs = pl.pallas_call(
        functools.partial(layer_kernel, dp, seq),
        out_shape=tuple(jax.ShapeDtypeStruct(shape, kind) for _, shape, kind in fields(LayerOut)),
        in_specs=[ANY] * 3 + [IN_VMEM, ANY] + [IN_VMEM] * 8 + [pl.BlockSpec(memory_space=pltpu.SMEM)],
        out_specs=(IN_VMEM,) * len(fields(LayerOut)),
        scratch_shapes=[
            pltpu.VMEM(shape, kind)
            for _, shape, kind in fields(FrontKept) + fields(FrontScratch) + fields(RestScratch)
        ]
        + [pltpu.SemaphoreType.DMA((500,))],
        compiler_params=pltpu.CompilerParams(collective_id=0, has_side_effects=True, vmem_limit_bytes=62 << 20),
        name="layer",
    )(*arrays)
    made = Box()
    for (name, shape, kind), out in zip(fields(LayerOut), outs):
        setattr(made, name, out)
    return made


class FinalOut:
    output = ((128, 1024), B16)
    input_grad = ((128, 1024), B16)
    gains_grad = ((2, 1024), F32)
    head_gain_grad = ((1, 256), F32)
    params_grad = ((3, 8), F32)
    head_w_grad = ((16, 1024), F32)
    conv_grad = ((4, 4096), F32)
    qkv_back = ((256, 512), F32)
    gate_back = ((256, 256), F32)
    in_back = ((704, 256), F32)
    out_back = ((512, 128), F32)
    down_back = ((704, 128), F32)


def final_kernel(*refs):
    count = len(fields(FinalOut))
    srcs, outs, held, sems = refs[:count], refs[count : 2 * count], refs[2 * count : -1], refs[-1]
    copies = [pltpu.make_async_copy(src, buf, sems.at[n]) for n, (src, buf) in enumerate(zip(srcs, held))]
    for copy in copies:
        copy.start()
    for n, ((name, shape, kind), copy, buf, out) in enumerate(zip(fields(FinalOut), copies, held, outs)):
        copy.wait()
        if n == 4:
            out[...] = jnp.transpose(buf[...])[0:3, :]
        else:
            out[...] = buf[0 : shape[0], :].astype(kind)


def final(made):
    names = fields(FinalOut)
    arrays = [getattr(made, name) for name, _, _ in names]
    outs = pl.pallas_call(
        final_kernel,
        out_shape=tuple(jax.ShapeDtypeStruct(shape, kind) for _, shape, kind in names),
        in_specs=[ANY] * len(names),
        out_specs=(IN_VMEM,) * len(names),
        scratch_shapes=[pltpu.VMEM(array.shape, array.dtype) for array in arrays]
        + [pltpu.SemaphoreType.DMA((len(names),))],
        compiler_params=pltpu.CompilerParams(vmem_limit_bytes=62 << 20),
        name="final",
    )(*arrays)
    done = Box()
    for (name, shape, kind), out in zip(names, outs):
        setattr(done, name, out)
    return done


def fast_body(
    dp,
    seq,
    tokens,
    lengths,
    cotangent,
    norm_gains,
    head_gain,
    head_params,
    qkv_weight,
    gate_weight,
    head_weight,
    conv_weight,
    out_weight,
    ffn_in,
    ffn_out,
):
    made = layer(
        dp,
        seq,
        tokens[0],
        qkv_weight,
        gate_weight,
        ffn_in.T,
        out_weight,
        ffn_out,
        norm_gains,
        head_gain[None],
        head_params,
        head_weight.T,
        conv_weight.T,
        tokens[0],
        cotangent[0],
        lengths,
    )
    r = final(made)
    return (
        r.output[None],
        r.input_grad[None],
        r.gains_grad,
        r.head_gain_grad[0],
        r.params_grad,
        r.qkv_back,
        r.gate_back,
        r.head_w_grad.T,
        r.conv_grad.T,
        r.out_back,
        r.in_back.T,
        r.down_back,
    )


def choose_body(dp, seq):
    def chosen(*arrays):
        tokens, head_params = arrays[0], arrays[5]
        if (dp, seq) == (4, 8) and tokens.shape[0] == 1 and head_params.shape[1] == seq:
            return fast_body(dp, seq, *arrays)
        return general_body(*arrays)

    return chosen


def solution(mesh):
    dp, seq = mesh.shape["dp"], mesh.shape["seq"]
    placed = (
        P("dp", "seq", None),
        P("dp"),
        P("dp", "seq", None),
        P(),
        P(),
        P(),
        P("dp", "seq"),
        P("dp", "seq"),
        P(),
        P(),
        P("dp", "seq"),
        P("dp", "seq"),
        P("dp", "seq"),
    )
    return jax.shard_map(
        choose_body(dp, seq),
        mesh=mesh,
        in_specs=placed,
        out_specs=(
            P("dp", "seq", None),
            P("dp", "seq", None),
            P(),
            P(),
            P(),
            P("dp", "seq"),
            P("dp", "seq"),
            P(),
            P(),
            P("dp", "seq"),
            P("dp", "seq"),
            P("dp", "seq"),
        ),
        check_vma=False,
    )
```

```python
import functools

import jax
import jax.numpy as jnp
from jax import lax
from jax.experimental import pallas as pl
from jax.experimental.pallas import tpu as pltpu
from jax.sharding import PartitionSpec as P

CH = 256
DK = 128
DV = 256
KCONV = 4
TILE = 64


HIGHEST = lax.Precision.HIGHEST
epsilon = 1e-06


def passed_along(block, axis, distance):
    devices = range(lax.axis_size(axis))
    route = [(i - distance, i) for i in devices if i - distance in devices]
    return lax.ppermute(block, axis, route)


def rms_scale(values, gain_row):
    return (
        values * lax.rsqrt(jnp.mean(values * values, axis=-1, keepdims=True) + epsilon) * gain_row
    )


def unit_rows(values):
    return values * lax.rsqrt(jnp.sum(values * values, axis=-1, keepdims=True) + epsilon)


def block_step(state_now, query_vecs, key_vecs, value_vecs, log_decay, erase_rate):
    length = query_vecs.shape[1]
    cumulative = jnp.cumsum(log_decay, axis=1)
    row_index = jnp.arange(length)[:, None]
    col_index = jnp.arange(length)[None, :]
    strict = col_index < row_index
    within = col_index <= row_index
    spread = cumulative[:, :, None] - cumulative[:, None, :]
    lower_decay = jnp.where(strict, jnp.exp(jnp.where(strict, spread, 0.0)), 0.0)
    causal = jnp.where(within, jnp.exp(jnp.where(within, spread, 0.0)), 0.0)
    key_gram = jnp.einsum("htk,hsk->hts", key_vecs, key_vecs, precision=HIGHEST)
    query_gram = jnp.einsum("htk,hsk->hts", query_vecs, key_vecs, precision=HIGHEST)
    negated = -(erase_rate[:, :, None] * key_gram * lower_decay)
    identity = jnp.eye(length, dtype=jnp.float32)
    inverse = identity + negated
    powered = negated
    for level_index in range(length.bit_length() - 2):
        powered = jnp.einsum("hts,hsr->htr", powered, powered, precision=HIGHEST)
        inverse = jnp.einsum("hts,hsr->htr", inverse, identity + powered, precision=HIGHEST)
    shrink = jnp.exp(cumulative)
    recalled = jnp.einsum("htk,hkw->htw", key_vecs, state_now, precision=HIGHEST)
    target = erase_rate[:, :, None] * value_vecs - (erase_rate * shrink)[:, :, None] * recalled
    updates = jnp.einsum("hts,hsw->htw", inverse, target, precision=HIGHEST)
    read_out = shrink[:, :, None] * jnp.einsum(
        "htk,hkw->htw", query_vecs, state_now, precision=HIGHEST
    )
    read_out = read_out + jnp.einsum(
        "hts,hsw->htw", query_gram * causal, updates, precision=HIGHEST
    )
    remain = jnp.exp(cumulative[:, -1:] - cumulative)
    state_next = jnp.exp(cumulative[:, -1])[:, None, None] * state_now
    state_next = state_next + jnp.einsum(
        "hsk,hsw->hkw", key_vecs * remain[:, :, None], updates, precision=HIGHEST
    )
    return (state_next, read_out)


def run_tiles(query_vecs, key_vecs, value_vecs, log_decay, erase_rate, state_start):
    row_count, head_count, key_width = query_vecs.shape
    tile_count = row_count // TILE

    def arrange(tensor):
        return jnp.swapaxes(tensor.reshape((tile_count, TILE, head_count) + tensor.shape[2:]), 1, 2)

    inputs = (
        arrange(query_vecs),
        arrange(key_vecs),
        arrange(value_vecs),
        arrange(log_decay),
        arrange(erase_rate),
    )

    def advance(state_now, sliced):
        return jax.checkpoint(block_step)(state_now, *sliced)

    state_end, outputs = lax.scan(advance, state_start, inputs)
    outputs = jnp.swapaxes(outputs, 1, 2).reshape(row_count, head_count, outputs.shape[-1])
    return (outputs, state_end)


def mixer_inputs(conv_in, edge_rows, head_in, conv_taps, head_params):
    block_len = conv_in.shape[1]
    head_count = head_params.shape[1]
    extended = jnp.concatenate([edge_rows, conv_in], axis=1)
    conv_sum = extended[:, 0:block_len] * conv_taps[:, 0]
    for offset in range(1, conv_taps.shape[1]):
        conv_sum = conv_sum + extended[:, offset : offset + block_len] * conv_taps[:, offset]
    activated = jax.nn.silu(conv_sum)
    key_span = head_count * DK
    lead = activated.shape[:2]
    query_vecs = unit_rows(activated[..., 0:key_span].reshape(lead + (head_count, DK))) * DK ** (
        -0.5
    )
    key_vecs = unit_rows(activated[..., key_span : 2 * key_span].reshape(lead + (head_count, DK)))
    value_vecs = activated[..., 2 * key_span :].reshape(lead + (head_count, DV))
    log_decay = -jnp.exp(head_params[0]) * jax.nn.softplus(
        head_in[..., 0:head_count] + head_params[1]
    )
    erase_rate = jax.nn.sigmoid(head_in[..., head_count : 2 * head_count] + head_params[2])
    return (query_vecs, key_vecs, value_vecs, log_decay, erase_rate)


def gated_norm(mixed, gate_in, head_gain):
    shaped = gate_in.reshape(mixed.shape)
    normed = (
        mixed * lax.rsqrt(jnp.mean(mixed * mixed, axis=-1, keepdims=True) + epsilon) * head_gain
    )
    return (normed * jax.nn.silu(shaped)).reshape(gate_in.shape)


def local_tiles(query_vecs, key_vecs, value_vecs, log_decay, erase_rate):
    key_width = key_vecs.shape[-1]
    value_width = value_vecs.shape[-1]
    head_count = key_vecs.shape[2]
    padded = jnp.concatenate(
        [jnp.zeros(value_vecs.shape[:3] + (key_width,), jnp.float32), value_vecs], axis=-1
    )
    start_map = jnp.concatenate(
        [jnp.eye(key_width, dtype=jnp.float32), jnp.zeros((key_width, value_width), jnp.float32)],
        axis=1,
    )
    start_map = jnp.broadcast_to(start_map, (head_count, key_width, key_width + value_width))

    def single(query_one, key_one, value_one, decay_one, erase_one):
        return run_tiles(query_one, key_one, value_one, decay_one, erase_one, start_map)

    return jax.vmap(single)(query_vecs, key_vecs, padded, log_decay, erase_rate)


def post_mix(local_out, incoming, gate_in, head_gain):
    mixed = local_out[..., DK:] + jnp.einsum(
        "snhk,shkv->snhv", local_out[..., 0:DK], incoming, precision=HIGHEST
    )
    return gated_norm(mixed, gate_in, head_gain)


def swiglu(gate_up):
    split_at = gate_up.shape[-1] // 2
    return jax.nn.silu(gate_up[:, 0:split_at]) * gate_up[:, split_at:]


def matmul_maps(left, right):
    return jnp.einsum("shij,shjk->shik", left, right, precision=HIGHEST)


def apply_map(maps, state_now):
    return matmul_maps(maps[0], state_now) + maps[1]


def general_body(
    tokens,
    lengths,
    cotangent,
    norm_gains,
    head_gain,
    head_params,
    qkv_weight,
    gate_weight,
    head_weight,
    conv_weight,
    out_weight,
    ffn_in,
    ffn_out,
):
    seq_count, block_len, model_width = tokens.shape
    row_count = seq_count * block_len
    position = lax.axis_index("seq") * block_len + jnp.arange(block_len, dtype=jnp.int32)
    valid_rows = (position[None, :] < lengths[:, None]).reshape(row_count, 1)
    col_parts = (
        lax.all_gather(qkv_weight, "seq", axis=1, tiled=True),
        lax.all_gather(gate_weight, "seq", axis=1, tiled=True),
        lax.all_gather(out_weight, "seq", axis=1, tiled=True),
        lax.all_gather(ffn_in, "seq", axis=1, tiled=True),
        lax.all_gather(ffn_out, "seq", axis=1, tiled=True),
    )
    gathered = (
        lax.all_gather(col_parts[0], "dp", axis=0, tiled=True),
        lax.all_gather(col_parts[1], "dp", axis=0, tiled=True),
        lax.all_gather(col_parts[2], "dp", axis=0, tiled=True),
        lax.all_gather(col_parts[3], "dp", axis=0, tiled=True),
        lax.all_gather(col_parts[4], "dp", axis=0, tiled=True),
    )
    w_qkv, w_gate, w_out, w_in, w_down = gathered
    inputs = tokens.reshape(row_count, model_width).astype(jnp.float32)
    first_norm = rms_scale(inputs, norm_gains[0]).astype(jnp.bfloat16)
    conv_in = jnp.dot(first_norm, w_qkv, preferred_element_type=jnp.float32).astype(jnp.bfloat16)
    head_in = jnp.dot(first_norm, head_weight, preferred_element_type=jnp.float32)
    gate_in = jnp.dot(first_norm, w_gate, preferred_element_type=jnp.float32)
    conv_width = conv_in.shape[-1]
    conv_rows = conv_in.reshape(seq_count, block_len, conv_width)
    edge_cut = block_len - (KCONV - 1)
    edge_rows = passed_along(conv_rows[:, edge_cut:], "seq", 1)
    mix_args = (
        conv_rows.astype(jnp.float32),
        edge_rows.astype(jnp.float32),
        head_in.reshape(seq_count, block_len, -1),
        conv_weight.astype(jnp.float32),
        head_params,
    )
    vectors = mixer_inputs(*mix_args)
    local_out, end_states = local_tiles(*vectors)
    carry_maps = (end_states[..., 0:DK], end_states[..., DK:])

    def relay_state(step_index, state_now):
        return passed_along(apply_map(carry_maps, state_now), "seq", 1)

    incoming = lax.fori_loop(
        0, lax.axis_size("seq") - 1, relay_state, jnp.zeros_like(carry_maps[1])
    )
    post_args = (local_out, incoming, gate_in, head_gain)
    normed = post_mix(*post_args).astype(jnp.bfloat16)
    attended = jnp.dot(normed, w_out, preferred_element_type=jnp.float32)
    middle = inputs + attended
    second_norm = rms_scale(middle, norm_gains[1]).astype(jnp.bfloat16)
    gate_up = jnp.dot(second_norm, w_in, preferred_element_type=jnp.float32)
    hidden = swiglu(gate_up).astype(jnp.bfloat16)
    carried = jnp.dot(hidden, w_down, preferred_element_type=jnp.float32)
    output = jnp.where(valid_rows, middle + carried, 0.0).astype(jnp.bfloat16)
    col_again = (
        lax.all_gather(qkv_weight, "seq", axis=1, tiled=True),
        lax.all_gather(gate_weight, "seq", axis=1, tiled=True),
        lax.all_gather(out_weight, "seq", axis=1, tiled=True),
        lax.all_gather(ffn_in, "seq", axis=1, tiled=True),
        lax.all_gather(ffn_out, "seq", axis=1, tiled=True),
    )
    regathered = (
        lax.all_gather(col_again[0], "dp", axis=0, tiled=True),
        lax.all_gather(col_again[1], "dp", axis=0, tiled=True),
        lax.all_gather(col_again[2], "dp", axis=0, tiled=True),
        lax.all_gather(col_again[3], "dp", axis=0, tiled=True),
        lax.all_gather(col_again[4], "dp", axis=0, tiled=True),
    )
    w_qkv, w_gate, w_out, w_in, w_down = regathered
    upstream = jnp.where(
        valid_rows, cotangent.reshape(row_count, model_width).astype(jnp.float32), 0.0
    )
    carried_grad = upstream.astype(jnp.bfloat16)
    grad_down = jnp.einsum("nf,nd->fd", hidden, carried_grad, preferred_element_type=jnp.float32)
    hidden_grad = jnp.einsum("nd,fd->nf", carried_grad, w_down, preferred_element_type=jnp.float32)
    unused, swiglu_back = jax.vjp(swiglu, gate_up)
    gate_up_grad = swiglu_back(hidden_grad)[0].astype(jnp.bfloat16)
    grad_in = jnp.einsum("nd,nf->df", second_norm, gate_up_grad, preferred_element_type=jnp.float32)
    second_grad = jnp.einsum("nf,df->nd", gate_up_grad, w_in, preferred_element_type=jnp.float32)
    unused, second_back = jax.vjp(rms_scale, middle, norm_gains[1])
    middle_back, gain_two = second_back(second_grad)
    middle_grad = upstream + middle_back
    attended_grad = middle_grad.astype(jnp.bfloat16)
    grad_out = jnp.einsum("nv,nd->vd", normed, attended_grad, preferred_element_type=jnp.float32)
    normed_grad = jnp.einsum("nd,vd->nv", attended_grad, w_out, preferred_element_type=jnp.float32)
    unused, post_back = jax.vjp(post_mix, *post_args)
    local_grad, incoming_local, gate_in_grad, head_gain_grad = post_back(normed_grad)
    flipped = (jnp.swapaxes(carry_maps[0], -1, -2), incoming_local)

    def relay_grad(step_index, grad_now):
        return passed_along(apply_map(flipped, grad_now).astype(jnp.bfloat16), "seq", -1).astype(
            jnp.float32
        )

    outgoing = lax.fori_loop(
        0, lax.axis_size("seq") - 1, relay_grad, jnp.zeros_like(incoming_local)
    )
    map_grad = jnp.einsum("shkv,shjv->shkj", outgoing, incoming, precision=HIGHEST)
    end_grad = jnp.concatenate([map_grad, outgoing], axis=-1)
    unused, tiles_back = jax.vjp(local_tiles, *vectors)
    vector_grads = tiles_back((local_grad, end_grad))
    unused, mix_back = jax.vjp(mixer_inputs, *mix_args)
    conv_own, edge_grad, head_in_grad, conv_taps_grad, params_grad = mix_back(vector_grads)
    edge_back = passed_along(edge_grad.astype(jnp.bfloat16), "seq", -1).astype(edge_grad.dtype)
    conv_total = jnp.concatenate(
        [conv_own[:, 0:edge_cut], conv_own[:, edge_cut:] + edge_back], axis=1
    )
    conv_grad = conv_total.reshape(row_count, conv_width).astype(jnp.bfloat16)
    head_grad = head_in_grad.reshape(row_count, -1).astype(jnp.bfloat16)
    gate_grad = gate_in_grad.astype(jnp.bfloat16)
    grad_qkv = jnp.einsum("nd,nc->dc", first_norm, conv_grad, preferred_element_type=jnp.float32)
    grad_head = jnp.einsum("nd,nc->dc", first_norm, head_grad, preferred_element_type=jnp.float32)
    grad_gate = jnp.einsum("nd,nc->dc", first_norm, gate_grad, preferred_element_type=jnp.float32)
    first_grad = jnp.einsum("nc,dc->nd", conv_grad, w_qkv, preferred_element_type=jnp.float32)
    first_grad = first_grad + jnp.einsum(
        "nc,dc->nd", head_grad, head_weight, preferred_element_type=jnp.float32
    )
    first_grad = first_grad + jnp.einsum(
        "nc,dc->nd", gate_grad, w_gate, preferred_element_type=jnp.float32
    )
    unused, first_back = jax.vjp(rms_scale, inputs, norm_gains[0])
    input_back, gain_one = first_back(first_grad)
    input_grad = (
        (middle_grad + input_back).astype(jnp.bfloat16).reshape(seq_count, block_len, model_width)
    )
    row_groups = (
        lax.psum_scatter(
            grad_qkv.astype(jnp.bfloat16), "dp", scatter_dimension=0, tiled=True
        ).astype(jnp.float32),
        lax.psum_scatter(
            grad_gate.astype(jnp.bfloat16), "dp", scatter_dimension=0, tiled=True
        ).astype(jnp.float32),
        lax.psum_scatter(
            grad_out.astype(jnp.bfloat16), "dp", scatter_dimension=0, tiled=True
        ).astype(jnp.float32),
        lax.psum_scatter(
            grad_in.astype(jnp.bfloat16), "dp", scatter_dimension=0, tiled=True
        ).astype(jnp.float32),
        lax.psum_scatter(
            grad_down.astype(jnp.bfloat16), "dp", scatter_dimension=0, tiled=True
        ).astype(jnp.float32),
    )
    weight_parts = (
        lax.psum_scatter(
            row_groups[0].astype(jnp.bfloat16), "seq", scatter_dimension=1, tiled=True
        ).astype(jnp.float32),
        lax.psum_scatter(
            row_groups[1].astype(jnp.bfloat16), "seq", scatter_dimension=1, tiled=True
        ).astype(jnp.float32),
        lax.psum_scatter(
            row_groups[2].astype(jnp.bfloat16), "seq", scatter_dimension=1, tiled=True
        ).astype(jnp.float32),
        lax.psum_scatter(
            row_groups[3].astype(jnp.bfloat16), "seq", scatter_dimension=1, tiled=True
        ).astype(jnp.float32),
        lax.psum_scatter(
            row_groups[4].astype(jnp.bfloat16), "seq", scatter_dimension=1, tiled=True
        ).astype(jnp.float32),
    )
    small_sums = lax.psum(
        (jnp.stack([gain_one, gain_two]), head_gain_grad, params_grad, grad_head, conv_taps_grad),
        ("dp", "seq"),
    )
    output = output.reshape(seq_count, block_len, model_width)
    return (
        output,
        input_grad,
        small_sums[0],
        small_sums[1],
        small_sums[2],
        weight_parts[0],
        weight_parts[1],
        small_sums[3],
        small_sums[4],
        weight_parts[2],
        weight_parts[3],
        weight_parts[4],
    )


MESH = pl.DeviceIdType.MESH
ANY = pl.BlockSpec(memory_space=pl.ANY)
IN_VMEM = pl.BlockSpec(memory_space=pltpu.VMEM)
B16 = jnp.bfloat16
F32 = jnp.float32
NN = ((1,), (0,))
NT = ((1,), (1,))
TN = ((0,), (0,))
HALO = 16


def low(v):
    return v.astype(jnp.bfloat16)


def mm(a, b, dims=NN):
    return lax.dot_general(low(a), low(b), (dims, ((), ())), preferred_element_type=jnp.float32)


def mmf(a, b, dims=NN):
    return lax.dot_general(
        a, b, (dims, ((), ())), precision=HIGHEST, preferred_element_type=jnp.float32
    )


def mm3(a, b, dims=NN):
    ah, bh = low(a), low(b)
    al, bl = low(a - ah.astype(jnp.float32)), low(b - bh.astype(jnp.float32))
    return mm(ah, bh, dims) + (mm(ah, bl, dims) + mm(al, bh, dims))


def sig(v):
    return 1.0 / (1.0 + jnp.exp(-v))


def soft_plus(v):
    tail = jnp.exp(-jnp.abs(v))
    series = tail * (1.0 - tail * (0.5 - tail * (1.0 / 3.0)))
    return jnp.maximum(v, 0.0) + jnp.where(tail < 1e-3, series, jnp.log(1.0 + tail))


def grid_masks():
    row = lax.broadcasted_iota(jnp.int32, (CH, CH), 0)
    col = lax.broadcasted_iota(jnp.int32, (CH, CH), 1)
    return row, col


def decay_parts(g, row, col):
    lower = (col <= row).astype(jnp.float32)
    cum = mmf(lower, g)
    cum_row = mmf(g, lower, ((0,), (1,)))
    within = col <= row
    decay = jnp.where(within, jnp.exp(jnp.where(within, cum - cum_row, 0.0)), 0.0)
    return cum, decay


def unit_inverse(attns, row, col):
    def same(width):
        return (row // width) == (col // width)

    eye = jnp.where(row == col, 1.0, 0.0)
    power = [jnp.where(same(64), -a, 0.0) for a in attns]
    inv = [eye + p for p in power]
    for level in range(5):
        power = [mm(p, p) for p in power]
        inv = [x + mm(x, p) for x, p in zip(inv, power)]
    for width in (128, 256):
        off = same(width) & jnp.logical_not(same(width // 2))
        part = [mm(jnp.where(off, a, 0.0), x) for a, x in zip(attns, inv)]
        inv = [x - mm(x, p) for x, p in zip(inv, part)]
    rest = [eye - x - mm3(a, x) for a, x in zip(attns, inv)]
    return [x + mm(x, r) for x, r in zip(inv, rest)]


def odd(t):
    return t % 2 if isinstance(t, int) else lax.rem(t, 2)


def tile(t, size=CH):
    return pl.ds(pl.multiple_of(t * size, size), size)


class Wires:
    def __init__(self, dp, seq, sems):
        self.dp, self.seq, self.sems, self.used = dp, seq, sems, 0
        self.i, self.s = lax.axis_index("dp"), lax.axis_index("seq")
        self.z, self.c = self.s // 2, lax.rem(self.s, 2)
        self.half, self.partner = self.z // 2, self.z + 1 - 2 * lax.rem(self.z, 2)
        self.inner = lax.rem((self.z + 1) // 2, 2)
        self.place = lax.rem(self.z, 2)
        self.beside = (self.i + 1 - 2 * lax.rem(self.i, 2), lax.rem(self.i + 2, 4))

    def take(self, count=1):
        start = self.used
        self.used += count
        return start

    def meet_all(self):
        barrier = pltpu.get_barrier_semaphore()
        for di in range(self.dp):
            for dj in range(self.seq):
                if di or dj:
                    pl.semaphore_signal(
                        barrier,
                        inc=1,
                        device_id=(lax.rem(self.i + di, self.dp), lax.rem(self.s + dj, self.seq)),
                        device_id_type=MESH,
                    )
        pl.semaphore_wait(barrier, self.dp * self.seq - 1)

    def remote(self, src, dst, send, recv, di, dj):
        return pltpu.make_async_remote_copy(
            src_ref=src,
            dst_ref=dst,
            send_sem=self.sems.at[send],
            recv_sem=self.sems.at[recv],
            device_id=(di, dj),
            device_id_type=MESH,
        )

    def local(self, src, dst, sem):
        return pltpu.make_async_copy(src, dst, self.sems.at[sem])

    def push(self, src, dst, send, recv, di, dj):
        here = (di == self.i) & (dj == self.s)
        away = self.remote(src, dst, send, recv, di, dj)

        @pl.when(here)
        def _():
            self.local(src, dst, recv).start()

        @pl.when(jnp.logical_not(here))
        def _():
            away.start()

        def sent():
            @pl.when(jnp.logical_not(here))
            def _():
                away.wait_send()

        return sent

    def arrived(self, dst, recv):
        pltpu.make_async_copy(dst, dst, self.sems.at[recv]).wait()

    def chip(self, z):
        return z * 2 + self.c

    def order(self, n):
        near = self.z + n * (1 - 2 * lax.rem(self.z, 2))
        return (1 - n // 2) * near + (n // 2) * (n + self.half * (3 - 2 * n))

    def sibling(self):
        return self.z * 2 + 1 - self.c


class LineGather:
    parts = 2

    def __init__(self, w, block_of):
        self.w, self.block_of = w, block_of
        n = 4 * self.parts
        self.send, self.recv = w.take(n), w.take(n)
        self.fsend, self.frecv = w.take(n), w.take(n)

    def piece(self, block, part):
        size = block.shape[0] // self.parts
        return block.at[part * size : part * size + size, :]

    def start(self, src):
        w = self.w
        dst = self.block_of(w.s)
        for part in range(self.parts):
            a, b = self.piece(src, part), self.piece(dst, part)
            slot = w.z * self.parts + part
            near, far = self.send + part, self.send + self.parts + part
            w.remote(a, b, near, self.recv + slot, w.i, w.chip(w.partner)).start()
            w.remote(a, b, far, self.recv + slot, w.i, w.chip(2 - w.half)).start()
        for part in range(self.parts):
            a, b = self.piece(src, part), self.piece(dst, part)
            slot = w.z * self.parts + part
            w.remote(a, b, self.fsend + slot, self.frecv + slot, w.i, w.sibling()).start()

    def arrive(self, t):
        w = self.w

        @pl.when(t != w.z)
        def _():
            block = self.block_of(w.chip(t))
            for part in range(self.parts):
                ref, slot = self.piece(block, part), t * self.parts + part
                w.arrived(ref, self.recv + slot)

                @pl.when((w.inner == 1) & (t // 2 != w.half))
                def _():
                    on = self.send + (2 + odd(t)) * self.parts + part
                    w.remote(ref, ref, on, self.recv + slot, w.i, w.chip(w.partner)).start()

                w.remote(ref, ref, self.fsend + slot, self.frecv + slot, w.i, w.sibling()).start()

    def other(self, t):
        w = self.w
        block = self.block_of(t * 2 + 1 - w.c)
        for part in range(self.parts):
            w.arrived(self.piece(block, part), self.frecv + t * self.parts + part)

    def finish(self):
        w = self.w
        block = self.block_of(w.s)
        for part in range(self.parts):
            ref = self.piece(block, part)
            for n in range(4):
                copy = w.remote(ref, ref, self.send + n * self.parts + part, self.recv, w.i, w.sibling())
                if n < 2:
                    copy.wait_send()
                else:
                    @pl.when(w.inner == 1)
                    def _():
                        copy.wait_send()

                w.remote(ref, ref, self.fsend + n * self.parts + part, self.recv, w.i, w.sibling()).wait_send()


class GroupGather:
    def __init__(self, w, part_of):
        self.w, self.part_of = w, part_of
        self.send, self.recv = w.take(4), w.take(4)

    def start(self, src):
        w = self.w
        w.local(src, self.part_of(w.i), self.recv).start()
        for d in (3, 1, 2):
            to = lax.rem(w.i + d, 4)
            w.remote(src, self.part_of(w.i), self.send + d, self.recv + d, to, w.s).start()

    def finish(self):
        w = self.w
        for d in range(4):
            w.arrived(self.part_of(lax.rem(w.i + 4 - d, 4)), self.recv + d)
        for d in range(1, 4):
            part = self.part_of(w.i)
            w.remote(part, part, self.send + d, self.recv + d, lax.rem(w.i + d, 4), w.s).wait_send()


class SquareGather:
    def __init__(self, w, part_of):
        self.w, self.part_of = w, part_of
        self.send, self.recv = w.take(4), w.take(5)

    def half(self, n, k):
        part = self.part_of(n)
        size = part.shape[0] // 2
        return part.at[size * k : size * k + size, :]

    def near(self, src):
        w = self.w
        part = self.part_of(w.i)
        return [w.remote(src, part, self.send + k, self.recv + k, w.beside[k], w.s) for k in range(2)]

    def far(self, k):
        w = self.w
        half = self.half(w.beside[k], k)
        return w.remote(half, half, self.send + 2 + k, self.recv + 2 + k, w.beside[1 - k], w.s)

    def start(self, src):
        w = self.w
        w.local(src, self.part_of(w.i), self.recv + 4).start()
        for copy in self.near(src):
            copy.start()

    def relay(self):
        w = self.w
        for k in range(2):
            w.arrived(self.part_of(w.beside[k]), self.recv + k)
            self.far(k).start()

    def finish(self):
        w = self.w
        w.arrived(self.part_of(w.i), self.recv + 4)
        for k in range(2):
            w.arrived(self.half(3 - w.i, k), self.recv + 2 + k)
        for copy in self.near(self.part_of(w.i)) + [self.far(0), self.far(1)]:
            copy.wait_send()


class LineScatter:
    def __init__(self, w, part, sib, chip, got):
        self.w, self.part, self.sib, self.chip, self.got = w, part, sib, chip, got
        self.ssend, self.srecv = w.take(4), w.take(4)
        self.send, self.recv = w.take(4), w.take(4)

    def swap(self, t):
        w = self.w
        src = self.part.at[pl.ds(pl.multiple_of(t * 256 + 128 * (1 - w.c), 128), 128), :]
        w.remote(src, self.sib.at[t], self.ssend + t, self.srecv + t, w.i, w.sibling()).start()

    def out(self, t, slot, chip):
        w = self.w
        w.remote(self.chip.at[t], self.got.at[slot], self.send + t, self.recv + slot, w.i, w.chip(chip)).start()

    def pass_on(self, t):
        w = self.w
        w.arrived(self.sib.at[t], self.srecv + t)
        mine = self.part[pl.ds(pl.multiple_of(t * 256 + 128 * w.c, 128), 128), :]
        self.chip[t] = low(mine.astype(jnp.float32) + self.sib[t].astype(jnp.float32))

        @pl.when(t == w.partner)
        def _():
            self.out(t, 0, t)

        @pl.when((t // 2 != w.half) & (w.inner == 0))
        def _():
            self.out(t, 2 + odd(t), w.partner)

    def relay(self, t):
        w = self.w

        @pl.when((t // 2 != w.half) & (w.inner == 1))
        def _():
            slot = 2 + odd(t)
            w.arrived(self.got.at[slot], self.recv + slot)
            self.chip[t] = low(self.chip[t].astype(jnp.float32) + self.got[slot].astype(jnp.float32))
            self.out(t, 1, t)

    def total(self):
        w = self.w
        total = self.chip[w.z].astype(jnp.float32)
        for slot in range(2):
            w.arrived(self.got.at[slot], self.recv + slot)
            total = total + self.got[slot].astype(jnp.float32)
        return total

    def finish(self):
        w = self.w
        for t in range(4):
            src = self.part.at[pl.ds(t * 256, 128), :]
            w.remote(src, self.sib.at[t], self.ssend + t, self.srecv + t, w.i, w.sibling()).wait_send()

            @pl.when(w.z != t)
            def _():
                w.remote(self.chip.at[t], self.got.at[0], self.send + t, self.recv, w.i, w.sibling()).wait_send()


class PairGather:
    def __init__(self, w, buffer):
        self.w, self.buffer = w, buffer
        self.send, self.recv = w.take(3), w.take(3)

    def block(self, q, c):
        return rows_of(self.buffer, 256 * q + 128 * c, 128)

    def copies(self):
        w = self.w
        mine, theirs = self.block(w.place, w.c), self.block(1 - w.place, w.c)
        send, recv = self.send, self.recv
        return (
            w.remote(mine, mine, send, recv, w.i, w.chip(w.partner)),
            w.remote(mine, mine, send + 1, recv + 1, w.i, w.sibling()),
            w.remote(theirs, theirs, send + 2, recv + 2, w.i, w.sibling()),
        )

    def start(self):
        near, core, unused = self.copies()
        near.start()
        core.start()

    def arrive(self):
        w = self.w
        w.arrived(self.block(1 - w.place, w.c), self.recv)
        self.copies()[2].start()

    def other(self, n):
        w = self.w
        q = w.place + n * (1 - 2 * w.place)
        w.arrived(self.block(q, 1 - w.c), self.recv + 1 + n)

    def finish(self):
        for copy in self.copies():
            copy.wait_send()


class PairScatter:
    def __init__(self, w, part, sib, chip, got):
        self.w, self.part, self.sib, self.chip, self.got = w, part, sib, chip, got
        self.ssend, self.srecv = w.take(2), w.take(2)
        self.send, self.recv = w.take(), w.take()

    def swapped(self, q):
        w = self.w
        src = rows_of(self.part, 256 * q + 128 * (1 - w.c), 128)
        return w.remote(src, self.sib.at[q], self.ssend + q, self.srecv + q, w.i, w.sibling())

    def away(self):
        w = self.w
        return w.remote(self.chip.at[1 - w.place], self.got, self.send, self.recv, w.i, w.chip(w.partner))

    def add(self, q):
        w = self.w
        w.arrived(self.sib.at[q], self.srecv + q)
        mine = rows_of(self.part, 256 * q + 128 * w.c, 128)[...]
        self.chip[q] = low(mine.astype(jnp.float32) + self.sib[q].astype(jnp.float32))

    def total(self):
        self.w.arrived(self.got, self.recv)
        return self.chip[self.w.place].astype(jnp.float32) + self.got[...].astype(jnp.float32)

    def finish(self):
        self.swapped(0).wait_send()
        self.swapped(1).wait_send()
        self.away().wait_send()


def cols(ref, start, size):
    return ref.at[:, pl.ds(pl.multiple_of(start, 128), size)]


def rows_of(ref, start, size):
    return ref.at[pl.ds(pl.multiple_of(start, 128), size), :]


class Box:
    pass


def fields(kind):
    return [(name, *value) for name, value in vars(kind).items() if name[0] != "_"]


class FrontKept:
    fn = ((1024, 1024), B16)
    ci = ((HALO + 1024, 512), B16)
    gi = ((1024, 256), F32)
    q = ((1024, 128), F32)
    k = ((1024, 128), F32)
    v = ((1024, 256), F32)
    ge = ((1024, 128), F32)
    mixed = ((1024, 256), F32)
    states = ((4, 128, 256), F32)
    tinv = ((1024, 256), B16)
    u = ((1024, 256), F32)
    wm = ((1024, 128), B16)
    normed = ((1024, 256), B16)
    middle = ((128, 1024), F32)
    sn = ((512, 1024), B16)
    cg = ((512, 1024), B16)
    w_qkv = ((1024, 512), B16)
    w_gate = ((1024, 256), B16)
    w_in = ((1536, 1024), B16)
    w_out = ((256, 1024), B16)
    w_down = ((768, 1024), B16)
class FrontScratch:
    x = ((1024, 1024), B16)
    qkv_p = ((256, 512), B16)
    in_p = ((1536, 256), B16)
    out_p = ((256, 256), B16)
    down_p = ((768, 256), B16)
    down_pad = ((768, 128), B16)
    taps32 = ((8, 4096), F32)
    own_cot = ((128, 1024), B16)
    qk = ((1024, 256), B16)
    cum = ((1024, 1), F32)
    part = ((1024, 1024), B16)
    sib = ((4, 128, 1024), B16)
    chip = ((4, 128, 1024), B16)
    got = ((4, 128, 1024), B16)


def start_weights(w, b):
    i, s = w.i, w.s
    qs, qr = w.take(4), w.take(3)
    lowhalf = s < 4
    b.qr = qr

    @pl.when(lowhalf)
    def _():
        for t in range(4):
            w.push(
                b.qkv.at[:, 128 * t : 128 * t + 128],
                cols(b.qkv_p, 128 * (s // 2), 128),
                qs + t,
                qr + s // 2,
                i,
                4 * lax.rem(s, 2) + t,
            )

    @pl.when(jnp.logical_not(lowhalf))
    def _():
        for t in range(2):
            w.push(b.qkv.at[:, 256 * t : 256 * t + 256], b.qkv_p.at[:, 256:512], qs + t, qr + 2, i, 2 * (s - 4) + t)

    def sent():
        @pl.when(lowhalf)
        def _():
            for t in range(4):
                @pl.when(4 * lax.rem(s, 2) + t != s)
                def _():
                    src = b.qkv.at[:, 128 * t : 128 * t + 128]
                    w.remote(src, b.qkv_p.at[:, 0:128], qs + t, qr, i, w.sibling()).wait_send()

        @pl.when(jnp.logical_not(lowhalf))
        def _():
            for t in range(2):
                @pl.when(2 * (s - 4) + t != s)
                def _():
                    src = b.qkv.at[:, 256 * t : 256 * t + 256]
                    w.remote(src, b.qkv_p.at[:, 256:512], qs + t, qr + 2, i, w.sibling()).wait_send()

    return sent


def start_out_weights(w, b):
    send, recv = w.take(2), w.take(2)
    odd = lax.rem(w.s, 2)
    waits = []
    for n in range(2):
        src = b.out.at[256 * n : 256 * n + 256, :]
        waits.append(w.push(src, cols(b.out_p, 128 * odd, 128), send + n, recv + odd, w.s // 2, 2 * w.i + n))

    def landed():
        for r in range(2):
            w.arrived(b.out_p.at[:, 128 * r : 128 * r + 128], recv + r)

    def sent():
        for wait in waits:
            wait()

    return landed, sent


def start_ffn_weights(w, b):
    i, s = w.i, w.s
    send, recv = w.take(3), w.take(3)
    own, half = lax.rem(s, 2), s // 4
    block = rows_of(b.in_p, 768 * half, 768)
    across = w.remote(block, block, send, recv, i, lax.rem(s + 4, 8))
    across.start()
    waits = [across.wait_send]
    for n in range(2):
        dst = cols(b.down_p, 128 * own, 128)
        waits.append(w.push(b.down_pad, dst, send + 1 + n, recv + 1 + own, s // 2, i + 4 * n))

    def landed():
        w.arrived(rows_of(b.in_p, 768 * (1 - half), 768), recv)
        for r in range(2):
            w.arrived(b.down_p.at[:, 128 * r : 128 * r + 128], recv + 1 + r)

    def sent():
        for wait in waits:
            wait()

    return landed, sent


def valid_rows(b, w):
    place = w.s * 128 + lax.broadcasted_iota(jnp.int32, (128, 1), 0)
    return place < b.lengths[0]


def first_norm_tile(b, t):
    rows = tile(t)
    x = b.x[rows, :].astype(jnp.float32)
    inv = lax.rsqrt(jnp.mean(x * x, axis=-1, keepdims=True) + epsilon)
    b.fn[rows, :] = low(x * inv * b.gains[0:1, :])


def own_head(b, w):
    pm = b.params[...]
    lane = lax.broadcasted_iota(jnp.int32, pm.shape, 1)
    return jnp.sum(jnp.where(lane == w.s, pm, 0.0), axis=1, keepdims=True)


def own_taps(b, w, n):
    s = w.s
    return jnp.concatenate(
        [
            b.taps32[n : n + 1, pl.ds(pl.multiple_of(128 * s, 128), 128)],
            b.taps32[n : n + 1, pl.ds(pl.multiple_of(1024 + 128 * s, 128), 128)],
            b.taps32[n : n + 1, pl.ds(pl.multiple_of(2048 + 256 * s, 128), 256)],
        ],
        axis=1,
    )


def conv_sums(b, w, t):
    window = b.ci[pl.ds(pl.multiple_of(t * CH, CH), CH + HALO), :].astype(jnp.float32)
    total = None
    for n in range(KCONV):
        at = HALO - (KCONV - 1) + n
        term = window[at : at + CH] * own_taps(b, w, n)
        total = term if total is None else total + term
    return total


def project_tile(b, w, t):
    rows = tile(t)
    f = b.fn[rows, :]
    b.ci[pl.ds(pl.multiple_of(t * CH + HALO, HALO), CH), :] = low(mm(f, b.w_qkv[...]))
    b.gi[rows, :] = mm(f, b.w_gate[...])
    hi = mm(f, b.head_w[...], NT)
    lane = lax.broadcasted_iota(jnp.int32, hi.shape, 1)
    pm = own_head(b, w)
    shift = jnp.sum(jnp.where(lane == w.s, hi, 0.0), axis=1, keepdims=True) + pm[1:2, :]
    erase = jnp.sum(jnp.where(lane == w.s + 8, hi, 0.0), axis=1, keepdims=True) + pm[2:3, :]
    line = lax.broadcasted_iota(jnp.int32, (CH, 128), 1)
    decay = -jnp.exp(pm[0:1, :]) * soft_plus(shift)
    b.ge[rows, :] = jnp.where(line == 0, decay, jnp.where(line == 1, sig(erase), shift))


def vectors_tile(b, w, t):
    rows = tile(t)
    total = conv_sums(b, w, t)
    act = total * sig(total)
    qa, ka = act[:, 0:DK], act[:, DK : 2 * DK]
    b.q[rows, :] = qa * lax.rsqrt(jnp.sum(qa * qa, axis=-1, keepdims=True) + epsilon) * DK ** (-0.5)
    b.k[rows, :] = ka * lax.rsqrt(jnp.sum(ka * ka, axis=-1, keepdims=True) + epsilon)
    b.v[rows, :] = act[:, 2 * DK :]


def rec_local(b, w, ts):
    row, col = grid_masks()
    attns = []
    for t in ts:
        vectors_tile(b, w, t)
        rows = tile(t)
        k = b.k[rows, :]
        cum, decay = decay_parts(b.ge[rows, 0:1], row, col)
        b.cum[rows, :] = cum
        b.qk[rows, :] = low(mm(b.q[rows, :], k, NT) * decay)
        attns.append(jnp.where(col < row, b.ge[rows, 1:2] * mm(k, k, NT) * decay, 0.0))
    for t, inv in zip(ts, unit_inverse(attns, row, col)):
        rows = tile(t)
        e, t16 = b.ge[rows, 1:2], low(inv)
        b.tinv[rows, :] = t16
        b.wm[rows, :] = low(mm(t16, (e * jnp.exp(b.cum[rows, :])) * b.k[rows, :]))
        b.u[rows, :] = mm(t16, e * b.v[rows, :])


def rec_step(b, t, state):
    rows = tile(t)
    b.states[t] = state
    cum = b.cum[rows, :]
    last = cum[CH - 1 : CH, :]
    s16 = low(state)
    u = b.u[rows, :] - mm(b.wm[rows, :], s16)
    b.u[rows, :] = u
    u16 = low(u)
    mixed = jnp.exp(cum) * mm(b.q[rows, :], s16) + mm(b.qk[rows, :], u16)
    b.mixed[rows, :] = mixed
    nxt = jnp.exp(last) * state + mm(b.k[rows, :] * jnp.exp(last - cum), u16, TN)
    gate = b.gi[rows, :]
    scale = lax.rsqrt(jnp.mean(mixed * mixed, axis=-1, keepdims=True) + epsilon)
    normed = low(mixed * scale * b.head_gain[...] * (gate * sig(gate)))
    b.normed[rows, :] = normed
    b.part[rows, :] = low(mm(normed, b.w_out[...]))
    return nxt


def front_phase(b, w):
    s, i = w.s, w.i
    own_rows = lambda ref: (lambda n: rows_of(ref, 128 * n, 128))
    x_gather = LineGather(w, own_rows(b.x))
    cg_gather = PairGather(w, b.cg)
    sn_gather = PairGather(w, b.sn)
    qkv_gather = GroupGather(w, lambda n: rows_of(b.w_qkv, 256 * n, 256))
    gate_gather = GroupGather(w, lambda n: rows_of(b.w_gate, 256 * n, 256))
    half = s // 4

    def in_block(n, start, size):
        return b.w_in.at[pl.ds(pl.multiple_of(start, 128), size), pl.ds(pl.multiple_of(256 * n, 256), 256)]

    def own_third(k):
        return GroupGather(w, lambda n: in_block(n, 768 * half + 256 * k, 256))

    in_gathers = [own_third(k) for k in range(3)]
    across_gather = SquareGather(w, lambda n: in_block(n, 768 * (1 - half), 768))

    def start_third(k):
        in_gathers[k].start(rows_of(b.in_p, 768 * half + 256 * k, 256))

    out_gather = GroupGather(w, lambda n: cols(b.w_out, 256 * n, 256))
    down_gather = SquareGather(w, lambda n: cols(b.w_down, 256 * n, 256))
    scatter = LineScatter(w, b.part, b.sib, b.chip, b.got)
    own_x, own_c = w.take(), w.take()

    ff_cols, ff_rows = b.ffn_in.shape[0], b.ffn_out.shape[0]
    b.in_p[pl.ds(pl.multiple_of(768 * half, 128), ff_cols), :] = b.ffn_in[...]
    b.in_p[pl.ds(pl.multiple_of(768 * half + ff_cols, 64), 768 - ff_cols), :] = jnp.zeros((768 - ff_cols, 256), B16)
    b.down_pad[0:ff_rows, :] = b.ffn_out[...]
    b.down_pad[ff_rows:, :] = jnp.zeros((768 - ff_rows, 128), B16)
    w.meet_all()
    qkv_sent = start_weights(w, b)
    out_landed, out_sent = start_out_weights(w, b)
    x_gather.start(b.tokens)
    gate_gather.start(b.gate)
    start_third(0)
    keep_x = w.local(b.tokens, rows_of(b.x, 128 * s, 128), own_x)
    keep_x.start()
    b.ci[0:HALO, :] = jnp.zeros((HALO, 512), B16)
    b.taps32[0:KCONV, :] = b.taps[...].astype(jnp.float32)
    cot = jnp.where(valid_rows(b, w), b.cot_v[...].astype(jnp.float32), 0.0)
    b.own_cot[...] = low(cot)
    rows_of(b.cg, 128 * lax.rem(s, 4), 128)[...] = low(cot)
    w.arrived(b.qkv_p.at[:, 0:128], b.qr)
    w.arrived(b.qkv_p.at[:, 128:256], b.qr + 1)
    w.arrived(b.qkv_p.at[:, 256:512], b.qr + 2)
    qkv_gather.start(b.qkv_p)
    out_landed()
    out_gather.start(b.out_p)
    ffn_landed, ffn_sent = start_ffn_weights(w, b)
    keep_x.wait()

    def norm_loop(n, carry):
        t = w.order(n)
        x_gather.arrive(t)
        x_gather.other(t)
        first_norm_tile(b, t)
        return carry

    lax.fori_loop(0, 4, norm_loop, 0)
    cg_gather.start()
    qkv_gather.finish()
    gate_gather.finish()
    start_third(1)
    start_third(2)

    def project_loop(t, carry):
        project_tile(b, w, t)
        return carry

    lax.fori_loop(0, 4, project_loop, 0)
    x_gather.finish()
    out_gather.finish()

    def pair_loop(pair, state):
        rec_local(b, w, (2 * pair, 2 * pair + 1))

        @pl.when(pair == 0)
        def _():
            ffn_landed()
            across_gather.start(rows_of(b.in_p, 768 * (1 - half), 768))
            down_gather.start(b.down_p)

        for k in range(2):
            t = 2 * pair + k
            state = rec_step(b, t, state)
            scatter.swap(t)
        scatter.pass_on(2 * pair)
        scatter.pass_on(2 * pair + 1)
        return state

    lax.fori_loop(0, 2, pair_loop, jnp.zeros((DK, DV), F32))

    scatter.relay(0)
    scatter.relay(1)
    scatter.relay(2)
    scatter.relay(3)
    across_gather.relay()
    down_gather.relay()

    def own_half(which):
        @pl.when(w.half == which)
        def _():
            middle = b.tokens_v[...].astype(jnp.float32) + scatter.total()
            b.middle[...] = middle
            inv = lax.rsqrt(jnp.mean(middle * middle, axis=-1, keepdims=True) + epsilon)
            rows_of(b.sn, 128 * lax.rem(s, 4), 128)[...] = low(middle * inv * b.gains[1:2, :])
            sn_gather.start()

    own_half(0)
    cg_gather.arrive()
    own_half(1)
    for third in in_gathers:
        third.finish()
    across_gather.finish()
    down_gather.finish()
    qkv_sent()
    out_sent()
    ffn_sent()
    scatter.finish()

    def finish():
        cg_gather.finish()
        sn_gather.finish()

    return sn_gather, cg_gather, finish


class SquareScatter:
    def __init__(self, w, out, got):
        self.w, self.out, self.got = w, out, got
        self.send, self.recv = w.take(6), w.take(6)

    def half(self, ref, n, k):
        size = ref.shape[1] // 2
        return ref.at[n, size * k : size * k + size, :]

    def copy(self, n, k):
        w = self.w
        to = k if n == 2 else n
        slot = 2 * n + k
        return w.remote(
            self.half(self.out, n, k), self.half(self.got, n, k), self.send + slot, self.recv + slot, w.beside[to], w.s
        )

    def start_far(self, piece_of):
        self.out[2] = low(piece_of(3 - self.w.i))
        self.copy(2, 0).start()
        self.copy(2, 1).start()

    def start_near(self, piece_of):
        for n in range(2):
            self.out[n] = low(piece_of(self.w.beside[n]))
            self.copy(n, n).start()

    def relay(self):
        w = self.w
        for k in range(2):
            half = self.half(self.out, 1 - k, k)
            w.arrived(self.half(self.got, 2, k), self.recv + 4 + k)
            half[...] = low(half[...].astype(jnp.float32) + self.half(self.got, 2, k)[...].astype(jnp.float32))
            self.copy(1 - k, k).start()

    def total(self, own):
        w = self.w
        total = own
        for n in range(2):
            for k in range(2):
                w.arrived(self.half(self.got, n, k), self.recv + 2 * n + k)
            total = total + self.got[n].astype(jnp.float32)
        return total

    def finish(self):
        for n in range(3):
            for k in range(2):
                self.copy(n, k).wait_send()


def ffn_tile(b, t):
    rows = tile(t)
    sn, cg = b.sn[rows, :], b.cg[rows, :]
    half = b.w_in.shape[0] // 2
    both = mm(sn, b.w_in[...], NT)
    gate, up = both[:, 0:half], both[:, half:]
    open_ = sig(gate)
    act = gate * open_
    hidden = low(act * up)
    b.hid[rows, :] = hidden
    b.part4[rows, :] = low(mm(hidden, b.w_down[...]))
    hgrad = mm(cg, b.w_down[...], NT)
    both_grad = jnp.concatenate(
        [low(hgrad * up * (open_ * (1.0 + gate * (1.0 - open_)))), low(hgrad * act)], axis=1
    )
    b.gug[rows, :] = both_grad
    b.part[rows, :] = low(mm(both_grad, b.w_in[...]))


def norm_back(x, gain, grad):
    inv = lax.rsqrt(jnp.mean(x * x, axis=-1, keepdims=True) + epsilon)
    unit = x * inv
    dunit = grad * gain
    return inv * (dunit - unit * jnp.mean(dunit * unit, axis=-1, keepdims=True)), grad * unit


def mixer_out_back(b, t, head_gain_sum):
    rows = tile(t)
    ng = mm(b.agr[rows, :], b.w_out[...], NT)
    gate = b.gi[rows, :]
    open_ = sig(gate)
    act = gate * open_
    gain = b.head_gain[...]
    mixed = b.mixed[rows, :]
    inv = lax.rsqrt(jnp.mean(mixed * mixed, axis=-1, keepdims=True) + epsilon)
    unit = mixed * inv
    dunit = ng * act * gain
    b.do[rows, :] = inv * (dunit - unit * jnp.mean(dunit * unit, axis=-1, keepdims=True))
    nu = ng * unit
    b.gg[rows, :] = low(nu * gain * (open_ * (1.0 + gate * (1.0 - open_))))
    return head_gain_sum + jnp.sum(nu * act, axis=0, keepdims=True)


def rec_back_chain(b, t, ds1, row, col):
    rows = tile(t)
    do = low(b.do[rows, :])
    b.dstates[t] = ds1
    cum = b.cum[rows, :]
    last = cum[CH - 1 : CH, :]
    du = mm(b.qk[rows, :], do, TN) + mm(b.k[rows, :] * jnp.exp(last - cum), ds1)
    du16 = low(du)
    b.dr[rows, :] = mm(b.tinv[rows, :], du16, TN)
    return jnp.exp(last) * ds1 + mm(b.q[rows, :] * jnp.exp(cum), do, TN) - mm(b.wm[rows, :], du16, TN)


def rec_back_tile(b, t, row, col):
    rows = tile(t)
    q, k, v, e = b.q[rows, :], b.k[rows, :], b.v[rows, :], b.ge[rows, 1:2]
    s0, ds1, u, do, dr = b.states[t], b.dstates[t], b.u[rows, :], b.do[rows, :], b.dr[rows, :]
    cum, decay = decay_parts(b.ge[rows, 0:1], row, col)
    last = cum[CH - 1 : CH, :]
    gamma, shrink, remain = jnp.exp(last), jnp.exp(cum), jnp.exp(last - cum)
    gram = jnp.where(col < row, mm(k, k, NT) * decay, 0.0)
    qk = mm(q, k, NT) * decay
    dp = jnp.where(col <= row, mm3(do, u, NT), 0.0)
    da = jnp.where(col < row, -mm3(dr, u, NT), 0.0)
    dqk = low(dp * decay)
    dag = da * gram
    zed = dp * qk + e * dag
    dgram = low(e * da * decay)
    nk = mm3(dr, s0, NT)
    m = mm3(do, s0, NT)
    lm = mm3(u, ds1, NT)
    row_nk = jnp.sum(nk * k, axis=1, keepdims=True)
    dv = e * dr
    de = (
        jnp.sum(dr * v, axis=1, keepdims=True)
        - shrink * row_nk
        + jnp.sum(dag, axis=1, keepdims=True)
    )
    dq = mm(dqk, k) + shrink * m
    dk = mm(dqk, q, TN) + mm(dgram, k) + mm(dgram, k, TN) - (e * shrink) * nk + remain * lm
    dshrink = jnp.sum(m * q, axis=1, keepdims=True) - e * row_nk
    rdr = remain * jnp.sum(lm * k, axis=1, keepdims=True)
    ones = jnp.ones((CH, 1), jnp.float32)
    dcum = jnp.sum(zed, axis=1, keepdims=True) - mmf(zed, ones, TN) + shrink * dshrink - rdr
    dlast = jnp.sum(rdr, axis=0, keepdims=True) + gamma * jnp.sum(
        jnp.sum(s0 * ds1, axis=1, keepdims=True), axis=0, keepdims=True
    )
    lower = (col <= row).astype(jnp.float32)
    dg = mmf(lower, dcum, TN) + dlast
    return dq, dk, dv, dg, de


def unit_back(x, grad):
    inv = lax.rsqrt(jnp.sum(x * x, axis=-1, keepdims=True) + epsilon)
    unit = x * inv
    return inv * (grad - unit * jnp.sum(grad * unit, axis=-1, keepdims=True))


def mixer_back_tile(b, w, t, row, col, sums):
    rows = tile(t)
    dq, dk, dv, dg, de = rec_back_tile(b, t, row, col)
    total = conv_sums(b, w, t)
    open_ = sig(total)
    act = total * open_
    dact = jnp.concatenate(
        [unit_back(act[:, 0:DK], dq * DK ** (-0.5)), unit_back(act[:, DK : 2 * DK], dk), dv], axis=1
    )
    dcs = dact * (open_ * (1.0 + total * (1.0 - open_)))
    b.dcs[0:CH, :] = dcs
    window = b.ci[pl.ds(pl.multiple_of(t * CH, CH), CH + HALO), :].astype(jnp.float32)
    ahead = b.dcs[...]
    taps_sums, p0, p1, p2, gain_sum = sums
    dci = None
    new_taps = []
    for n in range(KCONV):
        at = HALO - (KCONV - 1) + n
        new_taps.append(taps_sums[n] + jnp.sum(dcs * window[at : at + CH], axis=0, keepdims=True))
        back = KCONV - 1 - n
        term = ahead[back : back + CH] * own_taps(b, w, n)
        dci = term if dci is None else dci + term
    b.dcs[CH : CH + HALO, :] = dcs[0:HALO]
    dci16 = low(dci)
    b.cgd[rows, :] = dci16
    lane = lax.broadcasted_iota(jnp.int32, (CH, 16), 1)
    pm = own_head(b, w)
    shift = b.ge[rows, 2:3]
    dshift = dg * (-jnp.exp(pm[0:1, :])) * sig(shift)
    e = b.ge[rows, 1:2]
    dlogit = de * e * (1.0 - e)
    hg = low(jnp.where(lane == w.s, dshift, jnp.where(lane == w.s + 8, dlogit, 0.0)))
    b.hg[rows, :] = hg
    fp = mm(dci16, b.w_qkv[...], NT) + mm(hg, b.head_w[...]) + mm(b.gg[rows, :], b.w_gate[...], NT)
    b.part[rows, :] = low(fp)
    gain_part = jnp.sum(fp * b.fn[rows, :].astype(jnp.float32), axis=0, keepdims=True)
    return (
        tuple(new_taps),
        p0 + jnp.sum(dg * b.ge[rows, 0:1], axis=0, keepdims=True),
        p1 + jnp.sum(dshift, axis=0, keepdims=True),
        p2 + jnp.sum(dlogit, axis=0, keepdims=True),
        gain_sum + gain_part,
    )


class LayerOut:
    output = ((128, 1024), B16)
    input_grad = ((128, 1024), B16)
    gains_grad = ((2, 1024), F32)
    head_gain_grad = ((1, 256), F32)
    params_grad = ((8, 128), F32)
    head_w_grad = ((16, 1024), F32)
    conv_grad = ((4, 4096), F32)
    qkv_back = ((256, 512), B16)
    gate_back = ((256, 256), B16)
    in_back = ((768, 256), B16)
    out_back = ((512, 128), B16)
    down_back = ((768, 128), B16)
class RestScratch:
    hid = ((512, 768), B16)
    gug = ((512, 1536), B16)
    part4 = ((512, 1024), B16)
    sib4 = ((2, 128, 1024), B16)
    chip4 = ((2, 128, 1024), B16)
    got4 = ((128, 1024), B16)
    sib6 = ((2, 128, 1024), B16)
    chip6 = ((2, 128, 1024), B16)
    got6 = ((128, 1024), B16)
    own_ag = ((128, 1024), B16)
    mgrad = ((128, 1024), F32)
    gg = ((1024, 256), B16)
    dstates = ((4, 128, 256), F32)
    dcs = ((CH + HALO, 512), F32)
    cgd = ((1024, 512), B16)
    hg = ((1024, 16), B16)
    in_out = ((3, 1536, 256), B16)
    in_got = ((3, 1536, 256), B16)
    down_out = ((3, 768, 256), B16)
    down_got = ((3, 768, 256), B16)
    out_out = ((3, 256, 256), B16)
    out_got = ((3, 256, 256), B16)
    qkv_out = ((3, 256, 512), B16)
    qkv_got = ((3, 256, 512), B16)
    gate_out = ((3, 256, 256), B16)
    gate_got = ((3, 256, 256), B16)
    in_sum = ((1536, 256), B16)
    in_other = ((768, 256), B16)
    down_sum = ((768, 256), B16)
    down_parts = ((2, 768, 128), B16)
    out_sum = ((256, 256), B16)
    qkv_sum = ((256, 512), B16)
    small = ((8, 1024), F32)
    small_got = ((4, 8, 1024), F32)
    small_sum = ((8, 1024), F32)
    small_all = ((8, 8, 1024), F32)


def grads_home(w, b):
    i, h = w.i, w.s
    send, recv = w.take(9), w.take(10)
    quarter, pair, half = lax.rem(h, 4), lax.rem(h, 2), h // 4

    def across():
        block = rows_of(b.in_sum, 768 * (1 - half), 768)
        return w.remote(block, b.in_other, send, recv + 4, i, lax.rem(h + 4, 8))

    down_to = [(b.down_sum.at[:, 128 * r : 128 * r + 128], quarter, 2 * i + r) for r in range(2)]

    def ffn():
        across().start()
        for r, (src, di, dj) in enumerate(down_to):
            w.push(src, b.down_parts.at[half], send + 2 + r, recv + 8 + half, di, dj)

    def ffn_done():
        across().wait_send()
        for r, (src, di, dj) in enumerate(down_to):
            @pl.when((di != i) | (dj != h))
            def _():
                w.remote(src, src, send + 2 + r, recv, i, w.sibling()).wait_send()

        w.arrived(b.in_other, recv + 4)
        mine = rows_of(b.in_sum, 768 * half, 768)[...]
        b.in_back[...] = low(mine.astype(jnp.float32) + b.in_other[...].astype(jnp.float32))
        for r in range(2):
            w.arrived(b.down_parts.at[r], recv + 8 + r)
        b.down_back[...] = low(b.down_parts[0].astype(jnp.float32) + b.down_parts[1].astype(jnp.float32))

    def mixer():
        to = (
            (b.qkv_sum.at[:, 0:128], cols(b.qkv_back, 128 * quarter, 128), recv + quarter, half),
            (b.qkv_sum.at[:, 128:256], cols(b.qkv_back, 128 * quarter, 128), recv + quarter, 2 + half),
            (b.qkv_sum.at[:, 256:512], cols(b.qkv_back, 256 * pair, 256), recv + pair, 4 + h // 2),
        )
        return [w.push(src, dst, send + 4 + n, sem, i, dj) for n, (src, dst, sem, dj) in enumerate(to)]

    def mixer_out():
        waits = []
        for r in range(2):
            src = b.out_sum.at[:, 128 * r : 128 * r + 128]
            dst = rows_of(b.out_back, 256 * pair, 256)
            waits.append(w.push(src, dst, send + 7 + r, recv + 6 + pair, h // 2, 2 * i + r))
        return waits

    def landed():
        @pl.when(h < 4)
        def _():
            for t in range(4):
                w.arrived(b.qkv_back.at[:, 128 * t : 128 * t + 128], recv + t)

        @pl.when(h >= 4)
        def _():
            for t in range(2):
                w.arrived(b.qkv_back.at[:, 256 * t : 256 * t + 256], recv + t)

        for r in range(2):
            w.arrived(b.out_back.at[256 * r : 256 * r + 256, :], recv + 6 + r)

    return ffn, ffn_done, mixer, mixer_out, landed


def small_sums(w, b, send, recv, send2, recv2):
    copies = []
    for d in range(1, 4):
        copy = w.remote(b.small, b.small_got.at[d], send + d, recv + d, lax.rem(w.i + d, 4), w.s)
        copy.start()
        copies.append(copy)

    def middle():
        total = b.small[...]
        for d in range(1, 4):
            w.arrived(b.small_got.at[d], recv + d)
            total = total + b.small_got[d]
        b.small_sum[...] = total
        b.small_all[w.s] = total
        for d in range(1, 8):
            copy = w.remote(b.small_sum, b.small_all.at[w.s], send2 + d, recv2 + d, w.i, lax.rem(w.s + d, 8))
            copy.start()
            copies.append(copy)

    def end():
        for d in range(1, 8):
            w.arrived(b.small_all.at[lax.rem(w.s + 8 - d, 8)], recv2 + d)
        for copy in copies:
            copy.wait_send()
        gains = b.small_all[0, 0:2, :]
        head_gain = b.small_all[0, 2:3, 0:256]
        for n in range(1, 8):
            gains = gains + b.small_all[n, 0:2, :]
            head_gain = head_gain + b.small_all[n, 2:3, 0:256]
        b.gains_grad[...] = gains
        b.head_gain_grad[...] = head_gain
        for n in range(8):
            b.params_grad[n : n + 1, :] = b.small_all[n, 3:4, 0:128]
            b.head_w_grad[n : n + 1, :] = b.small_all[n, 4:5, :]
            b.head_w_grad[8 + n : 9 + n, :] = b.small_all[n, 5:6, :]
            for k in range(KCONV):
                line = b.small_all[n, 6 + k // 2 : 7 + k // 2, 512 * (k % 2) : 512 * (k % 2) + 512]
                b.conv_grad[k : k + 1, 128 * n : 128 * n + 128] = line[:, 0:128]
                b.conv_grad[k : k + 1, 1024 + 128 * n : 1152 + 128 * n] = line[:, 128:256]
                b.conv_grad[k : k + 1, 2048 + 256 * n : 2304 + 256 * n] = line[:, 256:512]

    return middle, end


def rest_phase(b, w, sn_gather, cg_gather, front_finish):
    s = w.s
    half_rows = lambda ref: (lambda n: rows_of(ref, 128 * n, 128))
    ag_gather = LineGather(w, half_rows(b.agr))
    scatter4 = PairScatter(w, b.part4, b.sib4, b.chip4, b.got4)
    scatter6 = PairScatter(w, b.part, b.sib6, b.chip6, b.got6)
    scatter8 = LineScatter(w, b.part, b.sib, b.chip, b.got)
    in_sum = SquareScatter(w, b.in_out, b.in_got)
    down_sum = SquareScatter(w, b.down_out, b.down_got)
    out_sum = SquareScatter(w, b.out_out, b.out_got)
    qkv_sum = SquareScatter(w, b.qkv_out, b.qkv_got)
    gate_sum = SquareScatter(w, b.gate_out, b.gate_got)
    home_ffn, home_ffn_done, home_qkv, home_out, home_landed = grads_home(w, b)
    sm = (w.take(4), w.take(4), w.take(8), w.take(8))

    def ffn_loop(n, carry):
        @pl.when(n == 1)
        def _():
            sn_gather.arrive()

        sn_gather.other(n)
        cg_gather.other(n)
        q = w.place + n * (1 - 2 * w.place)
        ffn_tile(b, q)
        scatter6.swapped(q).start()
        scatter4.swapped(q).start()
        return carry

    lax.fori_loop(0, 2, ffn_loop, 0)
    scatter6.add(1 - w.place)
    scatter6.away().start()
    scatter6.add(w.place)

    def in_piece(n):
        return mm(b.gug[...], cols(b.sn, 256 * n, 256)[...], TN)

    def down_piece(n):
        return mm(b.hid[...], cols(b.cg, 256 * n, 256)[...], TN)

    in_sum.start_far(in_piece)
    down_sum.start_far(down_piece)
    second_grad = scatter6.total()
    back, share = norm_back(b.middle[...], b.gains[1:2, :], second_grad)
    b.small[1:2, :] = jnp.sum(share, axis=0, keepdims=True)
    mgrad = b.own_cot[...].astype(jnp.float32) + back
    b.mgrad[...] = mgrad
    own = low(mgrad)
    b.own_ag[...] = own
    rows_of(b.agr, 128 * s, 128)[...] = own
    ag_gather.start(b.own_ag)
    in_sum.start_near(in_piece)
    down_sum.start_near(down_piece)
    scatter4.add(1 - w.place)
    scatter4.away().start()
    scatter4.add(w.place)
    row, col = grid_masks()

    def out_loop(n, head_gain_sum):
        t = w.order(n)
        ag_gather.arrive(t)
        ag_gather.other(t)
        out = mixer_out_back(b, t, head_gain_sum)

        @pl.when(n == 2)
        def _():
            in_sum.relay()
            down_sum.relay()

        return out

    head_gain_sum = lax.fori_loop(0, 4, out_loop, jnp.zeros((1, DV), F32))
    scatter6.finish()
    def out_piece(n):
        return mm(b.normed[...], cols(b.agr, 256 * n, 256)[...], TN)


    def gate_piece(n):
        return mm(cols(b.fn, 256 * n, 256)[...], b.gg[...], TN)

    out_sum.start_far(out_piece)
    gate_sum.start_far(gate_piece)
    out_sum.start_near(out_piece)
    gate_sum.start_near(gate_piece)

    def chain_loop(n, ds1):
        return rec_back_chain(b, 3 - n, ds1, row, col)

    lax.fori_loop(0, 4, chain_loop, jnp.zeros((DK, DV), F32))
    b.in_sum[...] = low(in_sum.total(in_piece(w.i)))
    b.down_sum[...] = low(down_sum.total(down_piece(w.i)))
    home_ffn()
    b.dcs[CH : CH + HALO, :] = jnp.zeros((HALO, 512), F32)

    def back_loop(n, sums):
        t = 3 - n
        sums = mixer_back_tile(b, w, t, row, col, sums)
        scatter8.swap(t)

        @pl.when(n == 1)
        def _():
            out_sum.relay()
            gate_sum.relay()

        @pl.when(n > 0)
        def _():
            scatter8.pass_on(t + 1)

        @pl.when(n > 1)
        def _():
            scatter8.relay(t + 2)

        return sums

    one = jnp.zeros((1, 1), F32)
    taps_sums, p0, p1, p2, gain_sum = lax.fori_loop(
        0, 4, back_loop, (tuple(jnp.zeros((1, 512), F32) for n in range(KCONV)), one, one, one, jnp.zeros((1, 1024), F32))
    )
    scatter8.pass_on(0)
    scatter8.relay(1)

    def qkv_piece(n):
        return mm(cols(b.fn, 256 * n, 256)[...], b.cgd[...], TN)

    qkv_sum.start_far(qkv_piece)
    qkv_sum.start_near(qkv_piece)
    scatter8.relay(0)
    b.small[0:1, :] = gain_sum / b.gains[0:1, :]
    b.small[2:3, :] = jnp.concatenate([head_gain_sum, jnp.zeros((1, 1024 - DV), F32)], axis=1)
    lane = lax.broadcasted_iota(jnp.int32, (1, 1024), 1)
    b.small[3:4, :] = jnp.where(lane == 0, p0, jnp.where(lane == 1, p1, jnp.where(lane == 2, p2, 0.0)))
    head_rows = mm(b.hg[...], b.fn[...], TN)
    line = lax.broadcasted_iota(jnp.int32, head_rows.shape, 0)
    b.small[4:5, :] = jnp.sum(jnp.where(line == s, head_rows, 0.0), axis=0, keepdims=True)
    b.small[5:6, :] = jnp.sum(jnp.where(line == s + 8, head_rows, 0.0), axis=0, keepdims=True)
    b.small[6:7, :] = jnp.concatenate([taps_sums[0], taps_sums[1]], axis=1)
    b.small[7:8, :] = jnp.concatenate([taps_sums[2], taps_sums[3]], axis=1)
    small_middle, small_end = small_sums(w, b, *sm)
    b.out_sum[...] = low(out_sum.total(out_piece(w.i)))
    waits = home_out()
    b.gate_back[...] = low(gate_sum.total(gate_piece(w.i)))
    qkv_sum.relay()
    small_middle()
    b.output[...] = low(jnp.where(valid_rows(b, w), b.middle[...] + scatter4.total(), 0.0))
    b.qkv_sum[...] = low(qkv_sum.total(qkv_piece(w.i)))
    waits = waits + home_qkv()
    first_grad = scatter8.total()
    back, unused_share = norm_back(b.tokens_v[...].astype(jnp.float32), b.gains[0:1, :], first_grad)
    b.input_grad[...] = low(b.mgrad[...] + back)
    home_ffn_done()
    small_end()
    home_landed()
    for wait in waits:
        wait()
    for part in (in_sum, down_sum, out_sum, qkv_sum, gate_sum):
        part.finish()
    scatter4.finish()
    scatter8.finish()
    ag_gather.finish()
    front_finish()


def layer_kernel(dp, seq, *refs):
    b = Box()
    (
        b.tokens,
        b.qkv,
        b.gate,
        b.ffn_in,
        b.out,
        b.ffn_out,
        b.gains,
        b.head_gain,
        b.params,
        b.head_w,
        b.taps,
        b.tokens_v,
        b.cot_v,
        b.lengths,
    ) = refs[:14]
    kinds = fields(LayerOut) + fields(FrontKept) + fields(FrontScratch) + fields(RestScratch)
    for (name, shape, kind), ref in zip(kinds, refs[14:]):
        setattr(b, name, ref)
    b.do, b.dr, b.agr = b.mixed, b.gi, b.x
    w = Wires(dp, seq, refs[-1])
    rest_phase(b, w, *front_phase(b, w))


def layer(dp, seq, *arrays):
    outs = pl.pallas_call(
        functools.partial(layer_kernel, dp, seq),
        out_shape=tuple(jax.ShapeDtypeStruct(shape, kind) for _, shape, kind in fields(LayerOut)),
        in_specs=[ANY] * 3 + [IN_VMEM, ANY] + [IN_VMEM] * 8 + [pl.BlockSpec(memory_space=pltpu.SMEM)],
        out_specs=(IN_VMEM,) * len(fields(LayerOut)),
        scratch_shapes=[
            pltpu.VMEM(shape, kind)
            for _, shape, kind in fields(FrontKept) + fields(FrontScratch) + fields(RestScratch)
        ]
        + [pltpu.SemaphoreType.DMA((500,))],
        compiler_params=pltpu.CompilerParams(collective_id=0, has_side_effects=True, vmem_limit_bytes=62 << 20),
        name="layer",
    )(*arrays)
    made = Box()
    for (name, shape, kind), out in zip(fields(LayerOut), outs):
        setattr(made, name, out)
    return made


class FinalOut:
    output = ((128, 1024), B16)
    input_grad = ((128, 1024), B16)
    gains_grad = ((2, 1024), F32)
    head_gain_grad = ((1, 256), F32)
    params_grad = ((3, 8), F32)
    head_w_grad = ((16, 1024), F32)
    conv_grad = ((4, 4096), F32)
    qkv_back = ((256, 512), F32)
    gate_back = ((256, 256), F32)
    in_back = ((704, 256), F32)
    out_back = ((512, 128), F32)
    down_back = ((704, 128), F32)


def final_kernel(*refs):
    count = len(fields(FinalOut))
    srcs, outs, held, sems = refs[:count], refs[count : 2 * count], refs[2 * count : -1], refs[-1]
    copies = [pltpu.make_async_copy(src, buf, sems.at[n]) for n, (src, buf) in enumerate(zip(srcs, held))]
    for copy in copies:
        copy.start()
    for n, ((name, shape, kind), copy, buf, out) in enumerate(zip(fields(FinalOut), copies, held, outs)):
        copy.wait()
        if n == 4:
            out[...] = jnp.transpose(buf[...])[0:3, :]
        else:
            out[...] = buf[0 : shape[0], :].astype(kind)


def final(made):
    names = fields(FinalOut)
    arrays = [getattr(made, name) for name, _, _ in names]
    outs = pl.pallas_call(
        final_kernel,
        out_shape=tuple(jax.ShapeDtypeStruct(shape, kind) for _, shape, kind in names),
        in_specs=[ANY] * len(names),
        out_specs=(IN_VMEM,) * len(names),
        scratch_shapes=[pltpu.VMEM(array.shape, array.dtype) for array in arrays]
        + [pltpu.SemaphoreType.DMA((len(names),))],
        compiler_params=pltpu.CompilerParams(vmem_limit_bytes=62 << 20),
        name="final",
    )(*arrays)
    done = Box()
    for (name, shape, kind), out in zip(names, outs):
        setattr(done, name, out)
    return done


def fast_body(
    dp,
    seq,
    tokens,
    lengths,
    cotangent,
    norm_gains,
    head_gain,
    head_params,
    qkv_weight,
    gate_weight,
    head_weight,
    conv_weight,
    out_weight,
    ffn_in,
    ffn_out,
):
    made = layer(
        dp,
        seq,
        tokens[0],
        qkv_weight,
        gate_weight,
        ffn_in.T,
        out_weight,
        ffn_out,
        norm_gains,
        head_gain[None],
        head_params,
        head_weight.T,
        conv_weight.T,
        tokens[0],
        cotangent[0],
        lengths,
    )
    r = final(made)
    return (
        r.output[None],
        r.input_grad[None],
        r.gains_grad,
        r.head_gain_grad[0],
        r.params_grad,
        r.qkv_back,
        r.gate_back,
        r.head_w_grad.T,
        r.conv_grad.T,
        r.out_back,
        r.in_back.T,
        r.down_back,
    )


def choose_body(dp, seq):
    def chosen(*arrays):
        tokens, head_params = arrays[0], arrays[5]
        if (dp, seq) == (4, 8) and tokens.shape[0] == 1 and head_params.shape[1] == seq:
            return fast_body(dp, seq, *arrays)
        return general_body(*arrays)

    return chosen


def solution(mesh):
    dp, seq = mesh.shape["dp"], mesh.shape["seq"]
    placed = (
        P("dp", "seq", None),
        P("dp"),
        P("dp", "seq", None),
        P(),
        P(),
        P(),
        P("dp", "seq"),
        P("dp", "seq"),
        P(),
        P(),
        P("dp", "seq"),
        P("dp", "seq"),
        P("dp", "seq"),
    )
    return jax.shard_map(
        choose_body(dp, seq),
        mesh=mesh,
        in_specs=placed,
        out_specs=(
            P("dp", "seq", None),
            P("dp", "seq", None),
            P(),
            P(),
            P(),
            P("dp", "seq"),
            P("dp", "seq"),
            P(),
            P(),
            P("dp", "seq"),
            P("dp", "seq"),
            P("dp", "seq"),
        ),
        check_vma=False,
    )
```

```python
import functools

import jax
import jax.numpy as jnp
from jax import lax
from jax.experimental import pallas as pl
from jax.experimental.pallas import tpu as pltpu
from jax.sharding import PartitionSpec as P

CH = 256
DK = 128
DV = 256
KCONV = 4
TILE = 64


HIGHEST = lax.Precision.HIGHEST
epsilon = 1e-06


def passed_along(block, axis, distance):
    devices = range(lax.axis_size(axis))
    route = [(i - distance, i) for i in devices if i - distance in devices]
    return lax.ppermute(block, axis, route)


def rms_scale(values, gain_row):
    return (
        values * lax.rsqrt(jnp.mean(values * values, axis=-1, keepdims=True) + epsilon) * gain_row
    )


def unit_rows(values):
    return values * lax.rsqrt(jnp.sum(values * values, axis=-1, keepdims=True) + epsilon)


def block_step(state_now, query_vecs, key_vecs, value_vecs, log_decay, erase_rate):
    length = query_vecs.shape[1]
    cumulative = jnp.cumsum(log_decay, axis=1)
    row_index = jnp.arange(length)[:, None]
    col_index = jnp.arange(length)[None, :]
    strict = col_index < row_index
    within = col_index <= row_index
    spread = cumulative[:, :, None] - cumulative[:, None, :]
    lower_decay = jnp.where(strict, jnp.exp(jnp.where(strict, spread, 0.0)), 0.0)
    causal = jnp.where(within, jnp.exp(jnp.where(within, spread, 0.0)), 0.0)
    key_gram = jnp.einsum("htk,hsk->hts", key_vecs, key_vecs, precision=HIGHEST)
    query_gram = jnp.einsum("htk,hsk->hts", query_vecs, key_vecs, precision=HIGHEST)
    negated = -(erase_rate[:, :, None] * key_gram * lower_decay)
    identity = jnp.eye(length, dtype=jnp.float32)
    inverse = identity + negated
    powered = negated
    for level_index in range(length.bit_length() - 2):
        powered = jnp.einsum("hts,hsr->htr", powered, powered, precision=HIGHEST)
        inverse = jnp.einsum("hts,hsr->htr", inverse, identity + powered, precision=HIGHEST)
    shrink = jnp.exp(cumulative)
    recalled = jnp.einsum("htk,hkw->htw", key_vecs, state_now, precision=HIGHEST)
    target = erase_rate[:, :, None] * value_vecs - (erase_rate * shrink)[:, :, None] * recalled
    updates = jnp.einsum("hts,hsw->htw", inverse, target, precision=HIGHEST)
    read_out = shrink[:, :, None] * jnp.einsum(
        "htk,hkw->htw", query_vecs, state_now, precision=HIGHEST
    )
    read_out = read_out + jnp.einsum(
        "hts,hsw->htw", query_gram * causal, updates, precision=HIGHEST
    )
    remain = jnp.exp(cumulative[:, -1:] - cumulative)
    state_next = jnp.exp(cumulative[:, -1])[:, None, None] * state_now
    state_next = state_next + jnp.einsum(
        "hsk,hsw->hkw", key_vecs * remain[:, :, None], updates, precision=HIGHEST
    )
    return (state_next, read_out)


def run_tiles(query_vecs, key_vecs, value_vecs, log_decay, erase_rate, state_start):
    row_count, head_count, key_width = query_vecs.shape
    tile_count = row_count // TILE

    def arrange(tensor):
        return jnp.swapaxes(tensor.reshape((tile_count, TILE, head_count) + tensor.shape[2:]), 1, 2)

    inputs = (
        arrange(query_vecs),
        arrange(key_vecs),
        arrange(value_vecs),
        arrange(log_decay),
        arrange(erase_rate),
    )

    def advance(state_now, sliced):
        return jax.checkpoint(block_step)(state_now, *sliced)

    state_end, outputs = lax.scan(advance, state_start, inputs)
    outputs = jnp.swapaxes(outputs, 1, 2).reshape(row_count, head_count, outputs.shape[-1])
    return (outputs, state_end)


def mixer_inputs(conv_in, edge_rows, head_in, conv_taps, head_params):
    block_len = conv_in.shape[1]
    head_count = head_params.shape[1]
    extended = jnp.concatenate([edge_rows, conv_in], axis=1)
    conv_sum = extended[:, 0:block_len] * conv_taps[:, 0]
    for offset in range(1, conv_taps.shape[1]):
        conv_sum = conv_sum + extended[:, offset : offset + block_len] * conv_taps[:, offset]
    activated = jax.nn.silu(conv_sum)
    key_span = head_count * DK
    lead = activated.shape[:2]
    query_vecs = unit_rows(activated[..., 0:key_span].reshape(lead + (head_count, DK))) * DK ** (
        -0.5
    )
    key_vecs = unit_rows(activated[..., key_span : 2 * key_span].reshape(lead + (head_count, DK)))
    value_vecs = activated[..., 2 * key_span :].reshape(lead + (head_count, DV))
    log_decay = -jnp.exp(head_params[0]) * jax.nn.softplus(
        head_in[..., 0:head_count] + head_params[1]
    )
    erase_rate = jax.nn.sigmoid(head_in[..., head_count : 2 * head_count] + head_params[2])
    return (query_vecs, key_vecs, value_vecs, log_decay, erase_rate)


def gated_norm(mixed, gate_in, head_gain):
    shaped = gate_in.reshape(mixed.shape)
    normed = (
        mixed * lax.rsqrt(jnp.mean(mixed * mixed, axis=-1, keepdims=True) + epsilon) * head_gain
    )
    return (normed * jax.nn.silu(shaped)).reshape(gate_in.shape)


def local_tiles(query_vecs, key_vecs, value_vecs, log_decay, erase_rate):
    key_width = key_vecs.shape[-1]
    value_width = value_vecs.shape[-1]
    head_count = key_vecs.shape[2]
    padded = jnp.concatenate(
        [jnp.zeros(value_vecs.shape[:3] + (key_width,), jnp.float32), value_vecs], axis=-1
    )
    start_map = jnp.concatenate(
        [jnp.eye(key_width, dtype=jnp.float32), jnp.zeros((key_width, value_width), jnp.float32)],
        axis=1,
    )
    start_map = jnp.broadcast_to(start_map, (head_count, key_width, key_width + value_width))

    def single(query_one, key_one, value_one, decay_one, erase_one):
        return run_tiles(query_one, key_one, value_one, decay_one, erase_one, start_map)

    return jax.vmap(single)(query_vecs, key_vecs, padded, log_decay, erase_rate)


def post_mix(local_out, incoming, gate_in, head_gain):
    mixed = local_out[..., DK:] + jnp.einsum(
        "snhk,shkv->snhv", local_out[..., 0:DK], incoming, precision=HIGHEST
    )
    return gated_norm(mixed, gate_in, head_gain)


def swiglu(gate_up):
    split_at = gate_up.shape[-1] // 2
    return jax.nn.silu(gate_up[:, 0:split_at]) * gate_up[:, split_at:]


def matmul_maps(left, right):
    return jnp.einsum("shij,shjk->shik", left, right, precision=HIGHEST)


def apply_map(maps, state_now):
    return matmul_maps(maps[0], state_now) + maps[1]


def general_body(
    tokens,
    lengths,
    cotangent,
    norm_gains,
    head_gain,
    head_params,
    qkv_weight,
    gate_weight,
    head_weight,
    conv_weight,
    out_weight,
    ffn_in,
    ffn_out,
):
    seq_count, block_len, model_width = tokens.shape
    row_count = seq_count * block_len
    position = lax.axis_index("seq") * block_len + jnp.arange(block_len, dtype=jnp.int32)
    valid_rows = (position[None, :] < lengths[:, None]).reshape(row_count, 1)
    col_parts = (
        lax.all_gather(qkv_weight, "seq", axis=1, tiled=True),
        lax.all_gather(gate_weight, "seq", axis=1, tiled=True),
        lax.all_gather(out_weight, "seq", axis=1, tiled=True),
        lax.all_gather(ffn_in, "seq", axis=1, tiled=True),
        lax.all_gather(ffn_out, "seq", axis=1, tiled=True),
    )
    gathered = (
        lax.all_gather(col_parts[0], "dp", axis=0, tiled=True),
        lax.all_gather(col_parts[1], "dp", axis=0, tiled=True),
        lax.all_gather(col_parts[2], "dp", axis=0, tiled=True),
        lax.all_gather(col_parts[3], "dp", axis=0, tiled=True),
        lax.all_gather(col_parts[4], "dp", axis=0, tiled=True),
    )
    w_qkv, w_gate, w_out, w_in, w_down = gathered
    inputs = tokens.reshape(row_count, model_width).astype(jnp.float32)
    first_norm = rms_scale(inputs, norm_gains[0]).astype(jnp.bfloat16)
    conv_in = jnp.dot(first_norm, w_qkv, preferred_element_type=jnp.float32).astype(jnp.bfloat16)
    head_in = jnp.dot(first_norm, head_weight, preferred_element_type=jnp.float32)
    gate_in = jnp.dot(first_norm, w_gate, preferred_element_type=jnp.float32)
    conv_width = conv_in.shape[-1]
    conv_rows = conv_in.reshape(seq_count, block_len, conv_width)
    edge_cut = block_len - (KCONV - 1)
    edge_rows = passed_along(conv_rows[:, edge_cut:], "seq", 1)
    mix_args = (
        conv_rows.astype(jnp.float32),
        edge_rows.astype(jnp.float32),
        head_in.reshape(seq_count, block_len, -1),
        conv_weight.astype(jnp.float32),
        head_params,
    )
    vectors = mixer_inputs(*mix_args)
    local_out, end_states = local_tiles(*vectors)
    carry_maps = (end_states[..., 0:DK], end_states[..., DK:])

    def relay_state(step_index, state_now):
        return passed_along(apply_map(carry_maps, state_now), "seq", 1)

    incoming = lax.fori_loop(
        0, lax.axis_size("seq") - 1, relay_state, jnp.zeros_like(carry_maps[1])
    )
    post_args = (local_out, incoming, gate_in, head_gain)
    normed = post_mix(*post_args).astype(jnp.bfloat16)
    attended = jnp.dot(normed, w_out, preferred_element_type=jnp.float32)
    middle = inputs + attended
    second_norm = rms_scale(middle, norm_gains[1]).astype(jnp.bfloat16)
    gate_up = jnp.dot(second_norm, w_in, preferred_element_type=jnp.float32)
    hidden = swiglu(gate_up).astype(jnp.bfloat16)
    carried = jnp.dot(hidden, w_down, preferred_element_type=jnp.float32)
    output = jnp.where(valid_rows, middle + carried, 0.0).astype(jnp.bfloat16)
    col_again = (
        lax.all_gather(qkv_weight, "seq", axis=1, tiled=True),
        lax.all_gather(gate_weight, "seq", axis=1, tiled=True),
        lax.all_gather(out_weight, "seq", axis=1, tiled=True),
        lax.all_gather(ffn_in, "seq", axis=1, tiled=True),
        lax.all_gather(ffn_out, "seq", axis=1, tiled=True),
    )
    regathered = (
        lax.all_gather(col_again[0], "dp", axis=0, tiled=True),
        lax.all_gather(col_again[1], "dp", axis=0, tiled=True),
        lax.all_gather(col_again[2], "dp", axis=0, tiled=True),
        lax.all_gather(col_again[3], "dp", axis=0, tiled=True),
        lax.all_gather(col_again[4], "dp", axis=0, tiled=True),
    )
    w_qkv, w_gate, w_out, w_in, w_down = regathered
    upstream = jnp.where(
        valid_rows, cotangent.reshape(row_count, model_width).astype(jnp.float32), 0.0
    )
    carried_grad = upstream.astype(jnp.bfloat16)
    grad_down = jnp.einsum("nf,nd->fd", hidden, carried_grad, preferred_element_type=jnp.float32)
    hidden_grad = jnp.einsum("nd,fd->nf", carried_grad, w_down, preferred_element_type=jnp.float32)
    unused, swiglu_back = jax.vjp(swiglu, gate_up)
    gate_up_grad = swiglu_back(hidden_grad)[0].astype(jnp.bfloat16)
    grad_in = jnp.einsum("nd,nf->df", second_norm, gate_up_grad, preferred_element_type=jnp.float32)
    second_grad = jnp.einsum("nf,df->nd", gate_up_grad, w_in, preferred_element_type=jnp.float32)
    unused, second_back = jax.vjp(rms_scale, middle, norm_gains[1])
    middle_back, gain_two = second_back(second_grad)
    middle_grad = upstream + middle_back
    attended_grad = middle_grad.astype(jnp.bfloat16)
    grad_out = jnp.einsum("nv,nd->vd", normed, attended_grad, preferred_element_type=jnp.float32)
    normed_grad = jnp.einsum("nd,vd->nv", attended_grad, w_out, preferred_element_type=jnp.float32)
    unused, post_back = jax.vjp(post_mix, *post_args)
    local_grad, incoming_local, gate_in_grad, head_gain_grad = post_back(normed_grad)
    flipped = (jnp.swapaxes(carry_maps[0], -1, -2), incoming_local)

    def relay_grad(step_index, grad_now):
        return passed_along(apply_map(flipped, grad_now).astype(jnp.bfloat16), "seq", -1).astype(
            jnp.float32
        )

    outgoing = lax.fori_loop(
        0, lax.axis_size("seq") - 1, relay_grad, jnp.zeros_like(incoming_local)
    )
    map_grad = jnp.einsum("shkv,shjv->shkj", outgoing, incoming, precision=HIGHEST)
    end_grad = jnp.concatenate([map_grad, outgoing], axis=-1)
    unused, tiles_back = jax.vjp(local_tiles, *vectors)
    vector_grads = tiles_back((local_grad, end_grad))
    unused, mix_back = jax.vjp(mixer_inputs, *mix_args)
    conv_own, edge_grad, head_in_grad, conv_taps_grad, params_grad = mix_back(vector_grads)
    edge_back = passed_along(edge_grad.astype(jnp.bfloat16), "seq", -1).astype(edge_grad.dtype)
    conv_total = jnp.concatenate(
        [conv_own[:, 0:edge_cut], conv_own[:, edge_cut:] + edge_back], axis=1
    )
    conv_grad = conv_total.reshape(row_count, conv_width).astype(jnp.bfloat16)
    head_grad = head_in_grad.reshape(row_count, -1).astype(jnp.bfloat16)
    gate_grad = gate_in_grad.astype(jnp.bfloat16)
    grad_qkv = jnp.einsum("nd,nc->dc", first_norm, conv_grad, preferred_element_type=jnp.float32)
    grad_head = jnp.einsum("nd,nc->dc", first_norm, head_grad, preferred_element_type=jnp.float32)
    grad_gate = jnp.einsum("nd,nc->dc", first_norm, gate_grad, preferred_element_type=jnp.float32)
    first_grad = jnp.einsum("nc,dc->nd", conv_grad, w_qkv, preferred_element_type=jnp.float32)
    first_grad = first_grad + jnp.einsum(
        "nc,dc->nd", head_grad, head_weight, preferred_element_type=jnp.float32
    )
    first_grad = first_grad + jnp.einsum(
        "nc,dc->nd", gate_grad, w_gate, preferred_element_type=jnp.float32
    )
    unused, first_back = jax.vjp(rms_scale, inputs, norm_gains[0])
    input_back, gain_one = first_back(first_grad)
    input_grad = (
        (middle_grad + input_back).astype(jnp.bfloat16).reshape(seq_count, block_len, model_width)
    )
    row_groups = (
        lax.psum_scatter(
            grad_qkv.astype(jnp.bfloat16), "dp", scatter_dimension=0, tiled=True
        ).astype(jnp.float32),
        lax.psum_scatter(
            grad_gate.astype(jnp.bfloat16), "dp", scatter_dimension=0, tiled=True
        ).astype(jnp.float32),
        lax.psum_scatter(
            grad_out.astype(jnp.bfloat16), "dp", scatter_dimension=0, tiled=True
        ).astype(jnp.float32),
        lax.psum_scatter(
            grad_in.astype(jnp.bfloat16), "dp", scatter_dimension=0, tiled=True
        ).astype(jnp.float32),
        lax.psum_scatter(
            grad_down.astype(jnp.bfloat16), "dp", scatter_dimension=0, tiled=True
        ).astype(jnp.float32),
    )
    weight_parts = (
        lax.psum_scatter(
            row_groups[0].astype(jnp.bfloat16), "seq", scatter_dimension=1, tiled=True
        ).astype(jnp.float32),
        lax.psum_scatter(
            row_groups[1].astype(jnp.bfloat16), "seq", scatter_dimension=1, tiled=True
        ).astype(jnp.float32),
        lax.psum_scatter(
            row_groups[2].astype(jnp.bfloat16), "seq", scatter_dimension=1, tiled=True
        ).astype(jnp.float32),
        lax.psum_scatter(
            row_groups[3].astype(jnp.bfloat16), "seq", scatter_dimension=1, tiled=True
        ).astype(jnp.float32),
        lax.psum_scatter(
            row_groups[4].astype(jnp.bfloat16), "seq", scatter_dimension=1, tiled=True
        ).astype(jnp.float32),
    )
    small_sums = lax.psum(
        (jnp.stack([gain_one, gain_two]), head_gain_grad, params_grad, grad_head, conv_taps_grad),
        ("dp", "seq"),
    )
    output = output.reshape(seq_count, block_len, model_width)
    return (
        output,
        input_grad,
        small_sums[0],
        small_sums[1],
        small_sums[2],
        weight_parts[0],
        weight_parts[1],
        small_sums[3],
        small_sums[4],
        weight_parts[2],
        weight_parts[3],
        weight_parts[4],
    )


MESH = pl.DeviceIdType.MESH
ANY = pl.BlockSpec(memory_space=pl.ANY)
IN_VMEM = pl.BlockSpec(memory_space=pltpu.VMEM)
B16 = jnp.bfloat16
F32 = jnp.float32
NN = ((1,), (0,))
NT = ((1,), (1,))
TN = ((0,), (0,))
HALO = 16


def low(v):
    return v.astype(jnp.bfloat16)


def mm(a, b, dims=NN):
    return lax.dot_general(low(a), low(b), (dims, ((), ())), preferred_element_type=jnp.float32)


def mmf(a, b, dims=NN):
    return lax.dot_general(
        a, b, (dims, ((), ())), precision=HIGHEST, preferred_element_type=jnp.float32
    )


def mm3(a, b, dims=NN):
    ah, bh = low(a), low(b)
    al, bl = low(a - ah.astype(jnp.float32)), low(b - bh.astype(jnp.float32))
    return mm(ah, bh, dims) + (mm(ah, bl, dims) + mm(al, bh, dims))


def sig(v):
    return 1.0 / (1.0 + jnp.exp(-v))


def soft_plus(v):
    tail = jnp.exp(-jnp.abs(v))
    series = tail * (1.0 - tail * (0.5 - tail * (1.0 / 3.0)))
    return jnp.maximum(v, 0.0) + jnp.where(tail < 1e-3, series, jnp.log(1.0 + tail))


def grid_masks():
    row = lax.broadcasted_iota(jnp.int32, (CH, CH), 0)
    col = lax.broadcasted_iota(jnp.int32, (CH, CH), 1)
    return row, col


def decay_parts(g, row, col):
    lower = (col <= row).astype(jnp.float32)
    cum = mmf(lower, g)
    cum_row = mmf(g, lower, ((0,), (1,)))
    within = col <= row
    decay = jnp.where(within, jnp.exp(jnp.where(within, cum - cum_row, 0.0)), 0.0)
    return cum, decay


def unit_inverse(attns, row, col):
    def same(width):
        return (row // width) == (col // width)

    eye = jnp.where(row == col, 1.0, 0.0)
    power = [jnp.where(same(64), -a, 0.0) for a in attns]
    inv = [eye + p for p in power]
    for level in range(5):
        power = [mm(p, p) for p in power]
        inv = [x + mm(x, p) for x, p in zip(inv, power)]
    for width in (128, 256):
        off = same(width) & jnp.logical_not(same(width // 2))
        part = [mm(jnp.where(off, a, 0.0), x) for a, x in zip(attns, inv)]
        inv = [x - mm(x, p) for x, p in zip(inv, part)]
    rest = [eye - x - mm3(a, x) for a, x in zip(attns, inv)]
    return [x + mm(x, r) for x, r in zip(inv, rest)]


def odd(t):
    return t % 2 if isinstance(t, int) else lax.rem(t, 2)


def tile(t, size=CH):
    return pl.ds(pl.multiple_of(t * size, size), size)


class Wires:
    def __init__(self, dp, seq, sems):
        self.dp, self.seq, self.sems, self.used = dp, seq, sems, 0
        self.i, self.s = lax.axis_index("dp"), lax.axis_index("seq")
        self.z, self.c = self.s // 2, lax.rem(self.s, 2)
        self.half, self.partner = self.z // 2, self.z + 1 - 2 * lax.rem(self.z, 2)
        self.inner = lax.rem((self.z + 1) // 2, 2)
        self.place = lax.rem(self.z, 2)
        self.beside = (self.i + 1 - 2 * lax.rem(self.i, 2), lax.rem(self.i + 2, 4))

    def take(self, count=1):
        start = self.used
        self.used += count
        return start

    def meet_all(self):
        barrier = pltpu.get_barrier_semaphore()
        for di in range(self.dp):
            for dj in range(self.seq):
                if di or dj:
                    pl.semaphore_signal(
                        barrier,
                        inc=1,
                        device_id=(lax.rem(self.i + di, self.dp), lax.rem(self.s + dj, self.seq)),
                        device_id_type=MESH,
                    )
        pl.semaphore_wait(barrier, self.dp * self.seq - 1)

    def remote(self, src, dst, send, recv, di, dj):
        return pltpu.make_async_remote_copy(
            src_ref=src,
            dst_ref=dst,
            send_sem=self.sems.at[send],
            recv_sem=self.sems.at[recv],
            device_id=(di, dj),
            device_id_type=MESH,
        )

    def local(self, src, dst, sem):
        return pltpu.make_async_copy(src, dst, self.sems.at[sem])

    def push(self, src, dst, send, recv, di, dj):
        here = (di == self.i) & (dj == self.s)
        away = self.remote(src, dst, send, recv, di, dj)

        @pl.when(here)
        def _():
            self.local(src, dst, recv).start()

        @pl.when(jnp.logical_not(here))
        def _():
            away.start()

        def sent():
            @pl.when(jnp.logical_not(here))
            def _():
                away.wait_send()

        return sent

    def arrived(self, dst, recv):
        pltpu.make_async_copy(dst, dst, self.sems.at[recv]).wait()

    def chip(self, z):
        return z * 2 + self.c

    def order(self, n):
        near = self.z + n * (1 - 2 * lax.rem(self.z, 2))
        return (1 - n // 2) * near + (n // 2) * (n + self.half * (3 - 2 * n))

    def sibling(self):
        return self.z * 2 + 1 - self.c


class LineGather:
    parts = 2

    def __init__(self, w, block_of):
        self.w, self.block_of = w, block_of
        n = 4 * self.parts
        self.send, self.recv = w.take(n), w.take(n)
        self.fsend, self.frecv = w.take(n), w.take(n)

    def piece(self, block, part):
        size = block.shape[0] // self.parts
        return block.at[part * size : part * size + size, :]

    def start(self, src):
        w = self.w
        dst = self.block_of(w.s)
        for part in range(self.parts):
            a, b = self.piece(src, part), self.piece(dst, part)
            slot = w.z * self.parts + part
            near, far = self.send + part, self.send + self.parts + part
            w.remote(a, b, near, self.recv + slot, w.i, w.chip(w.partner)).start()
            w.remote(a, b, far, self.recv + slot, w.i, w.chip(2 - w.half)).start()
        for part in range(self.parts):
            a, b = self.piece(src, part), self.piece(dst, part)
            slot = w.z * self.parts + part
            w.remote(a, b, self.fsend + slot, self.frecv + slot, w.i, w.sibling()).start()

    def arrive(self, t):
        w = self.w

        @pl.when(t != w.z)
        def _():
            block = self.block_of(w.chip(t))
            for part in range(self.parts):
                ref, slot = self.piece(block, part), t * self.parts + part
                w.arrived(ref, self.recv + slot)

                @pl.when((w.inner == 1) & (t // 2 != w.half))
                def _():
                    on = self.send + (2 + odd(t)) * self.parts + part
                    w.remote(ref, ref, on, self.recv + slot, w.i, w.chip(w.partner)).start()

                w.remote(ref, ref, self.fsend + slot, self.frecv + slot, w.i, w.sibling()).start()

    def other(self, t):
        w = self.w
        block = self.block_of(t * 2 + 1 - w.c)
        for part in range(self.parts):
            w.arrived(self.piece(block, part), self.frecv + t * self.parts + part)

    def finish(self):
        w = self.w
        block = self.block_of(w.s)
        for part in range(self.parts):
            ref = self.piece(block, part)
            for n in range(4):
                copy = w.remote(ref, ref, self.send + n * self.parts + part, self.recv, w.i, w.sibling())
                if n < 2:
                    copy.wait_send()
                else:
                    @pl.when(w.inner == 1)
                    def _():
                        copy.wait_send()

                w.remote(ref, ref, self.fsend + n * self.parts + part, self.recv, w.i, w.sibling()).wait_send()


class GroupGather:
    def __init__(self, w, part_of):
        self.w, self.part_of = w, part_of
        self.send, self.recv = w.take(4), w.take(4)

    def start(self, src):
        w = self.w
        w.local(src, self.part_of(w.i), self.recv).start()
        for d in (3, 1, 2):
            to = lax.rem(w.i + d, 4)
            w.remote(src, self.part_of(w.i), self.send + d, self.recv + d, to, w.s).start()

    def finish(self):
        w = self.w
        for d in range(4):
            w.arrived(self.part_of(lax.rem(w.i + 4 - d, 4)), self.recv + d)
        for d in range(1, 4):
            part = self.part_of(w.i)
            w.remote(part, part, self.send + d, self.recv + d, lax.rem(w.i + d, 4), w.s).wait_send()


class SquareGather:
    def __init__(self, w, part_of):
        self.w, self.part_of = w, part_of
        self.send, self.recv = w.take(4), w.take(5)

    def half(self, n, k):
        part = self.part_of(n)
        size = part.shape[0] // 2
        return part.at[size * k : size * k + size, :]

    def near(self, src):
        w = self.w
        part = self.part_of(w.i)
        return [w.remote(src, part, self.send + k, self.recv + k, w.beside[k], w.s) for k in range(2)]

    def far(self, k):
        w = self.w
        half = self.half(w.beside[k], k)
        return w.remote(half, half, self.send + 2 + k, self.recv + 2 + k, w.beside[1 - k], w.s)

    def start(self, src):
        w = self.w
        w.local(src, self.part_of(w.i), self.recv + 4).start()
        for copy in self.near(src):
            copy.start()

    def relay(self):
        w = self.w
        for k in range(2):
            w.arrived(self.part_of(w.beside[k]), self.recv + k)
            self.far(k).start()

    def finish(self):
        w = self.w
        w.arrived(self.part_of(w.i), self.recv + 4)
        for k in range(2):
            w.arrived(self.half(3 - w.i, k), self.recv + 2 + k)
        for copy in self.near(self.part_of(w.i)) + [self.far(0), self.far(1)]:
            copy.wait_send()


class LineScatter:
    def __init__(self, w, part, sib, chip, got):
        self.w, self.part, self.sib, self.chip, self.got = w, part, sib, chip, got
        self.ssend, self.srecv = w.take(4), w.take(4)
        self.send, self.recv = w.take(4), w.take(4)

    def swap(self, t):
        w = self.w
        src = self.part.at[pl.ds(pl.multiple_of(t * 256 + 128 * (1 - w.c), 128), 128), :]
        w.remote(src, self.sib.at[t], self.ssend + t, self.srecv + t, w.i, w.sibling()).start()

    def out(self, t, slot, chip):
        w = self.w
        w.remote(self.chip.at[t], self.got.at[slot], self.send + t, self.recv + slot, w.i, w.chip(chip)).start()

    def pass_on(self, t):
        w = self.w
        w.arrived(self.sib.at[t], self.srecv + t)
        mine = self.part[pl.ds(pl.multiple_of(t * 256 + 128 * w.c, 128), 128), :]
        self.chip[t] = low(mine.astype(jnp.float32) + self.sib[t].astype(jnp.float32))

        @pl.when(t == w.partner)
        def _():
            self.out(t, 0, t)

        @pl.when((t // 2 != w.half) & (w.inner == 0))
        def _():
            self.out(t, 2 + odd(t), w.partner)

    def relay(self, t):
        w = self.w

        @pl.when((t // 2 != w.half) & (w.inner == 1))
        def _():
            slot = 2 + odd(t)
            w.arrived(self.got.at[slot], self.recv + slot)
            self.chip[t] = low(self.chip[t].astype(jnp.float32) + self.got[slot].astype(jnp.float32))
            self.out(t, 1, t)

    def total(self):
        w = self.w
        total = self.chip[w.z].astype(jnp.float32)
        for slot in range(2):
            w.arrived(self.got.at[slot], self.recv + slot)
            total = total + self.got[slot].astype(jnp.float32)
        return total

    def finish(self):
        w = self.w
        for t in range(4):
            src = self.part.at[pl.ds(t * 256, 128), :]
            w.remote(src, self.sib.at[t], self.ssend + t, self.srecv + t, w.i, w.sibling()).wait_send()

            @pl.when(w.z != t)
            def _():
                w.remote(self.chip.at[t], self.got.at[0], self.send + t, self.recv, w.i, w.sibling()).wait_send()


class PairGather:
    def __init__(self, w, buffer):
        self.w, self.buffer = w, buffer
        self.send, self.recv = w.take(3), w.take(3)

    def block(self, q, c):
        return rows_of(self.buffer, 256 * q + 128 * c, 128)

    def copies(self):
        w = self.w
        mine, theirs = self.block(w.place, w.c), self.block(1 - w.place, w.c)
        send, recv = self.send, self.recv
        return (
            w.remote(mine, mine, send, recv, w.i, w.chip(w.partner)),
            w.remote(mine, mine, send + 1, recv + 1, w.i, w.sibling()),
            w.remote(theirs, theirs, send + 2, recv + 2, w.i, w.sibling()),
        )

    def start(self):
        near, core, unused = self.copies()
        near.start()
        core.start()

    def arrive(self):
        w = self.w
        w.arrived(self.block(1 - w.place, w.c), self.recv)
        self.copies()[2].start()

    def other(self, n):
        w = self.w
        q = w.place + n * (1 - 2 * w.place)
        w.arrived(self.block(q, 1 - w.c), self.recv + 1 + n)

    def finish(self):
        for copy in self.copies():
            copy.wait_send()


class PairScatter:
    def __init__(self, w, part, sib, chip, got):
        self.w, self.part, self.sib, self.chip, self.got = w, part, sib, chip, got
        self.ssend, self.srecv = w.take(2), w.take(2)
        self.send, self.recv = w.take(), w.take()

    def swapped(self, q):
        w = self.w
        src = rows_of(self.part, 256 * q + 128 * (1 - w.c), 128)
        return w.remote(src, self.sib.at[q], self.ssend + q, self.srecv + q, w.i, w.sibling())

    def away(self):
        w = self.w
        return w.remote(self.chip.at[1 - w.place], self.got, self.send, self.recv, w.i, w.chip(w.partner))

    def add(self, q):
        w = self.w
        w.arrived(self.sib.at[q], self.srecv + q)
        mine = rows_of(self.part, 256 * q + 128 * w.c, 128)[...]
        self.chip[q] = low(mine.astype(jnp.float32) + self.sib[q].astype(jnp.float32))

    def total(self):
        self.w.arrived(self.got, self.recv)
        return self.chip[self.w.place].astype(jnp.float32) + self.got[...].astype(jnp.float32)

    def finish(self):
        self.swapped(0).wait_send()
        self.swapped(1).wait_send()
        self.away().wait_send()


def cols(ref, start, size):
    return ref.at[:, pl.ds(pl.multiple_of(start, 128), size)]


def rows_of(ref, start, size):
    return ref.at[pl.ds(pl.multiple_of(start, 128), size), :]


class Box:
    pass


def fields(kind):
    return [(name, *value) for name, value in vars(kind).items() if name[0] != "_"]


class FrontKept:
    fn = ((1024, 1024), B16)
    ci = ((HALO + 1024, 512), B16)
    gi = ((1024, 256), F32)
    q = ((1024, 128), F32)
    k = ((1024, 128), F32)
    v = ((1024, 256), F32)
    ge = ((1024, 128), F32)
    mixed = ((1024, 256), F32)
    states = ((4, 128, 256), F32)
    tinv = ((1024, 256), B16)
    u = ((1024, 256), F32)
    wm = ((1024, 128), B16)
    normed = ((1024, 256), B16)
    middle = ((128, 1024), F32)
    sn = ((512, 1024), B16)
    cg = ((512, 1024), B16)
    w_qkv = ((1024, 512), B16)
    w_gate = ((1024, 256), B16)
    w_in = ((1536, 1024), B16)
    w_out = ((256, 1024), B16)
    w_down = ((768, 1024), B16)
class FrontScratch:
    x = ((1024, 1024), B16)
    qkv_p = ((256, 512), B16)
    in_p = ((704, 256), B16)
    out_p = ((256, 256), B16)
    down_p = ((704, 256), B16)
    taps32 = ((8, 4096), F32)
    own_cot = ((128, 1024), B16)
    qk = ((1024, 256), B16)
    cum = ((1024, 1), F32)
    part = ((1024, 1024), B16)
    sib = ((4, 128, 1024), B16)
    chip = ((4, 128, 1024), B16)
    got = ((4, 128, 1024), B16)


def start_weights(w, b):
    i, s = w.i, w.s
    qs, qr = w.take(4), w.take(3)
    lowhalf = s < 4
    b.qr = qr

    @pl.when(lowhalf)
    def _():
        for t in range(4):
            w.push(
                b.qkv.at[:, 128 * t : 128 * t + 128],
                cols(b.qkv_p, 128 * (s // 2), 128),
                qs + t,
                qr + s // 2,
                i,
                4 * lax.rem(s, 2) + t,
            )

    @pl.when(jnp.logical_not(lowhalf))
    def _():
        for t in range(2):
            w.push(b.qkv.at[:, 256 * t : 256 * t + 256], b.qkv_p.at[:, 256:512], qs + t, qr + 2, i, 2 * (s - 4) + t)

    def sent():
        @pl.when(lowhalf)
        def _():
            for t in range(4):
                @pl.when(4 * lax.rem(s, 2) + t != s)
                def _():
                    src = b.qkv.at[:, 128 * t : 128 * t + 128]
                    w.remote(src, b.qkv_p.at[:, 0:128], qs + t, qr, i, w.sibling()).wait_send()

        @pl.when(jnp.logical_not(lowhalf))
        def _():
            for t in range(2):
                @pl.when(2 * (s - 4) + t != s)
                def _():
                    src = b.qkv.at[:, 256 * t : 256 * t + 256]
                    w.remote(src, b.qkv_p.at[:, 256:512], qs + t, qr + 2, i, w.sibling()).wait_send()

    return sent


def start_out_weights(w, b):
    send, recv = w.take(2), w.take(2)
    odd = lax.rem(w.s, 2)
    waits = []
    for n in range(2):
        src = b.out.at[256 * n : 256 * n + 256, :]
        waits.append(w.push(src, cols(b.out_p, 128 * odd, 128), send + n, recv + odd, w.s // 2, 2 * w.i + n))

    def landed():
        for r in range(2):
            w.arrived(b.out_p.at[:, 128 * r : 128 * r + 128], recv + r)

    def sent():
        for wait in waits:
            wait()

    return landed, sent


def start_ffn_weights(w, b):
    i, s = w.i, w.s
    send, recv = w.take(3), w.take(3)
    own = lax.rem(s, 2)
    across = w.remote(b.ffn_in, b.in_p, send, recv, i, lax.rem(s + 4, 8))
    across.start()
    waits = [across.wait_send]
    for n in range(2):
        dst = cols(b.down_p, 128 * own, 128)
        waits.append(w.push(b.ffn_out, dst, send + 1 + n, recv + 1 + own, s // 2, i + 4 * n))

    def landed():
        w.arrived(b.in_p, recv)
        for r in range(2):
            w.arrived(b.down_p.at[:, 128 * r : 128 * r + 128], recv + 1 + r)

    def sent():
        for wait in waits:
            wait()

    return landed, sent


def valid_rows(b, w):
    place = w.s * 128 + lax.broadcasted_iota(jnp.int32, (128, 1), 0)
    return place < b.lengths[0]


def first_norm_tile(b, t):
    rows = tile(t)
    x = b.x[rows, :].astype(jnp.float32)
    inv = lax.rsqrt(jnp.mean(x * x, axis=-1, keepdims=True) + epsilon)
    b.fn[rows, :] = low(x * inv * b.gains[0:1, :])


def own_head(b, w):
    pm = b.params[...]
    lane = lax.broadcasted_iota(jnp.int32, pm.shape, 1)
    return jnp.sum(jnp.where(lane == w.s, pm, 0.0), axis=1, keepdims=True)


def own_taps(b, w, n):
    s = w.s
    return jnp.concatenate(
        [
            b.taps32[n : n + 1, pl.ds(pl.multiple_of(128 * s, 128), 128)],
            b.taps32[n : n + 1, pl.ds(pl.multiple_of(1024 + 128 * s, 128), 128)],
            b.taps32[n : n + 1, pl.ds(pl.multiple_of(2048 + 256 * s, 128), 256)],
        ],
        axis=1,
    )


def conv_sums(b, w, t):
    window = b.ci[pl.ds(pl.multiple_of(t * CH, CH), CH + HALO), :].astype(jnp.float32)
    total = None
    for n in range(KCONV):
        at = HALO - (KCONV - 1) + n
        term = window[at : at + CH] * own_taps(b, w, n)
        total = term if total is None else total + term
    return total


def project_tile(b, w, t):
    rows = tile(t)
    f = b.fn[rows, :]
    b.ci[pl.ds(pl.multiple_of(t * CH + HALO, HALO), CH), :] = low(mm(f, b.w_qkv[...]))
    b.gi[rows, :] = mm(f, b.w_gate[...])
    hi = mm(f, b.head_w[...], NT)
    lane = lax.broadcasted_iota(jnp.int32, hi.shape, 1)
    pm = own_head(b, w)
    shift = jnp.sum(jnp.where(lane == w.s, hi, 0.0), axis=1, keepdims=True) + pm[1:2, :]
    erase = jnp.sum(jnp.where(lane == w.s + 8, hi, 0.0), axis=1, keepdims=True) + pm[2:3, :]
    line = lax.broadcasted_iota(jnp.int32, (CH, 128), 1)
    decay = -jnp.exp(pm[0:1, :]) * soft_plus(shift)
    b.ge[rows, :] = jnp.where(line == 0, decay, jnp.where(line == 1, sig(erase), shift))


def vectors_tile(b, w, t):
    rows = tile(t)
    total = conv_sums(b, w, t)
    act = total * sig(total)
    qa, ka = act[:, 0:DK], act[:, DK : 2 * DK]
    b.q[rows, :] = qa * lax.rsqrt(jnp.sum(qa * qa, axis=-1, keepdims=True) + epsilon) * DK ** (-0.5)
    b.k[rows, :] = ka * lax.rsqrt(jnp.sum(ka * ka, axis=-1, keepdims=True) + epsilon)
    b.v[rows, :] = act[:, 2 * DK :]


def rec_local(b, w, ts):
    row, col = grid_masks()
    attns = []
    for t in ts:
        vectors_tile(b, w, t)
        rows = tile(t)
        k = b.k[rows, :]
        cum, decay = decay_parts(b.ge[rows, 0:1], row, col)
        b.cum[rows, :] = cum
        b.qk[rows, :] = low(mm(b.q[rows, :], k, NT) * decay)
        attns.append(jnp.where(col < row, b.ge[rows, 1:2] * mm(k, k, NT) * decay, 0.0))
    for t, inv in zip(ts, unit_inverse(attns, row, col)):
        rows = tile(t)
        e, t16 = b.ge[rows, 1:2], low(inv)
        b.tinv[rows, :] = t16
        b.wm[rows, :] = low(mm(t16, (e * jnp.exp(b.cum[rows, :])) * b.k[rows, :]))
        b.u[rows, :] = mm(t16, e * b.v[rows, :])


def rec_step(b, t, state):
    rows = tile(t)
    b.states[t] = state
    cum = b.cum[rows, :]
    last = cum[CH - 1 : CH, :]
    s16 = low(state)
    u = b.u[rows, :] - mm(b.wm[rows, :], s16)
    b.u[rows, :] = u
    u16 = low(u)
    mixed = jnp.exp(cum) * mm(b.q[rows, :], s16) + mm(b.qk[rows, :], u16)
    b.mixed[rows, :] = mixed
    nxt = jnp.exp(last) * state + mm(b.k[rows, :] * jnp.exp(last - cum), u16, TN)
    gate = b.gi[rows, :]
    scale = lax.rsqrt(jnp.mean(mixed * mixed, axis=-1, keepdims=True) + epsilon)
    normed = low(mixed * scale * b.head_gain[...] * (gate * sig(gate)))
    b.normed[rows, :] = normed
    b.part[rows, :] = low(mm(normed, b.w_out[...]))
    return nxt


def front_phase(b, w):
    s, i = w.s, w.i
    own_rows = lambda ref: (lambda n: rows_of(ref, 128 * n, 128))
    x_gather = LineGather(w, own_rows(b.x))
    cg_gather = PairGather(w, b.cg)
    sn_gather = PairGather(w, b.sn)
    qkv_gather = GroupGather(w, lambda n: rows_of(b.w_qkv, 256 * n, 256))
    gate_gather = GroupGather(w, lambda n: rows_of(b.w_gate, 256 * n, 256))
    half = s // 4

    def in_block(n, start, size):
        return b.w_in.at[pl.ds(pl.multiple_of(start, 128), size), pl.ds(pl.multiple_of(256 * n, 256), 256)]

    thirds = (256, 256, b.ffn_in.shape[0] - 512)

    def own_third(k):
        return GroupGather(w, lambda n: in_block(n, 768 * half + 256 * k, thirds[k]))

    in_gathers = [own_third(k) for k in range(3)]
    across_gather = SquareGather(w, lambda n: in_block(n, 768 * (1 - half), 704))

    def start_third(k):
        in_gathers[k].start(b.ffn_in.at[256 * k : 256 * k + thirds[k], :])

    out_gather = GroupGather(w, lambda n: cols(b.w_out, 256 * n, 256))
    down_gather = SquareGather(w, lambda n: b.w_down.at[0:704, pl.ds(pl.multiple_of(256 * n, 256), 256)])
    scatter = LineScatter(w, b.part, b.sib, b.chip, b.got)
    own_x, own_c = w.take(), w.take()

    for start in (704, 1472):
        b.w_in[start : start + 64, :] = jnp.zeros((64, 1024), B16)
    b.w_down[704:768, :] = jnp.zeros((64, 1024), B16)
    w.meet_all()
    qkv_sent = start_weights(w, b)
    out_landed, out_sent = start_out_weights(w, b)
    x_gather.start(b.tokens)
    gate_gather.start(b.gate)
    start_third(0)
    keep_x = w.local(b.tokens, rows_of(b.x, 128 * s, 128), own_x)
    keep_x.start()
    b.ci[0:HALO, :] = jnp.zeros((HALO, 512), B16)
    b.taps32[0:KCONV, :] = b.taps[...].astype(jnp.float32)
    cot = jnp.where(valid_rows(b, w), b.cot_v[...].astype(jnp.float32), 0.0)
    b.own_cot[...] = low(cot)
    rows_of(b.cg, 128 * lax.rem(s, 4), 128)[...] = low(cot)
    w.arrived(b.qkv_p.at[:, 0:128], b.qr)
    w.arrived(b.qkv_p.at[:, 128:256], b.qr + 1)
    w.arrived(b.qkv_p.at[:, 256:512], b.qr + 2)
    qkv_gather.start(b.qkv_p)
    out_landed()
    out_gather.start(b.out_p)
    keep_x.wait()

    def norm_loop(n, carry):
        t = w.order(n)
        x_gather.arrive(t)
        x_gather.other(t)
        first_norm_tile(b, t)
        return carry

    lax.fori_loop(0, 4, norm_loop, 0)
    ffn_landed, ffn_sent = start_ffn_weights(w, b)
    cg_gather.start()
    qkv_gather.finish()
    gate_gather.finish()
    start_third(1)
    start_third(2)

    def project_loop(t, carry):
        project_tile(b, w, t)
        return carry

    lax.fori_loop(0, 4, project_loop, 0)
    x_gather.finish()
    out_gather.finish()

    def pair_loop(pair, state):
        rec_local(b, w, (2 * pair, 2 * pair + 1))

        @pl.when(pair == 0)
        def _():
            ffn_landed()
            across_gather.start(b.in_p)
            down_gather.start(b.down_p)

        for k in range(2):
            t = 2 * pair + k
            state = rec_step(b, t, state)
            scatter.swap(t)
        scatter.pass_on(2 * pair)
        scatter.pass_on(2 * pair + 1)
        return state

    lax.fori_loop(0, 2, pair_loop, jnp.zeros((DK, DV), F32))

    scatter.relay(0)
    scatter.relay(1)
    scatter.relay(2)
    scatter.relay(3)
    across_gather.relay()
    down_gather.relay()

    def own_half(which):
        @pl.when(w.half == which)
        def _():
            middle = b.tokens_v[...].astype(jnp.float32) + scatter.total()
            b.middle[...] = middle
            inv = lax.rsqrt(jnp.mean(middle * middle, axis=-1, keepdims=True) + epsilon)
            rows_of(b.sn, 128 * lax.rem(s, 4), 128)[...] = low(middle * inv * b.gains[1:2, :])
            sn_gather.start()

    own_half(0)
    cg_gather.arrive()
    own_half(1)
    for third in in_gathers:
        third.finish()
    across_gather.finish()
    down_gather.finish()
    qkv_sent()
    out_sent()
    ffn_sent()
    scatter.finish()

    def finish():
        cg_gather.finish()
        sn_gather.finish()

    return sn_gather, cg_gather, finish


class SquareScatter:
    def __init__(self, w, out, got, step=None, size=None):
        self.w, self.out, self.got = w, out, got
        self.step = step or out.shape[1] // 2
        self.size = size or self.step
        self.send, self.recv = w.take(6), w.take(6)

    def half(self, ref, n, k):
        return ref.at[n, self.step * k : self.step * k + self.size, :]

    def copy(self, n, k):
        w = self.w
        to = k if n == 2 else n
        slot = 2 * n + k
        return w.remote(
            self.half(self.out, n, k), self.half(self.got, n, k), self.send + slot, self.recv + slot, w.beside[to], w.s
        )

    def start_far(self, piece_of):
        self.out[2] = low(piece_of(3 - self.w.i))
        self.copy(2, 0).start()
        self.copy(2, 1).start()

    def start_near(self, piece_of):
        for n in range(2):
            self.out[n] = low(piece_of(self.w.beside[n]))
            self.copy(n, n).start()

    def relay(self):
        w = self.w
        for k in range(2):
            half = self.half(self.out, 1 - k, k)
            w.arrived(self.half(self.got, 2, k), self.recv + 4 + k)
            half[...] = low(half[...].astype(jnp.float32) + self.half(self.got, 2, k)[...].astype(jnp.float32))
            self.copy(1 - k, k).start()

    def total(self, own, dst):
        w = self.w
        for k in range(2):
            start = self.step * k
            total = own[start : start + self.size]
            for n in range(2):
                half = self.half(self.got, n, k)
                w.arrived(half, self.recv + 2 * n + k)
                total = total + half[...].astype(jnp.float32)
            dst[start : start + self.size, :] = low(total)

    def finish(self):
        for n in range(3):
            for k in range(2):
                self.copy(n, k).wait_send()


def ffn_tile(b, t):
    rows = tile(t)
    sn, cg = b.sn[rows, :], b.cg[rows, :]
    half = b.w_in.shape[0] // 2
    both = mm(sn, b.w_in[...], NT)
    gate, up = both[:, 0:half], both[:, half:]
    open_ = sig(gate)
    act = gate * open_
    hidden = low(act * up)
    b.hid[rows, :] = hidden
    b.part4[rows, :] = low(mm(hidden, b.w_down[...]))
    hgrad = mm(cg, b.w_down[...], NT)
    both_grad = jnp.concatenate(
        [low(hgrad * up * (open_ * (1.0 + gate * (1.0 - open_)))), low(hgrad * act)], axis=1
    )
    b.gug[rows, :] = both_grad
    b.part[rows, :] = low(mm(both_grad, b.w_in[...]))


def norm_back(x, gain, grad):
    inv = lax.rsqrt(jnp.mean(x * x, axis=-1, keepdims=True) + epsilon)
    unit = x * inv
    dunit = grad * gain
    return inv * (dunit - unit * jnp.mean(dunit * unit, axis=-1, keepdims=True)), grad * unit


def mixer_out_back(b, t, head_gain_sum):
    rows = tile(t)
    ng = mm(b.agr[rows, :], b.w_out[...], NT)
    gate = b.gi[rows, :]
    open_ = sig(gate)
    act = gate * open_
    gain = b.head_gain[...]
    mixed = b.mixed[rows, :]
    inv = lax.rsqrt(jnp.mean(mixed * mixed, axis=-1, keepdims=True) + epsilon)
    unit = mixed * inv
    dunit = ng * act * gain
    b.do[rows, :] = inv * (dunit - unit * jnp.mean(dunit * unit, axis=-1, keepdims=True))
    nu = ng * unit
    b.gg[rows, :] = low(nu * gain * (open_ * (1.0 + gate * (1.0 - open_))))
    return head_gain_sum + jnp.sum(nu * act, axis=0, keepdims=True)


def rec_back_chain(b, t, ds1, row, col):
    rows = tile(t)
    do = low(b.do[rows, :])
    b.dstates[t] = ds1
    cum = b.cum[rows, :]
    last = cum[CH - 1 : CH, :]
    du = mm(b.qk[rows, :], do, TN) + mm(b.k[rows, :] * jnp.exp(last - cum), ds1)
    du16 = low(du)
    b.dr[rows, :] = mm(b.tinv[rows, :], du16, TN)
    return jnp.exp(last) * ds1 + mm(b.q[rows, :] * jnp.exp(cum), do, TN) - mm(b.wm[rows, :], du16, TN)


def rec_back_tile(b, t, row, col):
    rows = tile(t)
    q, k, v, e = b.q[rows, :], b.k[rows, :], b.v[rows, :], b.ge[rows, 1:2]
    s0, ds1, u, do, dr = b.states[t], b.dstates[t], b.u[rows, :], b.do[rows, :], b.dr[rows, :]
    cum, decay = decay_parts(b.ge[rows, 0:1], row, col)
    last = cum[CH - 1 : CH, :]
    gamma, shrink, remain = jnp.exp(last), jnp.exp(cum), jnp.exp(last - cum)
    gram = jnp.where(col < row, mm(k, k, NT) * decay, 0.0)
    qk = mm(q, k, NT) * decay
    dp = jnp.where(col <= row, mm3(do, u, NT), 0.0)
    da = jnp.where(col < row, -mm3(dr, u, NT), 0.0)
    dqk = low(dp * decay)
    dag = da * gram
    zed = dp * qk + e * dag
    dgram = low(e * da * decay)
    nk = mm3(dr, s0, NT)
    m = mm3(do, s0, NT)
    lm = mm3(u, ds1, NT)
    row_nk = jnp.sum(nk * k, axis=1, keepdims=True)
    dv = e * dr
    de = (
        jnp.sum(dr * v, axis=1, keepdims=True)
        - shrink * row_nk
        + jnp.sum(dag, axis=1, keepdims=True)
    )
    dq = mm(dqk, k) + shrink * m
    dk = mm(dqk, q, TN) + mm(dgram, k) + mm(dgram, k, TN) - (e * shrink) * nk + remain * lm
    dshrink = jnp.sum(m * q, axis=1, keepdims=True) - e * row_nk
    rdr = remain * jnp.sum(lm * k, axis=1, keepdims=True)
    ones = jnp.ones((CH, 1), jnp.float32)
    dcum = jnp.sum(zed, axis=1, keepdims=True) - mmf(zed, ones, TN) + shrink * dshrink - rdr
    dlast = jnp.sum(rdr, axis=0, keepdims=True) + gamma * jnp.sum(
        jnp.sum(s0 * ds1, axis=1, keepdims=True), axis=0, keepdims=True
    )
    lower = (col <= row).astype(jnp.float32)
    dg = mmf(lower, dcum, TN) + dlast
    return dq, dk, dv, dg, de


def unit_back(x, grad):
    inv = lax.rsqrt(jnp.sum(x * x, axis=-1, keepdims=True) + epsilon)
    unit = x * inv
    return inv * (grad - unit * jnp.sum(grad * unit, axis=-1, keepdims=True))


def mixer_back_tile(b, w, t, row, col, sums):
    rows = tile(t)
    dq, dk, dv, dg, de = rec_back_tile(b, t, row, col)
    total = conv_sums(b, w, t)
    open_ = sig(total)
    act = total * open_
    dact = jnp.concatenate(
        [unit_back(act[:, 0:DK], dq * DK ** (-0.5)), unit_back(act[:, DK : 2 * DK], dk), dv], axis=1
    )
    dcs = dact * (open_ * (1.0 + total * (1.0 - open_)))
    b.dcs[0:CH, :] = dcs
    window = b.ci[pl.ds(pl.multiple_of(t * CH, CH), CH + HALO), :].astype(jnp.float32)
    ahead = b.dcs[...]
    taps_sums, p0, p1, p2, gain_sum = sums
    dci = None
    new_taps = []
    for n in range(KCONV):
        at = HALO - (KCONV - 1) + n
        new_taps.append(taps_sums[n] + jnp.sum(dcs * window[at : at + CH], axis=0, keepdims=True))
        back = KCONV - 1 - n
        term = ahead[back : back + CH] * own_taps(b, w, n)
        dci = term if dci is None else dci + term
    b.dcs[CH : CH + HALO, :] = dcs[0:HALO]
    dci16 = low(dci)
    b.cgd[rows, :] = dci16
    lane = lax.broadcasted_iota(jnp.int32, (CH, 16), 1)
    pm = own_head(b, w)
    shift = b.ge[rows, 2:3]
    dshift = dg * (-jnp.exp(pm[0:1, :])) * sig(shift)
    e = b.ge[rows, 1:2]
    dlogit = de * e * (1.0 - e)
    hg = low(jnp.where(lane == w.s, dshift, jnp.where(lane == w.s + 8, dlogit, 0.0)))
    b.hg[rows, :] = hg
    fp = mm(dci16, b.w_qkv[...], NT) + mm(hg, b.head_w[...]) + mm(b.gg[rows, :], b.w_gate[...], NT)
    b.part[rows, :] = low(fp)
    gain_part = jnp.sum(fp * b.fn[rows, :].astype(jnp.float32), axis=0, keepdims=True)
    return (
        tuple(new_taps),
        p0 + jnp.sum(dg * b.ge[rows, 0:1], axis=0, keepdims=True),
        p1 + jnp.sum(dshift, axis=0, keepdims=True),
        p2 + jnp.sum(dlogit, axis=0, keepdims=True),
        gain_sum + gain_part,
    )


class LayerOut:
    output = ((128, 1024), B16)
    input_grad = ((128, 1024), B16)
    gains_grad = ((2, 1024), F32)
    head_gain_grad = ((1, 256), F32)
    params_grad = ((8, 128), F32)
    head_w_grad = ((16, 1024), F32)
    conv_grad = ((4, 4096), F32)
    qkv_back = ((256, 512), B16)
    gate_back = ((256, 256), B16)
    in_back = ((704, 256), B16)
    out_back = ((512, 128), B16)
    down_back = ((704, 128), B16)
class RestScratch:
    hid = ((512, 768), B16)
    gug = ((512, 1536), B16)
    part4 = ((512, 1024), B16)
    sib4 = ((2, 128, 1024), B16)
    chip4 = ((2, 128, 1024), B16)
    got4 = ((128, 1024), B16)
    sib6 = ((2, 128, 1024), B16)
    chip6 = ((2, 128, 1024), B16)
    got6 = ((128, 1024), B16)
    own_ag = ((128, 1024), B16)
    mgrad = ((128, 1024), F32)
    gg = ((1024, 256), B16)
    dstates = ((4, 128, 256), F32)
    dcs = ((CH + HALO, 512), F32)
    cgd = ((1024, 512), B16)
    hg = ((1024, 16), B16)
    in_out = ((3, 1536, 256), B16)
    in_got = ((3, 1536, 256), B16)
    down_out = ((3, 704, 256), B16)
    down_got = ((3, 704, 256), B16)
    out_out = ((3, 256, 256), B16)
    out_got = ((3, 256, 256), B16)
    qkv_out = ((3, 256, 512), B16)
    qkv_got = ((3, 256, 512), B16)
    gate_out = ((3, 256, 256), B16)
    gate_got = ((3, 256, 256), B16)
    in_sum = ((1536, 256), B16)
    in_other = ((704, 256), B16)
    down_sum = ((704, 256), B16)
    down_parts = ((2, 704, 128), B16)
    out_sum = ((256, 256), B16)
    qkv_sum = ((256, 512), B16)
    small = ((8, 1024), F32)
    small_got = ((4, 8, 1024), F32)
    small_sum = ((8, 1024), F32)
    small_all = ((8, 8, 1024), F32)


def grads_home(w, b):
    i, h = w.i, w.s
    send, recv = w.take(9), w.take(10)
    quarter, pair, half = lax.rem(h, 4), lax.rem(h, 2), h // 4

    def across():
        block = rows_of(b.in_sum, 768 * (1 - half), 704)
        return w.remote(block, b.in_other, send, recv + 4, i, lax.rem(h + 4, 8))

    down_to = [(b.down_sum.at[:, 128 * r : 128 * r + 128], quarter, 2 * i + r) for r in range(2)]

    def ffn():
        across().start()
        for r, (src, di, dj) in enumerate(down_to):
            w.push(src, b.down_parts.at[half], send + 2 + r, recv + 8 + half, di, dj)

    def ffn_done():
        across().wait_send()
        for r, (src, di, dj) in enumerate(down_to):
            @pl.when((di != i) | (dj != h))
            def _():
                w.remote(src, src, send + 2 + r, recv, i, w.sibling()).wait_send()

        w.arrived(b.in_other, recv + 4)
        mine = rows_of(b.in_sum, 768 * half, 704)[...]
        b.in_back[...] = low(mine.astype(jnp.float32) + b.in_other[...].astype(jnp.float32))
        for r in range(2):
            w.arrived(b.down_parts.at[r], recv + 8 + r)
        b.down_back[...] = low(b.down_parts[0].astype(jnp.float32) + b.down_parts[1].astype(jnp.float32))

    def mixer():
        to = (
            (b.qkv_sum.at[:, 0:128], cols(b.qkv_back, 128 * quarter, 128), recv + quarter, half),
            (b.qkv_sum.at[:, 128:256], cols(b.qkv_back, 128 * quarter, 128), recv + quarter, 2 + half),
            (b.qkv_sum.at[:, 256:512], cols(b.qkv_back, 256 * pair, 256), recv + pair, 4 + h // 2),
        )
        return [w.push(src, dst, send + 4 + n, sem, i, dj) for n, (src, dst, sem, dj) in enumerate(to)]

    def mixer_out():
        waits = []
        for r in range(2):
            src = b.out_sum.at[:, 128 * r : 128 * r + 128]
            dst = rows_of(b.out_back, 256 * pair, 256)
            waits.append(w.push(src, dst, send + 7 + r, recv + 6 + pair, h // 2, 2 * i + r))
        return waits

    def landed():
        @pl.when(h < 4)
        def _():
            for t in range(4):
                w.arrived(b.qkv_back.at[:, 128 * t : 128 * t + 128], recv + t)

        @pl.when(h >= 4)
        def _():
            for t in range(2):
                w.arrived(b.qkv_back.at[:, 256 * t : 256 * t + 256], recv + t)

        for r in range(2):
            w.arrived(b.out_back.at[256 * r : 256 * r + 256, :], recv + 6 + r)

    return ffn, ffn_done, mixer, mixer_out, landed


def small_sums(w, b, send, recv, send2, recv2):
    copies = []
    for d in range(1, 4):
        copy = w.remote(b.small, b.small_got.at[d], send + d, recv + d, lax.rem(w.i + d, 4), w.s)
        copy.start()
        copies.append(copy)

    def middle():
        total = b.small[...]
        for d in range(1, 4):
            w.arrived(b.small_got.at[d], recv + d)
            total = total + b.small_got[d]
        b.small_sum[...] = total
        b.small_all[w.s] = total
        for d in range(1, 8):
            copy = w.remote(b.small_sum, b.small_all.at[w.s], send2 + d, recv2 + d, w.i, lax.rem(w.s + d, 8))
            copy.start()
            copies.append(copy)

    def end():
        for d in range(1, 8):
            w.arrived(b.small_all.at[lax.rem(w.s + 8 - d, 8)], recv2 + d)
        for copy in copies:
            copy.wait_send()
        gains = b.small_all[0, 0:2, :]
        head_gain = b.small_all[0, 2:3, 0:256]
        for n in range(1, 8):
            gains = gains + b.small_all[n, 0:2, :]
            head_gain = head_gain + b.small_all[n, 2:3, 0:256]
        b.gains_grad[...] = gains
        b.head_gain_grad[...] = head_gain
        for n in range(8):
            b.params_grad[n : n + 1, :] = b.small_all[n, 3:4, 0:128]
            b.head_w_grad[n : n + 1, :] = b.small_all[n, 4:5, :]
            b.head_w_grad[8 + n : 9 + n, :] = b.small_all[n, 5:6, :]
            for k in range(KCONV):
                line = b.small_all[n, 6 + k // 2 : 7 + k // 2, 512 * (k % 2) : 512 * (k % 2) + 512]
                b.conv_grad[k : k + 1, 128 * n : 128 * n + 128] = line[:, 0:128]
                b.conv_grad[k : k + 1, 1024 + 128 * n : 1152 + 128 * n] = line[:, 128:256]
                b.conv_grad[k : k + 1, 2048 + 256 * n : 2304 + 256 * n] = line[:, 256:512]

    return middle, end


def rest_phase(b, w, sn_gather, cg_gather, front_finish):
    s = w.s
    half_rows = lambda ref: (lambda n: rows_of(ref, 128 * n, 128))
    ag_gather = LineGather(w, half_rows(b.agr))
    scatter4 = PairScatter(w, b.part4, b.sib4, b.chip4, b.got4)
    scatter6 = PairScatter(w, b.part, b.sib6, b.chip6, b.got6)
    scatter8 = LineScatter(w, b.part, b.sib, b.chip, b.got)
    in_sum = SquareScatter(w, b.in_out, b.in_got, 768, 704)
    down_sum = SquareScatter(w, b.down_out, b.down_got)
    out_sum = SquareScatter(w, b.out_out, b.out_got)
    qkv_sum = SquareScatter(w, b.qkv_out, b.qkv_got)
    gate_sum = SquareScatter(w, b.gate_out, b.gate_got)
    home_ffn, home_ffn_done, home_qkv, home_out, home_landed = grads_home(w, b)
    sm = (w.take(4), w.take(4), w.take(8), w.take(8))

    def ffn_loop(n, carry):
        @pl.when(n == 1)
        def _():
            sn_gather.arrive()

        sn_gather.other(n)
        cg_gather.other(n)
        q = w.place + n * (1 - 2 * w.place)
        ffn_tile(b, q)
        scatter6.swapped(q).start()
        scatter4.swapped(q).start()
        return carry

    lax.fori_loop(0, 2, ffn_loop, 0)
    scatter6.add(1 - w.place)
    scatter6.away().start()
    scatter6.add(w.place)

    def in_piece(n):
        return mm(b.gug[...], cols(b.sn, 256 * n, 256)[...], TN)

    def down_piece(n):
        return mm(b.hid[...], cols(b.cg, 256 * n, 256)[...], TN)[0:704]

    in_sum.start_far(in_piece)
    down_sum.start_far(down_piece)
    second_grad = scatter6.total()
    back, share = norm_back(b.middle[...], b.gains[1:2, :], second_grad)
    b.small[1:2, :] = jnp.sum(share, axis=0, keepdims=True)
    mgrad = b.own_cot[...].astype(jnp.float32) + back
    b.mgrad[...] = mgrad
    own = low(mgrad)
    b.own_ag[...] = own
    rows_of(b.agr, 128 * s, 128)[...] = own
    ag_gather.start(b.own_ag)
    in_sum.start_near(in_piece)
    down_sum.start_near(down_piece)
    scatter4.add(1 - w.place)
    scatter4.away().start()
    scatter4.add(w.place)
    row, col = grid_masks()

    def out_loop(n, head_gain_sum):
        t = w.order(n)
        ag_gather.arrive(t)
        ag_gather.other(t)
        out = mixer_out_back(b, t, head_gain_sum)

        @pl.when(n == 2)
        def _():
            in_sum.relay()
            down_sum.relay()

        return out

    head_gain_sum = lax.fori_loop(0, 4, out_loop, jnp.zeros((1, DV), F32))
    scatter6.finish()
    def out_piece(n):
        return mm(b.normed[...], cols(b.agr, 256 * n, 256)[...], TN)


    def gate_piece(n):
        return mm(cols(b.fn, 256 * n, 256)[...], b.gg[...], TN)

    out_sum.start_far(out_piece)
    gate_sum.start_far(gate_piece)
    out_sum.start_near(out_piece)
    gate_sum.start_near(gate_piece)

    def chain_loop(n, ds1):
        return rec_back_chain(b, 3 - n, ds1, row, col)

    lax.fori_loop(0, 4, chain_loop, jnp.zeros((DK, DV), F32))
    in_sum.total(in_piece(w.i), b.in_sum)
    down_sum.total(down_piece(w.i), b.down_sum)
    home_ffn()
    b.dcs[CH : CH + HALO, :] = jnp.zeros((HALO, 512), F32)

    def back_loop(n, sums):
        t = 3 - n
        sums = mixer_back_tile(b, w, t, row, col, sums)
        scatter8.swap(t)

        @pl.when(n == 1)
        def _():
            out_sum.relay()
            gate_sum.relay()

        @pl.when(n > 0)
        def _():
            scatter8.pass_on(t + 1)

        @pl.when(n > 1)
        def _():
            scatter8.relay(t + 2)

        return sums

    one = jnp.zeros((1, 1), F32)
    taps_sums, p0, p1, p2, gain_sum = lax.fori_loop(
        0, 4, back_loop, (tuple(jnp.zeros((1, 512), F32) for n in range(KCONV)), one, one, one, jnp.zeros((1, 1024), F32))
    )
    scatter8.pass_on(0)
    scatter8.relay(1)

    def qkv_piece(n):
        return mm(cols(b.fn, 256 * n, 256)[...], b.cgd[...], TN)

    qkv_sum.start_far(qkv_piece)
    qkv_sum.start_near(qkv_piece)
    scatter8.relay(0)
    b.small[0:1, :] = gain_sum / b.gains[0:1, :]
    b.small[2:3, :] = jnp.concatenate([head_gain_sum, jnp.zeros((1, 1024 - DV), F32)], axis=1)
    lane = lax.broadcasted_iota(jnp.int32, (1, 1024), 1)
    b.small[3:4, :] = jnp.where(lane == 0, p0, jnp.where(lane == 1, p1, jnp.where(lane == 2, p2, 0.0)))
    head_rows = mm(b.hg[...], b.fn[...], TN)
    line = lax.broadcasted_iota(jnp.int32, head_rows.shape, 0)
    b.small[4:5, :] = jnp.sum(jnp.where(line == s, head_rows, 0.0), axis=0, keepdims=True)
    b.small[5:6, :] = jnp.sum(jnp.where(line == s + 8, head_rows, 0.0), axis=0, keepdims=True)
    b.small[6:7, :] = jnp.concatenate([taps_sums[0], taps_sums[1]], axis=1)
    b.small[7:8, :] = jnp.concatenate([taps_sums[2], taps_sums[3]], axis=1)
    small_middle, small_end = small_sums(w, b, *sm)
    out_sum.total(out_piece(w.i), b.out_sum)
    waits = home_out()
    gate_sum.total(gate_piece(w.i), b.gate_back)
    qkv_sum.relay()
    small_middle()
    b.output[...] = low(jnp.where(valid_rows(b, w), b.middle[...] + scatter4.total(), 0.0))
    qkv_sum.total(qkv_piece(w.i), b.qkv_sum)
    waits = waits + home_qkv()
    first_grad = scatter8.total()
    back, unused_share = norm_back(b.tokens_v[...].astype(jnp.float32), b.gains[0:1, :], first_grad)
    b.input_grad[...] = low(b.mgrad[...] + back)
    home_ffn_done()
    small_end()
    home_landed()
    for wait in waits:
        wait()
    for part in (in_sum, down_sum, out_sum, qkv_sum, gate_sum):
        part.finish()
    scatter4.finish()
    scatter8.finish()
    ag_gather.finish()
    front_finish()


def layer_kernel(dp, seq, *refs):
    b = Box()
    (
        b.tokens,
        b.qkv,
        b.gate,
        b.ffn_in,
        b.out,
        b.ffn_out,
        b.gains,
        b.head_gain,
        b.params,
        b.head_w,
        b.taps,
        b.tokens_v,
        b.cot_v,
        b.lengths,
    ) = refs[:14]
    kinds = fields(LayerOut) + fields(FrontKept) + fields(FrontScratch) + fields(RestScratch)
    for (name, shape, kind), ref in zip(kinds, refs[14:]):
        setattr(b, name, ref)
    b.do, b.dr, b.agr = b.mixed, b.gi, b.x
    w = Wires(dp, seq, refs[-1])
    rest_phase(b, w, *front_phase(b, w))


def layer(dp, seq, *arrays):
    outs = pl.pallas_call(
        functools.partial(layer_kernel, dp, seq),
        out_shape=tuple(jax.ShapeDtypeStruct(shape, kind) for _, shape, kind in fields(LayerOut)),
        in_specs=[ANY] * 6 + [IN_VMEM] * 7 + [pl.BlockSpec(memory_space=pltpu.SMEM)],
        out_specs=(IN_VMEM,) * len(fields(LayerOut)),
        scratch_shapes=[
            pltpu.VMEM(shape, kind)
            for _, shape, kind in fields(FrontKept) + fields(FrontScratch) + fields(RestScratch)
        ]
        + [pltpu.SemaphoreType.DMA((500,))],
        compiler_params=pltpu.CompilerParams(collective_id=0, has_side_effects=True, vmem_limit_bytes=62 << 20),
        name="layer",
    )(*arrays)
    made = Box()
    for (name, shape, kind), out in zip(fields(LayerOut), outs):
        setattr(made, name, out)
    return made


class FinalOut:
    output = ((128, 1024), B16)
    input_grad = ((128, 1024), B16)
    gains_grad = ((2, 1024), F32)
    head_gain_grad = ((1, 256), F32)
    params_grad = ((3, 8), F32)
    head_w_grad = ((16, 1024), F32)
    conv_grad = ((4, 4096), F32)
    qkv_back = ((256, 512), F32)
    gate_back = ((256, 256), F32)
    in_back = ((704, 256), F32)
    out_back = ((512, 128), F32)
    down_back = ((704, 128), F32)


def final_kernel(*refs):
    count = len(fields(FinalOut))
    srcs, outs, held, sems = refs[:count], refs[count : 2 * count], refs[2 * count : -1], refs[-1]
    copies = [pltpu.make_async_copy(src, buf, sems.at[n]) for n, (src, buf) in enumerate(zip(srcs, held))]
    for copy in copies:
        copy.start()
    for n, ((name, shape, kind), copy, buf, out) in enumerate(zip(fields(FinalOut), copies, held, outs)):
        copy.wait()
        if n == 4:
            out[...] = jnp.transpose(buf[...])[0:3, :]
        else:
            out[...] = buf[0 : shape[0], :].astype(kind)


def final(made):
    names = fields(FinalOut)
    arrays = [getattr(made, name) for name, _, _ in names]
    outs = pl.pallas_call(
        final_kernel,
        out_shape=tuple(jax.ShapeDtypeStruct(shape, kind) for _, shape, kind in names),
        in_specs=[ANY] * len(names),
        out_specs=(IN_VMEM,) * len(names),
        scratch_shapes=[pltpu.VMEM(array.shape, array.dtype) for array in arrays]
        + [pltpu.SemaphoreType.DMA((len(names),))],
        compiler_params=pltpu.CompilerParams(vmem_limit_bytes=62 << 20),
        name="final",
    )(*arrays)
    done = Box()
    for (name, shape, kind), out in zip(names, outs):
        setattr(done, name, out)
    return done


def fast_body(
    dp,
    seq,
    tokens,
    lengths,
    cotangent,
    norm_gains,
    head_gain,
    head_params,
    qkv_weight,
    gate_weight,
    head_weight,
    conv_weight,
    out_weight,
    ffn_in,
    ffn_out,
):
    made = layer(
        dp,
        seq,
        tokens[0],
        qkv_weight,
        gate_weight,
        ffn_in.T,
        out_weight,
        ffn_out,
        norm_gains,
        head_gain[None],
        head_params,
        head_weight.T,
        conv_weight.T,
        tokens[0],
        cotangent[0],
        lengths,
    )
    r = final(made)
    return (
        r.output[None],
        r.input_grad[None],
        r.gains_grad,
        r.head_gain_grad[0],
        r.params_grad,
        r.qkv_back,
        r.gate_back,
        r.head_w_grad.T,
        r.conv_grad.T,
        r.out_back,
        r.in_back.T,
        r.down_back,
    )


def choose_body(dp, seq):
    def chosen(*arrays):
        tokens, head_params = arrays[0], arrays[5]
        if (dp, seq) == (4, 8) and tokens.shape[0] == 1 and head_params.shape[1] == seq:
            return fast_body(dp, seq, *arrays)
        return general_body(*arrays)

    return chosen


def solution(mesh):
    dp, seq = mesh.shape["dp"], mesh.shape["seq"]
    placed = (
        P("dp", "seq", None),
        P("dp"),
        P("dp", "seq", None),
        P(),
        P(),
        P(),
        P("dp", "seq"),
        P("dp", "seq"),
        P(),
        P(),
        P("dp", "seq"),
        P("dp", "seq"),
        P("dp", "seq"),
    )
    return jax.shard_map(
        choose_body(dp, seq),
        mesh=mesh,
        in_specs=placed,
        out_specs=(
            P("dp", "seq", None),
            P("dp", "seq", None),
            P(),
            P(),
            P(),
            P("dp", "seq"),
            P("dp", "seq"),
            P(),
            P(),
            P("dp", "seq"),
            P("dp", "seq"),
            P("dp", "seq"),
        ),
        check_vma=False,
    )
```

```python
import functools

import jax
import jax.numpy as jnp
from jax import lax
from jax.experimental import pallas as pl
from jax.experimental.pallas import tpu as pltpu
from jax.sharding import PartitionSpec as P

CH = 256
DK = 128
DV = 256
KCONV = 4
TILE = 64


HIGHEST = lax.Precision.HIGHEST
epsilon = 1e-06


def passed_along(block, axis, distance):
    devices = range(lax.axis_size(axis))
    route = [(i - distance, i) for i in devices if i - distance in devices]
    return lax.ppermute(block, axis, route)


def rms_scale(values, gain_row):
    return (
        values * lax.rsqrt(jnp.mean(values * values, axis=-1, keepdims=True) + epsilon) * gain_row
    )


def unit_rows(values):
    return values * lax.rsqrt(jnp.sum(values * values, axis=-1, keepdims=True) + epsilon)


def block_step(state_now, query_vecs, key_vecs, value_vecs, log_decay, erase_rate):
    length = query_vecs.shape[1]
    cumulative = jnp.cumsum(log_decay, axis=1)
    row_index = jnp.arange(length)[:, None]
    col_index = jnp.arange(length)[None, :]
    strict = col_index < row_index
    within = col_index <= row_index
    spread = cumulative[:, :, None] - cumulative[:, None, :]
    lower_decay = jnp.where(strict, jnp.exp(jnp.where(strict, spread, 0.0)), 0.0)
    causal = jnp.where(within, jnp.exp(jnp.where(within, spread, 0.0)), 0.0)
    key_gram = jnp.einsum("htk,hsk->hts", key_vecs, key_vecs, precision=HIGHEST)
    query_gram = jnp.einsum("htk,hsk->hts", query_vecs, key_vecs, precision=HIGHEST)
    negated = -(erase_rate[:, :, None] * key_gram * lower_decay)
    identity = jnp.eye(length, dtype=jnp.float32)
    inverse = identity + negated
    powered = negated
    for level_index in range(length.bit_length() - 2):
        powered = jnp.einsum("hts,hsr->htr", powered, powered, precision=HIGHEST)
        inverse = jnp.einsum("hts,hsr->htr", inverse, identity + powered, precision=HIGHEST)
    shrink = jnp.exp(cumulative)
    recalled = jnp.einsum("htk,hkw->htw", key_vecs, state_now, precision=HIGHEST)
    target = erase_rate[:, :, None] * value_vecs - (erase_rate * shrink)[:, :, None] * recalled
    updates = jnp.einsum("hts,hsw->htw", inverse, target, precision=HIGHEST)
    read_out = shrink[:, :, None] * jnp.einsum(
        "htk,hkw->htw", query_vecs, state_now, precision=HIGHEST
    )
    read_out = read_out + jnp.einsum(
        "hts,hsw->htw", query_gram * causal, updates, precision=HIGHEST
    )
    remain = jnp.exp(cumulative[:, -1:] - cumulative)
    state_next = jnp.exp(cumulative[:, -1])[:, None, None] * state_now
    state_next = state_next + jnp.einsum(
        "hsk,hsw->hkw", key_vecs * remain[:, :, None], updates, precision=HIGHEST
    )
    return (state_next, read_out)


def run_tiles(query_vecs, key_vecs, value_vecs, log_decay, erase_rate, state_start):
    row_count, head_count, key_width = query_vecs.shape
    tile_count = row_count // TILE

    def arrange(tensor):
        return jnp.swapaxes(tensor.reshape((tile_count, TILE, head_count) + tensor.shape[2:]), 1, 2)

    inputs = (
        arrange(query_vecs),
        arrange(key_vecs),
        arrange(value_vecs),
        arrange(log_decay),
        arrange(erase_rate),
    )

    def advance(state_now, sliced):
        return jax.checkpoint(block_step)(state_now, *sliced)

    state_end, outputs = lax.scan(advance, state_start, inputs)
    outputs = jnp.swapaxes(outputs, 1, 2).reshape(row_count, head_count, outputs.shape[-1])
    return (outputs, state_end)


def mixer_inputs(conv_in, edge_rows, head_in, conv_taps, head_params):
    block_len = conv_in.shape[1]
    head_count = head_params.shape[1]
    extended = jnp.concatenate([edge_rows, conv_in], axis=1)
    conv_sum = extended[:, 0:block_len] * conv_taps[:, 0]
    for offset in range(1, conv_taps.shape[1]):
        conv_sum = conv_sum + extended[:, offset : offset + block_len] * conv_taps[:, offset]
    activated = jax.nn.silu(conv_sum)
    key_span = head_count * DK
    lead = activated.shape[:2]
    query_vecs = unit_rows(activated[..., 0:key_span].reshape(lead + (head_count, DK))) * DK ** (
        -0.5
    )
    key_vecs = unit_rows(activated[..., key_span : 2 * key_span].reshape(lead + (head_count, DK)))
    value_vecs = activated[..., 2 * key_span :].reshape(lead + (head_count, DV))
    log_decay = -jnp.exp(head_params[0]) * jax.nn.softplus(
        head_in[..., 0:head_count] + head_params[1]
    )
    erase_rate = jax.nn.sigmoid(head_in[..., head_count : 2 * head_count] + head_params[2])
    return (query_vecs, key_vecs, value_vecs, log_decay, erase_rate)


def gated_norm(mixed, gate_in, head_gain):
    shaped = gate_in.reshape(mixed.shape)
    normed = (
        mixed * lax.rsqrt(jnp.mean(mixed * mixed, axis=-1, keepdims=True) + epsilon) * head_gain
    )
    return (normed * jax.nn.silu(shaped)).reshape(gate_in.shape)


def local_tiles(query_vecs, key_vecs, value_vecs, log_decay, erase_rate):
    key_width = key_vecs.shape[-1]
    value_width = value_vecs.shape[-1]
    head_count = key_vecs.shape[2]
    padded = jnp.concatenate(
        [jnp.zeros(value_vecs.shape[:3] + (key_width,), jnp.float32), value_vecs], axis=-1
    )
    start_map = jnp.concatenate(
        [jnp.eye(key_width, dtype=jnp.float32), jnp.zeros((key_width, value_width), jnp.float32)],
        axis=1,
    )
    start_map = jnp.broadcast_to(start_map, (head_count, key_width, key_width + value_width))

    def single(query_one, key_one, value_one, decay_one, erase_one):
        return run_tiles(query_one, key_one, value_one, decay_one, erase_one, start_map)

    return jax.vmap(single)(query_vecs, key_vecs, padded, log_decay, erase_rate)


def post_mix(local_out, incoming, gate_in, head_gain):
    mixed = local_out[..., DK:] + jnp.einsum(
        "snhk,shkv->snhv", local_out[..., 0:DK], incoming, precision=HIGHEST
    )
    return gated_norm(mixed, gate_in, head_gain)


def swiglu(gate_up):
    split_at = gate_up.shape[-1] // 2
    return jax.nn.silu(gate_up[:, 0:split_at]) * gate_up[:, split_at:]


def matmul_maps(left, right):
    return jnp.einsum("shij,shjk->shik", left, right, precision=HIGHEST)


def apply_map(maps, state_now):
    return matmul_maps(maps[0], state_now) + maps[1]


def general_body(
    tokens,
    lengths,
    cotangent,
    norm_gains,
    head_gain,
    head_params,
    qkv_weight,
    gate_weight,
    head_weight,
    conv_weight,
    out_weight,
    ffn_in,
    ffn_out,
):
    seq_count, block_len, model_width = tokens.shape
    row_count = seq_count * block_len
    position = lax.axis_index("seq") * block_len + jnp.arange(block_len, dtype=jnp.int32)
    valid_rows = (position[None, :] < lengths[:, None]).reshape(row_count, 1)
    col_parts = (
        lax.all_gather(qkv_weight, "seq", axis=1, tiled=True),
        lax.all_gather(gate_weight, "seq", axis=1, tiled=True),
        lax.all_gather(out_weight, "seq", axis=1, tiled=True),
        lax.all_gather(ffn_in, "seq", axis=1, tiled=True),
        lax.all_gather(ffn_out, "seq", axis=1, tiled=True),
    )
    gathered = (
        lax.all_gather(col_parts[0], "dp", axis=0, tiled=True),
        lax.all_gather(col_parts[1], "dp", axis=0, tiled=True),
        lax.all_gather(col_parts[2], "dp", axis=0, tiled=True),
        lax.all_gather(col_parts[3], "dp", axis=0, tiled=True),
        lax.all_gather(col_parts[4], "dp", axis=0, tiled=True),
    )
    w_qkv, w_gate, w_out, w_in, w_down = gathered
    inputs = tokens.reshape(row_count, model_width).astype(jnp.float32)
    first_norm = rms_scale(inputs, norm_gains[0]).astype(jnp.bfloat16)
    conv_in = jnp.dot(first_norm, w_qkv, preferred_element_type=jnp.float32).astype(jnp.bfloat16)
    head_in = jnp.dot(first_norm, head_weight, preferred_element_type=jnp.float32)
    gate_in = jnp.dot(first_norm, w_gate, preferred_element_type=jnp.float32)
    conv_width = conv_in.shape[-1]
    conv_rows = conv_in.reshape(seq_count, block_len, conv_width)
    edge_cut = block_len - (KCONV - 1)
    edge_rows = passed_along(conv_rows[:, edge_cut:], "seq", 1)
    mix_args = (
        conv_rows.astype(jnp.float32),
        edge_rows.astype(jnp.float32),
        head_in.reshape(seq_count, block_len, -1),
        conv_weight.astype(jnp.float32),
        head_params,
    )
    vectors = mixer_inputs(*mix_args)
    local_out, end_states = local_tiles(*vectors)
    carry_maps = (end_states[..., 0:DK], end_states[..., DK:])

    def relay_state(step_index, state_now):
        return passed_along(apply_map(carry_maps, state_now), "seq", 1)

    incoming = lax.fori_loop(
        0, lax.axis_size("seq") - 1, relay_state, jnp.zeros_like(carry_maps[1])
    )
    post_args = (local_out, incoming, gate_in, head_gain)
    normed = post_mix(*post_args).astype(jnp.bfloat16)
    attended = jnp.dot(normed, w_out, preferred_element_type=jnp.float32)
    middle = inputs + attended
    second_norm = rms_scale(middle, norm_gains[1]).astype(jnp.bfloat16)
    gate_up = jnp.dot(second_norm, w_in, preferred_element_type=jnp.float32)
    hidden = swiglu(gate_up).astype(jnp.bfloat16)
    carried = jnp.dot(hidden, w_down, preferred_element_type=jnp.float32)
    output = jnp.where(valid_rows, middle + carried, 0.0).astype(jnp.bfloat16)
    col_again = (
        lax.all_gather(qkv_weight, "seq", axis=1, tiled=True),
        lax.all_gather(gate_weight, "seq", axis=1, tiled=True),
        lax.all_gather(out_weight, "seq", axis=1, tiled=True),
        lax.all_gather(ffn_in, "seq", axis=1, tiled=True),
        lax.all_gather(ffn_out, "seq", axis=1, tiled=True),
    )
    regathered = (
        lax.all_gather(col_again[0], "dp", axis=0, tiled=True),
        lax.all_gather(col_again[1], "dp", axis=0, tiled=True),
        lax.all_gather(col_again[2], "dp", axis=0, tiled=True),
        lax.all_gather(col_again[3], "dp", axis=0, tiled=True),
        lax.all_gather(col_again[4], "dp", axis=0, tiled=True),
    )
    w_qkv, w_gate, w_out, w_in, w_down = regathered
    upstream = jnp.where(
        valid_rows, cotangent.reshape(row_count, model_width).astype(jnp.float32), 0.0
    )
    carried_grad = upstream.astype(jnp.bfloat16)
    grad_down = jnp.einsum("nf,nd->fd", hidden, carried_grad, preferred_element_type=jnp.float32)
    hidden_grad = jnp.einsum("nd,fd->nf", carried_grad, w_down, preferred_element_type=jnp.float32)
    unused, swiglu_back = jax.vjp(swiglu, gate_up)
    gate_up_grad = swiglu_back(hidden_grad)[0].astype(jnp.bfloat16)
    grad_in = jnp.einsum("nd,nf->df", second_norm, gate_up_grad, preferred_element_type=jnp.float32)
    second_grad = jnp.einsum("nf,df->nd", gate_up_grad, w_in, preferred_element_type=jnp.float32)
    unused, second_back = jax.vjp(rms_scale, middle, norm_gains[1])
    middle_back, gain_two = second_back(second_grad)
    middle_grad = upstream + middle_back
    attended_grad = middle_grad.astype(jnp.bfloat16)
    grad_out = jnp.einsum("nv,nd->vd", normed, attended_grad, preferred_element_type=jnp.float32)
    normed_grad = jnp.einsum("nd,vd->nv", attended_grad, w_out, preferred_element_type=jnp.float32)
    unused, post_back = jax.vjp(post_mix, *post_args)
    local_grad, incoming_local, gate_in_grad, head_gain_grad = post_back(normed_grad)
    flipped = (jnp.swapaxes(carry_maps[0], -1, -2), incoming_local)

    def relay_grad(step_index, grad_now):
        return passed_along(apply_map(flipped, grad_now).astype(jnp.bfloat16), "seq", -1).astype(
            jnp.float32
        )

    outgoing = lax.fori_loop(
        0, lax.axis_size("seq") - 1, relay_grad, jnp.zeros_like(incoming_local)
    )
    map_grad = jnp.einsum("shkv,shjv->shkj", outgoing, incoming, precision=HIGHEST)
    end_grad = jnp.concatenate([map_grad, outgoing], axis=-1)
    unused, tiles_back = jax.vjp(local_tiles, *vectors)
    vector_grads = tiles_back((local_grad, end_grad))
    unused, mix_back = jax.vjp(mixer_inputs, *mix_args)
    conv_own, edge_grad, head_in_grad, conv_taps_grad, params_grad = mix_back(vector_grads)
    edge_back = passed_along(edge_grad.astype(jnp.bfloat16), "seq", -1).astype(edge_grad.dtype)
    conv_total = jnp.concatenate(
        [conv_own[:, 0:edge_cut], conv_own[:, edge_cut:] + edge_back], axis=1
    )
    conv_grad = conv_total.reshape(row_count, conv_width).astype(jnp.bfloat16)
    head_grad = head_in_grad.reshape(row_count, -1).astype(jnp.bfloat16)
    gate_grad = gate_in_grad.astype(jnp.bfloat16)
    grad_qkv = jnp.einsum("nd,nc->dc", first_norm, conv_grad, preferred_element_type=jnp.float32)
    grad_head = jnp.einsum("nd,nc->dc", first_norm, head_grad, preferred_element_type=jnp.float32)
    grad_gate = jnp.einsum("nd,nc->dc", first_norm, gate_grad, preferred_element_type=jnp.float32)
    first_grad = jnp.einsum("nc,dc->nd", conv_grad, w_qkv, preferred_element_type=jnp.float32)
    first_grad = first_grad + jnp.einsum(
        "nc,dc->nd", head_grad, head_weight, preferred_element_type=jnp.float32
    )
    first_grad = first_grad + jnp.einsum(
        "nc,dc->nd", gate_grad, w_gate, preferred_element_type=jnp.float32
    )
    unused, first_back = jax.vjp(rms_scale, inputs, norm_gains[0])
    input_back, gain_one = first_back(first_grad)
    input_grad = (
        (middle_grad + input_back).astype(jnp.bfloat16).reshape(seq_count, block_len, model_width)
    )
    row_groups = (
        lax.psum_scatter(
            grad_qkv.astype(jnp.bfloat16), "dp", scatter_dimension=0, tiled=True
        ).astype(jnp.float32),
        lax.psum_scatter(
            grad_gate.astype(jnp.bfloat16), "dp", scatter_dimension=0, tiled=True
        ).astype(jnp.float32),
        lax.psum_scatter(
            grad_out.astype(jnp.bfloat16), "dp", scatter_dimension=0, tiled=True
        ).astype(jnp.float32),
        lax.psum_scatter(
            grad_in.astype(jnp.bfloat16), "dp", scatter_dimension=0, tiled=True
        ).astype(jnp.float32),
        lax.psum_scatter(
            grad_down.astype(jnp.bfloat16), "dp", scatter_dimension=0, tiled=True
        ).astype(jnp.float32),
    )
    weight_parts = (
        lax.psum_scatter(
            row_groups[0].astype(jnp.bfloat16), "seq", scatter_dimension=1, tiled=True
        ).astype(jnp.float32),
        lax.psum_scatter(
            row_groups[1].astype(jnp.bfloat16), "seq", scatter_dimension=1, tiled=True
        ).astype(jnp.float32),
        lax.psum_scatter(
            row_groups[2].astype(jnp.bfloat16), "seq", scatter_dimension=1, tiled=True
        ).astype(jnp.float32),
        lax.psum_scatter(
            row_groups[3].astype(jnp.bfloat16), "seq", scatter_dimension=1, tiled=True
        ).astype(jnp.float32),
        lax.psum_scatter(
            row_groups[4].astype(jnp.bfloat16), "seq", scatter_dimension=1, tiled=True
        ).astype(jnp.float32),
    )
    small_sums = lax.psum(
        (jnp.stack([gain_one, gain_two]), head_gain_grad, params_grad, grad_head, conv_taps_grad),
        ("dp", "seq"),
    )
    output = output.reshape(seq_count, block_len, model_width)
    return (
        output,
        input_grad,
        small_sums[0],
        small_sums[1],
        small_sums[2],
        weight_parts[0],
        weight_parts[1],
        small_sums[3],
        small_sums[4],
        weight_parts[2],
        weight_parts[3],
        weight_parts[4],
    )


MESH = pl.DeviceIdType.MESH
ANY = pl.BlockSpec(memory_space=pl.ANY)
IN_VMEM = pl.BlockSpec(memory_space=pltpu.VMEM)
B16 = jnp.bfloat16
F32 = jnp.float32
NN = ((1,), (0,))
NT = ((1,), (1,))
TN = ((0,), (0,))
HALO = 16


def low(v):
    return v.astype(jnp.bfloat16)


def mm(a, b, dims=NN):
    return lax.dot_general(low(a), low(b), (dims, ((), ())), preferred_element_type=jnp.float32)


def mmf(a, b, dims=NN):
    return lax.dot_general(
        a, b, (dims, ((), ())), precision=HIGHEST, preferred_element_type=jnp.float32
    )


def mm3(a, b, dims=NN):
    ah, bh = low(a), low(b)
    al, bl = low(a - ah.astype(jnp.float32)), low(b - bh.astype(jnp.float32))
    return mm(ah, bh, dims) + (mm(ah, bl, dims) + mm(al, bh, dims))


def sig(v):
    return 1.0 / (1.0 + jnp.exp(-v))


def soft_plus(v):
    tail = jnp.exp(-jnp.abs(v))
    series = tail * (1.0 - tail * (0.5 - tail * (1.0 / 3.0)))
    return jnp.maximum(v, 0.0) + jnp.where(tail < 1e-3, series, jnp.log(1.0 + tail))


def grid_masks():
    row = lax.broadcasted_iota(jnp.int32, (CH, CH), 0)
    col = lax.broadcasted_iota(jnp.int32, (CH, CH), 1)
    return row, col


def decay_parts(g, row, col):
    lower = (col <= row).astype(jnp.float32)
    cum = mmf(lower, g)
    cum_row = mmf(g, lower, ((0,), (1,)))
    within = col <= row
    decay = jnp.where(within, jnp.exp(jnp.where(within, cum - cum_row, 0.0)), 0.0)
    return cum, decay


def unit_inverse(attns, row, col):
    def same(width):
        return (row // width) == (col // width)

    eye = jnp.where(row == col, 1.0, 0.0)
    power = [jnp.where(same(64), -a, 0.0) for a in attns]
    inv = [eye + p for p in power]
    for level in range(5):
        power = [mm(p, p) for p in power]
        inv = [x + mm(x, p) for x, p in zip(inv, power)]
    for width in (128, 256):
        off = same(width) & jnp.logical_not(same(width // 2))
        part = [mm(jnp.where(off, a, 0.0), x) for a, x in zip(attns, inv)]
        inv = [x - mm(x, p) for x, p in zip(inv, part)]
    rest = [eye - x - mm3(a, x) for a, x in zip(attns, inv)]
    return [x + mm(x, r) for x, r in zip(inv, rest)]


def odd(t):
    return t % 2 if isinstance(t, int) else lax.rem(t, 2)


def tile(t, size=CH):
    return pl.ds(pl.multiple_of(t * size, size), size)


class Wires:
    def __init__(self, dp, seq, sems):
        self.dp, self.seq, self.sems, self.used = dp, seq, sems, 0
        self.i, self.s = lax.axis_index("dp"), lax.axis_index("seq")
        self.z, self.c = self.s // 2, lax.rem(self.s, 2)
        self.half, self.partner = self.z // 2, self.z + 1 - 2 * lax.rem(self.z, 2)
        self.inner = lax.rem((self.z + 1) // 2, 2)
        self.place = lax.rem(self.z, 2)
        self.beside = (self.i + 1 - 2 * lax.rem(self.i, 2), lax.rem(self.i + 2, 4))

    def take(self, count=1):
        start = self.used
        self.used += count
        return start

    def meet_all(self):
        barrier = pltpu.get_barrier_semaphore()
        for di in range(self.dp):
            for dj in range(self.seq):
                if di or dj:
                    pl.semaphore_signal(
                        barrier,
                        inc=1,
                        device_id=(lax.rem(self.i + di, self.dp), lax.rem(self.s + dj, self.seq)),
                        device_id_type=MESH,
                    )
        pl.semaphore_wait(barrier, self.dp * self.seq - 1)

    def remote(self, src, dst, send, recv, di, dj):
        return pltpu.make_async_remote_copy(
            src_ref=src,
            dst_ref=dst,
            send_sem=self.sems.at[send],
            recv_sem=self.sems.at[recv],
            device_id=(di, dj),
            device_id_type=MESH,
        )

    def local(self, src, dst, sem):
        return pltpu.make_async_copy(src, dst, self.sems.at[sem])

    def push(self, src, dst, send, recv, di, dj):
        here = (di == self.i) & (dj == self.s)
        away = self.remote(src, dst, send, recv, di, dj)

        @pl.when(here)
        def _():
            self.local(src, dst, recv).start()

        @pl.when(jnp.logical_not(here))
        def _():
            away.start()

        def sent():
            @pl.when(jnp.logical_not(here))
            def _():
                away.wait_send()

        return sent

    def arrived(self, dst, recv):
        pltpu.make_async_copy(dst, dst, self.sems.at[recv]).wait()

    def chip(self, z):
        return z * 2 + self.c

    def order(self, n):
        near = self.z + n * (1 - 2 * lax.rem(self.z, 2))
        return (1 - n // 2) * near + (n // 2) * (n + self.half * (3 - 2 * n))

    def sibling(self):
        return self.z * 2 + 1 - self.c


class LineGather:
    parts = 2

    def __init__(self, w, block_of):
        self.w, self.block_of = w, block_of
        n = 4 * self.parts
        self.send, self.recv = w.take(n), w.take(n)
        self.fsend, self.frecv = w.take(n), w.take(n)

    def piece(self, block, part):
        size = block.shape[0] // self.parts
        return block.at[part * size : part * size + size, :]

    def start(self, src):
        w = self.w
        dst = self.block_of(w.s)
        for part in range(self.parts):
            a, b = self.piece(src, part), self.piece(dst, part)
            slot = w.z * self.parts + part
            near, far = self.send + part, self.send + self.parts + part
            w.remote(a, b, near, self.recv + slot, w.i, w.chip(w.partner)).start()
            w.remote(a, b, far, self.recv + slot, w.i, w.chip(2 - w.half)).start()
        for part in range(self.parts):
            a, b = self.piece(src, part), self.piece(dst, part)
            slot = w.z * self.parts + part
            w.remote(a, b, self.fsend + slot, self.frecv + slot, w.i, w.sibling()).start()

    def arrive(self, t):
        w = self.w

        @pl.when(t != w.z)
        def _():
            block = self.block_of(w.chip(t))
            for part in range(self.parts):
                ref, slot = self.piece(block, part), t * self.parts + part
                w.arrived(ref, self.recv + slot)

                @pl.when((w.inner == 1) & (t // 2 != w.half))
                def _():
                    on = self.send + (2 + odd(t)) * self.parts + part
                    w.remote(ref, ref, on, self.recv + slot, w.i, w.chip(w.partner)).start()

                w.remote(ref, ref, self.fsend + slot, self.frecv + slot, w.i, w.sibling()).start()

    def other(self, t):
        w = self.w
        block = self.block_of(t * 2 + 1 - w.c)
        for part in range(self.parts):
            w.arrived(self.piece(block, part), self.frecv + t * self.parts + part)

    def finish(self):
        w = self.w
        block = self.block_of(w.s)
        for part in range(self.parts):
            ref = self.piece(block, part)
            for n in range(4):
                copy = w.remote(ref, ref, self.send + n * self.parts + part, self.recv, w.i, w.sibling())
                if n < 2:
                    copy.wait_send()
                else:
                    @pl.when(w.inner == 1)
                    def _():
                        copy.wait_send()

                w.remote(ref, ref, self.fsend + n * self.parts + part, self.recv, w.i, w.sibling()).wait_send()


class GroupGather:
    def __init__(self, w, part_of):
        self.w, self.part_of = w, part_of
        self.send, self.recv = w.take(4), w.take(4)

    def start(self, src):
        w = self.w
        w.local(src, self.part_of(w.i), self.recv).start()
        for d in (3, 1, 2):
            to = lax.rem(w.i + d, 4)
            w.remote(src, self.part_of(w.i), self.send + d, self.recv + d, to, w.s).start()

    def finish(self):
        w = self.w
        for d in range(4):
            w.arrived(self.part_of(lax.rem(w.i + 4 - d, 4)), self.recv + d)
        for d in range(1, 4):
            part = self.part_of(w.i)
            w.remote(part, part, self.send + d, self.recv + d, lax.rem(w.i + d, 4), w.s).wait_send()


class SquareGather:
    def __init__(self, w, part_of):
        self.w, self.part_of = w, part_of
        self.send, self.recv = w.take(4), w.take(5)

    def half(self, n, k):
        part = self.part_of(n)
        size = part.shape[0] // 2
        return part.at[size * k : size * k + size, :]

    def near(self, src):
        w = self.w
        part = self.part_of(w.i)
        return [w.remote(src, part, self.send + k, self.recv + k, w.beside[k], w.s) for k in range(2)]

    def far(self, k):
        w = self.w
        half = self.half(w.beside[k], k)
        return w.remote(half, half, self.send + 2 + k, self.recv + 2 + k, w.beside[1 - k], w.s)

    def start(self, src):
        w = self.w
        w.local(src, self.part_of(w.i), self.recv + 4).start()
        for copy in self.near(src):
            copy.start()

    def relay(self):
        w = self.w
        for k in range(2):
            w.arrived(self.part_of(w.beside[k]), self.recv + k)
            self.far(k).start()

    def finish(self):
        w = self.w
        w.arrived(self.part_of(w.i), self.recv + 4)
        for k in range(2):
            w.arrived(self.half(3 - w.i, k), self.recv + 2 + k)
        for copy in self.near(self.part_of(w.i)) + [self.far(0), self.far(1)]:
            copy.wait_send()


class LineScatter:
    def __init__(self, w, part, sib, chip, got):
        self.w, self.part, self.sib, self.chip, self.got = w, part, sib, chip, got
        self.ssend, self.srecv = w.take(4), w.take(4)
        self.send, self.recv = w.take(8), w.take(8)

    def swap(self, t):
        w = self.w
        src = self.part.at[pl.ds(pl.multiple_of(t * 256 + 128 * (1 - w.c), 128), 128), :]
        w.remote(src, self.sib.at[t], self.ssend + t, self.srecv + t, w.i, w.sibling()).start()

    def rows(self, ref, n, part):
        return ref.at[n, 64 * part : 64 * part + 64, :]

    def out(self, t, slot, chip, part):
        w = self.w
        src, dst = self.rows(self.chip, t, part), self.rows(self.got, slot, part)
        w.remote(src, dst, self.send + 2 * t + part, self.recv + 2 * slot + part, w.i, w.chip(chip)).start()

    def arrived(self, slot, part):
        half = self.rows(self.got, slot, part)
        self.w.arrived(half, self.recv + 2 * slot + part)
        return half[...].astype(jnp.float32)

    def pass_on(self, t):
        w = self.w
        w.arrived(self.sib.at[t], self.srecv + t)
        mine = self.part[pl.ds(pl.multiple_of(t * 256 + 128 * w.c, 128), 128), :]
        self.chip[t] = low(mine.astype(jnp.float32) + self.sib[t].astype(jnp.float32))

        @pl.when(t == w.partner)
        def _():
            for part in range(2):
                self.out(t, 0, t, part)

        @pl.when((t // 2 != w.half) & (w.inner == 0))
        def _():
            for part in range(2):
                self.out(t, 2 + odd(t), w.partner, part)

    def relay(self, t):
        w = self.w

        @pl.when((t // 2 != w.half) & (w.inner == 1))
        def _():
            for part in range(2):
                half = self.rows(self.chip, t, part)
                came = self.arrived(2 + odd(t), part)
                half[...] = low(half[...].astype(jnp.float32) + came)
                self.out(t, 1, t, part)

    def total(self):
        w = self.w
        came = [jnp.concatenate([self.arrived(slot, part) for part in range(2)], axis=0) for slot in range(2)]
        return self.chip[w.z].astype(jnp.float32) + came[0] + came[1]

    def finish(self):
        w = self.w
        for t in range(4):
            src = self.part.at[pl.ds(t * 256, 128), :]
            w.remote(src, self.sib.at[t], self.ssend + t, self.srecv + t, w.i, w.sibling()).wait_send()

            @pl.when(w.z != t)
            def _():
                for part in range(2):
                    half = self.rows(self.chip, t, part)
                    w.remote(half, half, self.send + 2 * t + part, self.recv, w.i, w.sibling()).wait_send()


class PairGather:
    def __init__(self, w, buffer):
        self.w, self.buffer = w, buffer
        self.send, self.recv = w.take(3), w.take(3)

    def block(self, q, c):
        return rows_of(self.buffer, 256 * q + 128 * c, 128)

    def copies(self):
        w = self.w
        mine, theirs = self.block(w.place, w.c), self.block(1 - w.place, w.c)
        send, recv = self.send, self.recv
        return (
            w.remote(mine, mine, send, recv, w.i, w.chip(w.partner)),
            w.remote(mine, mine, send + 1, recv + 1, w.i, w.sibling()),
            w.remote(theirs, theirs, send + 2, recv + 2, w.i, w.sibling()),
        )

    def start(self):
        near, core, unused = self.copies()
        near.start()
        core.start()

    def arrive(self):
        w = self.w
        w.arrived(self.block(1 - w.place, w.c), self.recv)
        self.copies()[2].start()

    def other(self, n):
        w = self.w
        q = w.place + n * (1 - 2 * w.place)
        w.arrived(self.block(q, 1 - w.c), self.recv + 1 + n)

    def finish(self):
        for copy in self.copies():
            copy.wait_send()


class PairScatter:
    def __init__(self, w, part, sib, chip, got):
        self.w, self.part, self.sib, self.chip, self.got = w, part, sib, chip, got
        self.ssend, self.srecv = w.take(2), w.take(2)
        self.send, self.recv = w.take(), w.take()

    def swapped(self, q):
        w = self.w
        src = rows_of(self.part, 256 * q + 128 * (1 - w.c), 128)
        return w.remote(src, self.sib.at[q], self.ssend + q, self.srecv + q, w.i, w.sibling())

    def away(self):
        w = self.w
        return w.remote(self.chip.at[1 - w.place], self.got, self.send, self.recv, w.i, w.chip(w.partner))

    def add(self, q):
        w = self.w
        w.arrived(self.sib.at[q], self.srecv + q)
        mine = rows_of(self.part, 256 * q + 128 * w.c, 128)[...]
        self.chip[q] = low(mine.astype(jnp.float32) + self.sib[q].astype(jnp.float32))

    def total(self):
        self.w.arrived(self.got, self.recv)
        return self.chip[self.w.place].astype(jnp.float32) + self.got[...].astype(jnp.float32)

    def finish(self):
        self.swapped(0).wait_send()
        self.swapped(1).wait_send()
        self.away().wait_send()


def cols(ref, start, size):
    return ref.at[:, pl.ds(pl.multiple_of(start, 128), size)]


def rows_of(ref, start, size):
    return ref.at[pl.ds(pl.multiple_of(start, 128), size), :]


class Box:
    pass


def fields(kind):
    return [(name, *value) for name, value in vars(kind).items() if name[0] != "_"]


class FrontKept:
    fn = ((1024, 1024), B16)
    ci = ((HALO + 1024, 512), B16)
    gi = ((1024, 256), F32)
    q = ((1024, 128), F32)
    k = ((1024, 128), F32)
    v = ((1024, 256), F32)
    ge = ((1024, 128), F32)
    mixed = ((1024, 256), F32)
    states = ((4, 128, 256), F32)
    tinv = ((1024, 256), B16)
    u = ((1024, 256), F32)
    wm = ((1024, 128), B16)
    normed = ((1024, 256), B16)
    middle = ((128, 1024), F32)
    sn = ((512, 1024), B16)
    cg = ((512, 1024), B16)
    w_qkv = ((1024, 512), B16)
    w_gate = ((1024, 256), B16)
    w_in = ((1536, 1024), B16)
    w_out = ((256, 1024), B16)
    w_down = ((768, 1024), B16)
class FrontScratch:
    x = ((1024, 1024), B16)
    qkv_p = ((256, 512), B16)
    in_p = ((704, 256), B16)
    out_p = ((256, 256), B16)
    down_p = ((704, 256), B16)
    taps32 = ((8, 4096), F32)
    own_cot = ((128, 1024), B16)
    qk = ((1024, 256), B16)
    cum = ((1024, 1), F32)
    part = ((1024, 1024), B16)
    sib = ((4, 128, 1024), B16)
    chip = ((4, 128, 1024), B16)
    got = ((4, 128, 1024), B16)


def start_weights(w, b):
    i, s = w.i, w.s
    qs, qr = w.take(4), w.take(3)
    lowhalf = s < 4
    b.qr = qr

    @pl.when(lowhalf)
    def _():
        for t in range(4):
            w.push(
                b.qkv.at[:, 128 * t : 128 * t + 128],
                cols(b.qkv_p, 128 * (s // 2), 128),
                qs + t,
                qr + s // 2,
                i,
                4 * lax.rem(s, 2) + t,
            )

    @pl.when(jnp.logical_not(lowhalf))
    def _():
        for t in range(2):
            w.push(b.qkv.at[:, 256 * t : 256 * t + 256], b.qkv_p.at[:, 256:512], qs + t, qr + 2, i, 2 * (s - 4) + t)

    def sent():
        @pl.when(lowhalf)
        def _():
            for t in range(4):
                @pl.when(4 * lax.rem(s, 2) + t != s)
                def _():
                    src = b.qkv.at[:, 128 * t : 128 * t + 128]
                    w.remote(src, b.qkv_p.at[:, 0:128], qs + t, qr, i, w.sibling()).wait_send()

        @pl.when(jnp.logical_not(lowhalf))
        def _():
            for t in range(2):
                @pl.when(2 * (s - 4) + t != s)
                def _():
                    src = b.qkv.at[:, 256 * t : 256 * t + 256]
                    w.remote(src, b.qkv_p.at[:, 256:512], qs + t, qr + 2, i, w.sibling()).wait_send()

    return sent


def start_out_weights(w, b):
    send, recv = w.take(2), w.take(2)
    odd = lax.rem(w.s, 2)
    waits = []
    for n in range(2):
        src = b.out.at[256 * n : 256 * n + 256, :]
        waits.append(w.push(src, cols(b.out_p, 128 * odd, 128), send + n, recv + odd, w.s // 2, 2 * w.i + n))

    def landed():
        for r in range(2):
            w.arrived(b.out_p.at[:, 128 * r : 128 * r + 128], recv + r)

    def sent():
        for wait in waits:
            wait()

    return landed, sent


def start_ffn_weights(w, b):
    i, s = w.i, w.s
    send, recv = w.take(3), w.take(3)
    own = lax.rem(s, 2)
    across = w.remote(b.ffn_in, b.in_p, send, recv, i, lax.rem(s + 4, 8))
    across.start()
    waits = [across.wait_send]
    for n in range(2):
        dst = cols(b.down_p, 128 * own, 128)
        waits.append(w.push(b.ffn_out, dst, send + 1 + n, recv + 1 + own, s // 2, i + 4 * n))

    def landed():
        w.arrived(b.in_p, recv)
        for r in range(2):
            w.arrived(b.down_p.at[:, 128 * r : 128 * r + 128], recv + 1 + r)

    def sent():
        for wait in waits:
            wait()

    return landed, sent


def valid_rows(b, w):
    place = w.s * 128 + lax.broadcasted_iota(jnp.int32, (128, 1), 0)
    return place < b.lengths[0]


def first_norm_tile(b, t):
    rows = tile(t)
    x = b.x[rows, :].astype(jnp.float32)
    inv = lax.rsqrt(jnp.mean(x * x, axis=-1, keepdims=True) + epsilon)
    b.fn[rows, :] = low(x * inv * b.gains[0:1, :])


def own_head(b, w):
    pm = b.params[...]
    lane = lax.broadcasted_iota(jnp.int32, pm.shape, 1)
    return jnp.sum(jnp.where(lane == w.s, pm, 0.0), axis=1, keepdims=True)


def own_taps(b, w, n):
    s = w.s
    return jnp.concatenate(
        [
            b.taps32[n : n + 1, pl.ds(pl.multiple_of(128 * s, 128), 128)],
            b.taps32[n : n + 1, pl.ds(pl.multiple_of(1024 + 128 * s, 128), 128)],
            b.taps32[n : n + 1, pl.ds(pl.multiple_of(2048 + 256 * s, 128), 256)],
        ],
        axis=1,
    )


def conv_sums(b, w, t):
    window = b.ci[pl.ds(pl.multiple_of(t * CH, CH), CH + HALO), :].astype(jnp.float32)
    total = None
    for n in range(KCONV):
        at = HALO - (KCONV - 1) + n
        term = window[at : at + CH] * own_taps(b, w, n)
        total = term if total is None else total + term
    return total


def project_tile(b, w, t):
    rows = tile(t)
    f = b.fn[rows, :]
    b.ci[pl.ds(pl.multiple_of(t * CH + HALO, HALO), CH), :] = low(mm(f, b.w_qkv[...]))
    b.gi[rows, :] = mm(f, b.w_gate[...])
    hi = mm(f, b.head_w[...], NT)
    lane = lax.broadcasted_iota(jnp.int32, hi.shape, 1)
    pm = own_head(b, w)
    shift = jnp.sum(jnp.where(lane == w.s, hi, 0.0), axis=1, keepdims=True) + pm[1:2, :]
    erase = jnp.sum(jnp.where(lane == w.s + 8, hi, 0.0), axis=1, keepdims=True) + pm[2:3, :]
    line = lax.broadcasted_iota(jnp.int32, (CH, 128), 1)
    decay = -jnp.exp(pm[0:1, :]) * soft_plus(shift)
    b.ge[rows, :] = jnp.where(line == 0, decay, jnp.where(line == 1, sig(erase), shift))


def vectors_tile(b, w, t):
    rows = tile(t)
    total = conv_sums(b, w, t)
    act = total * sig(total)
    qa, ka = act[:, 0:DK], act[:, DK : 2 * DK]
    b.q[rows, :] = qa * lax.rsqrt(jnp.sum(qa * qa, axis=-1, keepdims=True) + epsilon) * DK ** (-0.5)
    b.k[rows, :] = ka * lax.rsqrt(jnp.sum(ka * ka, axis=-1, keepdims=True) + epsilon)
    b.v[rows, :] = act[:, 2 * DK :]


def rec_local(b, w, ts):
    row, col = grid_masks()
    attns = []
    for t in ts:
        vectors_tile(b, w, t)
        rows = tile(t)
        k = b.k[rows, :]
        cum, decay = decay_parts(b.ge[rows, 0:1], row, col)
        b.cum[rows, :] = cum
        b.qk[rows, :] = low(mm(b.q[rows, :], k, NT) * decay)
        attns.append(jnp.where(col < row, b.ge[rows, 1:2] * mm(k, k, NT) * decay, 0.0))
    for t, inv in zip(ts, unit_inverse(attns, row, col)):
        rows = tile(t)
        e, t16 = b.ge[rows, 1:2], low(inv)
        b.tinv[rows, :] = t16
        b.wm[rows, :] = low(mm(t16, (e * jnp.exp(b.cum[rows, :])) * b.k[rows, :]))
        b.u[rows, :] = mm(t16, e * b.v[rows, :])


def rec_step(b, t, state):
    rows = tile(t)
    b.states[t] = state
    cum = b.cum[rows, :]
    last = cum[CH - 1 : CH, :]
    s16 = low(state)
    u = b.u[rows, :] - mm(b.wm[rows, :], s16)
    b.u[rows, :] = u
    u16 = low(u)
    mixed = jnp.exp(cum) * mm(b.q[rows, :], s16) + mm(b.qk[rows, :], u16)
    b.mixed[rows, :] = mixed
    nxt = jnp.exp(last) * state + mm(b.k[rows, :] * jnp.exp(last - cum), u16, TN)
    gate = b.gi[rows, :]
    scale = lax.rsqrt(jnp.mean(mixed * mixed, axis=-1, keepdims=True) + epsilon)
    normed = low(mixed * scale * b.head_gain[...] * (gate * sig(gate)))
    b.normed[rows, :] = normed
    b.part[rows, :] = low(mm(normed, b.w_out[...]))
    return nxt


def front_phase(b, w):
    s, i = w.s, w.i
    own_rows = lambda ref: (lambda n: rows_of(ref, 128 * n, 128))
    x_gather = LineGather(w, own_rows(b.x))
    cg_gather = PairGather(w, b.cg)
    sn_gather = PairGather(w, b.sn)
    qkv_gather = GroupGather(w, lambda n: rows_of(b.w_qkv, 256 * n, 256))
    gate_gather = GroupGather(w, lambda n: rows_of(b.w_gate, 256 * n, 256))
    half = s // 4

    def in_block(n, start, size):
        return b.w_in.at[pl.ds(pl.multiple_of(start, 128), size), pl.ds(pl.multiple_of(256 * n, 256), 256)]

    thirds = (256, 256, b.ffn_in.shape[0] - 512)

    def own_third(k):
        return GroupGather(w, lambda n: in_block(n, 768 * half + 256 * k, thirds[k]))

    in_gathers = [own_third(k) for k in range(3)]
    across_gather = SquareGather(w, lambda n: in_block(n, 768 * (1 - half), 704))

    def start_third(k):
        in_gathers[k].start(b.ffn_in.at[256 * k : 256 * k + thirds[k], :])

    out_gather = GroupGather(w, lambda n: cols(b.w_out, 256 * n, 256))
    down_gather = SquareGather(w, lambda n: b.w_down.at[0:704, pl.ds(pl.multiple_of(256 * n, 256), 256)])
    scatter = LineScatter(w, b.part, b.sib, b.chip, b.got)
    own_x, own_c = w.take(), w.take()

    for start in (704, 1472):
        b.w_in[start : start + 64, :] = jnp.zeros((64, 1024), B16)
    b.w_down[704:768, :] = jnp.zeros((64, 1024), B16)
    w.meet_all()
    qkv_sent = start_weights(w, b)
    out_landed, out_sent = start_out_weights(w, b)
    x_gather.start(b.tokens)
    gate_gather.start(b.gate)
    start_third(0)
    keep_x = w.local(b.tokens, rows_of(b.x, 128 * s, 128), own_x)
    keep_x.start()
    b.ci[0:HALO, :] = jnp.zeros((HALO, 512), B16)
    b.taps32[0:KCONV, :] = b.taps[...].astype(jnp.float32)
    cot = jnp.where(valid_rows(b, w), b.cot_v[...].astype(jnp.float32), 0.0)
    b.own_cot[...] = low(cot)
    rows_of(b.cg, 128 * lax.rem(s, 4), 128)[...] = low(cot)
    w.arrived(b.qkv_p.at[:, 0:128], b.qr)
    w.arrived(b.qkv_p.at[:, 128:256], b.qr + 1)
    w.arrived(b.qkv_p.at[:, 256:512], b.qr + 2)
    qkv_gather.start(b.qkv_p)
    out_landed()
    out_gather.start(b.out_p)
    keep_x.wait()

    def norm_loop(n, carry):
        t = w.order(n)
        x_gather.arrive(t)
        x_gather.other(t)
        first_norm_tile(b, t)
        return carry

    lax.fori_loop(0, 4, norm_loop, 0)
    ffn_landed, ffn_sent = start_ffn_weights(w, b)
    cg_gather.start()
    qkv_gather.finish()
    gate_gather.finish()
    start_third(1)
    start_third(2)

    def project_loop(t, carry):
        project_tile(b, w, t)
        return carry

    lax.fori_loop(0, 4, project_loop, 0)
    x_gather.finish()
    out_gather.finish()

    def pair_loop(pair, state):
        rec_local(b, w, (2 * pair, 2 * pair + 1))

        @pl.when(pair == 0)
        def _():
            ffn_landed()
            across_gather.start(b.in_p)
            down_gather.start(b.down_p)

        for k in range(2):
            t = 2 * pair + k
            state = rec_step(b, t, state)
            scatter.swap(t)
        scatter.pass_on(2 * pair)
        scatter.pass_on(2 * pair + 1)
        return state

    lax.fori_loop(0, 2, pair_loop, jnp.zeros((DK, DV), F32))

    scatter.relay(0)
    scatter.relay(1)
    scatter.relay(2)
    scatter.relay(3)
    across_gather.relay()
    down_gather.relay()

    def own_half(which):
        @pl.when(w.half == which)
        def _():
            middle = b.tokens_v[...].astype(jnp.float32) + scatter.total()
            b.middle[...] = middle
            inv = lax.rsqrt(jnp.mean(middle * middle, axis=-1, keepdims=True) + epsilon)
            rows_of(b.sn, 128 * lax.rem(s, 4), 128)[...] = low(middle * inv * b.gains[1:2, :])
            sn_gather.start()

    own_half(0)
    cg_gather.arrive()
    own_half(1)
    for third in in_gathers:
        third.finish()
    across_gather.finish()
    down_gather.finish()
    qkv_sent()
    out_sent()
    ffn_sent()
    scatter.finish()

    def finish():
        cg_gather.finish()
        sn_gather.finish()

    return sn_gather, cg_gather, finish


class SquareScatter:
    def __init__(self, w, out, got, step=None, size=None):
        self.w, self.out, self.got = w, out, got
        self.step = step or out.shape[1] // 2
        self.size = size or self.step
        self.send, self.recv = w.take(6), w.take(6)

    def half(self, ref, n, k):
        return ref.at[n, self.step * k : self.step * k + self.size, :]

    def copy(self, n, k):
        w = self.w
        to = k if n == 2 else n
        slot = 2 * n + k
        return w.remote(
            self.half(self.out, n, k), self.half(self.got, n, k), self.send + slot, self.recv + slot, w.beside[to], w.s
        )

    def start_far(self, piece_of):
        self.out[2] = low(piece_of(3 - self.w.i))
        self.copy(2, 0).start()
        self.copy(2, 1).start()

    def start_near(self, piece_of):
        for n in range(2):
            self.out[n] = low(piece_of(self.w.beside[n]))
            self.copy(n, n).start()

    def relay(self):
        w = self.w
        for k in range(2):
            half = self.half(self.out, 1 - k, k)
            w.arrived(self.half(self.got, 2, k), self.recv + 4 + k)
            half[...] = low(half[...].astype(jnp.float32) + self.half(self.got, 2, k)[...].astype(jnp.float32))
            self.copy(1 - k, k).start()

    def total(self, own, dst):
        w = self.w
        for k in range(2):
            start = self.step * k
            total = own[start : start + self.size]
            for n in range(2):
                half = self.half(self.got, n, k)
                w.arrived(half, self.recv + 2 * n + k)
                total = total + half[...].astype(jnp.float32)
            dst[start : start + self.size, :] = low(total)

    def finish(self):
        for n in range(3):
            for k in range(2):
                self.copy(n, k).wait_send()


def ffn_tile(b, t):
    rows = tile(t)
    sn, cg = b.sn[rows, :], b.cg[rows, :]
    half = b.w_in.shape[0] // 2
    both = mm(sn, b.w_in[...], NT)
    gate, up = both[:, 0:half], both[:, half:]
    open_ = sig(gate)
    act = gate * open_
    hidden = low(act * up)
    b.hid[rows, :] = hidden
    b.part4[rows, :] = low(mm(hidden, b.w_down[...]))
    hgrad = mm(cg, b.w_down[...], NT)
    both_grad = jnp.concatenate(
        [low(hgrad * up * (open_ * (1.0 + gate * (1.0 - open_)))), low(hgrad * act)], axis=1
    )
    b.gug[rows, :] = both_grad
    b.part[rows, :] = low(mm(both_grad, b.w_in[...]))


def norm_back(x, gain, grad):
    inv = lax.rsqrt(jnp.mean(x * x, axis=-1, keepdims=True) + epsilon)
    unit = x * inv
    dunit = grad * gain
    return inv * (dunit - unit * jnp.mean(dunit * unit, axis=-1, keepdims=True)), grad * unit


def mixer_out_back(b, t, head_gain_sum):
    rows = tile(t)
    ng = mm(b.agr[rows, :], b.w_out[...], NT)
    gate = b.gi[rows, :]
    open_ = sig(gate)
    act = gate * open_
    gain = b.head_gain[...]
    mixed = b.mixed[rows, :]
    inv = lax.rsqrt(jnp.mean(mixed * mixed, axis=-1, keepdims=True) + epsilon)
    unit = mixed * inv
    dunit = ng * act * gain
    b.do[rows, :] = inv * (dunit - unit * jnp.mean(dunit * unit, axis=-1, keepdims=True))
    nu = ng * unit
    b.gg[rows, :] = low(nu * gain * (open_ * (1.0 + gate * (1.0 - open_))))
    return head_gain_sum + jnp.sum(nu * act, axis=0, keepdims=True)


def rec_back_chain(b, t, ds1, row, col):
    rows = tile(t)
    do = low(b.do[rows, :])
    b.dstates[t] = ds1
    cum = b.cum[rows, :]
    last = cum[CH - 1 : CH, :]
    du = mm(b.qk[rows, :], do, TN) + mm(b.k[rows, :] * jnp.exp(last - cum), ds1)
    du16 = low(du)
    b.dr[rows, :] = mm(b.tinv[rows, :], du16, TN)
    return jnp.exp(last) * ds1 + mm(b.q[rows, :] * jnp.exp(cum), do, TN) - mm(b.wm[rows, :], du16, TN)


def rec_back_tile(b, t, row, col):
    rows = tile(t)
    q, k, v, e = b.q[rows, :], b.k[rows, :], b.v[rows, :], b.ge[rows, 1:2]
    s0, ds1, u, do, dr = b.states[t], b.dstates[t], b.u[rows, :], b.do[rows, :], b.dr[rows, :]
    cum, decay = decay_parts(b.ge[rows, 0:1], row, col)
    last = cum[CH - 1 : CH, :]
    gamma, shrink, remain = jnp.exp(last), jnp.exp(cum), jnp.exp(last - cum)
    gram = jnp.where(col < row, mm(k, k, NT) * decay, 0.0)
    qk = mm(q, k, NT) * decay
    dp = jnp.where(col <= row, mm3(do, u, NT), 0.0)
    da = jnp.where(col < row, -mm3(dr, u, NT), 0.0)
    dqk = low(dp * decay)
    dag = da * gram
    zed = dp * qk + e * dag
    dgram = low(e * da * decay)
    nk = mm3(dr, s0, NT)
    m = mm3(do, s0, NT)
    lm = mm3(u, ds1, NT)
    row_nk = jnp.sum(nk * k, axis=1, keepdims=True)
    dv = e * dr
    de = (
        jnp.sum(dr * v, axis=1, keepdims=True)
        - shrink * row_nk
        + jnp.sum(dag, axis=1, keepdims=True)
    )
    dq = mm(dqk, k) + shrink * m
    dk = mm(dqk, q, TN) + mm(dgram, k) + mm(dgram, k, TN) - (e * shrink) * nk + remain * lm
    dshrink = jnp.sum(m * q, axis=1, keepdims=True) - e * row_nk
    rdr = remain * jnp.sum(lm * k, axis=1, keepdims=True)
    ones = jnp.ones((CH, 1), jnp.float32)
    dcum = jnp.sum(zed, axis=1, keepdims=True) - mmf(zed, ones, TN) + shrink * dshrink - rdr
    dlast = jnp.sum(rdr, axis=0, keepdims=True) + gamma * jnp.sum(
        jnp.sum(s0 * ds1, axis=1, keepdims=True), axis=0, keepdims=True
    )
    lower = (col <= row).astype(jnp.float32)
    dg = mmf(lower, dcum, TN) + dlast
    return dq, dk, dv, dg, de


def unit_back(x, grad):
    inv = lax.rsqrt(jnp.sum(x * x, axis=-1, keepdims=True) + epsilon)
    unit = x * inv
    return inv * (grad - unit * jnp.sum(grad * unit, axis=-1, keepdims=True))


def mixer_back_tile(b, w, t, row, col, sums):
    rows = tile(t)
    dq, dk, dv, dg, de = rec_back_tile(b, t, row, col)
    total = conv_sums(b, w, t)
    open_ = sig(total)
    act = total * open_
    dact = jnp.concatenate(
        [unit_back(act[:, 0:DK], dq * DK ** (-0.5)), unit_back(act[:, DK : 2 * DK], dk), dv], axis=1
    )
    dcs = dact * (open_ * (1.0 + total * (1.0 - open_)))
    b.dcs[0:CH, :] = dcs
    window = b.ci[pl.ds(pl.multiple_of(t * CH, CH), CH + HALO), :].astype(jnp.float32)
    ahead = b.dcs[...]
    taps_sums, p0, p1, p2, gain_sum = sums
    dci = None
    new_taps = []
    for n in range(KCONV):
        at = HALO - (KCONV - 1) + n
        new_taps.append(taps_sums[n] + jnp.sum(dcs * window[at : at + CH], axis=0, keepdims=True))
        back = KCONV - 1 - n
        term = ahead[back : back + CH] * own_taps(b, w, n)
        dci = term if dci is None else dci + term
    b.dcs[CH : CH + HALO, :] = dcs[0:HALO]
    dci16 = low(dci)
    b.cgd[rows, :] = dci16
    lane = lax.broadcasted_iota(jnp.int32, (CH, 16), 1)
    pm = own_head(b, w)
    shift = b.ge[rows, 2:3]
    dshift = dg * (-jnp.exp(pm[0:1, :])) * sig(shift)
    e = b.ge[rows, 1:2]
    dlogit = de * e * (1.0 - e)
    hg = low(jnp.where(lane == w.s, dshift, jnp.where(lane == w.s + 8, dlogit, 0.0)))
    b.hg[rows, :] = hg
    fp = mm(dci16, b.w_qkv[...], NT) + mm(hg, b.head_w[...]) + mm(b.gg[rows, :], b.w_gate[...], NT)
    b.part[rows, :] = low(fp)
    gain_part = jnp.sum(fp * b.fn[rows, :].astype(jnp.float32), axis=0, keepdims=True)
    return (
        tuple(new_taps),
        p0 + jnp.sum(dg * b.ge[rows, 0:1], axis=0, keepdims=True),
        p1 + jnp.sum(dshift, axis=0, keepdims=True),
        p2 + jnp.sum(dlogit, axis=0, keepdims=True),
        gain_sum + gain_part,
    )


class LayerOut:
    output = ((128, 1024), B16)
    input_grad = ((128, 1024), B16)
    gains_grad = ((2, 1024), F32)
    head_gain_grad = ((1, 256), F32)
    params_grad = ((8, 128), F32)
    head_w_grad = ((16, 1024), F32)
    conv_grad = ((4, 4096), F32)
    qkv_back = ((256, 512), B16)
    gate_back = ((256, 256), B16)
    in_back = ((704, 256), B16)
    out_back = ((512, 128), B16)
    down_back = ((704, 128), B16)
class RestScratch:
    hid = ((512, 768), B16)
    gug = ((512, 1536), B16)
    part4 = ((512, 1024), B16)
    sib4 = ((2, 128, 1024), B16)
    chip4 = ((2, 128, 1024), B16)
    got4 = ((128, 1024), B16)
    sib6 = ((2, 128, 1024), B16)
    chip6 = ((2, 128, 1024), B16)
    got6 = ((128, 1024), B16)
    own_ag = ((128, 1024), B16)
    mgrad = ((128, 1024), F32)
    gg = ((1024, 256), B16)
    dstates = ((4, 128, 256), F32)
    dcs = ((CH + HALO, 512), F32)
    cgd = ((1024, 512), B16)
    hg = ((1024, 16), B16)
    in_out = ((3, 1536, 256), B16)
    in_got = ((3, 1536, 256), B16)
    down_out = ((3, 704, 256), B16)
    down_got = ((3, 704, 256), B16)
    out_out = ((3, 256, 256), B16)
    out_got = ((3, 256, 256), B16)
    qkv_out = ((3, 256, 512), B16)
    qkv_got = ((3, 256, 512), B16)
    gate_out = ((3, 256, 256), B16)
    gate_got = ((3, 256, 256), B16)
    in_sum = ((1536, 256), B16)
    in_other = ((704, 256), B16)
    down_sum = ((704, 256), B16)
    down_parts = ((2, 704, 128), B16)
    out_sum = ((256, 256), B16)
    qkv_sum = ((256, 512), B16)
    small = ((8, 1024), F32)
    small_got = ((4, 8, 1024), F32)
    small_sum = ((8, 1024), F32)
    small_all = ((8, 8, 1024), F32)


def grads_home(w, b):
    i, h = w.i, w.s
    send, recv = w.take(9), w.take(10)
    quarter, pair, half = lax.rem(h, 4), lax.rem(h, 2), h // 4

    def across():
        block = rows_of(b.in_sum, 768 * (1 - half), 704)
        return w.remote(block, b.in_other, send, recv + 4, i, lax.rem(h + 4, 8))

    down_to = [(b.down_sum.at[:, 128 * r : 128 * r + 128], quarter, 2 * i + r) for r in range(2)]

    def ffn():
        across().start()
        for r, (src, di, dj) in enumerate(down_to):
            w.push(src, b.down_parts.at[half], send + 2 + r, recv + 8 + half, di, dj)

    def ffn_done():
        across().wait_send()
        for r, (src, di, dj) in enumerate(down_to):
            @pl.when((di != i) | (dj != h))
            def _():
                w.remote(src, src, send + 2 + r, recv, i, w.sibling()).wait_send()

        w.arrived(b.in_other, recv + 4)
        mine = rows_of(b.in_sum, 768 * half, 704)[...]
        b.in_back[...] = low(mine.astype(jnp.float32) + b.in_other[...].astype(jnp.float32))
        for r in range(2):
            w.arrived(b.down_parts.at[r], recv + 8 + r)
        b.down_back[...] = low(b.down_parts[0].astype(jnp.float32) + b.down_parts[1].astype(jnp.float32))

    def mixer():
        to = (
            (b.qkv_sum.at[:, 0:128], cols(b.qkv_back, 128 * quarter, 128), recv + quarter, half),
            (b.qkv_sum.at[:, 128:256], cols(b.qkv_back, 128 * quarter, 128), recv + quarter, 2 + half),
            (b.qkv_sum.at[:, 256:512], cols(b.qkv_back, 256 * pair, 256), recv + pair, 4 + h // 2),
        )
        return [w.push(src, dst, send + 4 + n, sem, i, dj) for n, (src, dst, sem, dj) in enumerate(to)]

    def mixer_out():
        waits = []
        for r in range(2):
            src = b.out_sum.at[:, 128 * r : 128 * r + 128]
            dst = rows_of(b.out_back, 256 * pair, 256)
            waits.append(w.push(src, dst, send + 7 + r, recv + 6 + pair, h // 2, 2 * i + r))
        return waits

    def landed():
        @pl.when(h < 4)
        def _():
            for t in range(4):
                w.arrived(b.qkv_back.at[:, 128 * t : 128 * t + 128], recv + t)

        @pl.when(h >= 4)
        def _():
            for t in range(2):
                w.arrived(b.qkv_back.at[:, 256 * t : 256 * t + 256], recv + t)

        for r in range(2):
            w.arrived(b.out_back.at[256 * r : 256 * r + 256, :], recv + 6 + r)

    return ffn, ffn_done, mixer, mixer_out, landed


def small_sums(w, b, send, recv, send2, recv2):
    copies = []
    for d in range(1, 4):
        copy = w.remote(b.small, b.small_got.at[d], send + d, recv + d, lax.rem(w.i + d, 4), w.s)
        copy.start()
        copies.append(copy)

    def middle():
        total = b.small[...]
        for d in range(1, 4):
            w.arrived(b.small_got.at[d], recv + d)
            total = total + b.small_got[d]
        b.small_sum[...] = total
        b.small_all[w.s] = total
        for d in range(1, 8):
            copy = w.remote(b.small_sum, b.small_all.at[w.s], send2 + d, recv2 + d, w.i, lax.rem(w.s + d, 8))
            copy.start()
            copies.append(copy)

    def end():
        for d in range(1, 8):
            w.arrived(b.small_all.at[lax.rem(w.s + 8 - d, 8)], recv2 + d)
        for copy in copies:
            copy.wait_send()
        gains = b.small_all[0, 0:2, :]
        head_gain = b.small_all[0, 2:3, 0:256]
        for n in range(1, 8):
            gains = gains + b.small_all[n, 0:2, :]
            head_gain = head_gain + b.small_all[n, 2:3, 0:256]
        b.gains_grad[...] = gains
        b.head_gain_grad[...] = head_gain
        for n in range(8):
            b.params_grad[n : n + 1, :] = b.small_all[n, 3:4, 0:128]
            b.head_w_grad[n : n + 1, :] = b.small_all[n, 4:5, :]
            b.head_w_grad[8 + n : 9 + n, :] = b.small_all[n, 5:6, :]
            for k in range(KCONV):
                line = b.small_all[n, 6 + k // 2 : 7 + k // 2, 512 * (k % 2) : 512 * (k % 2) + 512]
                b.conv_grad[k : k + 1, 128 * n : 128 * n + 128] = line[:, 0:128]
                b.conv_grad[k : k + 1, 1024 + 128 * n : 1152 + 128 * n] = line[:, 128:256]
                b.conv_grad[k : k + 1, 2048 + 256 * n : 2304 + 256 * n] = line[:, 256:512]

    return middle, end


def rest_phase(b, w, sn_gather, cg_gather, front_finish):
    s = w.s
    half_rows = lambda ref: (lambda n: rows_of(ref, 128 * n, 128))
    ag_gather = LineGather(w, half_rows(b.agr))
    scatter4 = PairScatter(w, b.part4, b.sib4, b.chip4, b.got4)
    scatter6 = PairScatter(w, b.part, b.sib6, b.chip6, b.got6)
    scatter8 = LineScatter(w, b.part, b.sib, b.chip, b.got)
    in_sum = SquareScatter(w, b.in_out, b.in_got, 768, 704)
    down_sum = SquareScatter(w, b.down_out, b.down_got)
    out_sum = SquareScatter(w, b.out_out, b.out_got)
    qkv_sum = SquareScatter(w, b.qkv_out, b.qkv_got)
    gate_sum = SquareScatter(w, b.gate_out, b.gate_got)
    home_ffn, home_ffn_done, home_qkv, home_out, home_landed = grads_home(w, b)
    sm = (w.take(4), w.take(4), w.take(8), w.take(8))

    def ffn_loop(n, carry):
        @pl.when(n == 1)
        def _():
            sn_gather.arrive()

        sn_gather.other(n)
        cg_gather.other(n)
        q = w.place + n * (1 - 2 * w.place)
        ffn_tile(b, q)
        scatter6.swapped(q).start()
        scatter4.swapped(q).start()
        return carry

    lax.fori_loop(0, 2, ffn_loop, 0)
    scatter6.add(1 - w.place)
    scatter6.away().start()
    scatter6.add(w.place)

    def in_piece(n):
        return mm(b.gug[...], cols(b.sn, 256 * n, 256)[...], TN)

    def down_piece(n):
        return mm(b.hid[...], cols(b.cg, 256 * n, 256)[...], TN)[0:704]

    in_sum.start_far(in_piece)
    down_sum.start_far(down_piece)
    second_grad = scatter6.total()
    back, share = norm_back(b.middle[...], b.gains[1:2, :], second_grad)
    b.small[1:2, :] = jnp.sum(share, axis=0, keepdims=True)
    mgrad = b.own_cot[...].astype(jnp.float32) + back
    b.mgrad[...] = mgrad
    own = low(mgrad)
    b.own_ag[...] = own
    rows_of(b.agr, 128 * s, 128)[...] = own
    ag_gather.start(b.own_ag)
    in_sum.start_near(in_piece)
    down_sum.start_near(down_piece)
    scatter4.add(1 - w.place)
    scatter4.away().start()
    scatter4.add(w.place)
    row, col = grid_masks()

    def out_loop(n, head_gain_sum):
        t = w.order(n)
        ag_gather.arrive(t)
        ag_gather.other(t)
        out = mixer_out_back(b, t, head_gain_sum)

        @pl.when(n == 2)
        def _():
            in_sum.relay()
            down_sum.relay()

        return out

    head_gain_sum = lax.fori_loop(0, 4, out_loop, jnp.zeros((1, DV), F32))
    scatter6.finish()
    def out_piece(n):
        return mm(b.normed[...], cols(b.agr, 256 * n, 256)[...], TN)


    def gate_piece(n):
        return mm(cols(b.fn, 256 * n, 256)[...], b.gg[...], TN)

    out_sum.start_far(out_piece)
    gate_sum.start_far(gate_piece)
    out_sum.start_near(out_piece)
    gate_sum.start_near(gate_piece)

    def chain_loop(n, ds1):
        return rec_back_chain(b, 3 - n, ds1, row, col)

    lax.fori_loop(0, 4, chain_loop, jnp.zeros((DK, DV), F32))
    in_sum.total(in_piece(w.i), b.in_sum)
    down_sum.total(down_piece(w.i), b.down_sum)
    home_ffn()
    b.dcs[CH : CH + HALO, :] = jnp.zeros((HALO, 512), F32)

    def back_loop(n, sums):
        t = 3 - n
        sums = mixer_back_tile(b, w, t, row, col, sums)
        scatter8.swap(t)

        @pl.when(n == 1)
        def _():
            out_sum.relay()
            gate_sum.relay()

        @pl.when(n > 0)
        def _():
            scatter8.pass_on(t + 1)

        @pl.when(n > 1)
        def _():
            scatter8.relay(t + 2)

        return sums

    one = jnp.zeros((1, 1), F32)
    taps_sums, p0, p1, p2, gain_sum = lax.fori_loop(
        0, 4, back_loop, (tuple(jnp.zeros((1, 512), F32) for n in range(KCONV)), one, one, one, jnp.zeros((1, 1024), F32))
    )
    scatter8.pass_on(0)
    scatter8.relay(1)

    def qkv_piece(n):
        return mm(cols(b.fn, 256 * n, 256)[...], b.cgd[...], TN)

    qkv_sum.start_far(qkv_piece)
    qkv_sum.start_near(qkv_piece)
    scatter8.relay(0)
    b.small[0:1, :] = gain_sum / b.gains[0:1, :]
    b.small[2:3, :] = jnp.concatenate([head_gain_sum, jnp.zeros((1, 1024 - DV), F32)], axis=1)
    lane = lax.broadcasted_iota(jnp.int32, (1, 1024), 1)
    b.small[3:4, :] = jnp.where(lane == 0, p0, jnp.where(lane == 1, p1, jnp.where(lane == 2, p2, 0.0)))
    head_rows = mm(b.hg[...], b.fn[...], TN)
    line = lax.broadcasted_iota(jnp.int32, head_rows.shape, 0)
    b.small[4:5, :] = jnp.sum(jnp.where(line == s, head_rows, 0.0), axis=0, keepdims=True)
    b.small[5:6, :] = jnp.sum(jnp.where(line == s + 8, head_rows, 0.0), axis=0, keepdims=True)
    b.small[6:7, :] = jnp.concatenate([taps_sums[0], taps_sums[1]], axis=1)
    b.small[7:8, :] = jnp.concatenate([taps_sums[2], taps_sums[3]], axis=1)
    small_middle, small_end = small_sums(w, b, *sm)
    out_sum.total(out_piece(w.i), b.out_sum)
    waits = home_out()
    gate_sum.total(gate_piece(w.i), b.gate_back)
    qkv_sum.relay()
    small_middle()
    b.output[...] = low(jnp.where(valid_rows(b, w), b.middle[...] + scatter4.total(), 0.0))
    qkv_sum.total(qkv_piece(w.i), b.qkv_sum)
    waits = waits + home_qkv()
    first_grad = scatter8.total()
    back, unused_share = norm_back(b.tokens_v[...].astype(jnp.float32), b.gains[0:1, :], first_grad)
    b.input_grad[...] = low(b.mgrad[...] + back)
    home_ffn_done()
    small_end()
    home_landed()
    for wait in waits:
        wait()
    for part in (in_sum, down_sum, out_sum, qkv_sum, gate_sum):
        part.finish()
    scatter4.finish()
    scatter8.finish()
    ag_gather.finish()
    front_finish()


def layer_kernel(dp, seq, *refs):
    b = Box()
    (
        b.tokens,
        b.qkv,
        b.gate,
        b.ffn_in,
        b.out,
        b.ffn_out,
        b.gains,
        b.head_gain,
        b.params,
        b.head_w,
        b.taps,
        b.tokens_v,
        b.cot_v,
        b.lengths,
    ) = refs[:14]
    kinds = fields(LayerOut) + fields(FrontKept) + fields(FrontScratch) + fields(RestScratch)
    for (name, shape, kind), ref in zip(kinds, refs[14:]):
        setattr(b, name, ref)
    b.do, b.dr, b.agr = b.mixed, b.gi, b.x
    w = Wires(dp, seq, refs[-1])
    rest_phase(b, w, *front_phase(b, w))


def layer(dp, seq, *arrays):
    outs = pl.pallas_call(
        functools.partial(layer_kernel, dp, seq),
        out_shape=tuple(jax.ShapeDtypeStruct(shape, kind) for _, shape, kind in fields(LayerOut)),
        in_specs=[ANY] * 6 + [IN_VMEM] * 7 + [pl.BlockSpec(memory_space=pltpu.SMEM)],
        out_specs=(IN_VMEM,) * len(fields(LayerOut)),
        scratch_shapes=[
            pltpu.VMEM(shape, kind)
            for _, shape, kind in fields(FrontKept) + fields(FrontScratch) + fields(RestScratch)
        ]
        + [pltpu.SemaphoreType.DMA((500,))],
        compiler_params=pltpu.CompilerParams(collective_id=0, has_side_effects=True, vmem_limit_bytes=62 << 20),
        name="layer",
    )(*arrays)
    made = Box()
    for (name, shape, kind), out in zip(fields(LayerOut), outs):
        setattr(made, name, out)
    return made


class FinalOut:
    output = ((128, 1024), B16)
    input_grad = ((128, 1024), B16)
    gains_grad = ((2, 1024), F32)
    head_gain_grad = ((1, 256), F32)
    params_grad = ((3, 8), F32)
    head_w_grad = ((16, 1024), F32)
    conv_grad = ((4, 4096), F32)
    qkv_back = ((256, 512), F32)
    gate_back = ((256, 256), F32)
    in_back = ((704, 256), F32)
    out_back = ((512, 128), F32)
    down_back = ((704, 128), F32)


def final_kernel(*refs):
    count = len(fields(FinalOut))
    srcs, outs, held, sems = refs[:count], refs[count : 2 * count], refs[2 * count : -1], refs[-1]
    copies = [pltpu.make_async_copy(src, buf, sems.at[n]) for n, (src, buf) in enumerate(zip(srcs, held))]
    for copy in copies:
        copy.start()
    for n, ((name, shape, kind), copy, buf, out) in enumerate(zip(fields(FinalOut), copies, held, outs)):
        copy.wait()
        if n == 4:
            out[...] = jnp.transpose(buf[...])[0:3, :]
        else:
            out[...] = buf[0 : shape[0], :].astype(kind)


def final(made):
    names = fields(FinalOut)
    arrays = [getattr(made, name) for name, _, _ in names]
    outs = pl.pallas_call(
        final_kernel,
        out_shape=tuple(jax.ShapeDtypeStruct(shape, kind) for _, shape, kind in names),
        in_specs=[ANY] * len(names),
        out_specs=(IN_VMEM,) * len(names),
        scratch_shapes=[pltpu.VMEM(array.shape, array.dtype) for array in arrays]
        + [pltpu.SemaphoreType.DMA((len(names),))],
        compiler_params=pltpu.CompilerParams(vmem_limit_bytes=62 << 20),
        name="final",
    )(*arrays)
    done = Box()
    for (name, shape, kind), out in zip(names, outs):
        setattr(done, name, out)
    return done


def fast_body(
    dp,
    seq,
    tokens,
    lengths,
    cotangent,
    norm_gains,
    head_gain,
    head_params,
    qkv_weight,
    gate_weight,
    head_weight,
    conv_weight,
    out_weight,
    ffn_in,
    ffn_out,
):
    made = layer(
        dp,
        seq,
        tokens[0],
        qkv_weight,
        gate_weight,
        ffn_in.T,
        out_weight,
        ffn_out,
        norm_gains,
        head_gain[None],
        head_params,
        head_weight.T,
        conv_weight.T,
        tokens[0],
        cotangent[0],
        lengths,
    )
    r = final(made)
    return (
        r.output[None],
        r.input_grad[None],
        r.gains_grad,
        r.head_gain_grad[0],
        r.params_grad,
        r.qkv_back,
        r.gate_back,
        r.head_w_grad.T,
        r.conv_grad.T,
        r.out_back,
        r.in_back.T,
        r.down_back,
    )


def choose_body(dp, seq):
    def chosen(*arrays):
        tokens, head_params = arrays[0], arrays[5]
        if (dp, seq) == (4, 8) and tokens.shape[0] == 1 and head_params.shape[1] == seq:
            return fast_body(dp, seq, *arrays)
        return general_body(*arrays)

    return chosen


def solution(mesh):
    dp, seq = mesh.shape["dp"], mesh.shape["seq"]
    placed = (
        P("dp", "seq", None),
        P("dp"),
        P("dp", "seq", None),
        P(),
        P(),
        P(),
        P("dp", "seq"),
        P("dp", "seq"),
        P(),
        P(),
        P("dp", "seq"),
        P("dp", "seq"),
        P("dp", "seq"),
    )
    return jax.shard_map(
        choose_body(dp, seq),
        mesh=mesh,
        in_specs=placed,
        out_specs=(
            P("dp", "seq", None),
            P("dp", "seq", None),
            P(),
            P(),
            P(),
            P("dp", "seq"),
            P("dp", "seq"),
            P(),
            P(),
            P("dp", "seq"),
            P("dp", "seq"),
            P("dp", "seq"),
        ),
        check_vma=False,
    )
```

```python
import functools

import jax
import jax.numpy as jnp
from jax import lax
from jax.experimental import pallas as pl
from jax.experimental.pallas import tpu as pltpu
from jax.sharding import PartitionSpec as P

CH = 256
DK = 128
DV = 256
KCONV = 4
TILE = 64


HIGHEST = lax.Precision.HIGHEST
epsilon = 1e-06


def passed_along(block, axis, distance):
    devices = range(lax.axis_size(axis))
    route = [(i - distance, i) for i in devices if i - distance in devices]
    return lax.ppermute(block, axis, route)


def rms_scale(values, gain_row):
    return (
        values * lax.rsqrt(jnp.mean(values * values, axis=-1, keepdims=True) + epsilon) * gain_row
    )


def unit_rows(values):
    return values * lax.rsqrt(jnp.sum(values * values, axis=-1, keepdims=True) + epsilon)


def block_step(state_now, query_vecs, key_vecs, value_vecs, log_decay, erase_rate):
    length = query_vecs.shape[1]
    cumulative = jnp.cumsum(log_decay, axis=1)
    row_index = jnp.arange(length)[:, None]
    col_index = jnp.arange(length)[None, :]
    strict = col_index < row_index
    within = col_index <= row_index
    spread = cumulative[:, :, None] - cumulative[:, None, :]
    lower_decay = jnp.where(strict, jnp.exp(jnp.where(strict, spread, 0.0)), 0.0)
    causal = jnp.where(within, jnp.exp(jnp.where(within, spread, 0.0)), 0.0)
    key_gram = jnp.einsum("htk,hsk->hts", key_vecs, key_vecs, precision=HIGHEST)
    query_gram = jnp.einsum("htk,hsk->hts", query_vecs, key_vecs, precision=HIGHEST)
    negated = -(erase_rate[:, :, None] * key_gram * lower_decay)
    identity = jnp.eye(length, dtype=jnp.float32)
    inverse = identity + negated
    powered = negated
    for level_index in range(length.bit_length() - 2):
        powered = jnp.einsum("hts,hsr->htr", powered, powered, precision=HIGHEST)
        inverse = jnp.einsum("hts,hsr->htr", inverse, identity + powered, precision=HIGHEST)
    shrink = jnp.exp(cumulative)
    recalled = jnp.einsum("htk,hkw->htw", key_vecs, state_now, precision=HIGHEST)
    target = erase_rate[:, :, None] * value_vecs - (erase_rate * shrink)[:, :, None] * recalled
    updates = jnp.einsum("hts,hsw->htw", inverse, target, precision=HIGHEST)
    read_out = shrink[:, :, None] * jnp.einsum(
        "htk,hkw->htw", query_vecs, state_now, precision=HIGHEST
    )
    read_out = read_out + jnp.einsum(
        "hts,hsw->htw", query_gram * causal, updates, precision=HIGHEST
    )
    remain = jnp.exp(cumulative[:, -1:] - cumulative)
    state_next = jnp.exp(cumulative[:, -1])[:, None, None] * state_now
    state_next = state_next + jnp.einsum(
        "hsk,hsw->hkw", key_vecs * remain[:, :, None], updates, precision=HIGHEST
    )
    return (state_next, read_out)


def run_tiles(query_vecs, key_vecs, value_vecs, log_decay, erase_rate, state_start):
    row_count, head_count, key_width = query_vecs.shape
    tile_count = row_count // TILE

    def arrange(tensor):
        return jnp.swapaxes(tensor.reshape((tile_count, TILE, head_count) + tensor.shape[2:]), 1, 2)

    inputs = (
        arrange(query_vecs),
        arrange(key_vecs),
        arrange(value_vecs),
        arrange(log_decay),
        arrange(erase_rate),
    )

    def advance(state_now, sliced):
        return jax.checkpoint(block_step)(state_now, *sliced)

    state_end, outputs = lax.scan(advance, state_start, inputs)
    outputs = jnp.swapaxes(outputs, 1, 2).reshape(row_count, head_count, outputs.shape[-1])
    return (outputs, state_end)


def mixer_inputs(conv_in, edge_rows, head_in, conv_taps, head_params):
    block_len = conv_in.shape[1]
    head_count = head_params.shape[1]
    extended = jnp.concatenate([edge_rows, conv_in], axis=1)
    conv_sum = extended[:, 0:block_len] * conv_taps[:, 0]
    for offset in range(1, conv_taps.shape[1]):
        conv_sum = conv_sum + extended[:, offset : offset + block_len] * conv_taps[:, offset]
    activated = jax.nn.silu(conv_sum)
    key_span = head_count * DK
    lead = activated.shape[:2]
    query_vecs = unit_rows(activated[..., 0:key_span].reshape(lead + (head_count, DK))) * DK ** (
        -0.5
    )
    key_vecs = unit_rows(activated[..., key_span : 2 * key_span].reshape(lead + (head_count, DK)))
    value_vecs = activated[..., 2 * key_span :].reshape(lead + (head_count, DV))
    log_decay = -jnp.exp(head_params[0]) * jax.nn.softplus(
        head_in[..., 0:head_count] + head_params[1]
    )
    erase_rate = jax.nn.sigmoid(head_in[..., head_count : 2 * head_count] + head_params[2])
    return (query_vecs, key_vecs, value_vecs, log_decay, erase_rate)


def gated_norm(mixed, gate_in, head_gain):
    shaped = gate_in.reshape(mixed.shape)
    normed = (
        mixed * lax.rsqrt(jnp.mean(mixed * mixed, axis=-1, keepdims=True) + epsilon) * head_gain
    )
    return (normed * jax.nn.silu(shaped)).reshape(gate_in.shape)


def local_tiles(query_vecs, key_vecs, value_vecs, log_decay, erase_rate):
    key_width = key_vecs.shape[-1]
    value_width = value_vecs.shape[-1]
    head_count = key_vecs.shape[2]
    padded = jnp.concatenate(
        [jnp.zeros(value_vecs.shape[:3] + (key_width,), jnp.float32), value_vecs], axis=-1
    )
    start_map = jnp.concatenate(
        [jnp.eye(key_width, dtype=jnp.float32), jnp.zeros((key_width, value_width), jnp.float32)],
        axis=1,
    )
    start_map = jnp.broadcast_to(start_map, (head_count, key_width, key_width + value_width))

    def single(query_one, key_one, value_one, decay_one, erase_one):
        return run_tiles(query_one, key_one, value_one, decay_one, erase_one, start_map)

    return jax.vmap(single)(query_vecs, key_vecs, padded, log_decay, erase_rate)


def post_mix(local_out, incoming, gate_in, head_gain):
    mixed = local_out[..., DK:] + jnp.einsum(
        "snhk,shkv->snhv", local_out[..., 0:DK], incoming, precision=HIGHEST
    )
    return gated_norm(mixed, gate_in, head_gain)


def swiglu(gate_up):
    split_at = gate_up.shape[-1] // 2
    return jax.nn.silu(gate_up[:, 0:split_at]) * gate_up[:, split_at:]


def matmul_maps(left, right):
    return jnp.einsum("shij,shjk->shik", left, right, precision=HIGHEST)


def apply_map(maps, state_now):
    return matmul_maps(maps[0], state_now) + maps[1]


def general_body(
    tokens,
    lengths,
    cotangent,
    norm_gains,
    head_gain,
    head_params,
    qkv_weight,
    gate_weight,
    head_weight,
    conv_weight,
    out_weight,
    ffn_in,
    ffn_out,
):
    seq_count, block_len, model_width = tokens.shape
    row_count = seq_count * block_len
    position = lax.axis_index("seq") * block_len + jnp.arange(block_len, dtype=jnp.int32)
    valid_rows = (position[None, :] < lengths[:, None]).reshape(row_count, 1)
    col_parts = (
        lax.all_gather(qkv_weight, "seq", axis=1, tiled=True),
        lax.all_gather(gate_weight, "seq", axis=1, tiled=True),
        lax.all_gather(out_weight, "seq", axis=1, tiled=True),
        lax.all_gather(ffn_in, "seq", axis=1, tiled=True),
        lax.all_gather(ffn_out, "seq", axis=1, tiled=True),
    )
    gathered = (
        lax.all_gather(col_parts[0], "dp", axis=0, tiled=True),
        lax.all_gather(col_parts[1], "dp", axis=0, tiled=True),
        lax.all_gather(col_parts[2], "dp", axis=0, tiled=True),
        lax.all_gather(col_parts[3], "dp", axis=0, tiled=True),
        lax.all_gather(col_parts[4], "dp", axis=0, tiled=True),
    )
    w_qkv, w_gate, w_out, w_in, w_down = gathered
    inputs = tokens.reshape(row_count, model_width).astype(jnp.float32)
    first_norm = rms_scale(inputs, norm_gains[0]).astype(jnp.bfloat16)
    conv_in = jnp.dot(first_norm, w_qkv, preferred_element_type=jnp.float32).astype(jnp.bfloat16)
    head_in = jnp.dot(first_norm, head_weight, preferred_element_type=jnp.float32)
    gate_in = jnp.dot(first_norm, w_gate, preferred_element_type=jnp.float32)
    conv_width = conv_in.shape[-1]
    conv_rows = conv_in.reshape(seq_count, block_len, conv_width)
    edge_cut = block_len - (KCONV - 1)
    edge_rows = passed_along(conv_rows[:, edge_cut:], "seq", 1)
    mix_args = (
        conv_rows.astype(jnp.float32),
        edge_rows.astype(jnp.float32),
        head_in.reshape(seq_count, block_len, -1),
        conv_weight.astype(jnp.float32),
        head_params,
    )
    vectors = mixer_inputs(*mix_args)
    local_out, end_states = local_tiles(*vectors)
    carry_maps = (end_states[..., 0:DK], end_states[..., DK:])

    def relay_state(step_index, state_now):
        return passed_along(apply_map(carry_maps, state_now), "seq", 1)

    incoming = lax.fori_loop(
        0, lax.axis_size("seq") - 1, relay_state, jnp.zeros_like(carry_maps[1])
    )
    post_args = (local_out, incoming, gate_in, head_gain)
    normed = post_mix(*post_args).astype(jnp.bfloat16)
    attended = jnp.dot(normed, w_out, preferred_element_type=jnp.float32)
    middle = inputs + attended
    second_norm = rms_scale(middle, norm_gains[1]).astype(jnp.bfloat16)
    gate_up = jnp.dot(second_norm, w_in, preferred_element_type=jnp.float32)
    hidden = swiglu(gate_up).astype(jnp.bfloat16)
    carried = jnp.dot(hidden, w_down, preferred_element_type=jnp.float32)
    output = jnp.where(valid_rows, middle + carried, 0.0).astype(jnp.bfloat16)
    col_again = (
        lax.all_gather(qkv_weight, "seq", axis=1, tiled=True),
        lax.all_gather(gate_weight, "seq", axis=1, tiled=True),
        lax.all_gather(out_weight, "seq", axis=1, tiled=True),
        lax.all_gather(ffn_in, "seq", axis=1, tiled=True),
        lax.all_gather(ffn_out, "seq", axis=1, tiled=True),
    )
    regathered = (
        lax.all_gather(col_again[0], "dp", axis=0, tiled=True),
        lax.all_gather(col_again[1], "dp", axis=0, tiled=True),
        lax.all_gather(col_again[2], "dp", axis=0, tiled=True),
        lax.all_gather(col_again[3], "dp", axis=0, tiled=True),
        lax.all_gather(col_again[4], "dp", axis=0, tiled=True),
    )
    w_qkv, w_gate, w_out, w_in, w_down = regathered
    upstream = jnp.where(
        valid_rows, cotangent.reshape(row_count, model_width).astype(jnp.float32), 0.0
    )
    carried_grad = upstream.astype(jnp.bfloat16)
    grad_down = jnp.einsum("nf,nd->fd", hidden, carried_grad, preferred_element_type=jnp.float32)
    hidden_grad = jnp.einsum("nd,fd->nf", carried_grad, w_down, preferred_element_type=jnp.float32)
    unused, swiglu_back = jax.vjp(swiglu, gate_up)
    gate_up_grad = swiglu_back(hidden_grad)[0].astype(jnp.bfloat16)
    grad_in = jnp.einsum("nd,nf->df", second_norm, gate_up_grad, preferred_element_type=jnp.float32)
    second_grad = jnp.einsum("nf,df->nd", gate_up_grad, w_in, preferred_element_type=jnp.float32)
    unused, second_back = jax.vjp(rms_scale, middle, norm_gains[1])
    middle_back, gain_two = second_back(second_grad)
    middle_grad = upstream + middle_back
    attended_grad = middle_grad.astype(jnp.bfloat16)
    grad_out = jnp.einsum("nv,nd->vd", normed, attended_grad, preferred_element_type=jnp.float32)
    normed_grad = jnp.einsum("nd,vd->nv", attended_grad, w_out, preferred_element_type=jnp.float32)
    unused, post_back = jax.vjp(post_mix, *post_args)
    local_grad, incoming_local, gate_in_grad, head_gain_grad = post_back(normed_grad)
    flipped = (jnp.swapaxes(carry_maps[0], -1, -2), incoming_local)

    def relay_grad(step_index, grad_now):
        return passed_along(apply_map(flipped, grad_now).astype(jnp.bfloat16), "seq", -1).astype(
            jnp.float32
        )

    outgoing = lax.fori_loop(
        0, lax.axis_size("seq") - 1, relay_grad, jnp.zeros_like(incoming_local)
    )
    map_grad = jnp.einsum("shkv,shjv->shkj", outgoing, incoming, precision=HIGHEST)
    end_grad = jnp.concatenate([map_grad, outgoing], axis=-1)
    unused, tiles_back = jax.vjp(local_tiles, *vectors)
    vector_grads = tiles_back((local_grad, end_grad))
    unused, mix_back = jax.vjp(mixer_inputs, *mix_args)
    conv_own, edge_grad, head_in_grad, conv_taps_grad, params_grad = mix_back(vector_grads)
    edge_back = passed_along(edge_grad.astype(jnp.bfloat16), "seq", -1).astype(edge_grad.dtype)
    conv_total = jnp.concatenate(
        [conv_own[:, 0:edge_cut], conv_own[:, edge_cut:] + edge_back], axis=1
    )
    conv_grad = conv_total.reshape(row_count, conv_width).astype(jnp.bfloat16)
    head_grad = head_in_grad.reshape(row_count, -1).astype(jnp.bfloat16)
    gate_grad = gate_in_grad.astype(jnp.bfloat16)
    grad_qkv = jnp.einsum("nd,nc->dc", first_norm, conv_grad, preferred_element_type=jnp.float32)
    grad_head = jnp.einsum("nd,nc->dc", first_norm, head_grad, preferred_element_type=jnp.float32)
    grad_gate = jnp.einsum("nd,nc->dc", first_norm, gate_grad, preferred_element_type=jnp.float32)
    first_grad = jnp.einsum("nc,dc->nd", conv_grad, w_qkv, preferred_element_type=jnp.float32)
    first_grad = first_grad + jnp.einsum(
        "nc,dc->nd", head_grad, head_weight, preferred_element_type=jnp.float32
    )
    first_grad = first_grad + jnp.einsum(
        "nc,dc->nd", gate_grad, w_gate, preferred_element_type=jnp.float32
    )
    unused, first_back = jax.vjp(rms_scale, inputs, norm_gains[0])
    input_back, gain_one = first_back(first_grad)
    input_grad = (
        (middle_grad + input_back).astype(jnp.bfloat16).reshape(seq_count, block_len, model_width)
    )
    row_groups = (
        lax.psum_scatter(
            grad_qkv.astype(jnp.bfloat16), "dp", scatter_dimension=0, tiled=True
        ).astype(jnp.float32),
        lax.psum_scatter(
            grad_gate.astype(jnp.bfloat16), "dp", scatter_dimension=0, tiled=True
        ).astype(jnp.float32),
        lax.psum_scatter(
            grad_out.astype(jnp.bfloat16), "dp", scatter_dimension=0, tiled=True
        ).astype(jnp.float32),
        lax.psum_scatter(
            grad_in.astype(jnp.bfloat16), "dp", scatter_dimension=0, tiled=True
        ).astype(jnp.float32),
        lax.psum_scatter(
            grad_down.astype(jnp.bfloat16), "dp", scatter_dimension=0, tiled=True
        ).astype(jnp.float32),
    )
    weight_parts = (
        lax.psum_scatter(
            row_groups[0].astype(jnp.bfloat16), "seq", scatter_dimension=1, tiled=True
        ).astype(jnp.float32),
        lax.psum_scatter(
            row_groups[1].astype(jnp.bfloat16), "seq", scatter_dimension=1, tiled=True
        ).astype(jnp.float32),
        lax.psum_scatter(
            row_groups[2].astype(jnp.bfloat16), "seq", scatter_dimension=1, tiled=True
        ).astype(jnp.float32),
        lax.psum_scatter(
            row_groups[3].astype(jnp.bfloat16), "seq", scatter_dimension=1, tiled=True
        ).astype(jnp.float32),
        lax.psum_scatter(
            row_groups[4].astype(jnp.bfloat16), "seq", scatter_dimension=1, tiled=True
        ).astype(jnp.float32),
    )
    small_sums = lax.psum(
        (jnp.stack([gain_one, gain_two]), head_gain_grad, params_grad, grad_head, conv_taps_grad),
        ("dp", "seq"),
    )
    output = output.reshape(seq_count, block_len, model_width)
    return (
        output,
        input_grad,
        small_sums[0],
        small_sums[1],
        small_sums[2],
        weight_parts[0],
        weight_parts[1],
        small_sums[3],
        small_sums[4],
        weight_parts[2],
        weight_parts[3],
        weight_parts[4],
    )


MESH = pl.DeviceIdType.MESH
ANY = pl.BlockSpec(memory_space=pl.ANY)
IN_VMEM = pl.BlockSpec(memory_space=pltpu.VMEM)
B16 = jnp.bfloat16
F32 = jnp.float32
NN = ((1,), (0,))
NT = ((1,), (1,))
TN = ((0,), (0,))
HALO = 16


def low(v):
    return v.astype(jnp.bfloat16)


def mm(a, b, dims=NN):
    return lax.dot_general(low(a), low(b), (dims, ((), ())), preferred_element_type=jnp.float32)


def mmf(a, b, dims=NN):
    return lax.dot_general(
        a, b, (dims, ((), ())), precision=HIGHEST, preferred_element_type=jnp.float32
    )


def mm3(a, b, dims=NN):
    ah, bh = low(a), low(b)
    al, bl = low(a - ah.astype(jnp.float32)), low(b - bh.astype(jnp.float32))
    return mm(ah, bh, dims) + (mm(ah, bl, dims) + mm(al, bh, dims))


def sig(v):
    return 1.0 / (1.0 + jnp.exp(-v))


def soft_plus(v):
    tail = jnp.exp(-jnp.abs(v))
    series = tail * (1.0 - tail * (0.5 - tail * (1.0 / 3.0)))
    return jnp.maximum(v, 0.0) + jnp.where(tail < 1e-3, series, jnp.log(1.0 + tail))


def grid_masks():
    row = lax.broadcasted_iota(jnp.int32, (CH, CH), 0)
    col = lax.broadcasted_iota(jnp.int32, (CH, CH), 1)
    return row, col


def decay_parts(g, row, col):
    lower = (col <= row).astype(jnp.float32)
    cum = mmf(lower, g)
    cum_row = mmf(g, lower, ((0,), (1,)))
    within = col <= row
    decay = jnp.where(within, jnp.exp(jnp.where(within, cum - cum_row, 0.0)), 0.0)
    return cum, decay


def unit_inverse(attns, row, col):
    def same(width):
        return (row // width) == (col // width)

    eye = jnp.where(row == col, 1.0, 0.0)
    power = [jnp.where(same(64), -a, 0.0) for a in attns]
    inv = [eye + p for p in power]
    for level in range(5):
        power = [mm(p, p) for p in power]
        inv = [x + mm(x, p) for x, p in zip(inv, power)]
    for width in (128, 256):
        off = same(width) & jnp.logical_not(same(width // 2))
        part = [mm(jnp.where(off, a, 0.0), x) for a, x in zip(attns, inv)]
        inv = [x - mm(x, p) for x, p in zip(inv, part)]
    rest = [eye - x - mm3(a, x) for a, x in zip(attns, inv)]
    return [x + mm(x, r) for x, r in zip(inv, rest)]


def odd(t):
    return t % 2 if isinstance(t, int) else lax.rem(t, 2)


def tile(t, size=CH):
    return pl.ds(pl.multiple_of(t * size, size), size)


class Wires:
    def __init__(self, dp, seq, sems):
        self.dp, self.seq, self.sems, self.used = dp, seq, sems, 0
        self.i, self.s = lax.axis_index("dp"), lax.axis_index("seq")
        self.z, self.c = self.s // 2, lax.rem(self.s, 2)
        self.half, self.partner = self.z // 2, self.z + 1 - 2 * lax.rem(self.z, 2)
        self.inner = lax.rem((self.z + 1) // 2, 2)
        self.place = lax.rem(self.z, 2)
        self.beside = (self.i + 1 - 2 * lax.rem(self.i, 2), lax.rem(self.i + 2, 4))

    def take(self, count=1):
        start = self.used
        self.used += count
        return start

    def meet_all(self):
        barrier = pltpu.get_barrier_semaphore()
        for di in range(self.dp):
            for dj in range(self.seq):
                if di or dj:
                    pl.semaphore_signal(
                        barrier,
                        inc=1,
                        device_id=(lax.rem(self.i + di, self.dp), lax.rem(self.s + dj, self.seq)),
                        device_id_type=MESH,
                    )
        pl.semaphore_wait(barrier, self.dp * self.seq - 1)

    def remote(self, src, dst, send, recv, di, dj):
        return pltpu.make_async_remote_copy(
            src_ref=src,
            dst_ref=dst,
            send_sem=self.sems.at[send],
            recv_sem=self.sems.at[recv],
            device_id=(di, dj),
            device_id_type=MESH,
        )

    def local(self, src, dst, sem):
        return pltpu.make_async_copy(src, dst, self.sems.at[sem])

    def push(self, src, dst, send, recv, di, dj):
        here = (di == self.i) & (dj == self.s)
        away = self.remote(src, dst, send, recv, di, dj)

        @pl.when(here)
        def _():
            self.local(src, dst, recv).start()

        @pl.when(jnp.logical_not(here))
        def _():
            away.start()

        def sent():
            @pl.when(jnp.logical_not(here))
            def _():
                away.wait_send()

        return sent

    def arrived(self, dst, recv):
        pltpu.make_async_copy(dst, dst, self.sems.at[recv]).wait()

    def chip(self, z):
        return z * 2 + self.c

    def order(self, n):
        near = self.z + n * (1 - 2 * lax.rem(self.z, 2))
        return (1 - n // 2) * near + (n // 2) * (n + self.half * (3 - 2 * n))

    def sibling(self):
        return self.z * 2 + 1 - self.c


class LineGather:
    parts = 2

    def __init__(self, w, block_of):
        self.w, self.block_of = w, block_of
        n = 4 * self.parts
        self.send, self.recv = w.take(n), w.take(n)
        self.fsend, self.frecv = w.take(n), w.take(n)

    def piece(self, block, part):
        size = block.shape[0] // self.parts
        return block.at[part * size : part * size + size, :]

    def start(self, src):
        w = self.w
        dst = self.block_of(w.s)
        for part in range(self.parts):
            a, b = self.piece(src, part), self.piece(dst, part)
            slot = w.z * self.parts + part
            near, far = self.send + part, self.send + self.parts + part
            w.remote(a, b, near, self.recv + slot, w.i, w.chip(w.partner)).start()
            w.remote(a, b, far, self.recv + slot, w.i, w.chip(2 - w.half)).start()
        for part in range(self.parts):
            a, b = self.piece(src, part), self.piece(dst, part)
            slot = w.z * self.parts + part
            w.remote(a, b, self.fsend + slot, self.frecv + slot, w.i, w.sibling()).start()

    def arrive(self, t):
        w = self.w

        @pl.when(t != w.z)
        def _():
            block = self.block_of(w.chip(t))
            for part in range(self.parts):
                ref, slot = self.piece(block, part), t * self.parts + part
                w.arrived(ref, self.recv + slot)

                @pl.when((w.inner == 1) & (t // 2 != w.half))
                def _():
                    on = self.send + (2 + odd(t)) * self.parts + part
                    w.remote(ref, ref, on, self.recv + slot, w.i, w.chip(w.partner)).start()

                w.remote(ref, ref, self.fsend + slot, self.frecv + slot, w.i, w.sibling()).start()

    def other(self, t):
        w = self.w
        block = self.block_of(t * 2 + 1 - w.c)
        for part in range(self.parts):
            w.arrived(self.piece(block, part), self.frecv + t * self.parts + part)

    def finish(self):
        w = self.w
        block = self.block_of(w.s)
        for part in range(self.parts):
            ref = self.piece(block, part)
            for n in range(4):
                copy = w.remote(ref, ref, self.send + n * self.parts + part, self.recv, w.i, w.sibling())
                if n < 2:
                    copy.wait_send()
                else:
                    @pl.when(w.inner == 1)
                    def _():
                        copy.wait_send()

                w.remote(ref, ref, self.fsend + n * self.parts + part, self.recv, w.i, w.sibling()).wait_send()


class GroupGather:
    def __init__(self, w, part_of):
        self.w, self.part_of = w, part_of
        self.send, self.recv = w.take(4), w.take(4)

    def start(self, src):
        w = self.w
        w.local(src, self.part_of(w.i), self.recv).start()
        for d in (3, 1, 2):
            to = lax.rem(w.i + d, 4)
            w.remote(src, self.part_of(w.i), self.send + d, self.recv + d, to, w.s).start()

    def finish(self):
        w = self.w
        for d in range(4):
            w.arrived(self.part_of(lax.rem(w.i + 4 - d, 4)), self.recv + d)
        for d in range(1, 4):
            part = self.part_of(w.i)
            w.remote(part, part, self.send + d, self.recv + d, lax.rem(w.i + d, 4), w.s).wait_send()


class SquareGather:
    def __init__(self, w, part_of):
        self.w, self.part_of = w, part_of
        self.send, self.recv = w.take(4), w.take(5)

    def half(self, n, k):
        part = self.part_of(n)
        size = part.shape[0] // 2
        return part.at[size * k : size * k + size, :]

    def near(self, src):
        w = self.w
        part = self.part_of(w.i)
        return [w.remote(src, part, self.send + k, self.recv + k, w.beside[k], w.s) for k in range(2)]

    def far(self, k):
        w = self.w
        half = self.half(w.beside[k], k)
        return w.remote(half, half, self.send + 2 + k, self.recv + 2 + k, w.beside[1 - k], w.s)

    def start(self, src):
        w = self.w
        w.local(src, self.part_of(w.i), self.recv + 4).start()
        for copy in self.near(src):
            copy.start()

    def relay(self):
        w = self.w
        for k in range(2):
            w.arrived(self.part_of(w.beside[k]), self.recv + k)
            self.far(k).start()

    def finish(self):
        w = self.w
        w.arrived(self.part_of(w.i), self.recv + 4)
        for k in range(2):
            w.arrived(self.half(3 - w.i, k), self.recv + 2 + k)
        for copy in self.near(self.part_of(w.i)) + [self.far(0), self.far(1)]:
            copy.wait_send()


class LineScatter:
    def __init__(self, w, part, sib, chip, got):
        self.w, self.part, self.sib, self.chip, self.got = w, part, sib, chip, got
        self.ssend, self.srecv = w.take(4), w.take(4)
        self.send, self.recv = w.take(16), w.take(16)

    def swap(self, t):
        w = self.w
        src = self.part.at[pl.ds(pl.multiple_of(t * 256 + 128 * (1 - w.c), 128), 128), :]
        w.remote(src, self.sib.at[t], self.ssend + t, self.srecv + t, w.i, w.sibling()).start()

    def rows(self, ref, n, part):
        return ref.at[n, 32 * part : 32 * part + 32, :]

    def out(self, t, slot, chip, part):
        w = self.w
        src, dst = self.rows(self.chip, t, part), self.rows(self.got, slot, part)
        w.remote(src, dst, self.send + 4 * t + part, self.recv + 4 * slot + part, w.i, w.chip(chip)).start()

    def arrived(self, slot, part):
        half = self.rows(self.got, slot, part)
        self.w.arrived(half, self.recv + 4 * slot + part)
        return half[...].astype(jnp.float32)

    def pass_on(self, t):
        w = self.w
        w.arrived(self.sib.at[t], self.srecv + t)
        mine = self.part[pl.ds(pl.multiple_of(t * 256 + 128 * w.c, 128), 128), :]
        self.chip[t] = low(mine.astype(jnp.float32) + self.sib[t].astype(jnp.float32))

        @pl.when(t == w.partner)
        def _():
            for part in range(4):
                self.out(t, 0, t, part)

        @pl.when((t // 2 != w.half) & (w.inner == 0))
        def _():
            for part in range(4):
                self.out(t, 2 + odd(t), w.partner, part)

    def relay(self, t):
        w = self.w

        @pl.when((t // 2 != w.half) & (w.inner == 1))
        def _():
            for part in range(4):
                half = self.rows(self.chip, t, part)
                came = self.arrived(2 + odd(t), part)
                half[...] = low(half[...].astype(jnp.float32) + came)
                self.out(t, 1, t, part)

    def total(self):
        w = self.w
        came = [jnp.concatenate([self.arrived(slot, part) for part in range(4)], axis=0) for slot in range(2)]
        return self.chip[w.z].astype(jnp.float32) + came[0] + came[1]

    def finish(self):
        w = self.w
        for t in range(4):
            src = self.part.at[pl.ds(t * 256, 128), :]
            w.remote(src, self.sib.at[t], self.ssend + t, self.srecv + t, w.i, w.sibling()).wait_send()

            @pl.when(w.z != t)
            def _():
                for part in range(4):
                    half = self.rows(self.chip, t, part)
                    w.remote(half, half, self.send + 4 * t + part, self.recv, w.i, w.sibling()).wait_send()


class PairGather:
    def __init__(self, w, buffer):
        self.w, self.buffer = w, buffer
        self.send, self.recv = w.take(3), w.take(3)

    def block(self, q, c):
        return rows_of(self.buffer, 256 * q + 128 * c, 128)

    def copies(self):
        w = self.w
        mine, theirs = self.block(w.place, w.c), self.block(1 - w.place, w.c)
        send, recv = self.send, self.recv
        return (
            w.remote(mine, mine, send, recv, w.i, w.chip(w.partner)),
            w.remote(mine, mine, send + 1, recv + 1, w.i, w.sibling()),
            w.remote(theirs, theirs, send + 2, recv + 2, w.i, w.sibling()),
        )

    def start(self):
        near, core, unused = self.copies()
        near.start()
        core.start()

    def arrive(self):
        w = self.w
        w.arrived(self.block(1 - w.place, w.c), self.recv)
        self.copies()[2].start()

    def other(self, n):
        w = self.w
        q = w.place + n * (1 - 2 * w.place)
        w.arrived(self.block(q, 1 - w.c), self.recv + 1 + n)

    def finish(self):
        for copy in self.copies():
            copy.wait_send()


class PairScatter:
    def __init__(self, w, part, sib, chip, got):
        self.w, self.part, self.sib, self.chip, self.got = w, part, sib, chip, got
        self.ssend, self.srecv = w.take(2), w.take(2)
        self.send, self.recv = w.take(), w.take()

    def swapped(self, q):
        w = self.w
        src = rows_of(self.part, 256 * q + 128 * (1 - w.c), 128)
        return w.remote(src, self.sib.at[q], self.ssend + q, self.srecv + q, w.i, w.sibling())

    def away(self):
        w = self.w
        return w.remote(self.chip.at[1 - w.place], self.got, self.send, self.recv, w.i, w.chip(w.partner))

    def add(self, q):
        w = self.w
        w.arrived(self.sib.at[q], self.srecv + q)
        mine = rows_of(self.part, 256 * q + 128 * w.c, 128)[...]
        self.chip[q] = low(mine.astype(jnp.float32) + self.sib[q].astype(jnp.float32))

    def total(self):
        self.w.arrived(self.got, self.recv)
        return self.chip[self.w.place].astype(jnp.float32) + self.got[...].astype(jnp.float32)

    def finish(self):
        self.swapped(0).wait_send()
        self.swapped(1).wait_send()
        self.away().wait_send()


def cols(ref, start, size):
    return ref.at[:, pl.ds(pl.multiple_of(start, 128), size)]


def rows_of(ref, start, size):
    return ref.at[pl.ds(pl.multiple_of(start, 128), size), :]


class Box:
    pass


def fields(kind):
    return [(name, *value) for name, value in vars(kind).items() if name[0] != "_"]


class FrontKept:
    fn = ((1024, 1024), B16)
    ci = ((HALO + 1024, 512), B16)
    gi = ((1024, 256), F32)
    q = ((1024, 128), F32)
    k = ((1024, 128), F32)
    v = ((1024, 256), F32)
    ge = ((1024, 128), F32)
    mixed = ((1024, 256), F32)
    states = ((4, 128, 256), F32)
    tinv = ((1024, 256), B16)
    u = ((1024, 256), F32)
    wm = ((1024, 128), B16)
    normed = ((1024, 256), B16)
    middle = ((128, 1024), F32)
    sn = ((512, 1024), B16)
    cg = ((512, 1024), B16)
    w_qkv = ((1024, 512), B16)
    w_gate = ((1024, 256), B16)
    w_in = ((1536, 1024), B16)
    w_out = ((256, 1024), B16)
    w_down = ((768, 1024), B16)
class FrontScratch:
    x = ((1024, 1024), B16)
    qkv_p = ((256, 512), B16)
    in_p = ((704, 256), B16)
    out_p = ((256, 256), B16)
    down_p = ((704, 256), B16)
    taps32 = ((8, 4096), F32)
    own_cot = ((128, 1024), B16)
    qk = ((1024, 256), B16)
    cum = ((1024, 1), F32)
    part = ((1024, 1024), B16)
    sib = ((4, 128, 1024), B16)
    chip = ((4, 128, 1024), B16)
    got = ((4, 128, 1024), B16)


def start_weights(w, b):
    i, s = w.i, w.s
    qs, qr = w.take(4), w.take(3)
    lowhalf = s < 4
    b.qr = qr

    @pl.when(lowhalf)
    def _():
        for t in range(4):
            w.push(
                b.qkv.at[:, 128 * t : 128 * t + 128],
                cols(b.qkv_p, 128 * (s // 2), 128),
                qs + t,
                qr + s // 2,
                i,
                4 * lax.rem(s, 2) + t,
            )

    @pl.when(jnp.logical_not(lowhalf))
    def _():
        for t in range(2):
            w.push(b.qkv.at[:, 256 * t : 256 * t + 256], b.qkv_p.at[:, 256:512], qs + t, qr + 2, i, 2 * (s - 4) + t)

    def sent():
        @pl.when(lowhalf)
        def _():
            for t in range(4):
                @pl.when(4 * lax.rem(s, 2) + t != s)
                def _():
                    src = b.qkv.at[:, 128 * t : 128 * t + 128]
                    w.remote(src, b.qkv_p.at[:, 0:128], qs + t, qr, i, w.sibling()).wait_send()

        @pl.when(jnp.logical_not(lowhalf))
        def _():
            for t in range(2):
                @pl.when(2 * (s - 4) + t != s)
                def _():
                    src = b.qkv.at[:, 256 * t : 256 * t + 256]
                    w.remote(src, b.qkv_p.at[:, 256:512], qs + t, qr + 2, i, w.sibling()).wait_send()

    return sent


def start_out_weights(w, b):
    send, recv = w.take(2), w.take(2)
    odd = lax.rem(w.s, 2)
    waits = []
    for n in range(2):
        src = b.out.at[256 * n : 256 * n + 256, :]
        waits.append(w.push(src, cols(b.out_p, 128 * odd, 128), send + n, recv + odd, w.s // 2, 2 * w.i + n))

    def landed():
        for r in range(2):
            w.arrived(b.out_p.at[:, 128 * r : 128 * r + 128], recv + r)

    def sent():
        for wait in waits:
            wait()

    return landed, sent


def start_ffn_weights(w, b):
    i, s = w.i, w.s
    send, recv = w.take(3), w.take(3)
    own = lax.rem(s, 2)
    across = w.remote(b.ffn_in, b.in_p, send, recv, i, lax.rem(s + 4, 8))
    across.start()
    waits = [across.wait_send]
    for n in range(2):
        dst = cols(b.down_p, 128 * own, 128)
        waits.append(w.push(b.ffn_out, dst, send + 1 + n, recv + 1 + own, s // 2, i + 4 * n))

    def landed():
        w.arrived(b.in_p, recv)
        for r in range(2):
            w.arrived(b.down_p.at[:, 128 * r : 128 * r + 128], recv + 1 + r)

    def sent():
        for wait in waits:
            wait()

    return landed, sent


def valid_rows(b, w):
    place = w.s * 128 + lax.broadcasted_iota(jnp.int32, (128, 1), 0)
    return place < b.lengths[0]


def first_norm_tile(b, t):
    rows = tile(t)
    x = b.x[rows, :].astype(jnp.float32)
    inv = lax.rsqrt(jnp.mean(x * x, axis=-1, keepdims=True) + epsilon)
    b.fn[rows, :] = low(x * inv * b.gains[0:1, :])


def own_head(b, w):
    pm = b.params[...]
    lane = lax.broadcasted_iota(jnp.int32, pm.shape, 1)
    return jnp.sum(jnp.where(lane == w.s, pm, 0.0), axis=1, keepdims=True)


def own_taps(b, w, n):
    s = w.s
    return jnp.concatenate(
        [
            b.taps32[n : n + 1, pl.ds(pl.multiple_of(128 * s, 128), 128)],
            b.taps32[n : n + 1, pl.ds(pl.multiple_of(1024 + 128 * s, 128), 128)],
            b.taps32[n : n + 1, pl.ds(pl.multiple_of(2048 + 256 * s, 128), 256)],
        ],
        axis=1,
    )


def conv_sums(b, w, t):
    window = b.ci[pl.ds(pl.multiple_of(t * CH, CH), CH + HALO), :].astype(jnp.float32)
    total = None
    for n in range(KCONV):
        at = HALO - (KCONV - 1) + n
        term = window[at : at + CH] * own_taps(b, w, n)
        total = term if total is None else total + term
    return total


def project_tile(b, w, t):
    rows = tile(t)
    f = b.fn[rows, :]
    b.ci[pl.ds(pl.multiple_of(t * CH + HALO, HALO), CH), :] = low(mm(f, b.w_qkv[...]))
    b.gi[rows, :] = mm(f, b.w_gate[...])
    hi = mm(f, b.head_w[...], NT)
    lane = lax.broadcasted_iota(jnp.int32, hi.shape, 1)
    pm = own_head(b, w)
    shift = jnp.sum(jnp.where(lane == w.s, hi, 0.0), axis=1, keepdims=True) + pm[1:2, :]
    erase = jnp.sum(jnp.where(lane == w.s + 8, hi, 0.0), axis=1, keepdims=True) + pm[2:3, :]
    line = lax.broadcasted_iota(jnp.int32, (CH, 128), 1)
    decay = -jnp.exp(pm[0:1, :]) * soft_plus(shift)
    b.ge[rows, :] = jnp.where(line == 0, decay, jnp.where(line == 1, sig(erase), shift))


def vectors_tile(b, w, t):
    rows = tile(t)
    total = conv_sums(b, w, t)
    act = total * sig(total)
    qa, ka = act[:, 0:DK], act[:, DK : 2 * DK]
    b.q[rows, :] = qa * lax.rsqrt(jnp.sum(qa * qa, axis=-1, keepdims=True) + epsilon) * DK ** (-0.5)
    b.k[rows, :] = ka * lax.rsqrt(jnp.sum(ka * ka, axis=-1, keepdims=True) + epsilon)
    b.v[rows, :] = act[:, 2 * DK :]


def rec_local(b, w, ts):
    row, col = grid_masks()
    attns = []
    for t in ts:
        vectors_tile(b, w, t)
        rows = tile(t)
        k = b.k[rows, :]
        cum, decay = decay_parts(b.ge[rows, 0:1], row, col)
        b.cum[rows, :] = cum
        b.qk[rows, :] = low(mm(b.q[rows, :], k, NT) * decay)
        attns.append(jnp.where(col < row, b.ge[rows, 1:2] * mm(k, k, NT) * decay, 0.0))
    for t, inv in zip(ts, unit_inverse(attns, row, col)):
        rows = tile(t)
        e, t16 = b.ge[rows, 1:2], low(inv)
        b.tinv[rows, :] = t16
        b.wm[rows, :] = low(mm(t16, (e * jnp.exp(b.cum[rows, :])) * b.k[rows, :]))
        b.u[rows, :] = mm(t16, e * b.v[rows, :])


def rec_step(b, t, state):
    rows = tile(t)
    b.states[t] = state
    cum = b.cum[rows, :]
    last = cum[CH - 1 : CH, :]
    s16 = low(state)
    u = b.u[rows, :] - mm(b.wm[rows, :], s16)
    b.u[rows, :] = u
    u16 = low(u)
    mixed = jnp.exp(cum) * mm(b.q[rows, :], s16) + mm(b.qk[rows, :], u16)
    b.mixed[rows, :] = mixed
    nxt = jnp.exp(last) * state + mm(b.k[rows, :] * jnp.exp(last - cum), u16, TN)
    gate = b.gi[rows, :]
    scale = lax.rsqrt(jnp.mean(mixed * mixed, axis=-1, keepdims=True) + epsilon)
    normed = low(mixed * scale * b.head_gain[...] * (gate * sig(gate)))
    b.normed[rows, :] = normed
    b.part[rows, :] = low(mm(normed, b.w_out[...]))
    return nxt


def front_phase(b, w):
    s, i = w.s, w.i
    own_rows = lambda ref: (lambda n: rows_of(ref, 128 * n, 128))
    x_gather = LineGather(w, own_rows(b.x))
    cg_gather = PairGather(w, b.cg)
    sn_gather = PairGather(w, b.sn)
    qkv_gather = GroupGather(w, lambda n: rows_of(b.w_qkv, 256 * n, 256))
    gate_gather = GroupGather(w, lambda n: rows_of(b.w_gate, 256 * n, 256))
    half = s // 4

    def in_block(n, start, size):
        return b.w_in.at[pl.ds(pl.multiple_of(start, 128), size), pl.ds(pl.multiple_of(256 * n, 256), 256)]

    thirds = (256, 256, b.ffn_in.shape[0] - 512)

    def own_third(k):
        return GroupGather(w, lambda n: in_block(n, 768 * half + 256 * k, thirds[k]))

    in_gathers = [own_third(k) for k in range(3)]
    across_gather = SquareGather(w, lambda n: in_block(n, 768 * (1 - half), 704))

    def start_third(k):
        in_gathers[k].start(b.ffn_in.at[256 * k : 256 * k + thirds[k], :])

    out_gather = GroupGather(w, lambda n: cols(b.w_out, 256 * n, 256))
    down_gather = SquareGather(w, lambda n: b.w_down.at[0:704, pl.ds(pl.multiple_of(256 * n, 256), 256)])
    scatter = LineScatter(w, b.part, b.sib, b.chip, b.got)
    own_x, own_c = w.take(), w.take()

    for start in (704, 1472):
        b.w_in[start : start + 64, :] = jnp.zeros((64, 1024), B16)
    b.w_down[704:768, :] = jnp.zeros((64, 1024), B16)
    w.meet_all()
    qkv_sent = start_weights(w, b)
    out_landed, out_sent = start_out_weights(w, b)
    x_gather.start(b.tokens)
    gate_gather.start(b.gate)
    start_third(0)
    keep_x = w.local(b.tokens, rows_of(b.x, 128 * s, 128), own_x)
    keep_x.start()
    b.ci[0:HALO, :] = jnp.zeros((HALO, 512), B16)
    b.taps32[0:KCONV, :] = b.taps[...].astype(jnp.float32)
    cot = jnp.where(valid_rows(b, w), b.cot_v[...].astype(jnp.float32), 0.0)
    b.own_cot[...] = low(cot)
    rows_of(b.cg, 128 * lax.rem(s, 4), 128)[...] = low(cot)
    w.arrived(b.qkv_p.at[:, 0:128], b.qr)
    w.arrived(b.qkv_p.at[:, 128:256], b.qr + 1)
    w.arrived(b.qkv_p.at[:, 256:512], b.qr + 2)
    qkv_gather.start(b.qkv_p)
    out_landed()
    out_gather.start(b.out_p)
    keep_x.wait()

    def norm_loop(n, carry):
        t = w.order(n)
        x_gather.arrive(t)
        x_gather.other(t)
        first_norm_tile(b, t)
        return carry

    lax.fori_loop(0, 4, norm_loop, 0)
    ffn_landed, ffn_sent = start_ffn_weights(w, b)
    cg_gather.start()
    qkv_gather.finish()
    gate_gather.finish()
    start_third(1)
    start_third(2)

    def project_loop(t, carry):
        project_tile(b, w, t)
        return carry

    lax.fori_loop(0, 4, project_loop, 0)
    x_gather.finish()
    out_gather.finish()

    def pair_loop(pair, state):
        rec_local(b, w, (2 * pair, 2 * pair + 1))

        @pl.when(pair == 0)
        def _():
            ffn_landed()
            across_gather.start(b.in_p)
            down_gather.start(b.down_p)

        for k in range(2):
            t = 2 * pair + k
            state = rec_step(b, t, state)
            scatter.swap(t)
        scatter.pass_on(2 * pair)
        scatter.pass_on(2 * pair + 1)
        return state

    lax.fori_loop(0, 2, pair_loop, jnp.zeros((DK, DV), F32))

    scatter.relay(0)
    scatter.relay(1)
    scatter.relay(2)
    scatter.relay(3)
    across_gather.relay()
    down_gather.relay()

    def own_half(which):
        @pl.when(w.half == which)
        def _():
            middle = b.tokens_v[...].astype(jnp.float32) + scatter.total()
            b.middle[...] = middle
            inv = lax.rsqrt(jnp.mean(middle * middle, axis=-1, keepdims=True) + epsilon)
            rows_of(b.sn, 128 * lax.rem(s, 4), 128)[...] = low(middle * inv * b.gains[1:2, :])
            sn_gather.start()

    own_half(0)
    cg_gather.arrive()
    own_half(1)
    for third in in_gathers:
        third.finish()
    across_gather.finish()
    down_gather.finish()
    qkv_sent()
    out_sent()
    ffn_sent()
    scatter.finish()

    def finish():
        cg_gather.finish()
        sn_gather.finish()

    return sn_gather, cg_gather, finish


class SquareScatter:
    def __init__(self, w, out, got, step=None, size=None):
        self.w, self.out, self.got = w, out, got
        self.step = step or out.shape[1] // 2
        self.size = size or self.step
        self.send, self.recv = w.take(6), w.take(6)

    def half(self, ref, n, k):
        return ref.at[n, self.step * k : self.step * k + self.size, :]

    def copy(self, n, k):
        w = self.w
        to = k if n == 2 else n
        slot = 2 * n + k
        return w.remote(
            self.half(self.out, n, k), self.half(self.got, n, k), self.send + slot, self.recv + slot, w.beside[to], w.s
        )

    def start_far(self, piece_of):
        self.out[2] = low(piece_of(3 - self.w.i))
        self.copy(2, 0).start()
        self.copy(2, 1).start()

    def start_near(self, piece_of):
        for n in range(2):
            self.out[n] = low(piece_of(self.w.beside[n]))
            self.copy(n, n).start()

    def relay(self):
        w = self.w
        for k in range(2):
            half = self.half(self.out, 1 - k, k)
            w.arrived(self.half(self.got, 2, k), self.recv + 4 + k)
            half[...] = low(half[...].astype(jnp.float32) + self.half(self.got, 2, k)[...].astype(jnp.float32))
            self.copy(1 - k, k).start()

    def total(self, own, dst):
        w = self.w
        for k in range(2):
            start = self.step * k
            total = own[start : start + self.size]
            for n in range(2):
                half = self.half(self.got, n, k)
                w.arrived(half, self.recv + 2 * n + k)
                total = total + half[...].astype(jnp.float32)
            dst[start : start + self.size, :] = low(total)

    def finish(self):
        for n in range(3):
            for k in range(2):
                self.copy(n, k).wait_send()


def ffn_tile(b, t):
    rows = tile(t)
    sn, cg = b.sn[rows, :], b.cg[rows, :]
    half = b.w_in.shape[0] // 2
    both = mm(sn, b.w_in[...], NT)
    gate, up = both[:, 0:half], both[:, half:]
    open_ = sig(gate)
    act = gate * open_
    hidden = low(act * up)
    b.hid[rows, :] = hidden
    b.part4[rows, :] = low(mm(hidden, b.w_down[...]))
    hgrad = mm(cg, b.w_down[...], NT)
    both_grad = jnp.concatenate(
        [low(hgrad * up * (open_ * (1.0 + gate * (1.0 - open_)))), low(hgrad * act)], axis=1
    )
    b.gug[rows, :] = both_grad
    b.part[rows, :] = low(mm(both_grad, b.w_in[...]))


def norm_back(x, gain, grad):
    inv = lax.rsqrt(jnp.mean(x * x, axis=-1, keepdims=True) + epsilon)
    unit = x * inv
    dunit = grad * gain
    return inv * (dunit - unit * jnp.mean(dunit * unit, axis=-1, keepdims=True)), grad * unit


def mixer_out_back(b, t, head_gain_sum):
    rows = tile(t)
    ng = mm(b.agr[rows, :], b.w_out[...], NT)
    gate = b.gi[rows, :]
    open_ = sig(gate)
    act = gate * open_
    gain = b.head_gain[...]
    mixed = b.mixed[rows, :]
    inv = lax.rsqrt(jnp.mean(mixed * mixed, axis=-1, keepdims=True) + epsilon)
    unit = mixed * inv
    dunit = ng * act * gain
    b.do[rows, :] = inv * (dunit - unit * jnp.mean(dunit * unit, axis=-1, keepdims=True))
    nu = ng * unit
    b.gg[rows, :] = low(nu * gain * (open_ * (1.0 + gate * (1.0 - open_))))
    return head_gain_sum + jnp.sum(nu * act, axis=0, keepdims=True)


def rec_back_chain(b, t, ds1, row, col):
    rows = tile(t)
    do = low(b.do[rows, :])
    b.dstates[t] = ds1
    cum = b.cum[rows, :]
    last = cum[CH - 1 : CH, :]
    du = mm(b.qk[rows, :], do, TN) + mm(b.k[rows, :] * jnp.exp(last - cum), ds1)
    du16 = low(du)
    b.dr[rows, :] = mm(b.tinv[rows, :], du16, TN)
    return jnp.exp(last) * ds1 + mm(b.q[rows, :] * jnp.exp(cum), do, TN) - mm(b.wm[rows, :], du16, TN)


def rec_back_tile(b, t, row, col):
    rows = tile(t)
    q, k, v, e = b.q[rows, :], b.k[rows, :], b.v[rows, :], b.ge[rows, 1:2]
    s0, ds1, u, do, dr = b.states[t], b.dstates[t], b.u[rows, :], b.do[rows, :], b.dr[rows, :]
    cum, decay = decay_parts(b.ge[rows, 0:1], row, col)
    last = cum[CH - 1 : CH, :]
    gamma, shrink, remain = jnp.exp(last), jnp.exp(cum), jnp.exp(last - cum)
    gram = jnp.where(col < row, mm(k, k, NT) * decay, 0.0)
    qk = mm(q, k, NT) * decay
    dp = jnp.where(col <= row, mm3(do, u, NT), 0.0)
    da = jnp.where(col < row, -mm3(dr, u, NT), 0.0)
    dqk = low(dp * decay)
    dag = da * gram
    zed = dp * qk + e * dag
    dgram = low(e * da * decay)
    nk = mm3(dr, s0, NT)
    m = mm3(do, s0, NT)
    lm = mm3(u, ds1, NT)
    row_nk = jnp.sum(nk * k, axis=1, keepdims=True)
    dv = e * dr
    de = (
        jnp.sum(dr * v, axis=1, keepdims=True)
        - shrink * row_nk
        + jnp.sum(dag, axis=1, keepdims=True)
    )
    dq = mm(dqk, k) + shrink * m
    dk = mm(dqk, q, TN) + mm(dgram, k) + mm(dgram, k, TN) - (e * shrink) * nk + remain * lm
    dshrink = jnp.sum(m * q, axis=1, keepdims=True) - e * row_nk
    rdr = remain * jnp.sum(lm * k, axis=1, keepdims=True)
    ones = jnp.ones((CH, 1), jnp.float32)
    dcum = jnp.sum(zed, axis=1, keepdims=True) - mmf(zed, ones, TN) + shrink * dshrink - rdr
    dlast = jnp.sum(rdr, axis=0, keepdims=True) + gamma * jnp.sum(
        jnp.sum(s0 * ds1, axis=1, keepdims=True), axis=0, keepdims=True
    )
    lower = (col <= row).astype(jnp.float32)
    dg = mmf(lower, dcum, TN) + dlast
    return dq, dk, dv, dg, de


def unit_back(x, grad):
    inv = lax.rsqrt(jnp.sum(x * x, axis=-1, keepdims=True) + epsilon)
    unit = x * inv
    return inv * (grad - unit * jnp.sum(grad * unit, axis=-1, keepdims=True))


def mixer_back_tile(b, w, t, row, col, sums):
    rows = tile(t)
    dq, dk, dv, dg, de = rec_back_tile(b, t, row, col)
    total = conv_sums(b, w, t)
    open_ = sig(total)
    act = total * open_
    dact = jnp.concatenate(
        [unit_back(act[:, 0:DK], dq * DK ** (-0.5)), unit_back(act[:, DK : 2 * DK], dk), dv], axis=1
    )
    dcs = dact * (open_ * (1.0 + total * (1.0 - open_)))
    b.dcs[0:CH, :] = dcs
    window = b.ci[pl.ds(pl.multiple_of(t * CH, CH), CH + HALO), :].astype(jnp.float32)
    ahead = b.dcs[...]
    taps_sums, p0, p1, p2, gain_sum = sums
    dci = None
    new_taps = []
    for n in range(KCONV):
        at = HALO - (KCONV - 1) + n
        new_taps.append(taps_sums[n] + jnp.sum(dcs * window[at : at + CH], axis=0, keepdims=True))
        back = KCONV - 1 - n
        term = ahead[back : back + CH] * own_taps(b, w, n)
        dci = term if dci is None else dci + term
    b.dcs[CH : CH + HALO, :] = dcs[0:HALO]
    dci16 = low(dci)
    b.cgd[rows, :] = dci16
    lane = lax.broadcasted_iota(jnp.int32, (CH, 16), 1)
    pm = own_head(b, w)
    shift = b.ge[rows, 2:3]
    dshift = dg * (-jnp.exp(pm[0:1, :])) * sig(shift)
    e = b.ge[rows, 1:2]
    dlogit = de * e * (1.0 - e)
    hg = low(jnp.where(lane == w.s, dshift, jnp.where(lane == w.s + 8, dlogit, 0.0)))
    b.hg[rows, :] = hg
    fp = mm(dci16, b.w_qkv[...], NT) + mm(hg, b.head_w[...]) + mm(b.gg[rows, :], b.w_gate[...], NT)
    b.part[rows, :] = low(fp)
    gain_part = jnp.sum(fp * b.fn[rows, :].astype(jnp.float32), axis=0, keepdims=True)
    return (
        tuple(new_taps),
        p0 + jnp.sum(dg * b.ge[rows, 0:1], axis=0, keepdims=True),
        p1 + jnp.sum(dshift, axis=0, keepdims=True),
        p2 + jnp.sum(dlogit, axis=0, keepdims=True),
        gain_sum + gain_part,
    )


class LayerOut:
    output = ((128, 1024), B16)
    input_grad = ((128, 1024), B16)
    gains_grad = ((2, 1024), F32)
    head_gain_grad = ((1, 256), F32)
    params_grad = ((8, 128), F32)
    head_w_grad = ((16, 1024), F32)
    conv_grad = ((4, 4096), F32)
    qkv_back = ((256, 512), B16)
    gate_back = ((256, 256), B16)
    in_back = ((704, 256), B16)
    out_back = ((512, 128), B16)
    down_back = ((704, 128), B16)
class RestScratch:
    hid = ((512, 768), B16)
    gug = ((512, 1536), B16)
    part4 = ((512, 1024), B16)
    sib4 = ((2, 128, 1024), B16)
    chip4 = ((2, 128, 1024), B16)
    got4 = ((128, 1024), B16)
    sib6 = ((2, 128, 1024), B16)
    chip6 = ((2, 128, 1024), B16)
    got6 = ((128, 1024), B16)
    own_ag = ((128, 1024), B16)
    mgrad = ((128, 1024), F32)
    gg = ((1024, 256), B16)
    dstates = ((4, 128, 256), F32)
    dcs = ((CH + HALO, 512), F32)
    cgd = ((1024, 512), B16)
    hg = ((1024, 16), B16)
    in_out = ((3, 1536, 256), B16)
    in_got = ((3, 1536, 256), B16)
    down_out = ((3, 704, 256), B16)
    down_got = ((3, 704, 256), B16)
    out_out = ((3, 256, 256), B16)
    out_got = ((3, 256, 256), B16)
    qkv_out = ((3, 256, 512), B16)
    qkv_got = ((3, 256, 512), B16)
    gate_out = ((3, 256, 256), B16)
    gate_got = ((3, 256, 256), B16)
    in_sum = ((1536, 256), B16)
    in_other = ((704, 256), B16)
    down_sum = ((704, 256), B16)
    down_parts = ((2, 704, 128), B16)
    out_sum = ((256, 256), B16)
    qkv_sum = ((256, 512), B16)
    small = ((8, 1024), F32)
    small_got = ((4, 8, 1024), F32)
    small_sum = ((8, 1024), F32)
    small_all = ((8, 8, 1024), F32)


def grads_home(w, b):
    i, h = w.i, w.s
    send, recv = w.take(9), w.take(10)
    quarter, pair, half = lax.rem(h, 4), lax.rem(h, 2), h // 4

    def across():
        block = rows_of(b.in_sum, 768 * (1 - half), 704)
        return w.remote(block, b.in_other, send, recv + 4, i, lax.rem(h + 4, 8))

    down_to = [(b.down_sum.at[:, 128 * r : 128 * r + 128], quarter, 2 * i + r) for r in range(2)]

    def ffn():
        across().start()
        for r, (src, di, dj) in enumerate(down_to):
            w.push(src, b.down_parts.at[half], send + 2 + r, recv + 8 + half, di, dj)

    def ffn_done():
        across().wait_send()
        for r, (src, di, dj) in enumerate(down_to):
            @pl.when((di != i) | (dj != h))
            def _():
                w.remote(src, src, send + 2 + r, recv, i, w.sibling()).wait_send()

        w.arrived(b.in_other, recv + 4)
        mine = rows_of(b.in_sum, 768 * half, 704)[...]
        b.in_back[...] = low(mine.astype(jnp.float32) + b.in_other[...].astype(jnp.float32))
        for r in range(2):
            w.arrived(b.down_parts.at[r], recv + 8 + r)
        b.down_back[...] = low(b.down_parts[0].astype(jnp.float32) + b.down_parts[1].astype(jnp.float32))

    def mixer():
        to = (
            (b.qkv_sum.at[:, 0:128], cols(b.qkv_back, 128 * quarter, 128), recv + quarter, half),
            (b.qkv_sum.at[:, 128:256], cols(b.qkv_back, 128 * quarter, 128), recv + quarter, 2 + half),
            (b.qkv_sum.at[:, 256:512], cols(b.qkv_back, 256 * pair, 256), recv + pair, 4 + h // 2),
        )
        return [w.push(src, dst, send + 4 + n, sem, i, dj) for n, (src, dst, sem, dj) in enumerate(to)]

    def mixer_out():
        waits = []
        for r in range(2):
            src = b.out_sum.at[:, 128 * r : 128 * r + 128]
            dst = rows_of(b.out_back, 256 * pair, 256)
            waits.append(w.push(src, dst, send + 7 + r, recv + 6 + pair, h // 2, 2 * i + r))
        return waits

    def landed():
        @pl.when(h < 4)
        def _():
            for t in range(4):
                w.arrived(b.qkv_back.at[:, 128 * t : 128 * t + 128], recv + t)

        @pl.when(h >= 4)
        def _():
            for t in range(2):
                w.arrived(b.qkv_back.at[:, 256 * t : 256 * t + 256], recv + t)

        for r in range(2):
            w.arrived(b.out_back.at[256 * r : 256 * r + 256, :], recv + 6 + r)

    return ffn, ffn_done, mixer, mixer_out, landed


def small_sums(w, b, send, recv, send2, recv2):
    copies = []
    for d in range(1, 4):
        copy = w.remote(b.small, b.small_got.at[d], send + d, recv + d, lax.rem(w.i + d, 4), w.s)
        copy.start()
        copies.append(copy)

    def middle():
        total = b.small[...]
        for d in range(1, 4):
            w.arrived(b.small_got.at[d], recv + d)
            total = total + b.small_got[d]
        b.small_sum[...] = total
        b.small_all[w.s] = total
        for d in range(1, 8):
            copy = w.remote(b.small_sum, b.small_all.at[w.s], send2 + d, recv2 + d, w.i, lax.rem(w.s + d, 8))
            copy.start()
            copies.append(copy)

    def end():
        for d in range(1, 8):
            w.arrived(b.small_all.at[lax.rem(w.s + 8 - d, 8)], recv2 + d)
        for copy in copies:
            copy.wait_send()
        gains = b.small_all[0, 0:2, :]
        head_gain = b.small_all[0, 2:3, 0:256]
        for n in range(1, 8):
            gains = gains + b.small_all[n, 0:2, :]
            head_gain = head_gain + b.small_all[n, 2:3, 0:256]
        b.gains_grad[...] = gains
        b.head_gain_grad[...] = head_gain
        for n in range(8):
            b.params_grad[n : n + 1, :] = b.small_all[n, 3:4, 0:128]
            b.head_w_grad[n : n + 1, :] = b.small_all[n, 4:5, :]
            b.head_w_grad[8 + n : 9 + n, :] = b.small_all[n, 5:6, :]
            for k in range(KCONV):
                line = b.small_all[n, 6 + k // 2 : 7 + k // 2, 512 * (k % 2) : 512 * (k % 2) + 512]
                b.conv_grad[k : k + 1, 128 * n : 128 * n + 128] = line[:, 0:128]
                b.conv_grad[k : k + 1, 1024 + 128 * n : 1152 + 128 * n] = line[:, 128:256]
                b.conv_grad[k : k + 1, 2048 + 256 * n : 2304 + 256 * n] = line[:, 256:512]

    return middle, end


def rest_phase(b, w, sn_gather, cg_gather, front_finish):
    s = w.s
    half_rows = lambda ref: (lambda n: rows_of(ref, 128 * n, 128))
    ag_gather = LineGather(w, half_rows(b.agr))
    scatter4 = PairScatter(w, b.part4, b.sib4, b.chip4, b.got4)
    scatter6 = PairScatter(w, b.part, b.sib6, b.chip6, b.got6)
    scatter8 = LineScatter(w, b.part, b.sib, b.chip, b.got)
    in_sum = SquareScatter(w, b.in_out, b.in_got, 768, 704)
    down_sum = SquareScatter(w, b.down_out, b.down_got)
    out_sum = SquareScatter(w, b.out_out, b.out_got)
    qkv_sum = SquareScatter(w, b.qkv_out, b.qkv_got)
    gate_sum = SquareScatter(w, b.gate_out, b.gate_got)
    home_ffn, home_ffn_done, home_qkv, home_out, home_landed = grads_home(w, b)
    sm = (w.take(4), w.take(4), w.take(8), w.take(8))

    def ffn_loop(n, carry):
        @pl.when(n == 1)
        def _():
            sn_gather.arrive()

        sn_gather.other(n)
        cg_gather.other(n)
        q = w.place + n * (1 - 2 * w.place)
        ffn_tile(b, q)
        scatter6.swapped(q).start()
        scatter4.swapped(q).start()
        return carry

    lax.fori_loop(0, 2, ffn_loop, 0)
    scatter6.add(1 - w.place)
    scatter6.away().start()
    scatter6.add(w.place)

    def in_piece(n):
        return mm(b.gug[...], cols(b.sn, 256 * n, 256)[...], TN)

    def down_piece(n):
        return mm(b.hid[...], cols(b.cg, 256 * n, 256)[...], TN)[0:704]

    in_sum.start_far(in_piece)
    down_sum.start_far(down_piece)
    second_grad = scatter6.total()
    back, share = norm_back(b.middle[...], b.gains[1:2, :], second_grad)
    b.small[1:2, :] = jnp.sum(share, axis=0, keepdims=True)
    mgrad = b.own_cot[...].astype(jnp.float32) + back
    b.mgrad[...] = mgrad
    own = low(mgrad)
    b.own_ag[...] = own
    rows_of(b.agr, 128 * s, 128)[...] = own
    ag_gather.start(b.own_ag)
    in_sum.start_near(in_piece)
    down_sum.start_near(down_piece)
    scatter4.add(1 - w.place)
    scatter4.away().start()
    scatter4.add(w.place)
    row, col = grid_masks()

    def out_loop(n, head_gain_sum):
        t = w.order(n)
        ag_gather.arrive(t)
        ag_gather.other(t)
        out = mixer_out_back(b, t, head_gain_sum)

        @pl.when(n == 2)
        def _():
            in_sum.relay()
            down_sum.relay()

        return out

    head_gain_sum = lax.fori_loop(0, 4, out_loop, jnp.zeros((1, DV), F32))
    scatter6.finish()
    def out_piece(n):
        return mm(b.normed[...], cols(b.agr, 256 * n, 256)[...], TN)


    def gate_piece(n):
        return mm(cols(b.fn, 256 * n, 256)[...], b.gg[...], TN)

    out_sum.start_far(out_piece)
    gate_sum.start_far(gate_piece)
    out_sum.start_near(out_piece)
    gate_sum.start_near(gate_piece)

    def chain_loop(n, ds1):
        return rec_back_chain(b, 3 - n, ds1, row, col)

    lax.fori_loop(0, 4, chain_loop, jnp.zeros((DK, DV), F32))
    in_sum.total(in_piece(w.i), b.in_sum)
    down_sum.total(down_piece(w.i), b.down_sum)
    home_ffn()
    b.dcs[CH : CH + HALO, :] = jnp.zeros((HALO, 512), F32)

    def back_loop(n, sums):
        t = 3 - n
        sums = mixer_back_tile(b, w, t, row, col, sums)
        scatter8.swap(t)

        @pl.when(n == 1)
        def _():
            out_sum.relay()
            gate_sum.relay()

        @pl.when(n > 0)
        def _():
            scatter8.pass_on(t + 1)

        @pl.when(n > 1)
        def _():
            scatter8.relay(t + 2)

        return sums

    one = jnp.zeros((1, 1), F32)
    taps_sums, p0, p1, p2, gain_sum = lax.fori_loop(
        0, 4, back_loop, (tuple(jnp.zeros((1, 512), F32) for n in range(KCONV)), one, one, one, jnp.zeros((1, 1024), F32))
    )
    scatter8.pass_on(0)
    scatter8.relay(1)

    def qkv_piece(n):
        return mm(cols(b.fn, 256 * n, 256)[...], b.cgd[...], TN)

    qkv_sum.start_far(qkv_piece)
    qkv_sum.start_near(qkv_piece)
    scatter8.relay(0)
    b.small[0:1, :] = gain_sum / b.gains[0:1, :]
    b.small[2:3, :] = jnp.concatenate([head_gain_sum, jnp.zeros((1, 1024 - DV), F32)], axis=1)
    lane = lax.broadcasted_iota(jnp.int32, (1, 1024), 1)
    b.small[3:4, :] = jnp.where(lane == 0, p0, jnp.where(lane == 1, p1, jnp.where(lane == 2, p2, 0.0)))
    head_rows = mm(b.hg[...], b.fn[...], TN)
    line = lax.broadcasted_iota(jnp.int32, head_rows.shape, 0)
    b.small[4:5, :] = jnp.sum(jnp.where(line == s, head_rows, 0.0), axis=0, keepdims=True)
    b.small[5:6, :] = jnp.sum(jnp.where(line == s + 8, head_rows, 0.0), axis=0, keepdims=True)
    b.small[6:7, :] = jnp.concatenate([taps_sums[0], taps_sums[1]], axis=1)
    b.small[7:8, :] = jnp.concatenate([taps_sums[2], taps_sums[3]], axis=1)
    small_middle, small_end = small_sums(w, b, *sm)
    out_sum.total(out_piece(w.i), b.out_sum)
    waits = home_out()
    gate_sum.total(gate_piece(w.i), b.gate_back)
    qkv_sum.relay()
    small_middle()
    b.output[...] = low(jnp.where(valid_rows(b, w), b.middle[...] + scatter4.total(), 0.0))
    qkv_sum.total(qkv_piece(w.i), b.qkv_sum)
    waits = waits + home_qkv()
    first_grad = scatter8.total()
    back, unused_share = norm_back(b.tokens_v[...].astype(jnp.float32), b.gains[0:1, :], first_grad)
    b.input_grad[...] = low(b.mgrad[...] + back)
    home_ffn_done()
    small_end()
    home_landed()
    for wait in waits:
        wait()
    for part in (in_sum, down_sum, out_sum, qkv_sum, gate_sum):
        part.finish()
    scatter4.finish()
    scatter8.finish()
    ag_gather.finish()
    front_finish()


def layer_kernel(dp, seq, *refs):
    b = Box()
    (
        b.tokens,
        b.qkv,
        b.gate,
        b.ffn_in,
        b.out,
        b.ffn_out,
        b.gains,
        b.head_gain,
        b.params,
        b.head_w,
        b.taps,
        b.tokens_v,
        b.cot_v,
        b.lengths,
    ) = refs[:14]
    kinds = fields(LayerOut) + fields(FrontKept) + fields(FrontScratch) + fields(RestScratch)
    for (name, shape, kind), ref in zip(kinds, refs[14:]):
        setattr(b, name, ref)
    b.do, b.dr, b.agr = b.mixed, b.gi, b.x
    w = Wires(dp, seq, refs[-1])
    rest_phase(b, w, *front_phase(b, w))


def layer(dp, seq, *arrays):
    outs = pl.pallas_call(
        functools.partial(layer_kernel, dp, seq),
        out_shape=tuple(jax.ShapeDtypeStruct(shape, kind) for _, shape, kind in fields(LayerOut)),
        in_specs=[ANY] * 6 + [IN_VMEM] * 7 + [pl.BlockSpec(memory_space=pltpu.SMEM)],
        out_specs=(IN_VMEM,) * len(fields(LayerOut)),
        scratch_shapes=[
            pltpu.VMEM(shape, kind)
            for _, shape, kind in fields(FrontKept) + fields(FrontScratch) + fields(RestScratch)
        ]
        + [pltpu.SemaphoreType.DMA((500,))],
        compiler_params=pltpu.CompilerParams(collective_id=0, has_side_effects=True, vmem_limit_bytes=62 << 20),
        name="layer",
    )(*arrays)
    made = Box()
    for (name, shape, kind), out in zip(fields(LayerOut), outs):
        setattr(made, name, out)
    return made


class FinalOut:
    output = ((128, 1024), B16)
    input_grad = ((128, 1024), B16)
    gains_grad = ((2, 1024), F32)
    head_gain_grad = ((1, 256), F32)
    params_grad = ((3, 8), F32)
    head_w_grad = ((16, 1024), F32)
    conv_grad = ((4, 4096), F32)
    qkv_back = ((256, 512), F32)
    gate_back = ((256, 256), F32)
    in_back = ((704, 256), F32)
    out_back = ((512, 128), F32)
    down_back = ((704, 128), F32)


def final_kernel(*refs):
    count = len(fields(FinalOut))
    srcs, outs, held, sems = refs[:count], refs[count : 2 * count], refs[2 * count : -1], refs[-1]
    copies = [pltpu.make_async_copy(src, buf, sems.at[n]) for n, (src, buf) in enumerate(zip(srcs, held))]
    for copy in copies:
        copy.start()
    for n, ((name, shape, kind), copy, buf, out) in enumerate(zip(fields(FinalOut), copies, held, outs)):
        copy.wait()
        if n == 4:
            out[...] = jnp.transpose(buf[...])[0:3, :]
        else:
            out[...] = buf[0 : shape[0], :].astype(kind)


def final(made):
    names = fields(FinalOut)
    arrays = [getattr(made, name) for name, _, _ in names]
    outs = pl.pallas_call(
        final_kernel,
        out_shape=tuple(jax.ShapeDtypeStruct(shape, kind) for _, shape, kind in names),
        in_specs=[ANY] * len(names),
        out_specs=(IN_VMEM,) * len(names),
        scratch_shapes=[pltpu.VMEM(array.shape, array.dtype) for array in arrays]
        + [pltpu.SemaphoreType.DMA((len(names),))],
        compiler_params=pltpu.CompilerParams(vmem_limit_bytes=62 << 20),
        name="final",
    )(*arrays)
    done = Box()
    for (name, shape, kind), out in zip(names, outs):
        setattr(done, name, out)
    return done


def fast_body(
    dp,
    seq,
    tokens,
    lengths,
    cotangent,
    norm_gains,
    head_gain,
    head_params,
    qkv_weight,
    gate_weight,
    head_weight,
    conv_weight,
    out_weight,
    ffn_in,
    ffn_out,
):
    made = layer(
        dp,
        seq,
        tokens[0],
        qkv_weight,
        gate_weight,
        ffn_in.T,
        out_weight,
        ffn_out,
        norm_gains,
        head_gain[None],
        head_params,
        head_weight.T,
        conv_weight.T,
        tokens[0],
        cotangent[0],
        lengths,
    )
    r = final(made)
    return (
        r.output[None],
        r.input_grad[None],
        r.gains_grad,
        r.head_gain_grad[0],
        r.params_grad,
        r.qkv_back,
        r.gate_back,
        r.head_w_grad.T,
        r.conv_grad.T,
        r.out_back,
        r.in_back.T,
        r.down_back,
    )


def choose_body(dp, seq):
    def chosen(*arrays):
        tokens, head_params = arrays[0], arrays[5]
        if (dp, seq) == (4, 8) and tokens.shape[0] == 1 and head_params.shape[1] == seq:
            return fast_body(dp, seq, *arrays)
        return general_body(*arrays)

    return chosen


def solution(mesh):
    dp, seq = mesh.shape["dp"], mesh.shape["seq"]
    placed = (
        P("dp", "seq", None),
        P("dp"),
        P("dp", "seq", None),
        P(),
        P(),
        P(),
        P("dp", "seq"),
        P("dp", "seq"),
        P(),
        P(),
        P("dp", "seq"),
        P("dp", "seq"),
        P("dp", "seq"),
    )
    return jax.shard_map(
        choose_body(dp, seq),
        mesh=mesh,
        in_specs=placed,
        out_specs=(
            P("dp", "seq", None),
            P("dp", "seq", None),
            P(),
            P(),
            P(),
            P("dp", "seq"),
            P("dp", "seq"),
            P(),
            P(),
            P("dp", "seq"),
            P("dp", "seq"),
            P("dp", "seq"),
        ),
        check_vma=False,
    )
```
